32 devices in a mesh: seq: 8 (over z, y), fsdp: 4 (over x, core).
Axes of the slice: x: 2, y: 2, z: 4, core: 2. Of those that a mesh axis runs over, the one named last changes fastest.
Arguments:
- hidden_in: bfloat16 [4, 1024, 2048], P('fsdp', 'seq'), may hold values from -18 to 18
- ln1_gain: bfloat16 [2048], P(('seq', 'fsdp')), may hold values from 0.5 to 1.5
- ln1_bias: bfloat16 [2048], P(('seq', 'fsdp')), may hold values from -1.1953125 to 1.1953125
- qkv_weight: bfloat16 [2048, 6144], P(('seq', 'fsdp')), may hold values from -0.125 to 0.125
- qkv_bias: bfloat16 [3, 2048], P(None, ('seq', 'fsdp')), may hold values from -3 to 3
- out_weight: bfloat16 [2048, 2048], P(('seq', 'fsdp')), may hold values from -3 to 3
- ln2_gain: bfloat16 [2048], P(('seq', 'fsdp')), may hold values from 0.5 to 1.5
- ln2_bias: bfloat16 [2048], P(('seq', 'fsdp')), may hold values from -1.1953125 to 1.1953125
- gate_weight: bfloat16 [2048, 5632], P(('seq', 'fsdp')), may hold values from -0.125 to 0.125
- up_weight: bfloat16 [2048, 5632], P(('seq', 'fsdp')), may hold values from -0.125 to 0.125
- down_weight: bfloat16 [5632, 2048], P(('seq', 'fsdp')), may hold values from -0.078125 to 0.078125
- seq_lengths: int32 [4, 3], P('fsdp'), may hold values from 1 to 512, 640 in all within a row
- deal_order: int32 [4, 1024], P('fsdp'), may hold values from 0 to 1023, each once within a row
- out_grad: bfloat16 [4, 1024, 2048], P('fsdp', 'seq'), may hold values from -6 to 6
Outputs:
- layer_out: bfloat16 [4, 1024, 2048], P('fsdp', 'seq')
- input_grad: float32 [4, 1024, 2048], P('fsdp', 'seq')
- ln1_gain_grad: float32 [2048], P(('seq', 'fsdp'))
- ln1_bias_grad: float32 [2048], P(('seq', 'fsdp'))
- qkv_weight_grad: float32 [2048, 6144], P(('seq', 'fsdp'))
- qkv_bias_grad: float32 [3, 2048], P(None, ('seq', 'fsdp'))
- out_weight_grad: float32 [2048, 2048], P(('seq', 'fsdp'))
- ln2_gain_grad: float32 [2048], P(('seq', 'fsdp'))
- ln2_bias_grad: float32 [2048], P(('seq', 'fsdp'))
- gate_weight_grad: float32 [2048, 5632], P(('seq', 'fsdp'))
- up_weight_grad: float32 [2048, 5632], P(('seq', 'fsdp'))
- down_weight_grad: float32 [5632, 2048], P(('seq', 'fsdp'))
- branch_rms: float32 [3], replicated
The draws below stay inside these ranges and needn't reach their ends.
Inputs may be any that keep to these rules, and one draw needn't show every extreme that they name: `seq_lengths`: each group's lengths sum to 640, and its longest is exactly 512. `deal_order`: each group's row is a permutation of its positions.
All inputs are finite; a program needn't handle non-finite values.
Results may differ from the reference program's by a relative error of at most 0.00705.
The reference program's roundings to bfloat16 on the way count: a program that leaves them out, or rounds other values in their place, can miss the bound.
Values may be sent and summed in bfloat16 or wider, within the bound.
A program may use at most 384 MiB of HBM per device.

```python
import math
import jax
import jax.numpy as jnp
import numpy as np
from jax import lax

D = 2048
HEADS = 32
HEAD_DIM = 64
ROT = 16
FF = 5632
SEQS = 3
GROUPS = 4
GROUP_ROWS = 1024
VALID = 640
MOST = 512
BLOCK = 512


def draw_hidden_in(key, part):
    total = GROUPS * GROUP_ROWS
    index = jnp.arange(total, dtype=jnp.float32).reshape(GROUPS, GROUP_ROWS, 1)
    rising = jnp.exp(jnp.log(3.0) * index / max(total - 1, 1))
    base = jnp.clip(jax.random.normal(key, (GROUPS, GROUP_ROWS, D), jnp.float32), -6.0, 6.0)
    values = base * rising
    return values.astype(jnp.bfloat16)


def levels(stream_key, dims, split, low, high):
    factor_of, own = 1.0, jax.random.fold_in(stream_key, 6)
    for axis_at, shards_of in split:
        steps = jnp.exp(jax.random.uniform(jax.random.fold_in(own, axis_at), (shards_of,), jnp.float32, low / len(split), high / len(split)))
        factor_of = factor_of * jnp.repeat(steps, dims[axis_at] // shards_of).reshape([-1 if axis == axis_at else 1 for axis in range(len(dims))])
    return factor_of


def length_profile(number_of, total, reach, lean):
    loads = [(1 << 20) // math.isqrt(rank ** lean) + 1 for rank in range(2, number_of + 1)]
    surplus, given = total - reach - (number_of - 1), [1] * (number_of - 1)
    while surplus > 0:
        free = [i for i in range(number_of - 1) if given[i] < reach]
        pool, left = sum([loads[i] for i in free]), surplus
        for i in free:
            more = min(reach - given[i], max(1, left * loads[i] // pool), surplus)
            given[i] = given[i] + more
            surplus = surplus - more
    return np.array([reach] + given)


def uneven(key, count, total, bound, slope):
    if count == 2:
        one = jax.random.randint(key, (), max(1, total - bound), min(bound, total - 1) + 1)
        return jnp.stack([one, total - one])
    sizes = jnp.asarray(length_profile(count, total, bound, slope), jnp.int32)
    couples = (count - 1) // 2
    donor, taker = sizes[1:1 + 2 * couples:2], sizes[2:2 + 2 * couples:2]
    slack = jnp.minimum(donor - 1, bound - taker)
    moved = jax.random.randint(jax.random.fold_in(key, 1), (couples,), 0, 1 << 20) % (slack + 1)
    sizes = sizes.at[1:1 + 2 * couples:2].set(donor - moved).at[2:2 + 2 * couples:2].set(taker + moved)
    return sizes[jax.random.permutation(jax.random.fold_in(key, 2), count)]


def scatter_about(key, dims, width, most, cuts=(), held_as=jnp.bfloat16):
    drawn = jax.random.normal(key, dims, jnp.float32) * width
    if len(cuts) > 0:
        drawn = levels(key, dims, cuts, -0.22, 0.18) * drawn
    return jnp.clip(drawn, min=-most, max=most).astype(held_as)


def setup_inputs(seed: int = 0) -> dict:
    splits = jax.random.split(jax.random.key(seed), 15)
    hidden_in = draw_hidden_in(jax.random.fold_in(splits[14], 71), 0)
    ln1_gain = jnp.clip(1.0 + 0.1 * jax.random.normal(splits[1], (D,), jnp.float32), 0.5, 1.5).astype(jnp.bfloat16)
    ln1_bias = scatter_about(splits[2], (D,), 0.2, 1.1953125, ((0, 32),))
    qkv_weight = scatter_about(splits[3], (D, 3 * D), D ** -0.5, 0.125, ((0, 32),))
    qkv_bias = scatter_about(splits[4], (3, D), 0.5, 3.0, ((1, 32),))
    out_weight = scatter_about(splits[5], (D, D), (max(D // 512, 1)) ** -0.5, 3.0, ((0, 32),))
    ln2_gain = jnp.clip(1.0 + 0.1 * jax.random.normal(splits[6], (D,), jnp.float32), 0.5, 1.5).astype(jnp.bfloat16)
    ln2_bias = scatter_about(splits[7], (D,), 0.2, 1.1953125, ((0, 32),))
    gate_weight = scatter_about(splits[8], (D, FF), D ** -0.5, 0.125, ((0, 32),))
    up_weight = scatter_about(splits[9], (D, FF), D ** -0.5, 0.125, ((0, 32),))
    down_weight = scatter_about(splits[10], (FF, D), FF ** -0.5, 0.078125, ((0, 32),))
    seq_lengths = jax.vmap(lambda own: uneven(own, SEQS, VALID, MOST, 2))(jax.random.split(splits[11], GROUPS)).reshape((GROUPS, SEQS)).astype(jnp.int32)
    deal_order = jax.vmap(lambda own: jax.random.permutation(own, GROUP_ROWS))(jax.random.split(splits[12], GROUPS)).reshape((GROUPS, GROUP_ROWS)).astype(jnp.int32)
    out_grad = scatter_about(splits[13], (GROUPS, GROUP_ROWS, D), 1.0, 6.0, ((0, 4), (1, 8)))
    return dict(hidden_in=hidden_in, ln1_gain=ln1_gain, ln1_bias=ln1_bias, qkv_weight=qkv_weight, qkv_bias=qkv_bias, out_weight=out_weight, ln2_gain=ln2_gain, ln2_bias=ln2_bias, gate_weight=gate_weight, up_weight=up_weight, down_weight=down_weight, seq_lengths=seq_lengths, deal_order=deal_order, out_grad=out_grad)


EPS = 1e-05

@jax.custom_vjp
def low(v):
    return lax.optimization_barrier(v.astype(jnp.bfloat16)).astype(jnp.float32)

@jax.custom_vjp
def low_back(v):
    return v

def low_keep(v):
    return (low(v), None)

def low_pass(kept, grad):
    return (grad,)

def back_keep(v):
    return (v, None)

def back_low(kept, grad):
    return (low(grad),)
low.defvjp(low_keep, low_pass)
low_back.defvjp(back_keep, back_low)

def matmul(left, right):
    return jnp.dot(left, right, precision=lax.Precision.HIGHEST, preferred_element_type=jnp.float32)

def normalize(values):
    center = values - lax.optimization_barrier(jnp.mean(values, -1, keepdims=True))
    spread = lax.optimization_barrier(jnp.mean(center * center, -1, keepdims=True))
    return center * lax.rsqrt(spread + EPS)

def segment_of(pos, lengths):
    nseg = lengths.shape[0]
    ends = jnp.cumsum(lengths).astype(jnp.int32)
    seg = lax.optimization_barrier(jnp.sum((pos[:, None] >= ends[None, :]).astype(jnp.int32), 1)).astype(jnp.int32)
    starts = jnp.concatenate([jnp.zeros((1,), jnp.int32), ends[:-1]])
    start = lax.optimization_barrier(jnp.sum(jnp.where(seg[:, None] == jnp.arange(nseg, dtype=jnp.int32)[None, :], starts[None, :], 0), 1)).astype(jnp.int32)
    start = jnp.where(seg < nseg, start, pos)
    return (seg, start)

def rotate(values, rel, sign):
    count = values.shape[0]
    view = values.reshape(count, -1, HEAD_DIM)
    half = ROT // 2
    freq = 10000.0 ** (-2.0 * jnp.arange(half, dtype=jnp.float32) / ROT)
    angle = rel[:, None] * freq[None, :]
    cosine = jnp.cos(angle)[:, None, :]
    sine = jnp.sin(angle)[:, None, :]
    first = view[..., :half]
    second = view[..., half:ROT]
    turned = jnp.concatenate([first * cosine - sign * second * sine, second * cosine + sign * first * sine, view[..., ROT:]], -1)
    return turned.reshape(count, -1)

def group_attention(packed):
    query, keyset, valueset, pos, seg = packed
    scale = HEAD_DIM ** (-0.5)

    def one_block(index):
        first = index * BLOCK
        qblock = lax.dynamic_slice_in_dim(query, first, BLOCK)
        qpos = lax.dynamic_slice_in_dim(pos, first, BLOCK)
        qseg = lax.dynamic_slice_in_dim(seg, first, BLOCK)
        raw = jnp.einsum('qhd,khd->hqk', qblock, keyset, precision=lax.Precision.HIGHEST) * scale
        scores = low_back(raw)
        allowed = (qseg[:, None] == seg[None, :]) & (qseg[:, None] < SEQS) & (pos[None, :] <= qpos[:, None]) | (pos[None, :] == qpos[:, None])
        scores = jnp.where(allowed[None], scores, -1e+30)
        top = lax.optimization_barrier(jnp.max(scores, -1, keepdims=True))
        expo = jnp.exp(scores - top)
        probs = low(expo / lax.optimization_barrier(jnp.sum(expo, -1, keepdims=True)))
        return jnp.einsum('hqk,khd->qhd', probs, valueset, precision=lax.Precision.HIGHEST)
    blocks = lax.map(jax.checkpoint(one_block), jnp.arange(GROUP_ROWS // BLOCK, dtype=jnp.int32))
    return blocks.reshape(GROUP_ROWS, HEADS, HEAD_DIM)

def reference(hidden_in, ln1_gain, ln1_bias, qkv_weight, qkv_bias, out_weight, ln2_gain, ln2_bias, gate_weight, up_weight, down_weight, seq_lengths, deal_order, out_grad):
    segs, starts = jax.vmap(segment_of)(deal_order, seq_lengths)
    rel = (deal_order - starts).astype(jnp.float32).reshape(-1)
    params = [p.astype(jnp.float32) for p in (hidden_in, ln1_gain, ln1_bias, qkv_weight, qkv_bias, out_weight, ln2_gain, ln2_bias, gate_weight, up_weight, down_weight)]

    def forward(x, g1, b1, wqkv, bqkv, wout, g2, b2, wgate, wup, wdown):
        rows = x.reshape(-1, D)
        normed = low(normalize(rows) * g1 + b1)
        qkv = low_back(matmul(normed, wqkv) + bqkv.reshape(-1))
        query = low_back(low(rotate(qkv[:, :D], rel, 1.0)))
        keyset = low_back(low(rotate(qkv[:, D:2 * D], rel, 1.0)))
        valueset = low_back(low(qkv[:, 2 * D:]))
        shape4 = (GROUPS, GROUP_ROWS, HEADS, HEAD_DIM)
        mixed = lax.map(group_attention, (query.reshape(shape4), keyset.reshape(shape4), valueset.reshape(shape4), deal_order, segs))
        heads_out = low_back(low(mixed.reshape(-1, D)))
        attn = low_back(matmul(heads_out, wout))
        h1 = rows + attn
        second = low(normalize(h1) * g2 + b2)
        gate = low_back(matmul(second, wgate))
        upper = low_back(matmul(second, wup))
        hidden = low(jax.nn.silu(gate) * upper)
        mlp = low_back(matmul(hidden, wdown))
        return (h1 + mlp, (attn, mlp))
    result, pull, branches = jax.vjp(forward, *params, has_aux=True)
    grads = pull(out_grad.astype(jnp.float32).reshape(-1, D))
    valid = (deal_order < VALID).reshape(-1).astype(jnp.float32)[:, None]
    total = GROUPS * VALID * D
    sums = jnp.stack([jnp.sum(valid * result * result), jnp.sum(valid * branches[0] * branches[0]), jnp.sum(valid * branches[1] * branches[1])])
    rms = jnp.sqrt(sums / total)
    full = hidden_in.shape
    return (result.reshape(full).astype(jnp.bfloat16), grads[0].reshape(full), grads[1], grads[2], grads[3], grads[4], grads[5], grads[6], grads[7], grads[8], grads[9], grads[10], rms)
```

```python
import jax
import jax.numpy as jnp
from jax import lax
from jax.sharding import PartitionSpec as P

HEAD_DIM = 64
ROT = 16


EPS = 1e-05


def normalize(values):
    center = values - jnp.mean(values, -1, keepdims=True)
    spread = jnp.mean(center * center, -1, keepdims=True)
    rstd = lax.rsqrt(spread + EPS)
    return (center * rstd, rstd)


def norm_back(grad, normed, rstd, gain):
    scaled = grad * gain
    inner = (
        scaled
        - jnp.mean(scaled, -1, keepdims=True)
        - normed * jnp.mean(scaled * normed, -1, keepdims=True)
    )
    return (rstd * inner, jnp.sum(grad * normed, 0), jnp.sum(grad, 0))


def segment_of(pos, lengths):
    nseg = lengths.shape[0]
    ends = jnp.cumsum(lengths)
    seg = jnp.sum((pos[:, None] >= ends[None, :]).astype(jnp.int32), 1)
    starts = jnp.concatenate([jnp.zeros((1,), jnp.int32), ends[:-1]])
    start = jnp.sum(
        jnp.where(seg[:, None] == jnp.arange(nseg, dtype=jnp.int32)[None, :], starts[None, :], 0), 1
    )
    start = jnp.where(seg < nseg, start, pos)
    return (seg, start)


def rotate(values, rel, sign):
    count = values.shape[0]
    view = values.reshape(count, -1, HEAD_DIM)
    half = ROT // 2
    freq = 10000.0 ** (-2.0 * jnp.arange(half, dtype=jnp.float32) / ROT)
    angle = rel[:, None] * freq[None, :]
    cosine = jnp.cos(angle)[:, None, :]
    sine = jnp.sin(angle)[:, None, :]
    first = view[..., :half]
    second = view[..., half:ROT]
    turned = jnp.concatenate(
        [
            first * cosine - sign * second * sine,
            second * cosine + sign * first * sine,
            view[..., ROT:],
        ],
        -1,
    )
    return turned.reshape(count, -1)


def outer(left, right):
    return lax.dot_general(
        left, right, (((0,), (0,)), ((), ())), preferred_element_type=jnp.float32
    )


def times(left, right):
    return jnp.dot(left, right, preferred_element_type=jnp.float32)


def times_transposed(left, right):
    return lax.dot_general(
        left, right, (((1,), (1,)), ((), ())), preferred_element_type=jnp.float32
    )


def mlp_forward(gate, upper):
    sigma = jax.nn.sigmoid(gate)
    return ((gate * sigma * upper).astype(jnp.bfloat16), sigma)


def mlp_backward(hidden_grad, gate, upper, sigma):
    up_act = (hidden_grad * gate * sigma).astype(jnp.bfloat16)
    gate_act = (hidden_grad * upper * sigma * (1.0 + gate * (1.0 - sigma))).astype(jnp.bfloat16)
    return (gate_act, up_act)


def body(
    hidden_in,
    ln1_gain,
    ln1_bias,
    qkv_weight,
    qkv_bias,
    out_weight,
    ln2_gain,
    ln2_bias,
    gate_weight,
    up_weight,
    down_weight,
    seq_lengths,
    deal_order,
    out_grad,
):
    rows = hidden_in.shape[1]
    width = hidden_in.shape[2]
    nseq = lax.axis_size("seq")
    nfsdp = lax.axis_size("fsdp")
    local_width = width // nseq
    part = qkv_weight.shape[0]
    ff = gate_weight.shape[1]
    local_ff = ff // nseq
    stream = hidden_in[0].astype(jnp.float32)
    cotangent = out_grad[0].astype(jnp.float32)
    order = deal_order[0]
    lengths = seq_lengths[0]
    nseg = lengths.shape[0]
    group_rows = order.shape[0]
    valid_rows = group_rows * 5 // 8
    longest = valid_rows * 4 // 5
    blk = min(512, group_rows)
    keys = min(group_rows, longest + blk)
    nblocks = group_rows // blk
    scale = HEAD_DIM ** (-0.5)
    local_pos = lax.dynamic_slice_in_dim(order, lax.axis_index("seq") * rows, rows)
    valid = (local_pos < valid_rows).astype(jnp.float32)[:, None]
    dealt_seg, dealt_start = segment_of(order, lengths)
    rel = (order - dealt_start).astype(jnp.float32)
    inverse = (
        jnp.zeros((group_rows,), jnp.int32).at[order].set(jnp.arange(group_rows, dtype=jnp.int32))
    )
    seg_p, start_p = segment_of(jnp.arange(group_rows, dtype=jnp.int32), lengths)

    def gather_rows(values):
        return lax.all_gather(values, "seq", axis=0, tiled=True)

    def scatter_rows(partial):
        return lax.psum_scatter(
            partial.astype(jnp.bfloat16), "seq", scatter_dimension=0, tiled=True
        ).astype(jnp.float32)

    def column_slice(weight, blocks):
        cols = weight.shape[1] // (blocks * nseq)
        view = weight.reshape(part, blocks, nseq, cols).transpose(2, 0, 1, 3)
        mine = lax.all_to_all(
            view.reshape(nseq * part, blocks * cols), "seq", split_axis=0, concat_axis=0, tiled=True
        )
        full = lax.all_gather(mine.reshape(nseq, part, blocks * cols), "fsdp", axis=1)
        return full.reshape(width, blocks * cols)

    def row_slice(weight):
        return lax.all_gather(weight, "fsdp", axis=0, tiled=True)

    def column_shard(grad, blocks):
        cols = grad.shape[1] // blocks
        view = grad.astype(jnp.bfloat16).reshape(nseq, nfsdp, part, blocks * cols)
        mine = lax.psum_scatter(view.transpose(1, 0, 2, 3), "fsdp", scatter_dimension=0)
        got = lax.all_to_all(
            mine.reshape(nseq * part, blocks * cols), "seq", split_axis=0, concat_axis=0, tiled=True
        )
        view = got.reshape(nseq, part, blocks, cols).transpose(1, 2, 0, 3)
        return view.reshape(part, -1).astype(jnp.float32)

    def row_shard(grad):
        return lax.psum_scatter(
            grad.astype(jnp.bfloat16), "fsdp", scatter_dimension=0, tiled=True
        ).astype(jnp.float32)

    def to_pack(values):
        heads_here = values.shape[1] // HEAD_DIM
        return values[inverse].reshape(group_rows, heads_here, HEAD_DIM)

    def window(index, packed):
        query_p, key_p, value_p = packed
        first = index * blk
        key_first = jnp.clip(jnp.minimum(start_p[first], group_rows - keys), 0, group_rows - keys)
        qpos = first + jnp.arange(blk, dtype=jnp.int32)
        kpos = key_first + jnp.arange(keys, dtype=jnp.int32)
        qseg = lax.dynamic_slice_in_dim(seg_p, first, blk)
        kseg = lax.dynamic_slice_in_dim(seg_p, key_first, keys)
        allowed = (qseg[:, None] == kseg[None, :]) & (qseg[:, None] < nseg) & (
            kpos[None, :] <= qpos[:, None]
        ) | (kpos[None, :] == qpos[:, None])
        qblock = lax.dynamic_slice_in_dim(query_p, first, blk)
        kblock = lax.dynamic_slice_in_dim(key_p, key_first, keys)
        vblock = lax.dynamic_slice_in_dim(value_p, key_first, keys)
        scores = (
            jnp.einsum("qhd,khd->hqk", qblock, kblock, preferred_element_type=jnp.float32) * scale
        )
        scores = jnp.where(allowed[None], scores, -1e30)
        return (first, key_first, qblock, kblock, vblock, scores)

    both = ("seq", "fsdp")
    norms = lax.all_gather(
        jnp.stack([ln1_gain, ln1_bias, ln2_gain, ln2_bias, *qkv_bias]), both, axis=1, tiled=True
    )
    gain1, shift1, gain2, shift2 = norms[:4].astype(jnp.float32)
    qkv_shift = lax.dynamic_slice_in_dim(
        norms[4:], lax.axis_index("seq") * local_width, local_width, 1
    )
    qkv_shift = qkv_shift.reshape(-1).astype(jnp.float32)

    normed1, rstd1 = normalize(stream)
    first_local = (normed1 * gain1 + shift1).astype(jnp.bfloat16)
    first_in = gather_rows(first_local)
    qkv_w = column_slice(qkv_weight, 3)
    qkv = times(first_in, qkv_w) + qkv_shift
    query = rotate(qkv[:, :local_width], rel, 1.0).astype(jnp.bfloat16)
    keyset = rotate(qkv[:, local_width : 2 * local_width], rel, 1.0).astype(jnp.bfloat16)
    valueset = qkv[:, 2 * local_width :].astype(jnp.bfloat16)
    packed = (to_pack(query), to_pack(keyset), to_pack(valueset))

    def attend_block(index):
        first, key_first, qblock, kblock, vblock, scores = window(index, packed)
        top = jnp.max(scores, -1, keepdims=True)
        expo = jnp.exp(scores - top)
        total = jnp.sum(expo, -1, keepdims=True)
        probs = (expo / total).astype(jnp.bfloat16)
        mixed = jnp.einsum("hqk,khd->qhd", probs, vblock, preferred_element_type=jnp.float32)
        return (mixed.astype(jnp.bfloat16), (top + jnp.log(total))[..., 0])

    mixed_all, lse_all = lax.map(attend_block, jnp.arange(nblocks, dtype=jnp.int32))
    mixed = mixed_all.reshape(group_rows, -1)[order]
    heads_out = lax.all_to_all(mixed, "seq", split_axis=0, concat_axis=1, tiled=True)
    out_w = lax.all_gather(out_weight, both, axis=0, tiled=True)
    out_rows = row_slice(out_weight)
    attn = times(heads_out, out_w)
    resid = stream + attn
    normed2, rstd2 = normalize(resid)
    second_in = gather_rows((normed2 * gain2 + shift2).astype(jnp.bfloat16))
    gate_w = column_slice(gate_weight, 1)
    up_w = column_slice(up_weight, 1)
    down_w = row_slice(down_weight)
    gate = times(second_in, gate_w)
    upper = times(second_in, up_w)
    hidden, sigma = mlp_forward(gate, upper)
    mlp = scatter_rows(times(hidden, down_w))
    result = resid + mlp

    mlp_grad = gather_rows(out_grad[0])
    hidden_grad = times_transposed(mlp_grad, down_w)
    gate_act, up_act = mlp_backward(hidden_grad, gate, upper, sigma)
    second_grad = scatter_rows(times_transposed(gate_act, gate_w) + times_transposed(up_act, up_w))
    down_grad = row_shard(outer(hidden, mlp_grad))
    gate_grad = column_shard(outer(second_in, gate_act), 1)
    up_grad = column_shard(outer(second_in, up_act), 1)
    resid_part, gain2_grad, shift2_grad = norm_back(second_grad, normed2, rstd2, gain2)
    resid_grad = cotangent + resid_part

    attn_grad = gather_rows(resid_grad.astype(jnp.bfloat16))
    out_grad_w = row_shard(outer(mixed, attn_grad))
    mixed_grad_p = to_pack(times_transposed(attn_grad, out_rows).astype(jnp.bfloat16))

    def back_block(index, carry):
        query_acc, key_acc, value_acc = carry
        first, key_first, qblock, kblock, vblock, scores = window(index, packed)
        probs = jnp.exp(scores - lse_all[index][:, :, None])
        dblock = lax.dynamic_slice_in_dim(mixed_grad_p, first, blk)
        value_part = jnp.einsum(
            "hqk,qhd->khd", probs.astype(jnp.bfloat16), dblock, preferred_element_type=jnp.float32
        )
        prob_grad = jnp.einsum("qhd,khd->hqk", dblock, vblock, preferred_element_type=jnp.float32)
        inner = jnp.sum(probs * prob_grad, -1, keepdims=True)
        score_grad = (probs * (prob_grad - inner)).astype(jnp.bfloat16)
        query_part = (
            jnp.einsum("hqk,khd->qhd", score_grad, kblock, preferred_element_type=jnp.float32)
            * scale
        )
        key_part = (
            jnp.einsum("hqk,qhd->khd", score_grad, qblock, preferred_element_type=jnp.float32)
            * scale
        )
        query_acc = lax.dynamic_update_slice_in_dim(query_acc, query_part, first, 0)
        key_old = lax.dynamic_slice_in_dim(key_acc, key_first, keys)
        key_acc = lax.dynamic_update_slice_in_dim(key_acc, key_old + key_part, key_first, 0)
        value_old = lax.dynamic_slice_in_dim(value_acc, key_first, keys)
        value_acc = lax.dynamic_update_slice_in_dim(value_acc, value_old + value_part, key_first, 0)
        return (query_acc, key_acc, value_acc)

    zeros = jnp.zeros(packed[0].shape, jnp.float32)
    query_acc, key_acc, value_acc = lax.fori_loop(0, nblocks, back_block, (zeros, zeros, zeros))

    def to_dealt(values):
        return values.astype(jnp.bfloat16).reshape(group_rows, -1)[order]

    qkv_act = jnp.concatenate(
        [
            rotate(to_dealt(query_acc).astype(jnp.float32), rel, -1.0).astype(jnp.bfloat16),
            rotate(to_dealt(key_acc).astype(jnp.float32), rel, -1.0).astype(jnp.bfloat16),
            to_dealt(value_acc),
        ],
        1,
    )
    first_grad = scatter_rows(times_transposed(qkv_act, qkv_w))
    qkv_grad = column_shard(outer(first_in, qkv_act), 3)
    qkv_bias_grad = lax.psum_scatter(
        jnp.sum(qkv_act.astype(jnp.float32), 0).reshape(3, nfsdp, -1),
        "fsdp",
        scatter_dimension=1,
    )
    input_part, gain1_grad, shift1_grad = norm_back(first_grad, normed1, rstd1, gain1)
    input_grad = resid_grad + input_part

    norm_grads = lax.psum(
        (
            gain1_grad,
            shift1_grad,
            gain2_grad,
            shift2_grad,
            jnp.sum(valid * result * result),
            jnp.sum(valid * attn * attn),
            jnp.sum(valid * mlp * mlp),
        ),
        both,
    )
    count = valid_rows * nfsdp * width
    rms = jnp.sqrt(jnp.stack(norm_grads[4:]) / count)
    mine = (lax.axis_index("seq") * nfsdp + lax.axis_index("fsdp")) * part
    norm_shards = [lax.dynamic_slice_in_dim(value, mine, part) for value in norm_grads[:4]]
    return (
        result.astype(jnp.bfloat16)[None],
        input_grad[None],
        norm_shards[0],
        norm_shards[1],
        qkv_grad,
        qkv_bias_grad,
        out_grad_w,
        norm_shards[2],
        norm_shards[3],
        gate_grad,
        up_grad,
        down_grad,
        rms,
    )


def solution(mesh):
    in_specs = (
        P("fsdp", "seq", None),
        P(("seq", "fsdp")),
        P(("seq", "fsdp")),
        P(("seq", "fsdp"), None),
        P(None, ("seq", "fsdp")),
        P(("seq", "fsdp"), None),
        P(("seq", "fsdp")),
        P(("seq", "fsdp")),
        P(("seq", "fsdp"), None),
        P(("seq", "fsdp"), None),
        P(("seq", "fsdp"), None),
        P("fsdp", None),
        P("fsdp", None),
        P("fsdp", "seq", None),
    )
    out_specs = (
        P("fsdp", "seq", None),
        P("fsdp", "seq", None),
        P(("seq", "fsdp")),
        P(("seq", "fsdp")),
        P(("seq", "fsdp"), None),
        P(None, ("seq", "fsdp")),
        P(("seq", "fsdp"), None),
        P(("seq", "fsdp")),
        P(("seq", "fsdp")),
        P(("seq", "fsdp"), None),
        P(("seq", "fsdp"), None),
        P(("seq", "fsdp"), None),
        P(),
    )
    return jax.shard_map(body, mesh=mesh, in_specs=in_specs, out_specs=out_specs, check_vma=False)
```

```python
import functools

import jax
import jax.numpy as jnp
from jax import lax
from jax.experimental import pallas as pl
from jax.experimental.pallas import tpu as pltpu
from jax.sharding import PartitionSpec as P

HEAD_DIM = 64
ROT = 16


EPS = 1e-05


def normalize(values):
    center = values - jnp.mean(values, -1, keepdims=True)
    spread = jnp.mean(center * center, -1, keepdims=True)
    rstd = lax.rsqrt(spread + EPS)
    return (center * rstd, rstd)


def norm_back(grad, normed, rstd, gain):
    scaled = grad * gain
    inner = (
        scaled
        - jnp.mean(scaled, -1, keepdims=True)
        - normed * jnp.mean(scaled * normed, -1, keepdims=True)
    )
    return (rstd * inner, jnp.sum(grad * normed, 0), jnp.sum(grad, 0))


def segment_of(pos, lengths):
    nseg = lengths.shape[0]
    ends = jnp.cumsum(lengths)
    seg = jnp.sum((pos[:, None] >= ends[None, :]).astype(jnp.int32), 1)
    starts = jnp.concatenate([jnp.zeros((1,), jnp.int32), ends[:-1]])
    start = jnp.sum(
        jnp.where(seg[:, None] == jnp.arange(nseg, dtype=jnp.int32)[None, :], starts[None, :], 0), 1
    )
    start = jnp.where(seg < nseg, start, pos)
    return (seg, start)


def rotate(values, rel, sign):
    count = values.shape[0]
    view = values.reshape(count, -1, HEAD_DIM)
    half = ROT // 2
    freq = 10000.0 ** (-2.0 * jnp.arange(half, dtype=jnp.float32) / ROT)
    angle = rel[:, None] * freq[None, :]
    cosine = jnp.cos(angle)[:, None, :]
    sine = jnp.sin(angle)[:, None, :]
    first = view[..., :half]
    second = view[..., half:ROT]
    turned = jnp.concatenate(
        [
            first * cosine - sign * second * sine,
            second * cosine + sign * first * sine,
            view[..., ROT:],
        ],
        -1,
    )
    return turned.reshape(count, -1)


def outer(left, right):
    return lax.dot_general(
        left, right, (((0,), (0,)), ((), ())), preferred_element_type=jnp.float32
    )


def times(left, right):
    return jnp.dot(left, right, preferred_element_type=jnp.float32)


def times_transposed(left, right):
    return lax.dot_general(
        left, right, (((1,), (1,)), ((), ())), preferred_element_type=jnp.float32
    )


def mlp_forward(gate, upper):
    sigma = jax.nn.sigmoid(gate)
    return ((gate * sigma * upper).astype(jnp.bfloat16), sigma)


def mlp_backward(hidden_grad, gate, upper, sigma):
    up_act = (hidden_grad * gate * sigma).astype(jnp.bfloat16)
    gate_act = (hidden_grad * upper * sigma * (1.0 + gate * (1.0 - sigma))).astype(jnp.bfloat16)
    return (gate_act, up_act)


def body(
    hidden_in,
    ln1_gain,
    ln1_bias,
    qkv_weight,
    qkv_bias,
    out_weight,
    ln2_gain,
    ln2_bias,
    gate_weight,
    up_weight,
    down_weight,
    seq_lengths,
    deal_order,
    out_grad,
):
    rows = hidden_in.shape[1]
    width = hidden_in.shape[2]
    nseq = lax.axis_size("seq")
    nfsdp = lax.axis_size("fsdp")
    local_width = width // nseq
    part = qkv_weight.shape[0]
    ff = gate_weight.shape[1]
    local_ff = ff // nseq
    stream = hidden_in[0].astype(jnp.float32)
    cotangent = out_grad[0].astype(jnp.float32)
    order = deal_order[0]
    lengths = seq_lengths[0]
    nseg = lengths.shape[0]
    group_rows = order.shape[0]
    valid_rows = group_rows * 5 // 8
    longest = valid_rows * 4 // 5
    blk = min(512, group_rows)
    keys = min(group_rows, longest + blk)
    nblocks = group_rows // blk
    scale = HEAD_DIM ** (-0.5)
    local_pos = lax.dynamic_slice_in_dim(order, lax.axis_index("seq") * rows, rows)
    valid = (local_pos < valid_rows).astype(jnp.float32)[:, None]
    dealt_seg, dealt_start = segment_of(order, lengths)
    rel = (order - dealt_start).astype(jnp.float32)
    inverse = (
        jnp.zeros((group_rows,), jnp.int32).at[order].set(jnp.arange(group_rows, dtype=jnp.int32))
    )
    seg_p, start_p = segment_of(jnp.arange(group_rows, dtype=jnp.int32), lengths)

    def gather_rows(values):
        return lax.all_gather(values, "seq", axis=0, tiled=True)

    def scatter_rows(partial):
        return lax.psum_scatter(
            partial.astype(jnp.bfloat16), "seq", scatter_dimension=0, tiled=True
        ).astype(jnp.float32)

    def column_slice(weight, blocks):
        cols = weight.shape[1] // (blocks * nseq)
        view = weight.reshape(part, blocks, nseq, cols).transpose(2, 0, 1, 3)
        mine = lax.all_to_all(
            view.reshape(nseq * part, blocks * cols), "seq", split_axis=0, concat_axis=0, tiled=True
        )
        full = lax.all_gather(mine.reshape(nseq, part, blocks * cols), "fsdp", axis=1)
        return full.reshape(width, blocks * cols)

    def row_slice(weight):
        return lax.all_gather(weight, "fsdp", axis=0, tiled=True)

    def column_shard(grad, blocks):
        cols = grad.shape[1] // blocks
        view = grad.astype(jnp.bfloat16).reshape(nseq, nfsdp, part, blocks * cols)
        mine = lax.psum_scatter(view.transpose(1, 0, 2, 3), "fsdp", scatter_dimension=0)
        got = lax.all_to_all(
            mine.reshape(nseq * part, blocks * cols), "seq", split_axis=0, concat_axis=0, tiled=True
        )
        view = got.reshape(nseq, part, blocks, cols).transpose(1, 2, 0, 3)
        return view.reshape(part, -1).astype(jnp.float32)

    def row_shard(grad):
        return lax.psum_scatter(
            grad.astype(jnp.bfloat16), "fsdp", scatter_dimension=0, tiled=True
        ).astype(jnp.float32)

    def to_pack(values):
        heads_here = values.shape[1] // HEAD_DIM
        return values[inverse].reshape(group_rows, heads_here, HEAD_DIM)

    def window(index, packed):
        query_p, key_p, value_p = packed
        first = index * blk
        key_first = jnp.clip(jnp.minimum(start_p[first], group_rows - keys), 0, group_rows - keys)
        qpos = first + jnp.arange(blk, dtype=jnp.int32)
        kpos = key_first + jnp.arange(keys, dtype=jnp.int32)
        qseg = lax.dynamic_slice_in_dim(seg_p, first, blk)
        kseg = lax.dynamic_slice_in_dim(seg_p, key_first, keys)
        allowed = (qseg[:, None] == kseg[None, :]) & (qseg[:, None] < nseg) & (
            kpos[None, :] <= qpos[:, None]
        ) | (kpos[None, :] == qpos[:, None])
        qblock = lax.dynamic_slice_in_dim(query_p, first, blk)
        kblock = lax.dynamic_slice_in_dim(key_p, key_first, keys)
        vblock = lax.dynamic_slice_in_dim(value_p, key_first, keys)
        scores = (
            jnp.einsum("qhd,khd->hqk", qblock, kblock, preferred_element_type=jnp.float32) * scale
        )
        scores = jnp.where(allowed[None], scores, -1e30)
        return (first, key_first, qblock, kblock, vblock, scores)

    both = ("seq", "fsdp")
    norms = lax.all_gather(
        jnp.stack([ln1_gain, ln1_bias, ln2_gain, ln2_bias, *qkv_bias]), both, axis=1, tiled=True
    )
    gain1, shift1, gain2, shift2 = norms[:4].astype(jnp.float32)
    qkv_shift = lax.dynamic_slice_in_dim(
        norms[4:], lax.axis_index("seq") * local_width, local_width, 1
    )
    qkv_shift = qkv_shift.reshape(-1).astype(jnp.float32)

    normed1, rstd1 = normalize(stream)
    first_local = (normed1 * gain1 + shift1).astype(jnp.bfloat16)
    first_in = gather_rows(first_local)
    qkv_w = column_slice(qkv_weight, 3)
    qkv = times(first_in, qkv_w) + qkv_shift
    query = rotate(qkv[:, :local_width], rel, 1.0).astype(jnp.bfloat16)
    keyset = rotate(qkv[:, local_width : 2 * local_width], rel, 1.0).astype(jnp.bfloat16)
    valueset = qkv[:, 2 * local_width :].astype(jnp.bfloat16)
    packed = (to_pack(query), to_pack(keyset), to_pack(valueset))

    def attend_block(index):
        first, key_first, qblock, kblock, vblock, scores = window(index, packed)
        top = jnp.max(scores, -1, keepdims=True)
        expo = jnp.exp(scores - top)
        total = jnp.sum(expo, -1, keepdims=True)
        probs = (expo / total).astype(jnp.bfloat16)
        mixed = jnp.einsum("hqk,khd->qhd", probs, vblock, preferred_element_type=jnp.float32)
        return (mixed.astype(jnp.bfloat16), (top + jnp.log(total))[..., 0])

    mixed_all, lse_all = lax.map(attend_block, jnp.arange(nblocks, dtype=jnp.int32))
    mixed = mixed_all.reshape(group_rows, -1)[order]
    heads_out = lax.all_to_all(mixed, "seq", split_axis=0, concat_axis=1, tiled=True)
    out_w = lax.all_gather(out_weight, both, axis=0, tiled=True)
    out_rows = row_slice(out_weight)
    attn = times(heads_out, out_w)
    resid = stream + attn
    normed2, rstd2 = normalize(resid)
    second_in = gather_rows((normed2 * gain2 + shift2).astype(jnp.bfloat16))
    gate_w = column_slice(gate_weight, 1)
    up_w = column_slice(up_weight, 1)
    down_w = row_slice(down_weight)
    gate = times(second_in, gate_w)
    upper = times(second_in, up_w)
    hidden, sigma = mlp_forward(gate, upper)
    mlp = scatter_rows(times(hidden, down_w))
    result = resid + mlp

    mlp_grad = gather_rows(out_grad[0])
    hidden_grad = times_transposed(mlp_grad, down_w)
    gate_act, up_act = mlp_backward(hidden_grad, gate, upper, sigma)
    second_grad = scatter_rows(times_transposed(gate_act, gate_w) + times_transposed(up_act, up_w))
    down_grad = row_shard(outer(hidden, mlp_grad))
    gate_grad = column_shard(outer(second_in, gate_act), 1)
    up_grad = column_shard(outer(second_in, up_act), 1)
    resid_part, gain2_grad, shift2_grad = norm_back(second_grad, normed2, rstd2, gain2)
    resid_grad = cotangent + resid_part

    attn_grad = gather_rows(resid_grad.astype(jnp.bfloat16))
    out_grad_w = row_shard(outer(mixed, attn_grad))
    mixed_grad_p = to_pack(times_transposed(attn_grad, out_rows).astype(jnp.bfloat16))

    def back_block(index, carry):
        query_acc, key_acc, value_acc = carry
        first, key_first, qblock, kblock, vblock, scores = window(index, packed)
        probs = jnp.exp(scores - lse_all[index][:, :, None])
        dblock = lax.dynamic_slice_in_dim(mixed_grad_p, first, blk)
        value_part = jnp.einsum(
            "hqk,qhd->khd", probs.astype(jnp.bfloat16), dblock, preferred_element_type=jnp.float32
        )
        prob_grad = jnp.einsum("qhd,khd->hqk", dblock, vblock, preferred_element_type=jnp.float32)
        inner = jnp.sum(probs * prob_grad, -1, keepdims=True)
        score_grad = (probs * (prob_grad - inner)).astype(jnp.bfloat16)
        query_part = (
            jnp.einsum("hqk,khd->qhd", score_grad, kblock, preferred_element_type=jnp.float32)
            * scale
        )
        key_part = (
            jnp.einsum("hqk,qhd->khd", score_grad, qblock, preferred_element_type=jnp.float32)
            * scale
        )
        query_acc = lax.dynamic_update_slice_in_dim(query_acc, query_part, first, 0)
        key_old = lax.dynamic_slice_in_dim(key_acc, key_first, keys)
        key_acc = lax.dynamic_update_slice_in_dim(key_acc, key_old + key_part, key_first, 0)
        value_old = lax.dynamic_slice_in_dim(value_acc, key_first, keys)
        value_acc = lax.dynamic_update_slice_in_dim(value_acc, value_old + value_part, key_first, 0)
        return (query_acc, key_acc, value_acc)

    zeros = jnp.zeros(packed[0].shape, jnp.float32)
    query_acc, key_acc, value_acc = lax.fori_loop(0, nblocks, back_block, (zeros, zeros, zeros))

    def to_dealt(values):
        return values.astype(jnp.bfloat16).reshape(group_rows, -1)[order]

    qkv_act = jnp.concatenate(
        [
            rotate(to_dealt(query_acc).astype(jnp.float32), rel, -1.0).astype(jnp.bfloat16),
            rotate(to_dealt(key_acc).astype(jnp.float32), rel, -1.0).astype(jnp.bfloat16),
            to_dealt(value_acc),
        ],
        1,
    )
    first_grad = scatter_rows(times_transposed(qkv_act, qkv_w))
    qkv_grad = column_shard(outer(first_in, qkv_act), 3)
    qkv_bias_grad = lax.psum_scatter(
        jnp.sum(qkv_act.astype(jnp.float32), 0).reshape(3, nfsdp, -1),
        "fsdp",
        scatter_dimension=1,
    )
    input_part, gain1_grad, shift1_grad = norm_back(first_grad, normed1, rstd1, gain1)
    input_grad = resid_grad + input_part

    norm_grads = lax.psum(
        (
            gain1_grad,
            shift1_grad,
            gain2_grad,
            shift2_grad,
            jnp.sum(valid * result * result),
            jnp.sum(valid * attn * attn),
            jnp.sum(valid * mlp * mlp),
        ),
        both,
    )
    count = valid_rows * nfsdp * width
    rms = jnp.sqrt(jnp.stack(norm_grads[4:]) / count)
    mine = (lax.axis_index("seq") * nfsdp + lax.axis_index("fsdp")) * part
    norm_shards = [lax.dynamic_slice_in_dim(value, mine, part) for value in norm_grads[:4]]
    return (
        result.astype(jnp.bfloat16)[None],
        input_grad[None],
        norm_shards[0],
        norm_shards[1],
        qkv_grad,
        qkv_bias_grad,
        out_grad_w,
        norm_shards[2],
        norm_shards[3],
        gate_grad,
        up_grad,
        down_grad,
        rms,
    )


MESH = pl.DeviceIdType.MESH

def where_am_i():
    s = lax.axis_index("seq"); f = lax.axis_index("fsdp")
    return s, f, s // 2, s % 2

def remote(src, dst, ssem, rsem, dev):
    return pltpu.make_async_remote_copy(src, dst, ssem, rsem, device_id=dev, device_id_type=MESH)

def greet_line(s, f, z, y):
    bar = pltpu.get_barrier_semaphore()
    pl.semaphore_signal(bar, inc=1, device_id=(s + 1 - 2 * y, f), device_id_type=MESH)
    @pl.when(z > 0)
    def _(): pl.semaphore_signal(bar, inc=1, device_id=(s - 2, f), device_id_type=MESH)
    @pl.when(z < 3)
    def _(): pl.semaphore_signal(bar, inc=1, device_id=(s + 2, f), device_id_type=MESH)
    edge = jnp.where((z == 0) | (z == 3), 1, 0)
    pl.semaphore_wait(bar, 3 - edge)

def ag_kernel(x_ref, o_ref, own_sem, recv, sy, su, sd):
    s, f, z, y = where_am_i()
    greet_line(s, f, z, y)
    other = s + 1 - 2 * y
    own = pltpu.make_async_copy(x_ref, o_ref.at[s], own_sem)
    own.start()
    def ysend(zb, src): return remote(src, o_ref.at[2 * zb + y], sy.at[zb], recv.at[2 * zb + y], (other, f))
    def usend(zb, src): return remote(src, o_ref.at[2 * zb + y], su.at[zb], recv.at[2 * zb + y], (s + 2, f))
    def dsend(zb, src): return remote(src, o_ref.at[2 * zb + y], sd.at[zb], recv.at[2 * zb + y], (s - 2, f))
    def arrived(blk): return remote(o_ref.at[blk], o_ref.at[blk], sy.at[0], recv.at[blk], (other, f))
    @pl.when(z < 3)
    def _(): usend(z, x_ref).start()
    @pl.when(z > 0)
    def _(): dsend(z, x_ref).start()
    ysend(z, x_ref).start()
    for t in range(1, 4):
        @pl.when(z >= t)
        def _():
            zb = z - t
            arrived(2 * zb + y).wait_recv()
            @pl.when(z < 3)
            def _(): usend(zb, o_ref.at[2 * zb + y]).start()
            ysend(zb, o_ref.at[2 * zb + y]).start()
        @pl.when(z + t <= 3)
        def _():
            zb = z + t
            arrived(2 * zb + y).wait_recv()
            @pl.when(z > 0)
            def _(): dsend(zb, o_ref.at[2 * zb + y]).start()
            ysend(zb, o_ref.at[2 * zb + y]).start()
    for zb in range(4):
        arrived(2 * zb + 1 - y).wait_recv()
    own.wait()
    for zb in range(4):
        ysend(zb, x_ref).wait_send()
        @pl.when((z < 3) & (zb <= z))
        def _(): usend(zb, x_ref).wait_send()
        @pl.when((z > 0) & (zb >= z))
        def _(): dsend(zb, x_ref).wait_send()

def all_gather_rows(x, cid, vmem_in=True):
    return pl.pallas_call(ag_kernel, out_shape=jax.ShapeDtypeStruct((8,) + x.shape, x.dtype),
        in_specs=[pl.BlockSpec(memory_space=pltpu.VMEM)], out_specs=pl.BlockSpec(memory_space=pl.ANY),
        scratch_shapes=[pltpu.SemaphoreType.DMA, pltpu.SemaphoreType.DMA((8,)), pltpu.SemaphoreType.DMA((4,)), pltpu.SemaphoreType.DMA((4,)), pltpu.SemaphoreType.DMA((4,))],
        compiler_params=pltpu.CompilerParams(collective_id=cid, has_side_effects=True))(x)

CH = 2
def rs_kernel(p_ref, o_ref, mine, ybuf, up, down, send_up, send_down, load_sem, ry, ru, rd, sy, su, sd):
    s, f, z, y = where_am_i()
    rows = p_ref.shape[1]
    ch = rows // CH
    greet_line(s, f, z, y)
    other = s + 1 - 2 * y
    def order(k):
        a = [3, 2, 1, 0]; b = [3, 0, 2, 1]; c = [0, 3, 1, 2]; d = [0, 1, 2, 3]
        return jnp.where(z == 0, a[k], jnp.where(z == 1, b[k], jnp.where(z == 2, c[k], d[k])))
    def part(c): return pl.ds(c * ch, ch)
    def ysend(zb, c): return remote(p_ref.at[2 * zb + 1 - y, part(c)], ybuf.at[zb, part(c)], sy.at[zb, c], ry.at[zb, c], (other, f))
    def load(zb): return pltpu.make_async_copy(p_ref.at[2 * zb + y], mine.at[zb], load_sem.at[zb])
    def usend(zb, c): return remote(send_up.at[zb, part(c)], up.at[zb, part(c)], su.at[zb, c], ru.at[zb, c], (s + 2, f))
    def dsend(zb, c): return remote(send_down.at[zb, part(c)], down.at[zb, part(c)], sd.at[zb, c], rd.at[zb, c], (s - 2, f))
    for k in range(4):
        zb = order(k)
        for c in range(CH): ysend(zb, c).start()
        load(zb).start()
    STEP = 16
    def add2(dst, a, b):
        @pl.loop(0, ch // STEP)
        def _(i):
            r = pl.ds(pl.multiple_of(i * STEP, STEP), STEP)
            dst[r] = (a[r].astype(jnp.float32) + b[r].astype(jnp.float32)).astype(dst.dtype)
    def add3(dst, a, b, d):
        @pl.loop(0, ch // STEP)
        def _(i):
            r = pl.ds(pl.multiple_of(i * STEP, STEP), STEP)
            dst[r] = (a[r].astype(jnp.float32) + b[r].astype(jnp.float32) + d[r].astype(jnp.float32)).astype(dst.dtype)
    for k in range(4):
        zb = order(k)
        load(zb).wait()
        for c in range(CH):
            ysend(zb, c).wait_recv()
            a = mine.at[zb, part(c)]; b = ybuf.at[zb, part(c)]
            @pl.when(zb > z)
            def _():
                @pl.when(z == 0)
                def _(): add2(send_up.at[zb, part(c)], a, b)
                @pl.when(z > 0)
                def _():
                    usend(zb, c).wait_recv()
                    add3(send_up.at[zb, part(c)], a, b, up.at[zb, part(c)])
                usend(zb, c).start()
            @pl.when(zb < z)
            def _():
                @pl.when(z == 3)
                def _(): add2(send_down.at[zb, part(c)], a, b)
                @pl.when(z < 3)
                def _():
                    dsend(zb, c).wait_recv()
                    add3(send_down.at[zb, part(c)], a, b, down.at[zb, part(c)])
                dsend(zb, c).start()
            @pl.when(zb == z)
            def _():
                @pl.when(z > 0)
                def _(): usend(zb, c).wait_recv()
                @pl.when(z < 3)
                def _(): dsend(zb, c).wait_recv()
                o = o_ref.at[part(c)]
                @pl.when(z == 0)
                def _(): add3(o, a, b, down.at[zb, part(c)])
                @pl.when(z == 3)
                def _(): add3(o, a, b, up.at[zb, part(c)])
                @pl.when((z > 0) & (z < 3))
                def _():
                    @pl.loop(0, ch // STEP)
                    def _(i):
                        r = pl.ds(pl.multiple_of(i * STEP, STEP), STEP)
                        o[r] = (a[r].astype(jnp.float32) + b[r].astype(jnp.float32)) + (up[zb, part(c)][r] if False else up.at[zb, part(c)][r].astype(jnp.float32) + down.at[zb, part(c)][r].astype(jnp.float32))
    for zb in range(4):
        for c in range(CH):
            ysend(zb, c).wait_send()
            @pl.when(zb > z)
            def _(): usend(zb, c).wait_send()
            @pl.when(zb < z)
            def _(): dsend(zb, c).wait_send()

def reduce_scatter_rows(p, cid):
    _, rows, w = p.shape
    big = lambda: pltpu.VMEM((4, rows, w), p.dtype)
    sems = lambda: pltpu.SemaphoreType.DMA((4, CH))
    return pl.pallas_call(rs_kernel, out_shape=jax.ShapeDtypeStruct((rows, w), jnp.float32),
        in_specs=[pl.BlockSpec(memory_space=pl.ANY)], out_specs=pl.BlockSpec(memory_space=pltpu.VMEM),
        scratch_shapes=[big() for _ in range(6)] + [pltpu.SemaphoreType.DMA((4,))] + [sems() for _ in range(6)],
        compiler_params=pltpu.CompilerParams(collective_id=cid, has_side_effects=True, vmem_limit_bytes=40<<20))(p)

def flip(v, bit):
    return v + bit * (1 - 2 * ((v // bit) % 2))

def peer(s, k):
    for bit in (1, 2, 4):
        if k & bit:
            s = flip(s, bit)
    return s

def greet_columns(s, f):
    bar = pltpu.get_barrier_semaphore()
    for k in range(1, 8):
        pl.semaphore_signal(bar, inc=1, device_id=(peer(s, k), f), device_id_type=MESH)
    pl.semaphore_signal(bar, inc=1, device_id=(s, flip(f, 1)), device_id_type=MESH)
    pl.semaphore_signal(bar, inc=1, device_id=(s, flip(f, 2)), device_id_type=MESH)
    pl.semaphore_wait(bar, 9)

class ColGather:
    @staticmethod
    def sems():
        D = pltpu.SemaphoreType.DMA
        return [D, D((8, 4)), D((8,)), D((8, 2)), D((8,))]
    def __init__(self, x, o, own, recv, direct, core, xs, s, f):
        self.__dict__.update(locals())
        self.fc = flip(f, 1); self.fx = flip(f, 2); self.fd = flip(flip(f, 1), 2)
        self.mine = pltpu.make_async_copy(x.at[s], o.at[s, f], own)
    def send_direct(self, k):
        s, f = self.s, self.f; t = peer(s, k)
        return remote(self.x.at[t], self.o.at[s, f], self.direct.at[k], self.recv.at[s, f], (t, f))
    def send_core(self, k, which, src):
        t = peer(self.s, k); ff = self.f if which == 0 else self.fx
        return remote(src, self.o.at[t, ff], self.core.at[k, which], self.recv.at[t, ff], (self.s, self.fc))
    def send_x(self, k, src):
        t = peer(self.s, k)
        return remote(src, self.o.at[t, self.f], self.xs.at[k], self.recv.at[t, self.f], (self.s, self.fx))
    def arrived(self, k, ff):
        t = peer(self.s, k)
        return remote(self.o.at[t, ff], self.o.at[t, ff], self.own, self.recv.at[t, ff], (self.s, self.fc))
    def start(self):
        self.mine.start()
        for k in range(1, 8): self.send_direct(k).start()
        self.send_x(0, self.x.at[self.s]).start()
        self.send_core(0, 0, self.x.at[self.s]).start()
    def step(self, k):
        t = peer(self.s, k)
        self.arrived(k, self.f).wait_recv()
        self.send_x(k, self.o.at[t, self.f]).start()
        self.send_core(k, 0, self.o.at[t, self.f]).start()
    def xstep(self, k):
        t = peer(self.s, k)
        self.arrived(k, self.fx).wait_recv()
        self.send_core(k, 1, self.o.at[t, self.fx]).start()
    def finish(self):
        self.mine.wait()
        for k in range(8):
            self.arrived(k, self.fc).wait_recv()
            self.arrived(k, self.fd).wait_recv()
        for k in range(8):
            if k: self.send_direct(k).wait_send()
            self.send_x(k, self.x.at[0]).wait_send()
            self.send_core(k, 0, self.x.at[0]).wait_send()
            self.send_core(k, 1, self.x.at[0]).wait_send()

def cg_kernel(x_ref, o_ref, *sems):
    s, f, z, y = where_am_i()
    greet_columns(s, f)
    g = ColGather(x_ref, o_ref, *sems, s, f)
    g.start()
    for k in range(1, 8):
        g.step(k)
    for k in range(8):
        g.xstep(k)
    g.finish()

def column_gather(x, cid):
    return pl.pallas_call(cg_kernel, out_shape=jax.ShapeDtypeStruct((8, 4) + x.shape[1:], x.dtype),
        in_specs=[pl.BlockSpec(memory_space=pltpu.VMEM)], out_specs=pl.BlockSpec(memory_space=pl.ANY),
        scratch_shapes=ColGather.sems(),
        compiler_params=pltpu.CompilerParams(collective_id=cid, has_side_effects=True))(x)

def adder(dst, srcs, step=16):
    rows = dst.shape[0]
    @pl.loop(0, rows // step)
    def _(i):
        r = pl.ds(pl.multiple_of(i * step, step), step)
        tot = srcs[0][r].astype(jnp.float32)
        for v in srcs[1:]:
            tot = tot + v[r].astype(jnp.float32)
        dst[r] = tot.astype(dst.dtype)

class ColReduce:
    @staticmethod
    def scratch(n, r, c, exchange):
        V = lambda *lead: pltpu.VMEM(lead + (n, r, c), jnp.bfloat16)
        D = pltpu.SemaphoreType.DMA
        return [V(2), V(2), V(), V(), V() if exchange else pltpu.VMEM((8, 128), jnp.bfloat16),
                D((2, n)), D((2, n)), D((2, n)), D((n,)), D((n,)), D((n,)), D((n,))]
    def __init__(self, g, o, ld, cb, hx, xb, ob, ldsem, cs, cr, xs, xr, es, er, s, f, exchange):
        self.__dict__.update(locals())
        self.fc = flip(f, 1); self.fx = flip(f, 2); self.fd = flip(flip(f, 1), 2)
        self.n = g.shape[0]
    def idx(self, k): return peer(self.s, k) if self.exchange else k
    def core(self, w, k):
        i = self.idx(k)
        return remote(self.g.at[i, self.fd if w == 0 else self.fc], self.cb.at[w, i], self.cs.at[w, k], self.cr.at[w, k], (self.s, self.fc))
    def load(self, w, k):
        i = self.idx(k)
        return pltpu.make_async_copy(self.g.at[i, self.fx if w == 0 else self.f], self.ld.at[w, i], self.ldsem.at[w, k])
    def xsend(self, k):
        i = self.idx(k)
        return remote(self.hx.at[i], self.xb.at[i], self.xs.at[k], self.xr.at[k], (self.s, self.fx))
    def esend(self, k):
        t = peer(self.s, k)
        return remote(self.ob.at[t], self.o.at[self.s], self.es.at[k], self.er.at[k], (t, self.f))
    def start(self):
        for w in range(2):
            for k in reversed(range(self.n)):
                self.core(w, k).start(); self.load(w, k).start()
    def step(self, k):
        i = self.idx(k)
        self.core(0, k).wait_recv(); self.load(0, k).wait()
        adder(self.hx.at[i], [self.ld.at[0, i], self.cb.at[0, i]])
        self.xsend(k).start()
    def own(self, k):
        i = self.idx(k)
        self.core(1, k).wait_recv(); self.load(1, k).wait(); self.xsend(k).wait_recv()
        if self.exchange and k:
            adder(self.ob.at[i], [self.ld.at[1, i], self.cb.at[1, i], self.xb.at[i]])
            self.esend(k).start()
        else:
            adder(self.o.at[i], [self.ld.at[1, i], self.cb.at[1, i], self.xb.at[i]])
    def finish(self):
        for k in range(self.n):
            self.core(0, k).wait_send(); self.core(1, k).wait_send(); self.xsend(k).wait_send()
            if self.exchange and k:
                self.esend(k).wait_recv(); self.esend(k).wait_send()

def cr_kernel(exchange, g_ref, o_ref, *scr):
    s, f, z, y = where_am_i()
    greet_columns(s, f)
    g = ColReduce(g_ref, o_ref, *scr, s, f, exchange)
    g.start()
    for k in reversed(range(g.n)): g.step(k)
    for k in reversed(range(g.n)): g.own(k)
    g.finish()

def column_reduce(g, cid, exchange=True):
    n, _, r, c = g.shape
    return pl.pallas_call(functools.partial(cr_kernel, exchange), out_shape=jax.ShapeDtypeStruct((n, r, c), jnp.bfloat16 if exchange else jnp.float32),
        in_specs=[pl.BlockSpec(memory_space=pl.ANY)], out_specs=pl.BlockSpec(memory_space=pltpu.VMEM),
        scratch_shapes=ColReduce.scratch(n, r, c, exchange),
        compiler_params=pltpu.CompilerParams(collective_id=cid, has_side_effects=True, vmem_limit_bytes=40<<20))(g)
QB = 128
NEG = -1e30

def dot(a, b, ca=1, cb=0):
    return lax.dot_general(a, b, (((ca,), (cb,)), ((), ())), preferred_element_type=jnp.float32)

def starts_of(pos, lengths_ref, nseg):
    start = jnp.zeros_like(pos); end = 0
    for i in range(nseg - 1):
        end = end + lengths_ref[0, i]
        start = jnp.where(pos >= end, end, start)
    return start

def head_lanes(h):
    lane = lax.broadcasted_iota(jnp.int32, (1, 128), 1)
    return (lane // HEAD_DIM) == h

def turn(x, c, s1, s2, sign):
    return x * c + (pltpu.roll(x, 128 - ROT // 2, 1) * s1 + pltpu.roll(x, ROT // 2, 1) * s2) * sign

def block_mask(qb, lengths_ref, nseg):
    keys = (qb + 1) * QB
    row = qb * QB + lax.broadcasted_iota(jnp.int32, (QB, 1), 0)
    col = lax.broadcasted_iota(jnp.int32, (1, keys), 1)
    return (col >= starts_of(row, lengths_ref, nseg)) & (col <= row)

def attn_fwd_kernel(valid, qkv_ref, c_ref, s1_ref, s2_ref, orow_ref, ocol_ref, len_ref, o_ref, pk_ref, lse_ref, rot, opk):
    rows, w3 = qkv_ref.shape
    w = w3 // 3
    nseg = len_ref.shape[1]
    scale = HEAD_DIM ** -0.5
    @pl.loop(0, rows // QB)
    def _(i):
        r = pl.ds(pl.multiple_of(i * QB, QB), QB)
        c, s1, s2 = c_ref[r], s1_ref[r], s2_ref[r]
        for t in range(w3 // 128):
            cols = slice(t * 128, t * 128 + 128)
            x = qkv_ref[r, cols]
            if t < 2 * w // 128: x = turn(x, c, s1, s2, 1.0)
            rot[r, cols] = x.astype(jnp.bfloat16)
    @pl.loop(0, valid // QB)
    def _(i):
        r = pl.ds(pl.multiple_of(i * QB, QB), QB)
        p = (lax.broadcasted_iota(jnp.int32, (QB, 1), 0) + i * QB == orow_ref[...])
        pk_ref[r] = dot(jnp.where(p, 1.0, 0.0).astype(jnp.bfloat16), rot[...]).astype(jnp.bfloat16)
    nq = valid // QB
    for qb in range(nq):
        keys = (qb + 1) * QB
        rows_q = slice(qb * QB, qb * QB + QB)
        mask = block_mask(qb, len_ref, nseg)
        for t in range(w // 128):
            q = pk_ref[rows_q, t * 128:t * 128 + 128]
            k = pk_ref[0:keys, w + t * 128:w + t * 128 + 128]
            v = pk_ref[0:keys, 2 * w + t * 128:2 * w + t * 128 + 128]
            tot = None
            for h in range(2):
                qh = jnp.where(head_lanes(h), q, jnp.zeros_like(q))
                s = dot(qh, k, 1, 1) * scale
                s = jnp.where(mask, s, NEG)
                top = jnp.max(s, -1, keepdims=True)
                e = jnp.exp(s - top)
                total = jnp.sum(e, -1, keepdims=True)
                p = (e / total).astype(jnp.bfloat16)
                lse_ref[2 * t + h, rows_q] = top + jnp.log(total)
                oh = dot(p, v)
                tot = oh if h == 0 else jnp.where(head_lanes(1), oh, tot)
            opk[rows_q, t * 128:t * 128 + 128] = tot.astype(jnp.bfloat16)
    @pl.loop(0, rows // QB)
    def _(i):
        r = pl.ds(pl.multiple_of(i * QB, QB), QB)
        oc = ocol_ref[r]
        pt = jnp.where(oc == lax.broadcasted_iota(jnp.int32, (1, valid), 1), 1.0, 0.0).astype(jnp.bfloat16)
        back = dot(pt, opk[...])
        o_ref[r] = jnp.where(oc >= valid, rot[r, 2 * w:].astype(jnp.float32), back).astype(jnp.bfloat16)

VM = lambda: pl.BlockSpec(memory_space=pltpu.VMEM)
SM = lambda: pl.BlockSpec(memory_space=pltpu.SMEM)

def attn_fwd(qkv, tables, orow, ocol, lengths, valid):
    rows, w3 = qkv.shape
    heads = w3 // 3 // HEAD_DIM
    return pl.pallas_call(functools.partial(attn_fwd_kernel, valid),
        out_shape=(jax.ShapeDtypeStruct((rows, w3 // 3), jnp.bfloat16), jax.ShapeDtypeStruct((valid, w3), jnp.bfloat16), jax.ShapeDtypeStruct((heads, valid, 1), jnp.float32)),
        in_specs=[VM()] * 6 + [SM()], out_specs=(VM(), VM(), VM()),
        scratch_shapes=[pltpu.VMEM((rows, w3), jnp.bfloat16), pltpu.VMEM((valid, w3 // 3), jnp.bfloat16)],
        compiler_params=pltpu.CompilerParams(vmem_limit_bytes=40 << 20))(qkv, *tables, orow, ocol, lengths)

def attn_bwd_kernel(valid, pk_ref, do_ref, lse_ref, c_ref, s1_ref, s2_ref, orow_ref, ocol_ref, len_ref, g_ref, b_ref, dpk, dq, dk, dv, gpk):
    rows, w = do_ref.shape
    nseg = len_ref.shape[1]
    scale = HEAD_DIM ** -0.5
    @pl.loop(0, valid // QB)
    def _(i):
        r = pl.ds(pl.multiple_of(i * QB, QB), QB)
        p = (lax.broadcasted_iota(jnp.int32, (QB, 1), 0) + i * QB == orow_ref[...])
        dpk[r] = dot(jnp.where(p, 1.0, 0.0).astype(jnp.bfloat16), do_ref[...]).astype(jnp.bfloat16)
        dk[r] = jnp.zeros((QB, w), jnp.float32)
        dv[r] = jnp.zeros((QB, w), jnp.float32)
    for qb in range(valid // QB):
        keys = (qb + 1) * QB
        rows_q = slice(qb * QB, qb * QB + QB)
        mask = block_mask(qb, len_ref, nseg)
        for t in range(w // 128):
            ct = slice(t * 128, t * 128 + 128)
            q = pk_ref[rows_q, ct]
            k = pk_ref[0:keys, w + t * 128:w + t * 128 + 128]
            v = pk_ref[0:keys, 2 * w + t * 128:2 * w + t * 128 + 128]
            d = dpk[rows_q, ct]
            tq = None
            for h in range(2):
                hl = head_lanes(h)
                qh = jnp.where(hl, q, jnp.zeros_like(q))
                dh = jnp.where(hl, d, jnp.zeros_like(d))
                s = dot(qh, k, 1, 1) * scale
                s = jnp.where(mask, s, NEG)
                p = jnp.exp(s - lse_ref[2 * t + h, rows_q])
                dp = dot(dh, v, 1, 1)
                inner = jnp.sum(p * dp, -1, keepdims=True)
                ds = (p * (dp - inner)).astype(jnp.bfloat16)
                dv[0:keys, ct] += dot(p.astype(jnp.bfloat16), dh, 0, 0)
                dk[0:keys, ct] += dot(ds, qh, 0, 0)
                qp = dot(ds, k)
                tq = qp if h == 0 else jnp.where(head_lanes(1), qp, tq)
            dq[rows_q, ct] = tq
    @pl.loop(0, valid // QB)
    def _(i):
        r = pl.ds(pl.multiple_of(i * QB, QB), QB)
        c, s1, s2 = c_ref[r], s1_ref[r], s2_ref[r]
        for t in range(w // 128):
            ct = slice(t * 128, t * 128 + 128)
            for j, src in ((0, dq), (1, dk)):
                x = (src[r, ct] * scale).astype(jnp.bfloat16).astype(jnp.float32)
                gpk[r, j * w + t * 128:j * w + t * 128 + 128] = turn(x, c, s1, s2, -1.0).astype(jnp.bfloat16)
            gpk[r, 2 * w + t * 128:2 * w + t * 128 + 128] = dv[r, ct].astype(jnp.bfloat16)
    b_ref[...] = jnp.zeros_like(b_ref)
    @pl.loop(0, rows // QB)
    def _(i):
        r = pl.ds(pl.multiple_of(i * QB, QB), QB)
        oc = ocol_ref[r]
        pt = jnp.where(oc == lax.broadcasted_iota(jnp.int32, (1, valid), 1), 1.0, 0.0).astype(jnp.bfloat16)
        back = dot(pt, gpk[...])
        pad = jnp.where(oc >= valid, do_ref[r].astype(jnp.float32), 0.0)
        back = jnp.concatenate([back[:, :2 * w], back[:, 2 * w:] + pad], 1)
        g_ref[r] = back.astype(jnp.bfloat16)
        b_ref[...] += jnp.sum(back, 0, keepdims=True)

def attn_bwd(pk, do, lse, tables, orow, ocol, lengths):
    rows, w = do.shape
    valid = pk.shape[0]
    F = lambda c: pltpu.VMEM((valid, c), jnp.float32)
    return pl.pallas_call(functools.partial(attn_bwd_kernel, valid),
        out_shape=(jax.ShapeDtypeStruct((rows, 3 * w), jnp.bfloat16), jax.ShapeDtypeStruct((1, 3 * w), jnp.float32)),
        in_specs=[VM()] * 8 + [SM()], out_specs=(VM(), VM()),
        scratch_shapes=[pltpu.VMEM((valid, w), jnp.bfloat16), F(w), F(w), F(w), pltpu.VMEM((valid, 3 * w), jnp.bfloat16)],
        compiler_params=pltpu.CompilerParams(vmem_limit_bytes=48 << 20))(pk, do, lse, *tables, orow, ocol, lengths)

def rotary_tables(rel):
    half = ROT // 2
    d = jnp.arange(128, dtype=jnp.int32) % HEAD_DIM
    freq = 10000.0 ** (-2.0 * (d % half).astype(jnp.float32) / ROT)
    angle = rel[:, None] * freq[None, :]
    c, s = jnp.cos(angle), jnp.sin(angle)
    return (jnp.where(d < ROT, c, 1.0), jnp.where(d < half, -s, 0.0), jnp.where((d >= half) & (d < ROT), s, 0.0))

def a2a_kernel(x_ref, o_ref, own, send, recv):
    s, f, z, y = where_am_i()
    bar = pltpu.get_barrier_semaphore()
    for k in range(1, 8):
        pl.semaphore_signal(bar, inc=1, device_id=(peer(s, k), f), device_id_type=MESH)
    pl.semaphore_wait(bar, 7)
    mine = pltpu.make_async_copy(x_ref.at[s], o_ref.at[s], own)
    mine.start()
    def piece(k):
        t = peer(s, k)
        return remote(x_ref.at[t], o_ref.at[s], send.at[k], recv.at[k], (t, f))
    for k in reversed(range(1, 8)): piece(k).start()
    mine.wait()
    for k in reversed(range(1, 8)):
        piece(k).wait_recv()
        piece(k).wait_send()

def exchange_rows(x, cid):
    D = pltpu.SemaphoreType.DMA
    return pl.pallas_call(a2a_kernel, out_shape=jax.ShapeDtypeStruct(x.shape, x.dtype), in_specs=[VM()], out_specs=VM(),
        scratch_shapes=[D, D((8,)), D((8,))],
        compiler_params=pltpu.CompilerParams(collective_id=cid, has_side_effects=True))(x)

def sum_kernel(x_ref, o_ref, got, send, recv):
    s, f, z, y = where_am_i()
    me = s * 4 + f
    bar = pltpu.get_barrier_semaphore()
    def dev(i): return (i // 4, i % 4)
    @pl.loop(1, 32)
    def _(k):
        pl.semaphore_signal(bar, inc=1, device_id=dev((me + k) % 32), device_id_type=MESH)
    pl.semaphore_wait(bar, 31)
    def piece(k):
        i = (me + k) % 32
        return remote(x_ref.at[i], got.at[k], send.at[k], recv.at[k], dev(i))
    @pl.loop(1, 32)
    def _(k): piece(k).start()
    @pl.loop(1, 32)
    def _(k):
        piece(k).wait_recv()
        piece(k).wait_send()
    o_ref[...] = x_ref[me]
    @pl.loop(1, 32)
    def _(k): o_ref[...] += got[k]

def sum_parts(x, cid):
    D = pltpu.SemaphoreType.DMA
    return pl.pallas_call(sum_kernel, out_shape=jax.ShapeDtypeStruct(x.shape[1:], x.dtype), in_specs=[VM()], out_specs=VM(),
        scratch_shapes=[pltpu.VMEM(x.shape, x.dtype), D((32,)), D((32,))],
        compiler_params=pltpu.CompilerParams(collective_id=cid, has_side_effects=True))(x)


def line_body(
    hidden_in,
    ln1_gain,
    ln1_bias,
    qkv_weight,
    qkv_bias,
    out_weight,
    ln2_gain,
    ln2_bias,
    gate_weight,
    up_weight,
    down_weight,
    seq_lengths,
    deal_order,
    out_grad,
):
    rows = hidden_in.shape[1]
    width = hidden_in.shape[2]
    nseq = lax.axis_size("seq")
    nfsdp = lax.axis_size("fsdp")
    lw = width // nseq
    part = qkv_weight.shape[0]
    ff = gate_weight.shape[1]
    lf = ff // nseq
    both = ("seq", "fsdp")
    seq_at, fsdp_at = lax.axis_index("seq"), lax.axis_index("fsdp")
    stream = hidden_in[0].astype(jnp.float32)
    cotangent = out_grad[0].astype(jnp.float32)
    order = deal_order[0]
    lengths = seq_lengths[0]
    group_rows = order.shape[0]
    valid_rows = group_rows * 5 // 8
    orow, ocol = order[None, :], order[:, None]
    local_pos = lax.dynamic_slice_in_dim(order, seq_at * rows, rows)
    valid = (local_pos < valid_rows).astype(jnp.float32)[:, None]
    dealt_seg, dealt_start = segment_of(order, lengths)
    dealt_tables = rotary_tables((order - dealt_start).astype(jnp.float32))
    packed_pos = jnp.arange(valid_rows, dtype=jnp.int32)
    packed_seg, packed_start = segment_of(packed_pos, lengths)
    packed_tables = rotary_tables((packed_pos - packed_start).astype(jnp.float32))

    def column_parts(weights):
        views = [w.reshape(part, nseq, -1) for w in weights]
        return jnp.concatenate(views, 2).transpose(1, 0, 2)

    def full_columns(weights, cid):
        return column_gather(column_parts(weights), cid).reshape(width, -1)

    norms = lax.all_gather(
        jnp.stack([ln1_gain, ln1_bias, ln2_gain, ln2_bias, *qkv_bias]), both, axis=1, tiled=True
    )
    gain1, shift1, gain2, shift2 = norms[:4].astype(jnp.float32)
    qkv_shift = lax.dynamic_slice_in_dim(norms[4:], seq_at * lw, lw, 1)
    qkv_shift = qkv_shift.reshape(-1).astype(jnp.float32)

    stream_full = all_gather_rows(hidden_in[0], 1).reshape(group_rows, width)
    qkv_parts = qkv_weight.reshape(part, 3, nseq, lw).transpose(2, 0, 1, 3).reshape(nseq, part, -1)
    qkv_w = column_gather(qkv_parts, 2).reshape(width, 3 * lw)
    normed_full, _ = normalize(stream_full.astype(jnp.float32))
    first_in = (normed_full * gain1 + shift1).astype(jnp.bfloat16)
    normed1, rstd1 = normalize(stream)
    qkv = times(first_in, qkv_w) + qkv_shift
    mixed, packed, lse = attn_fwd(qkv, dealt_tables, orow, ocol, seq_lengths, valid_rows)
    heads_out = exchange_rows(mixed.reshape(nseq, rows, lw), 3)
    heads_out = heads_out.transpose(1, 0, 2).reshape(rows, width)
    out_w = lax.all_gather(out_weight, both, axis=0, tiled=True)
    out_rows = lax.all_gather(out_weight, "fsdp", axis=0, tiled=True)
    down_w = lax.all_gather(down_weight, "fsdp", axis=0, tiled=True)
    wide_w = full_columns([gate_weight, up_weight], 4)
    attn = times(heads_out, out_w)
    resid = stream + attn
    normed2, rstd2 = normalize(resid)
    second_local = (normed2 * gain2 + shift2).astype(jnp.bfloat16)
    second_in = all_gather_rows(second_local, 5).reshape(group_rows, width)
    mlp_grad = all_gather_rows(out_grad[0], 6).reshape(group_rows, width)
    wide = times(second_in, wide_w)
    gate, upper = wide[:, :lf], wide[:, lf:]
    hidden, sigma = mlp_forward(gate, upper)
    mlp_part = times(hidden, down_w).astype(jnp.bfloat16).reshape(nseq, rows, width)
    hidden_grad = times_transposed(mlp_grad, down_w)
    wide_act = jnp.concatenate(mlp_backward(hidden_grad, gate, upper, sigma), 1)
    second_part = times_transposed(wide_act, wide_w).astype(jnp.bfloat16)
    second_grad = reduce_scatter_rows(second_part.reshape(nseq, rows, width), 7)
    resid_part, gain2_grad, shift2_grad = norm_back(second_grad, normed2, rstd2, gain2)
    resid_grad = cotangent + resid_part
    attn_grad = all_gather_rows(resid_grad.astype(jnp.bfloat16), 8).reshape(group_rows, width)
    mixed_grad = times_transposed(attn_grad, out_rows).astype(jnp.bfloat16)
    qkv_act, bias_sums = attn_bwd(packed, mixed_grad, lse, packed_tables, orow, ocol, seq_lengths)
    first_part = times_transposed(qkv_act, qkv_w).astype(jnp.bfloat16)
    first_grad = reduce_scatter_rows(first_part.reshape(nseq, rows, width), 9)
    input_part, gain1_grad, shift1_grad = norm_back(first_grad, normed1, rstd1, gain1)
    input_grad = resid_grad + input_part

    mlp = reduce_scatter_rows(mlp_part, 10)
    result = resid + mlp

    def column_shard(left, right, cid):
        grad = outer(left, right).astype(jnp.bfloat16).reshape(nseq, nfsdp, part, -1)
        return column_reduce(grad, cid).astype(jnp.float32)

    def row_shard(left, right, cid):
        grad = outer(left, right).astype(jnp.bfloat16).reshape(1, nfsdp, -1, width)
        return column_reduce(grad, cid, False)[0]

    down_grad = row_shard(hidden, mlp_grad, 11)
    wide_grad = column_shard(second_in, wide_act, 12)
    gate_grad = wide_grad[:, :, :lf].transpose(1, 0, 2).reshape(part, ff)
    up_grad = wide_grad[:, :, lf:].transpose(1, 0, 2).reshape(part, ff)
    out_grad_w = row_shard(mixed, attn_grad, 13)
    qkv_grad = column_shard(first_in, qkv_act, 14)
    qkv_grad = qkv_grad.reshape(nseq, part, 3, lw).transpose(1, 2, 0, 3).reshape(part, 3 * width)

    vectors = jnp.stack([gain1_grad, shift1_grad, gain2_grad, shift2_grad])
    vectors = vectors.reshape(4, nseq * nfsdp, part).transpose(1, 0, 2).reshape(-1, 2, 128)
    sums = jnp.stack(
        [
            jnp.sum(valid * result * result),
            jnp.sum(valid * attn * attn),
            jnp.sum(valid * mlp * mlp),
        ]
    )
    sums = jnp.broadcast_to(jnp.pad(sums, (0, 125)), (nseq * nfsdp, 1, 128))
    bias = bias_sums.reshape(3, nfsdp, part).transpose(1, 0, 2).reshape(nfsdp, 3 * part)
    bias = jnp.pad(bias, ((0, 0), (0, 64))).reshape(1, nfsdp, 2, 128)
    here = (jnp.arange(nseq) == seq_at)[:, None, None, None]
    bias = jnp.where(here, bias, 0.0).reshape(-1, 2, 128)
    message = jnp.concatenate([vectors, sums, bias, jnp.zeros_like(vectors), sums], 1)
    total = sum_parts(message, 15)
    count = valid_rows * nfsdp * width
    rms = jnp.sqrt(total[2, :3] / count)
    shards = total[:2].reshape(4, part)
    qkv_bias_grad = total[3:5].reshape(4, part)[:3]
    return (
        result.astype(jnp.bfloat16)[None],
        input_grad[None],
        shards[0],
        shards[1],
        qkv_grad,
        qkv_bias_grad,
        out_grad_w,
        shards[2],
        shards[3],
        gate_grad,
        up_grad,
        down_grad,
        rms,
    )


def solution(mesh):
    in_specs = (
        P("fsdp", "seq", None),
        P(("seq", "fsdp")),
        P(("seq", "fsdp")),
        P(("seq", "fsdp"), None),
        P(None, ("seq", "fsdp")),
        P(("seq", "fsdp"), None),
        P(("seq", "fsdp")),
        P(("seq", "fsdp")),
        P(("seq", "fsdp"), None),
        P(("seq", "fsdp"), None),
        P(("seq", "fsdp"), None),
        P("fsdp", None),
        P("fsdp", None),
        P("fsdp", "seq", None),
    )
    out_specs = (
        P("fsdp", "seq", None),
        P("fsdp", "seq", None),
        P(("seq", "fsdp")),
        P(("seq", "fsdp")),
        P(("seq", "fsdp"), None),
        P(None, ("seq", "fsdp")),
        P(("seq", "fsdp"), None),
        P(("seq", "fsdp")),
        P(("seq", "fsdp")),
        P(("seq", "fsdp"), None),
        P(("seq", "fsdp"), None),
        P(("seq", "fsdp"), None),
        P(),
    )
    line = dict(mesh.shape) == {"seq": 8, "fsdp": 4}
    return jax.shard_map(
        line_body if line else body,
        mesh=mesh,
        in_specs=in_specs,
        out_specs=out_specs,
        check_vma=False,
    )
```

```python
import functools

import jax
import jax.numpy as jnp
from jax import lax
from jax.experimental import pallas as pl
from jax.experimental.pallas import tpu as pltpu
from jax.sharding import PartitionSpec as P

HEAD_DIM = 64
ROT = 16


EPS = 1e-05


def normalize(values):
    center = values - jnp.mean(values, -1, keepdims=True)
    spread = jnp.mean(center * center, -1, keepdims=True)
    rstd = lax.rsqrt(spread + EPS)
    return (center * rstd, rstd)


def norm_back(grad, normed, rstd, gain):
    scaled = grad * gain
    inner = (
        scaled
        - jnp.mean(scaled, -1, keepdims=True)
        - normed * jnp.mean(scaled * normed, -1, keepdims=True)
    )
    return (rstd * inner, jnp.sum(grad * normed, 0), jnp.sum(grad, 0))


def segment_of(pos, lengths):
    nseg = lengths.shape[0]
    ends = jnp.cumsum(lengths)
    seg = jnp.sum((pos[:, None] >= ends[None, :]).astype(jnp.int32), 1)
    starts = jnp.concatenate([jnp.zeros((1,), jnp.int32), ends[:-1]])
    start = jnp.sum(
        jnp.where(seg[:, None] == jnp.arange(nseg, dtype=jnp.int32)[None, :], starts[None, :], 0), 1
    )
    start = jnp.where(seg < nseg, start, pos)
    return (seg, start)


def rotate(values, rel, sign):
    count = values.shape[0]
    view = values.reshape(count, -1, HEAD_DIM)
    half = ROT // 2
    freq = 10000.0 ** (-2.0 * jnp.arange(half, dtype=jnp.float32) / ROT)
    angle = rel[:, None] * freq[None, :]
    cosine = jnp.cos(angle)[:, None, :]
    sine = jnp.sin(angle)[:, None, :]
    first = view[..., :half]
    second = view[..., half:ROT]
    turned = jnp.concatenate(
        [
            first * cosine - sign * second * sine,
            second * cosine + sign * first * sine,
            view[..., ROT:],
        ],
        -1,
    )
    return turned.reshape(count, -1)


def outer(left, right):
    return lax.dot_general(
        left, right, (((0,), (0,)), ((), ())), preferred_element_type=jnp.float32
    )


def times(left, right):
    return jnp.dot(left, right, preferred_element_type=jnp.float32)


def times_transposed(left, right):
    return lax.dot_general(
        left, right, (((1,), (1,)), ((), ())), preferred_element_type=jnp.float32
    )


def mlp_forward(gate, upper):
    sigma = jax.nn.sigmoid(gate)
    return ((gate * sigma * upper).astype(jnp.bfloat16), sigma)


def mlp_backward(hidden_grad, gate, upper, sigma):
    up_act = (hidden_grad * gate * sigma).astype(jnp.bfloat16)
    gate_act = (hidden_grad * upper * sigma * (1.0 + gate * (1.0 - sigma))).astype(jnp.bfloat16)
    return (gate_act, up_act)


def body(
    hidden_in,
    ln1_gain,
    ln1_bias,
    qkv_weight,
    qkv_bias,
    out_weight,
    ln2_gain,
    ln2_bias,
    gate_weight,
    up_weight,
    down_weight,
    seq_lengths,
    deal_order,
    out_grad,
):
    rows = hidden_in.shape[1]
    width = hidden_in.shape[2]
    nseq = lax.axis_size("seq")
    nfsdp = lax.axis_size("fsdp")
    local_width = width // nseq
    part = qkv_weight.shape[0]
    ff = gate_weight.shape[1]
    local_ff = ff // nseq
    stream = hidden_in[0].astype(jnp.float32)
    cotangent = out_grad[0].astype(jnp.float32)
    order = deal_order[0]
    lengths = seq_lengths[0]
    nseg = lengths.shape[0]
    group_rows = order.shape[0]
    valid_rows = group_rows * 5 // 8
    longest = valid_rows * 4 // 5
    blk = min(512, group_rows)
    keys = min(group_rows, longest + blk)
    nblocks = group_rows // blk
    scale = HEAD_DIM ** (-0.5)
    local_pos = lax.dynamic_slice_in_dim(order, lax.axis_index("seq") * rows, rows)
    valid = (local_pos < valid_rows).astype(jnp.float32)[:, None]
    dealt_seg, dealt_start = segment_of(order, lengths)
    rel = (order - dealt_start).astype(jnp.float32)
    inverse = (
        jnp.zeros((group_rows,), jnp.int32).at[order].set(jnp.arange(group_rows, dtype=jnp.int32))
    )
    seg_p, start_p = segment_of(jnp.arange(group_rows, dtype=jnp.int32), lengths)

    def gather_rows(values):
        return lax.all_gather(values, "seq", axis=0, tiled=True)

    def scatter_rows(partial):
        return lax.psum_scatter(
            partial.astype(jnp.bfloat16), "seq", scatter_dimension=0, tiled=True
        ).astype(jnp.float32)

    def column_slice(weight, blocks):
        cols = weight.shape[1] // (blocks * nseq)
        view = weight.reshape(part, blocks, nseq, cols).transpose(2, 0, 1, 3)
        mine = lax.all_to_all(
            view.reshape(nseq * part, blocks * cols), "seq", split_axis=0, concat_axis=0, tiled=True
        )
        full = lax.all_gather(mine.reshape(nseq, part, blocks * cols), "fsdp", axis=1)
        return full.reshape(width, blocks * cols)

    def row_slice(weight):
        return lax.all_gather(weight, "fsdp", axis=0, tiled=True)

    def column_shard(grad, blocks):
        cols = grad.shape[1] // blocks
        view = grad.astype(jnp.bfloat16).reshape(nseq, nfsdp, part, blocks * cols)
        mine = lax.psum_scatter(view.transpose(1, 0, 2, 3), "fsdp", scatter_dimension=0)
        got = lax.all_to_all(
            mine.reshape(nseq * part, blocks * cols), "seq", split_axis=0, concat_axis=0, tiled=True
        )
        view = got.reshape(nseq, part, blocks, cols).transpose(1, 2, 0, 3)
        return view.reshape(part, -1).astype(jnp.float32)

    def row_shard(grad):
        return lax.psum_scatter(
            grad.astype(jnp.bfloat16), "fsdp", scatter_dimension=0, tiled=True
        ).astype(jnp.float32)

    def to_pack(values):
        heads_here = values.shape[1] // HEAD_DIM
        return values[inverse].reshape(group_rows, heads_here, HEAD_DIM)

    def window(index, packed):
        query_p, key_p, value_p = packed
        first = index * blk
        key_first = jnp.clip(jnp.minimum(start_p[first], group_rows - keys), 0, group_rows - keys)
        qpos = first + jnp.arange(blk, dtype=jnp.int32)
        kpos = key_first + jnp.arange(keys, dtype=jnp.int32)
        qseg = lax.dynamic_slice_in_dim(seg_p, first, blk)
        kseg = lax.dynamic_slice_in_dim(seg_p, key_first, keys)
        allowed = (qseg[:, None] == kseg[None, :]) & (qseg[:, None] < nseg) & (
            kpos[None, :] <= qpos[:, None]
        ) | (kpos[None, :] == qpos[:, None])
        qblock = lax.dynamic_slice_in_dim(query_p, first, blk)
        kblock = lax.dynamic_slice_in_dim(key_p, key_first, keys)
        vblock = lax.dynamic_slice_in_dim(value_p, key_first, keys)
        scores = (
            jnp.einsum("qhd,khd->hqk", qblock, kblock, preferred_element_type=jnp.float32) * scale
        )
        scores = jnp.where(allowed[None], scores, -1e30)
        return (first, key_first, qblock, kblock, vblock, scores)

    both = ("seq", "fsdp")
    norms = lax.all_gather(
        jnp.stack([ln1_gain, ln1_bias, ln2_gain, ln2_bias, *qkv_bias]), both, axis=1, tiled=True
    )
    gain1, shift1, gain2, shift2 = norms[:4].astype(jnp.float32)
    qkv_shift = lax.dynamic_slice_in_dim(
        norms[4:], lax.axis_index("seq") * local_width, local_width, 1
    )
    qkv_shift = qkv_shift.reshape(-1).astype(jnp.float32)

    normed1, rstd1 = normalize(stream)
    first_local = (normed1 * gain1 + shift1).astype(jnp.bfloat16)
    first_in = gather_rows(first_local)
    qkv_w = column_slice(qkv_weight, 3)
    qkv = times(first_in, qkv_w) + qkv_shift
    query = rotate(qkv[:, :local_width], rel, 1.0).astype(jnp.bfloat16)
    keyset = rotate(qkv[:, local_width : 2 * local_width], rel, 1.0).astype(jnp.bfloat16)
    valueset = qkv[:, 2 * local_width :].astype(jnp.bfloat16)
    packed = (to_pack(query), to_pack(keyset), to_pack(valueset))

    def attend_block(index):
        first, key_first, qblock, kblock, vblock, scores = window(index, packed)
        top = jnp.max(scores, -1, keepdims=True)
        expo = jnp.exp(scores - top)
        total = jnp.sum(expo, -1, keepdims=True)
        probs = (expo / total).astype(jnp.bfloat16)
        mixed = jnp.einsum("hqk,khd->qhd", probs, vblock, preferred_element_type=jnp.float32)
        return (mixed.astype(jnp.bfloat16), (top + jnp.log(total))[..., 0])

    mixed_all, lse_all = lax.map(attend_block, jnp.arange(nblocks, dtype=jnp.int32))
    mixed = mixed_all.reshape(group_rows, -1)[order]
    heads_out = lax.all_to_all(mixed, "seq", split_axis=0, concat_axis=1, tiled=True)
    out_w = lax.all_gather(out_weight, both, axis=0, tiled=True)
    out_rows = row_slice(out_weight)
    attn = times(heads_out, out_w)
    resid = stream + attn
    normed2, rstd2 = normalize(resid)
    second_in = gather_rows((normed2 * gain2 + shift2).astype(jnp.bfloat16))
    gate_w = column_slice(gate_weight, 1)
    up_w = column_slice(up_weight, 1)
    down_w = row_slice(down_weight)
    gate = times(second_in, gate_w)
    upper = times(second_in, up_w)
    hidden, sigma = mlp_forward(gate, upper)
    mlp = scatter_rows(times(hidden, down_w))
    result = resid + mlp

    mlp_grad = gather_rows(out_grad[0])
    hidden_grad = times_transposed(mlp_grad, down_w)
    gate_act, up_act = mlp_backward(hidden_grad, gate, upper, sigma)
    second_grad = scatter_rows(times_transposed(gate_act, gate_w) + times_transposed(up_act, up_w))
    down_grad = row_shard(outer(hidden, mlp_grad))
    gate_grad = column_shard(outer(second_in, gate_act), 1)
    up_grad = column_shard(outer(second_in, up_act), 1)
    resid_part, gain2_grad, shift2_grad = norm_back(second_grad, normed2, rstd2, gain2)
    resid_grad = cotangent + resid_part

    attn_grad = gather_rows(resid_grad.astype(jnp.bfloat16))
    out_grad_w = row_shard(outer(mixed, attn_grad))
    mixed_grad_p = to_pack(times_transposed(attn_grad, out_rows).astype(jnp.bfloat16))

    def back_block(index, carry):
        query_acc, key_acc, value_acc = carry
        first, key_first, qblock, kblock, vblock, scores = window(index, packed)
        probs = jnp.exp(scores - lse_all[index][:, :, None])
        dblock = lax.dynamic_slice_in_dim(mixed_grad_p, first, blk)
        value_part = jnp.einsum(
            "hqk,qhd->khd", probs.astype(jnp.bfloat16), dblock, preferred_element_type=jnp.float32
        )
        prob_grad = jnp.einsum("qhd,khd->hqk", dblock, vblock, preferred_element_type=jnp.float32)
        inner = jnp.sum(probs * prob_grad, -1, keepdims=True)
        score_grad = (probs * (prob_grad - inner)).astype(jnp.bfloat16)
        query_part = (
            jnp.einsum("hqk,khd->qhd", score_grad, kblock, preferred_element_type=jnp.float32)
            * scale
        )
        key_part = (
            jnp.einsum("hqk,qhd->khd", score_grad, qblock, preferred_element_type=jnp.float32)
            * scale
        )
        query_acc = lax.dynamic_update_slice_in_dim(query_acc, query_part, first, 0)
        key_old = lax.dynamic_slice_in_dim(key_acc, key_first, keys)
        key_acc = lax.dynamic_update_slice_in_dim(key_acc, key_old + key_part, key_first, 0)
        value_old = lax.dynamic_slice_in_dim(value_acc, key_first, keys)
        value_acc = lax.dynamic_update_slice_in_dim(value_acc, value_old + value_part, key_first, 0)
        return (query_acc, key_acc, value_acc)

    zeros = jnp.zeros(packed[0].shape, jnp.float32)
    query_acc, key_acc, value_acc = lax.fori_loop(0, nblocks, back_block, (zeros, zeros, zeros))

    def to_dealt(values):
        return values.astype(jnp.bfloat16).reshape(group_rows, -1)[order]

    qkv_act = jnp.concatenate(
        [
            rotate(to_dealt(query_acc).astype(jnp.float32), rel, -1.0).astype(jnp.bfloat16),
            rotate(to_dealt(key_acc).astype(jnp.float32), rel, -1.0).astype(jnp.bfloat16),
            to_dealt(value_acc),
        ],
        1,
    )
    first_grad = scatter_rows(times_transposed(qkv_act, qkv_w))
    qkv_grad = column_shard(outer(first_in, qkv_act), 3)
    qkv_bias_grad = lax.psum_scatter(
        jnp.sum(qkv_act.astype(jnp.float32), 0).reshape(3, nfsdp, -1),
        "fsdp",
        scatter_dimension=1,
    )
    input_part, gain1_grad, shift1_grad = norm_back(first_grad, normed1, rstd1, gain1)
    input_grad = resid_grad + input_part

    norm_grads = lax.psum(
        (
            gain1_grad,
            shift1_grad,
            gain2_grad,
            shift2_grad,
            jnp.sum(valid * result * result),
            jnp.sum(valid * attn * attn),
            jnp.sum(valid * mlp * mlp),
        ),
        both,
    )
    count = valid_rows * nfsdp * width
    rms = jnp.sqrt(jnp.stack(norm_grads[4:]) / count)
    mine = (lax.axis_index("seq") * nfsdp + lax.axis_index("fsdp")) * part
    norm_shards = [lax.dynamic_slice_in_dim(value, mine, part) for value in norm_grads[:4]]
    return (
        result.astype(jnp.bfloat16)[None],
        input_grad[None],
        norm_shards[0],
        norm_shards[1],
        qkv_grad,
        qkv_bias_grad,
        out_grad_w,
        norm_shards[2],
        norm_shards[3],
        gate_grad,
        up_grad,
        down_grad,
        rms,
    )


MESH = pl.DeviceIdType.MESH
QB = 128
NEG = -1e30
CH = 2
VMEM_SPEC = pl.BlockSpec(memory_space=pltpu.VMEM)
SMEM_SPEC = pl.BlockSpec(memory_space=pltpu.SMEM)
ANY_SPEC = pl.BlockSpec(memory_space=pl.ANY)
DMA = pltpu.SemaphoreType.DMA


def comm_params(collective, limit=48):
    return pltpu.CompilerParams(
        collective_id=collective, has_side_effects=True, vmem_limit_bytes=limit << 20
    )


def where_am_i():
    s = lax.axis_index("seq")
    f = lax.axis_index("fsdp")
    return s, f, s // 2, s % 2


def remote(src, dst, send, recv, device):
    return pltpu.make_async_remote_copy(
        src, dst, send, recv, device_id=device, device_id_type=MESH
    )


def flip(v, bit):
    return v + bit * (1 - 2 * ((v // bit) % 2))


def peer(s, k):
    for bit in (1, 2, 4):
        if k & bit:
            s = flip(s, bit)
    return s


def dealer(i):
    return (i // 4, i % 4)


def greet_all(s, f):
    bar = pltpu.get_barrier_semaphore()
    me = s * 4 + f

    @pl.loop(1, 32)
    def _(k):
        pl.semaphore_signal(bar, inc=1, device_id=dealer((me + k) % 32), device_id_type=MESH)

    pl.semaphore_wait(bar, 31)


def greet_line(s, f, z, y):
    bar = pltpu.get_barrier_semaphore()
    pl.semaphore_signal(bar, inc=1, device_id=(flip(s, 1), f), device_id_type=MESH)

    @pl.when(z > 0)
    def _():
        pl.semaphore_signal(bar, inc=1, device_id=(s - 2, f), device_id_type=MESH)

    @pl.when(z < 3)
    def _():
        pl.semaphore_signal(bar, inc=1, device_id=(s + 2, f), device_id_type=MESH)

    edge = jnp.where((z == 0) | (z == 3), 1, 0)
    pl.semaphore_wait(bar, 3 - edge)


def greet_columns(s, f):
    bar = pltpu.get_barrier_semaphore()
    for k in range(1, 8):
        pl.semaphore_signal(bar, inc=1, device_id=(peer(s, k), f), device_id_type=MESH)
    pl.semaphore_signal(bar, inc=1, device_id=(s, flip(f, 1)), device_id_type=MESH)
    pl.semaphore_signal(bar, inc=1, device_id=(s, flip(f, 2)), device_id_type=MESH)
    pl.semaphore_wait(bar, 9)


def adder(dst, srcs, step=16):
    @pl.loop(0, dst.shape[0] // step)
    def _(i):
        r = pl.ds(pl.multiple_of(i * step, step), step)
        total = srcs[0][r].astype(jnp.float32)
        for v in srcs[1:]:
            total = total + v[r].astype(jnp.float32)
        dst[r] = total.astype(dst.dtype)


class SeqGather:
    @staticmethod
    def scratch():
        return [DMA, DMA((8,)), DMA((4,)), DMA((4,)), DMA((4,))]

    def __init__(self, x, o, own, recv, sy, su, sd):
        self.x, self.o, self.recv, self.sy, self.su, self.sd = x, o, recv, sy, su, sd
        self.s, self.f, self.z, self.y = where_am_i()
        self.other = flip(self.s, 1)
        self.own = pltpu.make_async_copy(x, o.at[self.s], own)

    def at(self, zb):
        return 2 * zb + self.y

    def ysend(self, zb, src):
        b = self.at(zb)
        return remote(src, self.o.at[b], self.sy.at[zb], self.recv.at[b], (self.other, self.f))

    def usend(self, zb, src):
        b = self.at(zb)
        return remote(src, self.o.at[b], self.su.at[zb], self.recv.at[b], (self.s + 2, self.f))

    def dsend(self, zb, src):
        b = self.at(zb)
        return remote(src, self.o.at[b], self.sd.at[zb], self.recv.at[b], (self.s - 2, self.f))

    def arrived(self, b):
        o = self.o.at[b]
        return remote(o, o, self.sy.at[0], self.recv.at[b], (self.other, self.f))

    def start(self):
        @pl.when(self.z < 3)
        def _():
            self.usend(self.z, self.x).start()

        @pl.when(self.z > 0)
        def _():
            self.dsend(self.z, self.x).start()

        self.ysend(self.z, self.x).start()
        self.own.start()

    def below(self, t, use=None):
        @pl.when(self.z >= t)
        def _():
            zb = self.z - t
            b = self.at(zb)
            self.arrived(b).wait_recv()

            @pl.when(self.z < 3)
            def _():
                self.usend(zb, self.o.at[b]).start()

            self.ysend(zb, self.o.at[b]).start()
            if use is not None:
                use(b)

    def above(self, t, use=None):
        @pl.when(self.z + t <= 3)
        def _():
            zb = self.z + t
            b = self.at(zb)
            self.arrived(b).wait_recv()

            @pl.when(self.z > 0)
            def _():
                self.dsend(zb, self.o.at[b]).start()

            self.ysend(zb, self.o.at[b]).start()
            if use is not None:
                use(b)

    def across(self, t, use=None):
        for sign in (0,) if t == 0 else (-1, 1):
            zb = self.z + sign * t

            @pl.when((zb >= 0) & (zb <= 3))
            def _():
                b = 2 * zb + 1 - self.y
                self.arrived(b).wait_recv()
                if use is not None:
                    use(b)

    def steps(self):
        out = []
        for t in (1, 2, 3):
            out.append(functools.partial(self.below, t))
            out.append(functools.partial(self.above, t))
        return out

    def finish(self):
        self.own.wait()
        for zb in range(4):
            self.ysend(zb, self.x).wait_send()

            @pl.when((self.z < 3) & (zb <= self.z))
            def _():
                self.usend(zb, self.x).wait_send()

            @pl.when((self.z > 0) & (zb >= self.z))
            def _():
                self.dsend(zb, self.x).wait_send()


class SeqReduce:
    @staticmethod
    def scratch(rows, w):
        big = [pltpu.VMEM((4, rows, w), jnp.bfloat16) for _ in range(6)]
        return big + [DMA((4,))] + [DMA((4, CH)) for _ in range(6)]

    def __init__(self, p, o, mine, ybuf, up, down, send_up, send_down, load, ry, ru, rd, sy, su, sd):
        self.p, self.o, self.mine, self.ybuf, self.up, self.down = p, o, mine, ybuf, up, down
        self.send_up, self.send_down, self.load_sem = send_up, send_down, load
        self.ry, self.ru, self.rd, self.sy, self.su, self.sd = ry, ru, rd, sy, su, sd
        self.s, self.f, self.z, self.y = where_am_i()
        self.other = flip(self.s, 1)
        self.ch = p.shape[1] // CH

    def order(self, k):
        a, b, c, d = [3, 2, 1, 0][k], [3, 0, 2, 1][k], [0, 3, 1, 2][k], [0, 1, 2, 3][k]
        z = self.z
        return jnp.where(z == 0, a, jnp.where(z == 1, b, jnp.where(z == 2, c, d)))

    def rows(self, c):
        return pl.ds(c * self.ch, self.ch)

    def ysend(self, zb, c):
        r = self.rows(c)
        src = self.p.at[2 * zb + 1 - self.y, r]
        dst = self.ybuf.at[zb, r]
        return remote(src, dst, self.sy.at[zb, c], self.ry.at[zb, c], (self.other, self.f))

    def load(self, zb):
        src = self.p.at[2 * zb + self.y]
        return pltpu.make_async_copy(src, self.mine.at[zb], self.load_sem.at[zb])

    def usend(self, zb, c):
        r = self.rows(c)
        src, dst = self.send_up.at[zb, r], self.up.at[zb, r]
        return remote(src, dst, self.su.at[zb, c], self.ru.at[zb, c], (self.s + 2, self.f))

    def dsend(self, zb, c):
        r = self.rows(c)
        src, dst = self.send_down.at[zb, r], self.down.at[zb, r]
        return remote(src, dst, self.sd.at[zb, c], self.rd.at[zb, c], (self.s - 2, self.f))

    def start(self):
        for k in range(4):
            zb = self.order(k)
            for c in range(CH):
                self.ysend(zb, c).start()
            self.load(zb).start()

    def step(self, k, c):
        z, zb, r = self.z, self.order(k), self.rows(c)
        if c == 0:
            self.load(zb).wait()
        self.ysend(zb, c).wait_recv()
        a, b = self.mine.at[zb, r], self.ybuf.at[zb, r]
        u, d = self.up.at[zb, r], self.down.at[zb, r]

        @pl.when(zb > z)
        def _():
            @pl.when(z == 0)
            def _():
                adder(self.send_up.at[zb, r], [a, b])

            @pl.when(z > 0)
            def _():
                self.usend(zb, c).wait_recv()
                adder(self.send_up.at[zb, r], [a, b, u])

            self.usend(zb, c).start()

        @pl.when(zb < z)
        def _():
            @pl.when(z == 3)
            def _():
                adder(self.send_down.at[zb, r], [a, b])

            @pl.when(z < 3)
            def _():
                self.dsend(zb, c).wait_recv()
                adder(self.send_down.at[zb, r], [a, b, d])

            self.dsend(zb, c).start()

        @pl.when(zb == z)
        def _():
            @pl.when(z > 0)
            def _():
                self.usend(zb, c).wait_recv()

            @pl.when(z < 3)
            def _():
                self.dsend(zb, c).wait_recv()

            o = self.o.at[r]

            @pl.when(z == 0)
            def _():
                adder(o, [a, b, d])

            @pl.when(z == 3)
            def _():
                adder(o, [a, b, u])

            @pl.when((z > 0) & (z < 3))
            def _():
                adder(o, [a, b, u, d])

    def steps(self):
        return [functools.partial(self.step, k, c) for k in range(4) for c in range(CH)]

    def finish(self):
        for zb in range(4):
            for c in range(CH):
                self.ysend(zb, c).wait_send()

                @pl.when(zb > self.z)
                def _():
                    self.usend(zb, c).wait_send()

                @pl.when(zb < self.z)
                def _():
                    self.dsend(zb, c).wait_send()


class ColGather:
    @staticmethod
    def scratch():
        return [DMA, DMA((8, 4)), DMA((8,)), DMA((8, 2)), DMA((8,))]

    def __init__(self, x, o, own, recv, direct, core, xs):
        self.x, self.o, self.own, self.recv = x, o, own, recv
        self.direct, self.core, self.xs = direct, core, xs
        self.s, self.f, _, _ = where_am_i()
        self.fc, self.fx = flip(self.f, 1), flip(self.f, 2)
        self.fd = flip(self.fc, 2)
        self.mine = pltpu.make_async_copy(x.at[self.s], o.at[self.s, self.f], own)

    def send_direct(self, k):
        s, f, t = self.s, self.f, peer(self.s, k)
        return remote(self.x.at[t], self.o.at[s, f], self.direct.at[k], self.recv.at[s, f], (t, f))

    def send_core(self, k, which, src):
        t, ff = peer(self.s, k), self.f if which == 0 else self.fx
        dst = self.o.at[t, ff]
        return remote(src, dst, self.core.at[k, which], self.recv.at[t, ff], (self.s, self.fc))

    def send_x(self, k, src):
        t = peer(self.s, k)
        dst = self.o.at[t, self.f]
        return remote(src, dst, self.xs.at[k], self.recv.at[t, self.f], (self.s, self.fx))

    def arrived(self, k, ff):
        t = peer(self.s, k)
        o = self.o.at[t, ff]
        return remote(o, o, self.own, self.recv.at[t, ff], (self.s, self.fc))

    def start(self):
        for k in reversed(range(1, 8)):
            self.send_direct(k).start()
        self.send_x(0, self.x.at[self.s]).start()
        self.send_core(0, 0, self.x.at[self.s]).start()
        self.mine.start()

    def step(self, k):
        t = peer(self.s, k)
        self.arrived(k, self.f).wait_recv()
        self.send_x(k, self.o.at[t, self.f]).start()
        self.send_core(k, 0, self.o.at[t, self.f]).start()

    def xstep(self, k):
        t = peer(self.s, k)
        self.arrived(k, self.fx).wait_recv()
        self.send_core(k, 1, self.o.at[t, self.fx]).start()

    def steps(self):
        first = [functools.partial(self.step, k) for k in reversed(range(1, 8))]
        then = [functools.partial(self.xstep, k) for k in (0, 7, 6, 5, 4, 3, 2, 1)]
        return first + then

    def finish(self):
        self.mine.wait()
        for k in range(8):
            self.arrived(k, self.fc).wait_recv()
            self.arrived(k, self.fd).wait_recv()
        for k in range(8):
            if k:
                self.send_direct(k).wait_send()
            self.send_x(k, self.x.at[0]).wait_send()
            self.send_core(k, 0, self.x.at[0]).wait_send()
            self.send_core(k, 1, self.x.at[0]).wait_send()


class ColReduce:
    @staticmethod
    def scratch(r, c):
        def v(*lead):
            return pltpu.VMEM(lead + (8, r, c), jnp.bfloat16)

        return [v(2), v(2), v(), v(), v()] + [DMA((2, 8)) for _ in range(3)] + [DMA((8,)) for _ in range(4)]

    def __init__(self, g, o, ld, cb, hx, xb, ob, ldsem, cs, cr, xs, xr, es, er):
        self.g, self.o, self.ld, self.cb, self.hx, self.xb, self.ob = g, o, ld, cb, hx, xb, ob
        self.ldsem, self.cs, self.cr, self.xs, self.xr, self.es, self.er = ldsem, cs, cr, xs, xr, es, er
        self.s, self.f, _, _ = where_am_i()
        self.fc, self.fx = flip(self.f, 1), flip(self.f, 2)
        self.fd = flip(self.fc, 2)

    def core(self, w, k):
        i = peer(self.s, k)
        src = self.g.at[i, self.fd if w == 0 else self.fc]
        dst = self.cb.at[w, i]
        return remote(src, dst, self.cs.at[w, k], self.cr.at[w, k], (self.s, self.fc))

    def load(self, w, k):
        i = peer(self.s, k)
        src = self.g.at[i, self.fx if w == 0 else self.f]
        return pltpu.make_async_copy(src, self.ld.at[w, i], self.ldsem.at[w, k])

    def xsend(self, k):
        i = peer(self.s, k)
        return remote(self.hx.at[i], self.xb.at[i], self.xs.at[k], self.xr.at[k], (self.s, self.fx))

    def esend(self, k):
        t = peer(self.s, k)
        dst = self.o.at[self.s]
        return remote(self.ob.at[t], dst, self.es.at[k], self.er.at[k], (t, self.f))

    def start(self):
        for w in range(2):
            for k in reversed(range(8)):
                self.core(w, k).start()
                self.load(w, k).start()

    def step(self, k):
        i = peer(self.s, k)
        self.core(0, k).wait_recv()
        self.load(0, k).wait()
        adder(self.hx.at[i], [self.ld.at[0, i], self.cb.at[0, i]])
        self.xsend(k).start()

    def total(self, k):
        i = peer(self.s, k)
        self.core(1, k).wait_recv()
        self.load(1, k).wait()
        self.xsend(k).wait_recv()
        dst = self.ob if k else self.o
        adder(dst.at[i], [self.ld.at[1, i], self.cb.at[1, i], self.xb.at[i]])
        if k:
            self.esend(k).start()

    def steps(self):
        first = [functools.partial(self.step, k) for k in reversed(range(8))]
        then = [functools.partial(self.total, k) for k in reversed(range(8))]
        return first + then

    def finish(self):
        for k in range(8):
            self.core(0, k).wait_send()
            self.core(1, k).wait_send()
            self.xsend(k).wait_send()
            if k:
                self.esend(k).wait_recv()
                self.esend(k).wait_send()


class FsdpGather:
    @staticmethod
    def scratch():
        return [DMA, DMA((4,)), DMA((3,))]

    def __init__(self, x, o, own, recv, send):
        self.x, self.o, self.own, self.recv, self.send = x, o, own, recv, send
        self.s, self.f, _, _ = where_am_i()
        self.fc, self.fx = flip(self.f, 1), flip(self.f, 2)
        self.fd = flip(self.fc, 2)
        self.mine = pltpu.make_async_copy(x, o.at[self.f], own)

    def pass_on(self, n, src, ff, to):
        return remote(src, self.o.at[ff], self.send.at[n], self.recv.at[ff], (self.s, to))

    def arrived(self, ff):
        o = self.o.at[ff]
        return remote(o, o, self.own, self.recv.at[ff], (self.s, self.fc))

    def start(self):
        self.pass_on(0, self.x, self.f, self.fx).start()
        self.pass_on(1, self.x, self.f, self.fc).start()
        self.mine.start()

    def step(self):
        self.arrived(self.fx).wait_recv()
        self.pass_on(2, self.o.at[self.fx], self.fx, self.fc).start()

    def finish(self):
        self.mine.wait()
        self.arrived(self.fc).wait_recv()
        self.arrived(self.fd).wait_recv()
        for n in range(3):
            self.pass_on(n, self.x, self.f, self.fc).wait_send()


class WholeGather:
    @staticmethod
    def scratch():
        return [DMA, DMA((32,)), DMA((4,)), DMA((4,)), DMA((4,)), DMA((4, 2)), DMA((4, 2, 2))]

    def __init__(self, x, o, own, recv, su, sd, sy, sx, sc):
        self.x, self.o, self.own, self.recv = x, o, own, recv
        self.su, self.sd, self.sy, self.sx, self.sc = su, sd, sy, sx, sc
        self.s, self.f, self.z, self.y = where_am_i()
        self.fc, self.fx = flip(self.f, 1), flip(self.f, 2)
        self.fd = flip(self.fc, 2)
        self.me = self.s * 4 + self.f
        self.mine = pltpu.make_async_copy(x, o.at[self.me], own)

    def at(self, zb, yy, ff):
        return (2 * zb + (self.y if yy == 0 else 1 - self.y)) * 4 + ff

    def src(self, b, first):
        return self.x if first else self.o.at[b]

    def up(self, zb, first=False):
        b = self.at(zb, 0, self.f)
        to = (self.s + 2, self.f)
        return remote(self.src(b, first), self.o.at[b], self.su.at[zb], self.recv.at[b], to)

    def down(self, zb, first=False):
        b = self.at(zb, 0, self.f)
        to = (self.s - 2, self.f)
        return remote(self.src(b, first), self.o.at[b], self.sd.at[zb], self.recv.at[b], to)

    def over_y(self, zb, first=False):
        b = self.at(zb, 0, self.f)
        to = (flip(self.s, 1), self.f)
        return remote(self.src(b, first), self.o.at[b], self.sy.at[zb], self.recv.at[b], to)

    def over_x(self, zb, yy, first=False):
        b = self.at(zb, yy, self.f)
        to = (self.s, self.fx)
        return remote(self.src(b, first), self.o.at[b], self.sx.at[zb, yy], self.recv.at[b], to)

    def over_core(self, zb, yy, xx, first=False):
        b = self.at(zb, yy, self.f if xx == 0 else self.fx)
        to = (self.s, self.fc)
        return remote(self.src(b, first), self.o.at[b], self.sc.at[zb, yy, xx], self.recv.at[b], to)

    def arrived(self, b):
        o = self.o.at[b]
        return remote(o, o, self.own, self.recv.at[b], (self.s, self.fc))

    def start(self):
        z = self.z

        @pl.when(z < 3)
        def _():
            self.up(z, True).start()

        @pl.when(z > 0)
        def _():
            self.down(z, True).start()

        self.over_y(z, True).start()
        self.over_x(z, 0, True).start()
        self.over_core(z, 0, 0, True).start()
        self.mine.start()

    def line(self, sign, t):
        zb = self.z + sign * t

        @pl.when((zb >= 0) & (zb <= 3))
        def _():
            self.arrived(self.at(zb, 0, self.f)).wait_recv()
            if sign < 0:

                @pl.when(self.z < 3)
                def _():
                    self.up(zb).start()

            else:

                @pl.when(self.z > 0)
                def _():
                    self.down(zb).start()

            self.over_y(zb).start()
            self.over_x(zb, 0).start()
            self.over_core(zb, 0, 0).start()

    def column(self, sign, t):
        zb = self.z + sign * t

        @pl.when((zb >= 0) & (zb <= 3))
        def _():
            self.arrived(self.at(zb, 1, self.f)).wait_recv()
            self.over_x(zb, 1).start()
            self.over_core(zb, 1, 0).start()

    def side(self, sign, t, yy):
        zb = self.z + sign * t

        @pl.when((zb >= 0) & (zb <= 3))
        def _():
            self.arrived(self.at(zb, yy, self.fx)).wait_recv()
            self.over_core(zb, yy, 1).start()

    def steps(self):
        p = functools.partial
        out = []
        for t in range(4):
            for sign in (-1, 1) if t else (1,):
                if t:
                    out.append(p(self.line, sign, t))
        for t in range(4):
            for sign in (-1, 1) if t else (1,):
                out.append(p(self.column, sign, t))
                out.append(p(self.side, sign, t, 0))
        for t in range(4):
            for sign in (-1, 1) if t else (1,):
                out.append(p(self.side, sign, t, 1))
        return out

    def finish(self):
        self.mine.wait()
        for zb in range(4):
            for yy in range(2):
                self.arrived(self.at(zb, yy, self.fc)).wait_recv()
                self.arrived(self.at(zb, yy, self.fd)).wait_recv()
        for zb in range(4):
            self.over_y(zb).wait_send()

            @pl.when((self.z < 3) & (zb <= self.z))
            def _():
                self.up(zb).wait_send()

            @pl.when((self.z > 0) & (zb >= self.z))
            def _():
                self.down(zb).wait_send()

            for yy in range(2):
                self.over_x(zb, yy).wait_send()
                for xx in range(2):
                    self.over_core(zb, yy, xx).wait_send()


class RowExchange:
    @staticmethod
    def scratch():
        return [DMA, DMA((8,)), DMA((8,))]

    def __init__(self, x, o, own, send, recv):
        self.x, self.o, self.send, self.recv = x, o, send, recv
        self.s, self.f, _, _ = where_am_i()
        self.mine = pltpu.make_async_copy(x.at[self.s], o.at[self.s], own)

    def piece(self, k):
        t = peer(self.s, k)
        dst = self.o.at[self.s]
        return remote(self.x.at[t], dst, self.send.at[k], self.recv.at[k], (t, self.f))

    def start(self):
        for k in reversed(range(1, 8)):
            self.piece(k).start()
        self.mine.start()

    def finish(self):
        self.mine.wait()
        for k in reversed(range(1, 8)):
            self.piece(k).wait_recv()
            self.piece(k).wait_send()


def merged(*lists):
    keyed = []
    for n, items in enumerate(lists):
        keyed += [((i + 0.5) / len(items), n, item) for i, item in enumerate(items)]
    return [item for _, _, item in sorted(keyed, key=lambda v: v[:2])]


def entry_kernel(
    x_ref, p_ref, w_ref, ow_ref, a_ref, wo_ref, g_ref, oo_ref, xs, got, psend, precv, *sems
):
    s, f, z, y = where_am_i()
    me = s * 4 + f
    greet_all(s, f)
    gather = SeqGather(x_ref, xs, *sems[:5])
    slices = ColGather(w_ref, wo_ref, *sems[5:10])
    whole = WholeGather(ow_ref, oo_ref, *sems[10:])

    def param(k):
        i = (me + k) % 32
        return remote(p_ref, got.at[me], psend.at[k], precv.at[k], dealer(i))

    @pl.loop(1, 32)
    def _(k):
        param(k).start()

    gather.start()
    slices.start()
    whole.start()
    got[me] = p_ref[...]

    @pl.loop(1, 32)
    def _(k):
        param(k).wait_recv()

    for i in range(16):
        g_ref[:, i * 128 : i * 128 + 128] = got[2 * i] + got[2 * i + 1]
    step = 16

    def norm(b):
        gain, shift = g_ref[0:1], g_ref[1:2]

        @pl.loop(0, x_ref.shape[0] // step)
        def _(i):
            r = pl.ds(pl.multiple_of(i * step, step), step)
            normed, _ = normalize(xs[b, r].astype(jnp.float32))
            a_ref[b, r] = (normed * gain + shift).astype(jnp.bfloat16)

    gather.own.wait()
    norm(s)
    todo = slices.steps()
    lines = whole.steps()
    for t in (1, 2, 3):
        gather.below(t)
        gather.above(t)
        for item in todo[:3] + lines[:2]:
            item()
        todo, lines = todo[3:], lines[2:]
        gather.across(t - 1, norm)
        for zb in (z - t, z + t):

            @pl.when((zb >= 0) & (zb <= 3))
            def _():
                norm(2 * zb + y)

    for item in todo[:2]:
        item()
    gather.across(3, norm)
    for item in merged(todo[2:], lines):
        item()
    slices.finish()
    whole.finish()

    @pl.loop(1, 32)
    def _(k):
        param(k).wait_send()

    for zb in range(4):
        gather.ysend(zb, x_ref).wait_send()

        @pl.when((z < 3) & (zb <= z))
        def _():
            gather.usend(zb, x_ref).wait_send()

        @pl.when((z > 0) & (zb >= z))
        def _():
            gather.dsend(zb, x_ref).wait_send()


def entry(x, params, weight, rows_weight, collective):
    rows, width = x.shape
    return pl.pallas_call(
        entry_kernel,
        out_shape=(
            jax.ShapeDtypeStruct((8, rows, width), jnp.bfloat16),
            jax.ShapeDtypeStruct((8, 4) + weight.shape[1:], weight.dtype),
            jax.ShapeDtypeStruct((8, width), jnp.float32),
            jax.ShapeDtypeStruct((32,) + rows_weight.shape, rows_weight.dtype),
        ),
        in_specs=[VMEM_SPEC] * 4,
        out_specs=(VMEM_SPEC, ANY_SPEC, VMEM_SPEC, ANY_SPEC),
        scratch_shapes=[
            pltpu.VMEM((8, rows, width), x.dtype),
            pltpu.VMEM((32, 8, 128), jnp.float32),
            DMA((32,)),
            DMA((32,)),
        ]
        + SeqGather.scratch()
        + ColGather.scratch()
        + WholeGather.scratch(),
        compiler_params=comm_params(collective),
    )(x, params, weight, rows_weight)


def gather_kernel(x_ref, o_ref, *sems):
    s, f, z, y = where_am_i()
    greet_line(s, f, z, y)
    task = SeqGather(x_ref, o_ref, *sems)
    task.start()
    for item in task.steps():
        item()
    for t in range(4):
        task.across(t)
    task.finish()


def gather_rows_line(x, collective):
    return pl.pallas_call(
        gather_kernel,
        out_shape=jax.ShapeDtypeStruct((8,) + x.shape, x.dtype),
        in_specs=[VMEM_SPEC],
        out_specs=ANY_SPEC,
        scratch_shapes=SeqGather.scratch(),
        compiler_params=comm_params(collective),
    )(x)


def reduce_kernel(p_ref, o_ref, *scratch):
    s, f, z, y = where_am_i()
    greet_line(s, f, z, y)
    task = SeqReduce(p_ref, o_ref, *scratch)
    task.start()
    for item in task.steps():
        item()
    task.finish()


def reduce_rows_line(p, collective):
    _, rows, width = p.shape
    return pl.pallas_call(
        reduce_kernel,
        out_shape=jax.ShapeDtypeStruct((rows, width), jnp.float32),
        in_specs=[ANY_SPEC],
        out_specs=VMEM_SPEC,
        scratch_shapes=SeqReduce.scratch(rows, width),
        compiler_params=comm_params(collective),
    )(p)


def dot(a, b, ca=1, cb=0):
    return lax.dot_general(a, b, (((ca,), (cb,)), ((), ())), preferred_element_type=jnp.float32)


def starts_of(pos, lengths_ref, nseg):
    start = jnp.zeros_like(pos)
    end = 0
    for i in range(nseg - 1):
        end = end + lengths_ref[0, i]
        start = jnp.where(pos >= end, end, start)
    return start


def head_lanes(h):
    lane = lax.broadcasted_iota(jnp.int32, (1, 128), 1)
    return (lane // HEAD_DIM) == h


def turn(x, c, s1, s2, sign):
    half = ROT // 2
    return x * c + (pltpu.roll(x, 128 - half, 1) * s1 + pltpu.roll(x, half, 1) * s2) * sign


def block_mask(qb, lengths_ref):
    keys = (qb + 1) * QB
    row = qb * QB + lax.broadcasted_iota(jnp.int32, (QB, 1), 0)
    col = lax.broadcasted_iota(jnp.int32, (1, keys), 1)
    return (col >= starts_of(row, lengths_ref, lengths_ref.shape[1])) & (col <= row)


def row_at(i, step=QB):
    return pl.ds(pl.multiple_of(i * step, step), step)


def picks(orow_ref, i):
    p = lax.broadcasted_iota(jnp.int32, (QB, 1), 0) + i * QB == orow_ref[...]
    return jnp.where(p, 1.0, 0.0).astype(jnp.bfloat16)


def puts(oc, valid):
    p = oc == lax.broadcasted_iota(jnp.int32, (1, valid), 1)
    return jnp.where(p, 1.0, 0.0).astype(jnp.bfloat16)


def attend(
    a_ref, w_ref, shift_ref, tables, orow_ref, ocol_ref, len_ref, o_ref, pk_ref, lse_ref, rot, opk
):
    rows, w3 = rot.shape
    w = w3 // 3
    valid = pk_ref.shape[0]
    scale = HEAD_DIM**-0.5
    c_ref, s1_ref, s2_ref = tables

    def project():
        @pl.loop(0, rows // 256)
        def _(i):
            r = row_at(i, 256)
            c, s1, s2 = c_ref[r], s1_ref[r], s2_ref[r]
            qkv = dot(a_ref[r], w_ref[...]) + shift_ref[...]
            for t in range(w3 // 128):
                cols = slice(t * 128, t * 128 + 128)
                x = qkv[:, cols]
                if t < 2 * w // 128:
                    x = turn(x, c, s1, s2, 1.0)
                rot[r, cols] = x.astype(jnp.bfloat16)

    def pack():
        @pl.loop(0, valid // QB)
        def _(i):
            pk_ref[row_at(i)] = dot(picks(orow_ref, i), rot[...]).astype(jnp.bfloat16)

    def block(qb, t):
        keys = (qb + 1) * QB
        rq = slice(qb * QB, qb * QB + QB)
        ct = slice(t * 128, t * 128 + 128)
        mask = block_mask(qb, len_ref)
        q = pk_ref[rq, ct]
        k = pk_ref[0:keys, w + t * 128 : w + t * 128 + 128]
        v = pk_ref[0:keys, 2 * w + t * 128 : 2 * w + t * 128 + 128]
        total = None
        for h in range(2):
            qh = jnp.where(head_lanes(h), q, jnp.zeros_like(q))
            scores = jnp.where(mask, dot(qh, k, 1, 1) * scale, NEG)
            top = jnp.max(scores, -1, keepdims=True)
            expo = jnp.exp(scores - top)
            norm = jnp.sum(expo, -1, keepdims=True)
            probs = (expo / norm).astype(jnp.bfloat16)
            lse_ref[2 * t + h, rq] = top + jnp.log(norm)
            out = dot(probs, v)
            total = out if h == 0 else jnp.where(head_lanes(1), out, total)
        opk[rq, ct] = total.astype(jnp.bfloat16)

    def unpack():
        per = o_ref.shape[1]

        @pl.loop(0, rows // per)
        def _(i):
            r = row_at(i, per)
            oc = ocol_ref[r]
            back = dot(puts(oc, valid), opk[...])
            pad = rot[r, 2 * w :].astype(jnp.float32)
            o_ref[i] = jnp.where(oc >= valid, pad, back).astype(jnp.bfloat16)

    blocks = [
        functools.partial(block, qb, t) for qb in range(valid // QB) for t in range(w // 128)
    ]
    return [project, pack] + blocks + [unpack]


def attend_back(
    pk_ref, do_ref, lse_ref, tables, orow_ref, ocol_ref, len_ref, g_ref, b_ref, dpk, dq, dk, dv, gpk
):
    rows, w = do_ref.shape
    valid = pk_ref.shape[0]
    scale = HEAD_DIM**-0.5
    c_ref, s1_ref, s2_ref = tables

    def pack():
        @pl.loop(0, valid // QB)
        def _(i):
            r = row_at(i)
            dpk[r] = dot(picks(orow_ref, i), do_ref[...]).astype(jnp.bfloat16)
            dk[r] = jnp.zeros((QB, w), jnp.float32)
            dv[r] = jnp.zeros((QB, w), jnp.float32)

    def block(qb, t):
        keys = (qb + 1) * QB
        rq = slice(qb * QB, qb * QB + QB)
        ct = slice(t * 128, t * 128 + 128)
        mask = block_mask(qb, len_ref)
        q, d = pk_ref[rq, ct], dpk[rq, ct]
        k = pk_ref[0:keys, w + t * 128 : w + t * 128 + 128]
        v = pk_ref[0:keys, 2 * w + t * 128 : 2 * w + t * 128 + 128]
        total = None
        for h in range(2):
            hl = head_lanes(h)
            qh = jnp.where(hl, q, jnp.zeros_like(q))
            dh = jnp.where(hl, d, jnp.zeros_like(d))
            scores = jnp.where(mask, dot(qh, k, 1, 1) * scale, NEG)
            p = jnp.exp(scores - lse_ref[2 * t + h, rq])
            dp = dot(dh, v, 1, 1)
            inner = jnp.sum(p * dp, -1, keepdims=True)
            ds = (p * (dp - inner)).astype(jnp.bfloat16)
            dv[0:keys, ct] += dot(p.astype(jnp.bfloat16), dh, 0, 0)
            dk[0:keys, ct] += dot(ds, qh, 0, 0)
            part = dot(ds, k)
            total = part if h == 0 else jnp.where(head_lanes(1), part, total)
        dq[rq, ct] = total

    def rotary():
        @pl.loop(0, valid // QB)
        def _(i):
            r = row_at(i)
            c, s1, s2 = c_ref[r], s1_ref[r], s2_ref[r]
            for t in range(w // 128):
                ct = slice(t * 128, t * 128 + 128)
                for j, src in ((0, dq), (1, dk)):
                    x = (src[r, ct] * scale).astype(jnp.bfloat16).astype(jnp.float32)
                    at = j * w + t * 128
                    gpk[r, at : at + 128] = turn(x, c, s1, s2, -1.0).astype(jnp.bfloat16)
                at = 2 * w + t * 128
                gpk[r, at : at + 128] = dv[r, ct].astype(jnp.bfloat16)

    def unpack():
        b_ref[...] = jnp.zeros_like(b_ref)

        @pl.loop(0, rows // QB)
        def _(i):
            r = row_at(i)
            oc = ocol_ref[r]
            back = dot(puts(oc, valid), gpk[...])
            pad = jnp.where(oc >= valid, do_ref[r].astype(jnp.float32), 0.0)
            back = jnp.concatenate([back[:, : 2 * w], back[:, 2 * w :] + pad], 1)
            g_ref[r] = back.astype(jnp.bfloat16)
            b_ref[...] += jnp.sum(back, 0, keepdims=True)

    blocks = [
        functools.partial(block, qb, t) for qb in range(valid // QB) for t in range(w // 128)
    ]
    return [pack] + blocks + [rotary, unpack]


def forward_kernel(
    a_ref,
    qw_ref,
    shift_ref,
    c_ref,
    s1_ref,
    s2_ref,
    orow_ref,
    ocol_ref,
    len_ref,
    dm_ref,
    w_ref,
    dw_ref,
    ho_ref,
    pk_ref,
    lse_ref,
    dmo_ref,
    wo_ref,
    dwo_ref,
    mix_ref,
    rot,
    opk,
    *sems,
):
    s, f, z, y = where_am_i()
    greet_columns(s, f)
    gather = SeqGather(dm_ref, dmo_ref, *sems[:5])
    slices = ColGather(w_ref, wo_ref, *sems[5:10])
    side = FsdpGather(dw_ref, dwo_ref, *sems[10:13])
    swap = RowExchange(mix_ref, ho_ref, *sems[13:])
    work = attend(
        a_ref,
        qw_ref,
        shift_ref,
        (c_ref, s1_ref, s2_ref),
        orow_ref,
        ocol_ref,
        len_ref,
        mix_ref,
        pk_ref,
        lse_ref,
        rot,
        opk,
    )
    gather.start()
    slices.start()
    side.start()
    for item in work[:-6]:
        item()
    gather.below(1)
    gather.above(1)
    todo = slices.steps()
    for item in merged(work[-6:], todo[:3]):
        item()
    swap.start()
    todo = todo[3:] + [side.step]
    for t in (2, 3):
        gather.below(t)
        gather.above(t)
        for item in todo[:4]:
            item()
        todo = todo[4:]
    for item in todo:
        item()
    for t in range(4):
        gather.across(t)
    swap.finish()
    slices.finish()
    side.finish()
    gather.finish()


def attention_forward(
    a, w_qkv, shift, tables, orow, ocol, lengths, valid, dm, weight, rows_weight, collective
):
    rows, w3 = a.shape[0], w_qkv.shape[1]
    w = w3 // 3
    heads = w // HEAD_DIM
    mixed = jax.ShapeDtypeStruct((8, rows // 8, w), jnp.bfloat16)
    return pl.pallas_call(
        forward_kernel,
        out_shape=(
            mixed,
            jax.ShapeDtypeStruct((valid, w3), jnp.bfloat16),
            jax.ShapeDtypeStruct((heads, valid, 1), jnp.float32),
            jax.ShapeDtypeStruct((8,) + dm.shape, dm.dtype),
            jax.ShapeDtypeStruct((8, 4) + weight.shape[1:], weight.dtype),
            jax.ShapeDtypeStruct((4,) + rows_weight.shape, rows_weight.dtype),
            mixed,
        ),
        in_specs=[VMEM_SPEC] * 8 + [SMEM_SPEC] + [VMEM_SPEC] * 3,
        out_specs=(VMEM_SPEC,) * 3 + (ANY_SPEC,) * 3 + (VMEM_SPEC,),
        scratch_shapes=[
            pltpu.VMEM((rows, w3), jnp.bfloat16),
            pltpu.VMEM((valid, w), jnp.bfloat16),
        ]
        + SeqGather.scratch()
        + ColGather.scratch()
        + FsdpGather.scratch()
        + RowExchange.scratch(),
        compiler_params=comm_params(collective),
    )(a, w_qkv, shift, *tables, orow, ocol, lengths, dm, weight, rows_weight)


def backward_kernel(
    pk_ref,
    do_ref,
    lse_ref,
    c_ref,
    s1_ref,
    s2_ref,
    orow_ref,
    ocol_ref,
    len_ref,
    p_ref,
    wg_ref,
    g_ref,
    b_ref,
    o_ref,
    wo_ref,
    dpk,
    dq,
    dk,
    dv,
    gpk,
    *scratch,
):
    s, f, z, y = where_am_i()
    greet_columns(s, f)
    reduce = SeqReduce(p_ref, o_ref, *scratch[:13])
    slices = ColReduce(wg_ref, wo_ref, *scratch[13:])
    work = attend_back(
        pk_ref,
        do_ref,
        lse_ref,
        (c_ref, s1_ref, s2_ref),
        orow_ref,
        ocol_ref,
        len_ref,
        g_ref,
        b_ref,
        dpk,
        dq,
        dk,
        dv,
        gpk,
    )
    reduce.start()
    slices.start()
    for item in merged(work, slices.steps()[:8]):
        item()
    for item in merged(reduce.steps(), slices.steps()[8:]):
        item()
    reduce.finish()
    slices.finish()


def attention_backward(pk, do, lse, tables, orow, ocol, lengths, partial, wide_grad, collective):
    rows, w = do.shape
    valid = pk.shape[0]
    width = partial.shape[2]

    def acc(c):
        return pltpu.VMEM((valid, c), jnp.float32)

    return pl.pallas_call(
        backward_kernel,
        out_shape=(
            jax.ShapeDtypeStruct((rows, 3 * w), jnp.bfloat16),
            jax.ShapeDtypeStruct((1, 3 * w), jnp.float32),
            jax.ShapeDtypeStruct((rows // 8, width), jnp.float32),
            jax.ShapeDtypeStruct((8,) + wide_grad.shape[2:], jnp.bfloat16),
        ),
        in_specs=[VMEM_SPEC] * 8 + [SMEM_SPEC] + [ANY_SPEC] * 2,
        out_specs=(VMEM_SPEC,) * 4,
        scratch_shapes=[
            pltpu.VMEM((valid, w), jnp.bfloat16),
            acc(w),
            acc(w),
            acc(w),
            pltpu.VMEM((valid, 3 * w), jnp.bfloat16),
        ]
        + SeqReduce.scratch(rows // 8, width)
        + ColReduce.scratch(*wide_grad.shape[2:]),
        compiler_params=comm_params(collective, 56),
    )(pk, do, lse, *tables, orow, ocol, lengths, partial, wide_grad)


def last_kernel(p_ref, wg_ref, o_ref, wo_ref, *scratch):
    s, f, z, y = where_am_i()
    greet_columns(s, f)
    reduce = SeqReduce(p_ref, o_ref, *scratch[:13])
    slices = ColReduce(wg_ref, wo_ref, *scratch[13:])
    reduce.start()
    slices.start()
    for item in slices.steps()[:8]:
        item()
    for item in merged(reduce.steps(), slices.steps()[8:]):
        item()
    reduce.finish()
    slices.finish()


def last_reduce(partial, grad, collective):
    _, rows, width = partial.shape
    return pl.pallas_call(
        last_kernel,
        out_shape=(
            jax.ShapeDtypeStruct((rows, width), jnp.float32),
            jax.ShapeDtypeStruct((8,) + grad.shape[2:], jnp.bfloat16),
        ),
        in_specs=[ANY_SPEC] * 2,
        out_specs=(VMEM_SPEC,) * 2,
        scratch_shapes=SeqReduce.scratch(rows, width) + ColReduce.scratch(*grad.shape[2:]),
        compiler_params=comm_params(collective),
    )(partial, grad)


def sum_kernel(x_ref, o_ref, got, send, recv):
    s, f, z, y = where_am_i()
    me = s * 4 + f
    greet_all(s, f)

    def piece(k):
        i = (me + k) % 32
        return remote(x_ref.at[i], got.at[k], send.at[k], recv.at[k], dealer(i))

    @pl.loop(1, 32)
    def _(k):
        piece(k).start()

    @pl.loop(1, 32)
    def _(k):
        piece(k).wait_recv()
        piece(k).wait_send()

    o_ref[...] = x_ref[me]

    @pl.loop(1, 32)
    def _(k):
        o_ref[...] += got[k]


def sum_parts(x, collective):
    return pl.pallas_call(
        sum_kernel,
        out_shape=jax.ShapeDtypeStruct(x.shape[1:], x.dtype),
        in_specs=[VMEM_SPEC],
        out_specs=VMEM_SPEC,
        scratch_shapes=[pltpu.VMEM(x.shape, x.dtype), DMA((32,)), DMA((32,))],
        compiler_params=comm_params(collective),
    )(x)


def rotary_tables(rel):
    half = ROT // 2
    d = jnp.arange(128, dtype=jnp.int32) % HEAD_DIM
    freq = 10000.0 ** (-2.0 * (d % half).astype(jnp.float32) / ROT)
    angle = rel[:, None] * freq[None, :]
    c, s = jnp.cos(angle), jnp.sin(angle)
    second = (d >= half) & (d < ROT)
    return (jnp.where(d < ROT, c, 1.0), jnp.where(d < half, -s, 0.0), jnp.where(second, s, 0.0))


def line_body(
    hidden_in,
    ln1_gain,
    ln1_bias,
    qkv_weight,
    qkv_bias,
    out_weight,
    ln2_gain,
    ln2_bias,
    gate_weight,
    up_weight,
    down_weight,
    seq_lengths,
    deal_order,
    out_grad,
):
    rows = hidden_in.shape[1]
    width = hidden_in.shape[2]
    nseq = lax.axis_size("seq")
    nfsdp = lax.axis_size("fsdp")
    lw = width // nseq
    part = qkv_weight.shape[0]
    ff = gate_weight.shape[1]
    lf = ff // nseq
    seq_at, fsdp_at = lax.axis_index("seq"), lax.axis_index("fsdp")
    stream = hidden_in[0].astype(jnp.float32)
    cotangent = out_grad[0].astype(jnp.float32)
    order = deal_order[0]
    lengths = seq_lengths[0]
    group_rows = order.shape[0]
    valid_rows = group_rows * 5 // 8
    orow, ocol = order[None, :], order[:, None]
    local_pos = lax.dynamic_slice_in_dim(order, seq_at * rows, rows)
    valid = (local_pos < valid_rows).astype(jnp.float32)[:, None]
    dealt_seg, dealt_start = segment_of(order, lengths)
    dealt_tables = rotary_tables((order - dealt_start).astype(jnp.float32))
    packed_pos = jnp.arange(valid_rows, dtype=jnp.int32)
    packed_seg, packed_start = segment_of(packed_pos, lengths)
    packed_tables = rotary_tables((packed_pos - packed_start).astype(jnp.float32))

    def column_parts(weights):
        views = [w.reshape(part, nseq, -1) for w in weights]
        return jnp.concatenate(views, 2).transpose(1, 0, 2)

    params = jnp.stack([ln1_gain, ln1_bias, ln2_gain, ln2_bias, *qkv_bias])
    params = jnp.pad(params.astype(jnp.float32), ((0, 1), (0, 64)))
    params = jnp.where(fsdp_at % 2 == 0, params, jnp.roll(params, part, 1))
    qkv_parts = qkv_weight.reshape(part, 3, nseq, lw).transpose(2, 0, 1, 3).reshape(nseq, part, -1)
    first_in, qkv_w, norms, out_w = entry(hidden_in[0], params, qkv_parts, out_weight, 1)
    first_in = first_in.reshape(group_rows, width)
    qkv_w = qkv_w.reshape(width, 3 * lw)
    gain1, shift1, gain2, shift2 = norms[:4]
    qkv_shift = lax.dynamic_slice_in_dim(norms[4:7], seq_at * lw, lw, 1).reshape(1, -1)
    normed1, rstd1 = normalize(stream)
    heads_out, packed, lse, mlp_grad, wide_w, down_w, mixed = attention_forward(
        first_in,
        qkv_w,
        qkv_shift,
        dealt_tables,
        orow,
        ocol,
        seq_lengths,
        valid_rows,
        out_grad[0],
        column_parts([gate_weight, up_weight]),
        down_weight,
        2,
    )
    mixed = mixed.reshape(group_rows, lw)
    heads_out = heads_out.transpose(1, 0, 2).reshape(rows, width)
    wide_w = wide_w.reshape(width, 2 * lf)
    mlp_grad = mlp_grad.reshape(group_rows, width)
    out_rows = lax.dynamic_slice_in_dim(out_w, seq_at * nfsdp, nfsdp).reshape(lw, width)
    out_w = out_w.reshape(width, width)
    down_w = down_w.reshape(lf, width)
    attn = times(heads_out, out_w)
    resid = stream + attn
    normed2, rstd2 = normalize(resid)
    second_local = (normed2 * gain2 + shift2).astype(jnp.bfloat16)
    second_in = gather_rows_line(second_local, 3).reshape(group_rows, width)
    wide = times(second_in, wide_w)
    gate, upper = wide[:, :lf], wide[:, lf:]
    hidden, sigma = mlp_forward(gate, upper)
    hidden_grad = times_transposed(mlp_grad, down_w)
    wide_act = jnp.concatenate(mlp_backward(hidden_grad, gate, upper, sigma), 1)
    second_part = times_transposed(wide_act, wide_w).astype(jnp.bfloat16)
    second_grad = reduce_rows_line(second_part.reshape(nseq, rows, width), 4)
    resid_part, gain2_grad, shift2_grad = norm_back(second_grad, normed2, rstd2, gain2)
    resid_grad = cotangent + resid_part
    attn_grad = gather_rows_line(resid_grad.astype(jnp.bfloat16), 5).reshape(group_rows, width)
    mixed_grad = times_transposed(attn_grad, out_rows).astype(jnp.bfloat16)

    def row_shard(left, right):
        grad = outer(left, right).astype(jnp.bfloat16)
        return lax.psum_scatter(grad, "fsdp", scatter_dimension=0, tiled=True).astype(jnp.float32)

    def column_parts_grad(left, right):
        return outer(left, right).astype(jnp.bfloat16).reshape(nseq, nfsdp, part, -1)

    down_grad = row_shard(hidden, mlp_grad)
    mlp_part = times(hidden, down_w).astype(jnp.bfloat16).reshape(nseq, rows, width)
    qkv_act, bias_sums, mlp, wide_grad = attention_backward(
        packed,
        mixed_grad,
        lse,
        packed_tables,
        orow,
        ocol,
        seq_lengths,
        mlp_part,
        column_parts_grad(second_in, wide_act),
        6,
    )
    result = resid + mlp
    out_grad_w = row_shard(mixed, attn_grad)
    first_part = times_transposed(qkv_act, qkv_w).astype(jnp.bfloat16)
    first_grad, qkv_grad = last_reduce(
        first_part.reshape(nseq, rows, width), column_parts_grad(first_in, qkv_act), 7
    )
    input_part, gain1_grad, shift1_grad = norm_back(first_grad, normed1, rstd1, gain1)
    input_grad = resid_grad + input_part
    wide_grad = wide_grad.astype(jnp.float32)
    gate_grad = wide_grad[:, :, :lf].transpose(1, 0, 2).reshape(part, ff)
    up_grad = wide_grad[:, :, lf:].transpose(1, 0, 2).reshape(part, ff)
    qkv_grad = qkv_grad.astype(jnp.float32).reshape(nseq, part, 3, lw)
    qkv_grad = qkv_grad.transpose(1, 2, 0, 3).reshape(part, 3 * width)

    vectors = jnp.stack([gain1_grad, shift1_grad, gain2_grad, shift2_grad])
    vectors = vectors.reshape(4, nseq * nfsdp, part).transpose(1, 0, 2).reshape(-1, 2, 128)
    sums = jnp.stack(
        [
            jnp.sum(valid * result * result),
            jnp.sum(valid * attn * attn),
            jnp.sum(valid * mlp * mlp),
        ]
    )
    sums = jnp.broadcast_to(jnp.pad(sums, (0, 125)), (nseq * nfsdp, 1, 128))
    bias = bias_sums.reshape(3, nfsdp, part).transpose(1, 0, 2).reshape(nfsdp, 3 * part)
    bias = jnp.pad(bias, ((0, 0), (0, 64))).reshape(1, nfsdp, 2, 128)
    here = (jnp.arange(nseq) == seq_at)[:, None, None, None]
    bias = jnp.where(here, bias, 0.0).reshape(-1, 2, 128)
    message = jnp.concatenate([vectors, sums, bias, jnp.zeros_like(vectors), sums], 1)
    total = sum_parts(message, 8)
    count = valid_rows * nfsdp * width
    rms = jnp.sqrt(total[2, :3] / count)
    shards = total[:2].reshape(4, part)
    qkv_bias_grad = total[3:5].reshape(4, part)[:3]
    return (
        result.astype(jnp.bfloat16)[None],
        input_grad[None],
        shards[0],
        shards[1],
        qkv_grad,
        qkv_bias_grad,
        out_grad_w,
        shards[2],
        shards[3],
        gate_grad,
        up_grad,
        down_grad,
        rms,
    )


def solution(mesh):
    in_specs = (
        P("fsdp", "seq", None),
        P(("seq", "fsdp")),
        P(("seq", "fsdp")),
        P(("seq", "fsdp"), None),
        P(None, ("seq", "fsdp")),
        P(("seq", "fsdp"), None),
        P(("seq", "fsdp")),
        P(("seq", "fsdp")),
        P(("seq", "fsdp"), None),
        P(("seq", "fsdp"), None),
        P(("seq", "fsdp"), None),
        P("fsdp", None),
        P("fsdp", None),
        P("fsdp", "seq", None),
    )
    out_specs = (
        P("fsdp", "seq", None),
        P("fsdp", "seq", None),
        P(("seq", "fsdp")),
        P(("seq", "fsdp")),
        P(("seq", "fsdp"), None),
        P(None, ("seq", "fsdp")),
        P(("seq", "fsdp"), None),
        P(("seq", "fsdp")),
        P(("seq", "fsdp")),
        P(("seq", "fsdp"), None),
        P(("seq", "fsdp"), None),
        P(("seq", "fsdp"), None),
        P(),
    )
    line = dict(mesh.shape) == {"seq": 8, "fsdp": 4}
    return jax.shard_map(
        line_body if line else body,
        mesh=mesh,
        in_specs=in_specs,
        out_specs=out_specs,
        check_vma=False,
    )
```

```python
import functools

import jax
import jax.numpy as jnp
from jax import lax
from jax.experimental import pallas as pl
from jax.experimental.pallas import tpu as pltpu
from jax.sharding import PartitionSpec as P

HEAD_DIM = 64
ROT = 16


EPS = 1e-05


def normalize(values):
    center = values - jnp.mean(values, -1, keepdims=True)
    spread = jnp.mean(center * center, -1, keepdims=True)
    rstd = lax.rsqrt(spread + EPS)
    return (center * rstd, rstd)


def norm_back(grad, normed, rstd, gain):
    scaled = grad * gain
    inner = (
        scaled
        - jnp.mean(scaled, -1, keepdims=True)
        - normed * jnp.mean(scaled * normed, -1, keepdims=True)
    )
    return (rstd * inner, jnp.sum(grad * normed, 0), jnp.sum(grad, 0))


def segment_of(pos, lengths):
    nseg = lengths.shape[0]
    ends = jnp.cumsum(lengths)
    seg = jnp.sum((pos[:, None] >= ends[None, :]).astype(jnp.int32), 1)
    starts = jnp.concatenate([jnp.zeros((1,), jnp.int32), ends[:-1]])
    start = jnp.sum(
        jnp.where(seg[:, None] == jnp.arange(nseg, dtype=jnp.int32)[None, :], starts[None, :], 0), 1
    )
    start = jnp.where(seg < nseg, start, pos)
    return (seg, start)


def rotate(values, rel, sign):
    count = values.shape[0]
    view = values.reshape(count, -1, HEAD_DIM)
    half = ROT // 2
    freq = 10000.0 ** (-2.0 * jnp.arange(half, dtype=jnp.float32) / ROT)
    angle = rel[:, None] * freq[None, :]
    cosine = jnp.cos(angle)[:, None, :]
    sine = jnp.sin(angle)[:, None, :]
    first = view[..., :half]
    second = view[..., half:ROT]
    turned = jnp.concatenate(
        [
            first * cosine - sign * second * sine,
            second * cosine + sign * first * sine,
            view[..., ROT:],
        ],
        -1,
    )
    return turned.reshape(count, -1)


def outer(left, right):
    return lax.dot_general(
        left, right, (((0,), (0,)), ((), ())), preferred_element_type=jnp.float32
    )


def times(left, right):
    return jnp.dot(left, right, preferred_element_type=jnp.float32)


def times_transposed(left, right):
    return lax.dot_general(
        left, right, (((1,), (1,)), ((), ())), preferred_element_type=jnp.float32
    )


def mlp_forward(gate, upper):
    sigma = jax.nn.sigmoid(gate)
    return ((gate * sigma * upper).astype(jnp.bfloat16), sigma)


def mlp_backward(hidden_grad, gate, upper, sigma):
    up_act = (hidden_grad * gate * sigma).astype(jnp.bfloat16)
    gate_act = (hidden_grad * upper * sigma * (1.0 + gate * (1.0 - sigma))).astype(jnp.bfloat16)
    return (gate_act, up_act)


def body(
    hidden_in,
    ln1_gain,
    ln1_bias,
    qkv_weight,
    qkv_bias,
    out_weight,
    ln2_gain,
    ln2_bias,
    gate_weight,
    up_weight,
    down_weight,
    seq_lengths,
    deal_order,
    out_grad,
):
    rows = hidden_in.shape[1]
    width = hidden_in.shape[2]
    nseq = lax.axis_size("seq")
    nfsdp = lax.axis_size("fsdp")
    local_width = width // nseq
    part = qkv_weight.shape[0]
    ff = gate_weight.shape[1]
    local_ff = ff // nseq
    stream = hidden_in[0].astype(jnp.float32)
    cotangent = out_grad[0].astype(jnp.float32)
    order = deal_order[0]
    lengths = seq_lengths[0]
    nseg = lengths.shape[0]
    group_rows = order.shape[0]
    valid_rows = group_rows * 5 // 8
    longest = valid_rows * 4 // 5
    blk = min(512, group_rows)
    keys = min(group_rows, longest + blk)
    nblocks = group_rows // blk
    scale = HEAD_DIM ** (-0.5)
    local_pos = lax.dynamic_slice_in_dim(order, lax.axis_index("seq") * rows, rows)
    valid = (local_pos < valid_rows).astype(jnp.float32)[:, None]
    dealt_seg, dealt_start = segment_of(order, lengths)
    rel = (order - dealt_start).astype(jnp.float32)
    inverse = (
        jnp.zeros((group_rows,), jnp.int32).at[order].set(jnp.arange(group_rows, dtype=jnp.int32))
    )
    seg_p, start_p = segment_of(jnp.arange(group_rows, dtype=jnp.int32), lengths)

    def gather_rows(values):
        return lax.all_gather(values, "seq", axis=0, tiled=True)

    def scatter_rows(partial):
        return lax.psum_scatter(
            partial.astype(jnp.bfloat16), "seq", scatter_dimension=0, tiled=True
        ).astype(jnp.float32)

    def column_slice(weight, blocks):
        cols = weight.shape[1] // (blocks * nseq)
        view = weight.reshape(part, blocks, nseq, cols).transpose(2, 0, 1, 3)
        mine = lax.all_to_all(
            view.reshape(nseq * part, blocks * cols), "seq", split_axis=0, concat_axis=0, tiled=True
        )
        full = lax.all_gather(mine.reshape(nseq, part, blocks * cols), "fsdp", axis=1)
        return full.reshape(width, blocks * cols)

    def row_slice(weight):
        return lax.all_gather(weight, "fsdp", axis=0, tiled=True)

    def column_shard(grad, blocks):
        cols = grad.shape[1] // blocks
        view = grad.astype(jnp.bfloat16).reshape(nseq, nfsdp, part, blocks * cols)
        mine = lax.psum_scatter(view.transpose(1, 0, 2, 3), "fsdp", scatter_dimension=0)
        got = lax.all_to_all(
            mine.reshape(nseq * part, blocks * cols), "seq", split_axis=0, concat_axis=0, tiled=True
        )
        view = got.reshape(nseq, part, blocks, cols).transpose(1, 2, 0, 3)
        return view.reshape(part, -1).astype(jnp.float32)

    def row_shard(grad):
        return lax.psum_scatter(
            grad.astype(jnp.bfloat16), "fsdp", scatter_dimension=0, tiled=True
        ).astype(jnp.float32)

    def to_pack(values):
        heads_here = values.shape[1] // HEAD_DIM
        return values[inverse].reshape(group_rows, heads_here, HEAD_DIM)

    def window(index, packed):
        query_p, key_p, value_p = packed
        first = index * blk
        key_first = jnp.clip(jnp.minimum(start_p[first], group_rows - keys), 0, group_rows - keys)
        qpos = first + jnp.arange(blk, dtype=jnp.int32)
        kpos = key_first + jnp.arange(keys, dtype=jnp.int32)
        qseg = lax.dynamic_slice_in_dim(seg_p, first, blk)
        kseg = lax.dynamic_slice_in_dim(seg_p, key_first, keys)
        allowed = (qseg[:, None] == kseg[None, :]) & (qseg[:, None] < nseg) & (
            kpos[None, :] <= qpos[:, None]
        ) | (kpos[None, :] == qpos[:, None])
        qblock = lax.dynamic_slice_in_dim(query_p, first, blk)
        kblock = lax.dynamic_slice_in_dim(key_p, key_first, keys)
        vblock = lax.dynamic_slice_in_dim(value_p, key_first, keys)
        scores = (
            jnp.einsum("qhd,khd->hqk", qblock, kblock, preferred_element_type=jnp.float32) * scale
        )
        scores = jnp.where(allowed[None], scores, -1e30)
        return (first, key_first, qblock, kblock, vblock, scores)

    both = ("seq", "fsdp")
    norms = lax.all_gather(
        jnp.stack([ln1_gain, ln1_bias, ln2_gain, ln2_bias, *qkv_bias]), both, axis=1, tiled=True
    )
    gain1, shift1, gain2, shift2 = norms[:4].astype(jnp.float32)
    qkv_shift = lax.dynamic_slice_in_dim(
        norms[4:], lax.axis_index("seq") * local_width, local_width, 1
    )
    qkv_shift = qkv_shift.reshape(-1).astype(jnp.float32)

    normed1, rstd1 = normalize(stream)
    first_local = (normed1 * gain1 + shift1).astype(jnp.bfloat16)
    first_in = gather_rows(first_local)
    qkv_w = column_slice(qkv_weight, 3)
    qkv = times(first_in, qkv_w) + qkv_shift
    query = rotate(qkv[:, :local_width], rel, 1.0).astype(jnp.bfloat16)
    keyset = rotate(qkv[:, local_width : 2 * local_width], rel, 1.0).astype(jnp.bfloat16)
    valueset = qkv[:, 2 * local_width :].astype(jnp.bfloat16)
    packed = (to_pack(query), to_pack(keyset), to_pack(valueset))

    def attend_block(index):
        first, key_first, qblock, kblock, vblock, scores = window(index, packed)
        top = jnp.max(scores, -1, keepdims=True)
        expo = jnp.exp(scores - top)
        total = jnp.sum(expo, -1, keepdims=True)
        probs = (expo / total).astype(jnp.bfloat16)
        mixed = jnp.einsum("hqk,khd->qhd", probs, vblock, preferred_element_type=jnp.float32)
        return (mixed.astype(jnp.bfloat16), (top + jnp.log(total))[..., 0])

    mixed_all, lse_all = lax.map(attend_block, jnp.arange(nblocks, dtype=jnp.int32))
    mixed = mixed_all.reshape(group_rows, -1)[order]
    heads_out = lax.all_to_all(mixed, "seq", split_axis=0, concat_axis=1, tiled=True)
    out_w = lax.all_gather(out_weight, both, axis=0, tiled=True)
    out_rows = row_slice(out_weight)
    attn = times(heads_out, out_w)
    resid = stream + attn
    normed2, rstd2 = normalize(resid)
    second_in = gather_rows((normed2 * gain2 + shift2).astype(jnp.bfloat16))
    gate_w = column_slice(gate_weight, 1)
    up_w = column_slice(up_weight, 1)
    down_w = row_slice(down_weight)
    gate = times(second_in, gate_w)
    upper = times(second_in, up_w)
    hidden, sigma = mlp_forward(gate, upper)
    mlp = scatter_rows(times(hidden, down_w))
    result = resid + mlp

    mlp_grad = gather_rows(out_grad[0])
    hidden_grad = times_transposed(mlp_grad, down_w)
    gate_act, up_act = mlp_backward(hidden_grad, gate, upper, sigma)
    second_grad = scatter_rows(times_transposed(gate_act, gate_w) + times_transposed(up_act, up_w))
    down_grad = row_shard(outer(hidden, mlp_grad))
    gate_grad = column_shard(outer(second_in, gate_act), 1)
    up_grad = column_shard(outer(second_in, up_act), 1)
    resid_part, gain2_grad, shift2_grad = norm_back(second_grad, normed2, rstd2, gain2)
    resid_grad = cotangent + resid_part

    attn_grad = gather_rows(resid_grad.astype(jnp.bfloat16))
    out_grad_w = row_shard(outer(mixed, attn_grad))
    mixed_grad_p = to_pack(times_transposed(attn_grad, out_rows).astype(jnp.bfloat16))

    def back_block(index, carry):
        query_acc, key_acc, value_acc = carry
        first, key_first, qblock, kblock, vblock, scores = window(index, packed)
        probs = jnp.exp(scores - lse_all[index][:, :, None])
        dblock = lax.dynamic_slice_in_dim(mixed_grad_p, first, blk)
        value_part = jnp.einsum(
            "hqk,qhd->khd", probs.astype(jnp.bfloat16), dblock, preferred_element_type=jnp.float32
        )
        prob_grad = jnp.einsum("qhd,khd->hqk", dblock, vblock, preferred_element_type=jnp.float32)
        inner = jnp.sum(probs * prob_grad, -1, keepdims=True)
        score_grad = (probs * (prob_grad - inner)).astype(jnp.bfloat16)
        query_part = (
            jnp.einsum("hqk,khd->qhd", score_grad, kblock, preferred_element_type=jnp.float32)
            * scale
        )
        key_part = (
            jnp.einsum("hqk,qhd->khd", score_grad, qblock, preferred_element_type=jnp.float32)
            * scale
        )
        query_acc = lax.dynamic_update_slice_in_dim(query_acc, query_part, first, 0)
        key_old = lax.dynamic_slice_in_dim(key_acc, key_first, keys)
        key_acc = lax.dynamic_update_slice_in_dim(key_acc, key_old + key_part, key_first, 0)
        value_old = lax.dynamic_slice_in_dim(value_acc, key_first, keys)
        value_acc = lax.dynamic_update_slice_in_dim(value_acc, value_old + value_part, key_first, 0)
        return (query_acc, key_acc, value_acc)

    zeros = jnp.zeros(packed[0].shape, jnp.float32)
    query_acc, key_acc, value_acc = lax.fori_loop(0, nblocks, back_block, (zeros, zeros, zeros))

    def to_dealt(values):
        return values.astype(jnp.bfloat16).reshape(group_rows, -1)[order]

    qkv_act = jnp.concatenate(
        [
            rotate(to_dealt(query_acc).astype(jnp.float32), rel, -1.0).astype(jnp.bfloat16),
            rotate(to_dealt(key_acc).astype(jnp.float32), rel, -1.0).astype(jnp.bfloat16),
            to_dealt(value_acc),
        ],
        1,
    )
    first_grad = scatter_rows(times_transposed(qkv_act, qkv_w))
    qkv_grad = column_shard(outer(first_in, qkv_act), 3)
    qkv_bias_grad = lax.psum_scatter(
        jnp.sum(qkv_act.astype(jnp.float32), 0).reshape(3, nfsdp, -1),
        "fsdp",
        scatter_dimension=1,
    )
    input_part, gain1_grad, shift1_grad = norm_back(first_grad, normed1, rstd1, gain1)
    input_grad = resid_grad + input_part

    norm_grads = lax.psum(
        (
            gain1_grad,
            shift1_grad,
            gain2_grad,
            shift2_grad,
            jnp.sum(valid * result * result),
            jnp.sum(valid * attn * attn),
            jnp.sum(valid * mlp * mlp),
        ),
        both,
    )
    count = valid_rows * nfsdp * width
    rms = jnp.sqrt(jnp.stack(norm_grads[4:]) / count)
    mine = (lax.axis_index("seq") * nfsdp + lax.axis_index("fsdp")) * part
    norm_shards = [lax.dynamic_slice_in_dim(value, mine, part) for value in norm_grads[:4]]
    return (
        result.astype(jnp.bfloat16)[None],
        input_grad[None],
        norm_shards[0],
        norm_shards[1],
        qkv_grad,
        qkv_bias_grad,
        out_grad_w,
        norm_shards[2],
        norm_shards[3],
        gate_grad,
        up_grad,
        down_grad,
        rms,
    )


MESH = pl.DeviceIdType.MESH
QB = 128
NEG = -1e30
CH = 2
VMEM_SPEC = pl.BlockSpec(memory_space=pltpu.VMEM)
SMEM_SPEC = pl.BlockSpec(memory_space=pltpu.SMEM)
ANY_SPEC = pl.BlockSpec(memory_space=pl.ANY)
DMA = pltpu.SemaphoreType.DMA


def comm_params(collective, limit=48):
    return pltpu.CompilerParams(
        collective_id=collective, has_side_effects=True, vmem_limit_bytes=limit << 20
    )


def where_am_i():
    s = lax.axis_index("seq")
    f = lax.axis_index("fsdp")
    return s, f, s // 2, s % 2


def remote(src, dst, send, recv, device):
    return pltpu.make_async_remote_copy(
        src, dst, send, recv, device_id=device, device_id_type=MESH
    )


def flip(v, bit):
    return v + bit * (1 - 2 * ((v // bit) % 2))


def peer(s, k):
    for bit in (1, 2, 4):
        if k & bit:
            s = flip(s, bit)
    return s


def dealer(i):
    return (i // 4, i % 4)


def greet_all(s, f):
    bar = pltpu.get_barrier_semaphore()
    me = s * 4 + f

    @pl.loop(1, 32)
    def _(k):
        pl.semaphore_signal(bar, inc=1, device_id=dealer((me + k) % 32), device_id_type=MESH)

    pl.semaphore_wait(bar, 31)


def greet_line(s, f, z, y):
    bar = pltpu.get_barrier_semaphore()
    pl.semaphore_signal(bar, inc=1, device_id=(flip(s, 1), f), device_id_type=MESH)

    @pl.when(z > 0)
    def _():
        pl.semaphore_signal(bar, inc=1, device_id=(s - 2, f), device_id_type=MESH)

    @pl.when(z < 3)
    def _():
        pl.semaphore_signal(bar, inc=1, device_id=(s + 2, f), device_id_type=MESH)

    edge = jnp.where((z == 0) | (z == 3), 1, 0)
    pl.semaphore_wait(bar, 3 - edge)


def greet_columns(s, f):
    bar = pltpu.get_barrier_semaphore()
    for k in range(1, 8):
        pl.semaphore_signal(bar, inc=1, device_id=(peer(s, k), f), device_id_type=MESH)
    pl.semaphore_signal(bar, inc=1, device_id=(s, flip(f, 1)), device_id_type=MESH)
    pl.semaphore_signal(bar, inc=1, device_id=(s, flip(f, 2)), device_id_type=MESH)
    pl.semaphore_wait(bar, 9)


def adder(dst, srcs, step=16):
    @pl.loop(0, dst.shape[0] // step)
    def _(i):
        r = pl.ds(pl.multiple_of(i * step, step), step)
        total = srcs[0][r].astype(jnp.float32)
        for v in srcs[1:]:
            total = total + v[r].astype(jnp.float32)
        dst[r] = total.astype(dst.dtype)


class SeqGather:
    @staticmethod
    def scratch():
        return [DMA, DMA((8,)), DMA((4,)), DMA((4,)), DMA((4,))]

    def __init__(self, x, o, own, recv, sy, su, sd):
        self.x, self.o, self.recv, self.sy, self.su, self.sd = x, o, recv, sy, su, sd
        self.s, self.f, self.z, self.y = where_am_i()
        self.other = flip(self.s, 1)
        self.own = pltpu.make_async_copy(x, o.at[self.s], own)

    def at(self, zb):
        return 2 * zb + self.y

    def ysend(self, zb, src):
        b = self.at(zb)
        return remote(src, self.o.at[b], self.sy.at[zb], self.recv.at[b], (self.other, self.f))

    def usend(self, zb, src):
        b = self.at(zb)
        return remote(src, self.o.at[b], self.su.at[zb], self.recv.at[b], (self.s + 2, self.f))

    def dsend(self, zb, src):
        b = self.at(zb)
        return remote(src, self.o.at[b], self.sd.at[zb], self.recv.at[b], (self.s - 2, self.f))

    def arrived(self, b):
        o = self.o.at[b]
        return remote(o, o, self.sy.at[0], self.recv.at[b], (self.other, self.f))

    def start(self):
        @pl.when(self.z < 3)
        def _():
            self.usend(self.z, self.x).start()

        @pl.when(self.z > 0)
        def _():
            self.dsend(self.z, self.x).start()

        self.ysend(self.z, self.x).start()
        self.own.start()

    def near(self, i):
        low = jnp.where(self.z < 2, self.z, 3 - self.z)
        base = jnp.where(low == 0, i, jnp.where(i < 2, 1 - i, i))
        return jnp.where(self.z < 2, base, 3 - base)

    def arrive(self, i):
        zb = self.near(i)
        b = self.at(zb)
        self.arrived(b).wait_recv()

        @pl.when((zb < self.z) & (self.z < 3))
        def _():
            self.usend(zb, self.o.at[b]).start()

        @pl.when((zb > self.z) & (self.z > 0))
        def _():
            self.dsend(zb, self.o.at[b]).start()

        self.ysend(zb, self.o.at[b]).start()
        return b

    def cross(self, i):
        b = 2 * self.near(i) + 1 - self.y
        self.arrived(b).wait_recv()
        return b

    def steps(self):
        return [functools.partial(self.arrive, i) for i in (1, 2, 3)]

    def each(self, use):
        @pl.loop(0, 8)
        def _(j):
            i = (j + 1) // 2
            column = (j == 0) | ((j % 2 == 1) & (j < 7))

            @pl.when(column & (j > 0))
            def _():
                self.arrive(i)

            other = jnp.where(j == 7, 3, j // 2 - 1)

            @pl.when(jnp.logical_not(column))
            def _():
                self.cross(other)

            zb = self.near(jnp.where(column, i, other))
            use(2 * zb + jnp.where(column, self.y, 1 - self.y))

    def finish(self, own=True):
        if own:
            self.own.wait()
        for zb in range(4):
            self.ysend(zb, self.x).wait_send()

            @pl.when((self.z < 3) & (zb <= self.z))
            def _():
                self.usend(zb, self.x).wait_send()

            @pl.when((self.z > 0) & (zb >= self.z))
            def _():
                self.dsend(zb, self.x).wait_send()


class SeqReduce:
    @staticmethod
    def scratch(rows, w):
        big = [pltpu.VMEM((n, rows, w), jnp.bfloat16) for n in (4, 5)]
        return big + [DMA((4, CH)), DMA((5, CH)), DMA((4, CH)), DMA((4, CH))]

    def __init__(self, p, o, ybuf, got, ry, rl, sy, sl):
        self.p, self.o, self.ybuf, self.got = p, o, ybuf, got
        self.ry, self.rl, self.sy, self.sl = ry, rl, sy, sl
        self.s, self.f, self.z, self.y = where_am_i()
        self.other = flip(self.s, 1)
        self.ch = p.shape[1] // CH

    def order(self, k):
        a, b, c, d = [3, 2, 1, 0][k], [3, 0, 2, 1][k], [0, 3, 1, 2][k], [0, 1, 2, 3][k]
        z = self.z
        return jnp.where(z == 0, a, jnp.where(z == 1, b, jnp.where(z == 2, c, d)))

    def rows(self, c):
        return pl.ds(c * self.ch, self.ch)

    def ysend(self, zb, c):
        r = self.rows(c)
        src = self.p.at[2 * zb + 1 - self.y, r]
        dst = self.ybuf.at[zb, r]
        return remote(src, dst, self.sy.at[zb, c], self.ry.at[zb, c], (self.other, self.f))

    def usend(self, zb, c):
        r = self.rows(c)
        src, dst = self.ybuf.at[zb, r], self.got.at[zb, r]
        return remote(src, dst, self.sl.at[zb, c], self.rl.at[zb, c], (self.s + 2, self.f))

    def dsend(self, zb, c):
        r = self.rows(c)
        slot = jnp.where(zb == self.z - 1, 4, zb)
        src, dst = self.ybuf.at[zb, r], self.got.at[slot, r]
        return remote(src, dst, self.sl.at[zb, c], self.rl.at[slot, c], (self.s - 2, self.f))

    def landed(self, slot, c):
        v = self.got.at[slot, self.rows(c)]
        return remote(v, v, self.sl.at[0, c], self.rl.at[slot, c], (self.other, self.f))

    def send(self, k):
        for c in range(CH):
            self.ysend(self.order(k), c).start()

    def start(self):
        for k in range(4):
            self.send(k)

    def step(self, k, c):
        z, zb, r = self.z, self.order(k), self.rows(c)
        self.ysend(zb, c).wait_recv()
        a, b = self.p.at[2 * zb + self.y, r], self.ybuf.at[zb, r]
        u, d = self.got.at[zb, r], self.got.at[4, r]
        alone = ((zb > z) & (z == 0)) | ((zb < z) & (z == 3))

        @pl.when(alone)
        def _():
            adder(b, [a, b])

        @pl.when((zb != z) & jnp.logical_not(alone))
        def _():
            self.landed(zb, c).wait_recv()
            adder(b, [a, b, u])

        @pl.when(zb > z)
        def _():
            self.usend(zb, c).start()

        @pl.when(zb < z)
        def _():
            self.dsend(zb, c).start()

        @pl.when(zb == z)
        def _():
            o = self.o.at[r]

            @pl.when(z == 0)
            def _():
                self.landed(4, c).wait_recv()
                adder(o, [a, b, d])

            @pl.when(z == 3)
            def _():
                self.landed(zb, c).wait_recv()
                adder(o, [a, b, u])

            @pl.when((z > 0) & (z < 3))
            def _():
                self.landed(zb, c).wait_recv()
                self.landed(4, c).wait_recv()
                adder(o, [a, b, u, d])

    def steps(self):
        return [functools.partial(self.step, k, c) for k in range(4) for c in range(CH)]

    def finish(self):
        for zb in range(4):
            for c in range(CH):
                self.ysend(zb, c).wait_send()

                @pl.when(zb != self.z)
                def _():
                    self.usend(zb, c).wait_send()


class ColGather:
    @staticmethod
    def scratch():
        return [DMA, DMA((8, 4)), DMA((8,)), DMA((8, 2)), DMA((8,))]

    def __init__(self, x, o, own, recv, direct, core, xs):
        self.x, self.o, self.own, self.recv = x, o, own, recv
        self.direct, self.core, self.xs = direct, core, xs
        self.s, self.f, _, _ = where_am_i()
        self.fc, self.fx = flip(self.f, 1), flip(self.f, 2)
        self.fd = flip(self.fc, 2)
        self.mine = pltpu.make_async_copy(x.at[self.s], self.piece(self.s, self.f), own)

    def piece(self, t, ff):
        r = self.x.shape[1]
        return self.o.at[pl.ds(pl.multiple_of((t * 4 + ff) * r, r), r)]

    def send_direct(self, k):
        s, f, t = self.s, self.f, peer(self.s, k)
        return remote(self.x.at[t], self.piece(s, f), self.direct.at[k], self.recv.at[s, f], (t, f))

    def send_core(self, k, which, src):
        t, ff = peer(self.s, k), self.f if which == 0 else self.fx
        dst = self.piece(t, ff)
        return remote(src, dst, self.core.at[k, which], self.recv.at[t, ff], (self.s, self.fc))

    def send_x(self, k, src):
        t = peer(self.s, k)
        dst = self.piece(t, self.f)
        return remote(src, dst, self.xs.at[k], self.recv.at[t, self.f], (self.s, self.fx))

    def arrived(self, k, ff):
        t = peer(self.s, k)
        o = self.piece(t, ff)
        return remote(o, o, self.own, self.recv.at[t, ff], (self.s, self.fc))

    def start(self):
        for k in reversed(range(1, 8)):
            self.send_direct(k).start()
        self.send_x(0, self.x.at[self.s]).start()
        self.send_core(0, 0, self.x.at[self.s]).start()
        self.mine.start()

    def step(self, k):
        t = peer(self.s, k)
        self.arrived(k, self.f).wait_recv()
        self.send_x(k, self.piece(t, self.f)).start()
        self.send_core(k, 0, self.piece(t, self.f)).start()

    def xstep(self, k):
        t = peer(self.s, k)
        self.arrived(k, self.fx).wait_recv()
        self.send_core(k, 1, self.piece(t, self.fx)).start()

    def steps(self):
        first = [functools.partial(self.step, k) for k in reversed(range(1, 8))]
        then = [functools.partial(self.xstep, k) for k in (0, 7, 6, 5, 4, 3, 2, 1)]
        return first + then

    def finish(self):
        self.mine.wait()
        for k in range(8):
            self.arrived(k, self.fc).wait_recv()
            self.arrived(k, self.fd).wait_recv()
        for k in range(8):
            if k:
                self.send_direct(k).wait_send()
            self.send_x(k, self.x.at[0]).wait_send()
            self.send_core(k, 0, self.x.at[0]).wait_send()
            self.send_core(k, 1, self.x.at[0]).wait_send()


class ColSum:
    @staticmethod
    def scratch(r, c):
        def v(*lead):
            return pltpu.VMEM(lead + (8, r, c), jnp.bfloat16)

        return [v(2), v(), DMA((2, 8)), DMA((2, 8)), DMA((8,)), DMA((8,))]

    def __init__(self, g, h, cb, xb, cs, cr, xs, xr):
        self.g, self.h, self.cb, self.xb = g, h, cb, xb
        self.cs, self.cr, self.xs, self.xr = cs, cr, xs, xr
        self.s, self.f, _, _ = where_am_i()
        self.fc, self.fx = flip(self.f, 1), flip(self.f, 2)
        self.fd = flip(self.fc, 2)
        self.r, self.c = h.shape[1:]

    def piece(self, i, ff):
        at = pl.multiple_of((i * 4 + ff) * self.r, self.r)
        return self.g.at[pl.ds(at, self.r), pl.ds(0, self.c)]

    def core(self, w, i):
        src = self.piece(i, self.fd if w == 0 else self.fc)
        dst = self.cb.at[w, i]
        return remote(src, dst, self.cs.at[w, i], self.cr.at[w, i], (self.s, self.fc))

    def xsend(self, i):
        src, dst = self.cb.at[0, i], self.xb.at[i]
        return remote(src, dst, self.xs.at[i], self.xr.at[i], (self.s, self.fx))

    def send(self, i):
        self.core(0, i).start()
        self.core(1, i).start()

    def step(self, i):
        self.core(0, i).wait_recv()
        adder(self.cb.at[0, i], [self.piece(i, self.fx), self.cb.at[0, i]])
        self.xsend(i).start()

    def total(self, i):
        self.core(1, i).wait_recv()
        self.xsend(i).wait_recv()
        adder(self.h.at[i], [self.piece(i, self.f), self.cb.at[1, i], self.xb.at[i]])

    def finish(self):
        for i in range(8):
            self.core(0, i).wait_send()
            self.core(1, i).wait_send()
            self.xsend(i).wait_send()


class FsdpReduce:
    @staticmethod
    def scratch(r, c):
        return [pltpu.VMEM((2, r, c), jnp.bfloat16), pltpu.VMEM((r, c), jnp.bfloat16), DMA((3,)), DMA((3,))]

    def __init__(self, g, o, cb, xb, send, recv):
        self.g, self.o, self.cb, self.xb = g, o, cb, xb
        self.s, self.f, _, _ = where_am_i()
        f = self.f
        self.fx = flip(f, 2)
        fc = flip(f, 1)
        core = (self.s, fc)
        self.far = remote(g.at[flip(fc, 2)], cb.at[0], send.at[0], recv.at[0], core)
        self.near = remote(g.at[fc], cb.at[1], send.at[1], recv.at[1], core)
        self.over = remote(cb.at[0], xb, send.at[2], recv.at[2], (self.s, self.fx))

    def start(self):
        self.far.start()
        self.near.start()

    def step(self):
        self.far.wait_recv()
        adder(self.cb.at[0], [self.g.at[self.fx], self.cb.at[0]])
        self.over.start()

    def total(self):
        self.near.wait_recv()
        self.over.wait_recv()
        adder(self.o, [self.g.at[self.f], self.cb.at[1], self.xb])

    def finish(self):
        self.far.wait_send()
        self.near.wait_send()
        self.over.wait_send()


class FsdpGather:
    @staticmethod
    def scratch():
        return [DMA, DMA((4,)), DMA((3,))]

    def __init__(self, x, o, own, recv, send):
        self.x, self.o, self.own, self.recv, self.send = x, o, own, recv, send
        self.s, self.f, _, _ = where_am_i()
        self.fc, self.fx = flip(self.f, 1), flip(self.f, 2)
        self.fd = flip(self.fc, 2)
        self.mine = pltpu.make_async_copy(x, o.at[self.f], own)

    def pass_on(self, n, src, ff, to):
        return remote(src, self.o.at[ff], self.send.at[n], self.recv.at[ff], (self.s, to))

    def arrived(self, ff):
        o = self.o.at[ff]
        return remote(o, o, self.own, self.recv.at[ff], (self.s, self.fc))

    def start(self):
        self.pass_on(0, self.x, self.f, self.fx).start()
        self.pass_on(1, self.x, self.f, self.fc).start()
        self.mine.start()

    def step(self):
        self.arrived(self.fx).wait_recv()
        self.pass_on(2, self.o.at[self.fx], self.fx, self.fc).start()

    def finish(self):
        self.mine.wait()
        self.arrived(self.fc).wait_recv()
        self.arrived(self.fd).wait_recv()
        for n in range(3):
            self.pass_on(n, self.x, self.f, self.fc).wait_send()


class WholeGather:
    @staticmethod
    def scratch():
        return [DMA, DMA((32,)), DMA((4,)), DMA((4,)), DMA((4,)), DMA((4, 2)), DMA((4, 2, 2))]

    def __init__(self, x, o, own, recv, su, sd, sy, sx, sc):
        self.x, self.o, self.own, self.recv = x, o, own, recv
        self.su, self.sd, self.sy, self.sx, self.sc = su, sd, sy, sx, sc
        self.s, self.f, self.z, self.y = where_am_i()
        self.fc, self.fx = flip(self.f, 1), flip(self.f, 2)
        self.fd = flip(self.fc, 2)
        self.me = self.s * 4 + self.f
        self.mine = pltpu.make_async_copy(x, o.at[self.me], own)

    def at(self, zb, yy, ff):
        return (2 * zb + (self.y if yy == 0 else 1 - self.y)) * 4 + ff

    def src(self, b, first):
        return self.x if first else self.o.at[b]

    def up(self, zb, first=False):
        b = self.at(zb, 0, self.f)
        to = (self.s + 2, self.f)
        return remote(self.src(b, first), self.o.at[b], self.su.at[zb], self.recv.at[b], to)

    def down(self, zb, first=False):
        b = self.at(zb, 0, self.f)
        to = (self.s - 2, self.f)
        return remote(self.src(b, first), self.o.at[b], self.sd.at[zb], self.recv.at[b], to)

    def over_y(self, zb, first=False):
        b = self.at(zb, 0, self.f)
        to = (flip(self.s, 1), self.f)
        return remote(self.src(b, first), self.o.at[b], self.sy.at[zb], self.recv.at[b], to)

    def over_x(self, zb, yy, first=False):
        b = self.at(zb, yy, self.f)
        to = (self.s, self.fx)
        return remote(self.src(b, first), self.o.at[b], self.sx.at[zb, yy], self.recv.at[b], to)

    def over_core(self, zb, yy, xx, first=False):
        b = self.at(zb, yy, self.f if xx == 0 else self.fx)
        to = (self.s, self.fc)
        return remote(self.src(b, first), self.o.at[b], self.sc.at[zb, yy, xx], self.recv.at[b], to)

    def arrived(self, b):
        o = self.o.at[b]
        return remote(o, o, self.own, self.recv.at[b], (self.s, self.fc))

    def start(self):
        z = self.z

        @pl.when(z < 3)
        def _():
            self.up(z, True).start()

        @pl.when(z > 0)
        def _():
            self.down(z, True).start()

        self.over_y(z, True).start()
        self.over_x(z, 0, True).start()
        self.over_core(z, 0, 0, True).start()
        self.mine.start()

    def line(self, sign, t):
        zb = self.z + sign * t

        @pl.when((zb >= 0) & (zb <= 3))
        def _():
            self.arrived(self.at(zb, 0, self.f)).wait_recv()
            if sign < 0:

                @pl.when(self.z < 3)
                def _():
                    self.up(zb).start()

            else:

                @pl.when(self.z > 0)
                def _():
                    self.down(zb).start()

            self.over_y(zb).start()
            self.over_x(zb, 0).start()
            self.over_core(zb, 0, 0).start()

    def column(self, sign, t):
        zb = self.z + sign * t

        @pl.when((zb >= 0) & (zb <= 3))
        def _():
            self.arrived(self.at(zb, 1, self.f)).wait_recv()
            self.over_x(zb, 1).start()
            self.over_core(zb, 1, 0).start()

    def side(self, sign, t, yy):
        zb = self.z + sign * t

        @pl.when((zb >= 0) & (zb <= 3))
        def _():
            self.arrived(self.at(zb, yy, self.fx)).wait_recv()
            self.over_core(zb, yy, 1).start()

    def steps(self):
        p = functools.partial
        out = []
        for t in range(4):
            for sign in (-1, 1) if t else (1,):
                if t:
                    out.append(p(self.line, sign, t))
        for t in range(4):
            for sign in (-1, 1) if t else (1,):
                out.append(p(self.column, sign, t))
                out.append(p(self.side, sign, t, 0))
        for t in range(4):
            for sign in (-1, 1) if t else (1,):
                out.append(p(self.side, sign, t, 1))
        return out

    def finish(self):
        self.mine.wait()
        for zb in range(4):
            for yy in range(2):
                self.arrived(self.at(zb, yy, self.fc)).wait_recv()
                self.arrived(self.at(zb, yy, self.fd)).wait_recv()
        for zb in range(4):
            self.over_y(zb).wait_send()

            @pl.when((self.z < 3) & (zb <= self.z))
            def _():
                self.up(zb).wait_send()

            @pl.when((self.z > 0) & (zb >= self.z))
            def _():
                self.down(zb).wait_send()

            for yy in range(2):
                self.over_x(zb, yy).wait_send()
                for xx in range(2):
                    self.over_core(zb, yy, xx).wait_send()


class RowExchange:
    @staticmethod
    def scratch():
        return [DMA, DMA((8,)), DMA((8,))]

    def __init__(self, x, o, own, send, recv):
        self.x, self.o, self.send, self.recv = x, o, send, recv
        self.s, self.f, _, _ = where_am_i()
        self.mine = pltpu.make_async_copy(x.at[self.s], o.at[self.s], own)

    def piece(self, k):
        t = peer(self.s, k)
        dst = self.o.at[self.s]
        return remote(self.x.at[t], dst, self.send.at[k], self.recv.at[k], (t, self.f))

    def start(self):
        for k in reversed(range(1, 8)):
            self.piece(k).start()
        self.mine.start()

    def finish(self):
        self.mine.wait()
        for k in reversed(range(1, 8)):
            self.piece(k).wait_recv()
            self.piece(k).wait_send()


def merged(*lists):
    keyed = []
    for n, items in enumerate(lists):
        keyed += [((i + 0.5) / len(items), n, item) for i, item in enumerate(items)]
    return [item for _, _, item in sorted(keyed, key=lambda v: v[:2])]


def dot(a, b, ca=1, cb=0):
    return lax.dot_general(a, b, (((ca,), (cb,)), ((), ())), preferred_element_type=jnp.float32)


def starts_of(pos, lengths_ref, nseg):
    start = jnp.zeros_like(pos)
    end = 0
    for i in range(nseg - 1):
        end = end + lengths_ref[0, i]
        start = jnp.where(pos >= end, end, start)
    return start


def head_lanes(h):
    lane = lax.broadcasted_iota(jnp.int32, (1, 128), 1)
    return (lane // HEAD_DIM) == h


def turn(x, c, s1, s2, sign):
    half = ROT // 2
    return x * c + (pltpu.roll(x, 128 - half, 1) * s1 + pltpu.roll(x, half, 1) * s2) * sign


def block_mask(qb, lengths_ref):
    keys = (qb + 1) * QB
    row = qb * QB + lax.broadcasted_iota(jnp.int32, (QB, 1), 0)
    col = lax.broadcasted_iota(jnp.int32, (1, keys), 1)
    return (col >= starts_of(row, lengths_ref, lengths_ref.shape[1])) & (col <= row)


def row_at(i, step=QB):
    return pl.ds(pl.multiple_of(i * step, step), step)


def picks(orow_ref, i):
    p = lax.broadcasted_iota(jnp.int32, (QB, 1), 0) + i * QB == orow_ref[...]
    return jnp.where(p, 1.0, 0.0).astype(jnp.bfloat16)


def puts(oc, valid):
    p = oc == lax.broadcasted_iota(jnp.int32, (1, valid), 1)
    return jnp.where(p, 1.0, 0.0).astype(jnp.bfloat16)


def attend(
    a_ref, w_ref, shift_of, tables, orow_ref, ocol_ref, len_ref, o_ref, pk_ref, lse_ref, rot, opk
):
    rows, w3 = rot.shape
    w = w3 // 3
    valid = pk_ref.shape[0]
    scale = HEAD_DIM**-0.5
    c_ref, s1_ref, s2_ref = tables

    def project():
        shift = shift_of()

        @pl.loop(0, rows // 256)
        def _(i):
            r = row_at(i, 256)
            c, s1, s2 = c_ref[r], s1_ref[r], s2_ref[r]
            left = jnp.concatenate([a_ref[2 * i], a_ref[2 * i + 1]], 0)
            qkv = dot(left, w_ref[...]) + shift
            for t in range(w3 // 128):
                cols = slice(t * 128, t * 128 + 128)
                x = qkv[:, cols]
                if t < 2 * w // 128:
                    x = turn(x, c, s1, s2, 1.0)
                rot[r, cols] = x.astype(jnp.bfloat16)

    def pack():
        @pl.loop(0, valid // QB)
        def _(i):
            pk_ref[row_at(i)] = dot(picks(orow_ref, i), rot[...]).astype(jnp.bfloat16)

    def block(qb, t):
        keys = (qb + 1) * QB
        rq = slice(qb * QB, qb * QB + QB)
        ct = slice(t * 128, t * 128 + 128)
        mask = block_mask(qb, len_ref)
        q = pk_ref[rq, ct]
        k = pk_ref[0:keys, w + t * 128 : w + t * 128 + 128]
        v = pk_ref[0:keys, 2 * w + t * 128 : 2 * w + t * 128 + 128]
        total = None
        for h in range(2):
            qh = jnp.where(head_lanes(h), q, jnp.zeros_like(q))
            scores = jnp.where(mask, dot(qh, k, 1, 1) * scale, NEG)
            top = jnp.max(scores, -1, keepdims=True)
            expo = jnp.exp(scores - top)
            norm = jnp.sum(expo, -1, keepdims=True)
            probs = (expo / norm).astype(jnp.bfloat16)
            lse_ref[2 * t + h, rq] = top + jnp.log(norm)
            out = dot(probs, v)
            total = out if h == 0 else jnp.where(head_lanes(1), out, total)
        opk[rq, ct] = total.astype(jnp.bfloat16)

    def unpack():
        per = o_ref.shape[1]

        @pl.loop(0, rows // per)
        def _(i):
            r = row_at(i, per)
            oc = ocol_ref[r]
            back = dot(puts(oc, valid), opk[...])
            pad = rot[r, 2 * w :].astype(jnp.float32)
            o_ref[i] = jnp.where(oc >= valid, pad, back).astype(jnp.bfloat16)

    blocks = [
        functools.partial(block, qb, t) for qb in range(valid // QB) for t in range(w // 128)
    ]
    return [project, pack] + blocks + [unpack]


def attend_back(
    pk_ref, do_ref, lse_ref, tables, orow_ref, ocol_ref, len_ref, g_ref, b_ref, dpk, dq, dk, dv, gpk
):
    rows, w = do_ref.shape
    valid = pk_ref.shape[0]
    scale = HEAD_DIM**-0.5
    c_ref, s1_ref, s2_ref = tables

    def pack():
        @pl.loop(0, valid // QB)
        def _(i):
            r = row_at(i)
            dpk[r] = dot(picks(orow_ref, i), do_ref[...]).astype(jnp.bfloat16)
            dk[r] = jnp.zeros((QB, w), jnp.float32)
            dv[r] = jnp.zeros((QB, w), jnp.float32)

    def block(qb, t):
        keys = (qb + 1) * QB
        rq = slice(qb * QB, qb * QB + QB)
        ct = slice(t * 128, t * 128 + 128)
        mask = block_mask(qb, len_ref)
        q, d = pk_ref[rq, ct], dpk[rq, ct]
        k = pk_ref[0:keys, w + t * 128 : w + t * 128 + 128]
        v = pk_ref[0:keys, 2 * w + t * 128 : 2 * w + t * 128 + 128]
        total = None
        for h in range(2):
            hl = head_lanes(h)
            qh = jnp.where(hl, q, jnp.zeros_like(q))
            dh = jnp.where(hl, d, jnp.zeros_like(d))
            scores = jnp.where(mask, dot(qh, k, 1, 1) * scale, NEG)
            p = jnp.exp(scores - lse_ref[2 * t + h, rq])
            dp = dot(dh, v, 1, 1)
            inner = jnp.sum(p * dp, -1, keepdims=True)
            ds = (p * (dp - inner)).astype(jnp.bfloat16)
            dv[0:keys, ct] += dot(p.astype(jnp.bfloat16), dh, 0, 0)
            dk[0:keys, ct] += dot(ds, qh, 0, 0)
            part = dot(ds, k)
            total = part if h == 0 else jnp.where(head_lanes(1), part, total)
        dq[rq, ct] = total

    def rotary():
        @pl.loop(0, valid // QB)
        def _(i):
            r = row_at(i)
            c, s1, s2 = c_ref[r], s1_ref[r], s2_ref[r]
            for t in range(w // 128):
                ct = slice(t * 128, t * 128 + 128)
                for j, src in ((0, dq), (1, dk)):
                    x = (src[r, ct] * scale).astype(jnp.bfloat16).astype(jnp.float32)
                    at = j * w + t * 128
                    gpk[r, at : at + 128] = turn(x, c, s1, s2, -1.0).astype(jnp.bfloat16)
                at = 2 * w + t * 128
                gpk[r, at : at + 128] = dv[r, ct].astype(jnp.bfloat16)

    def unpack():
        b_ref[...] = jnp.zeros_like(b_ref)

        @pl.loop(0, rows // QB)
        def _(i):
            r = row_at(i)
            oc = ocol_ref[r]
            back = dot(puts(oc, valid), gpk[...])
            pad = jnp.where(oc >= valid, do_ref[r].astype(jnp.float32), 0.0)
            back = jnp.concatenate([back[:, : 2 * w], back[:, 2 * w :] + pad], 1)
            g_ref[r] = back.astype(jnp.bfloat16)
            b_ref[...] += jnp.sum(back, 0, keepdims=True)

    blocks = [
        functools.partial(block, qb, t) for qb in range(valid // QB) for t in range(w // 128)
    ]
    return [pack] + blocks + [rotary, unpack]


def forward_kernel(
    x_ref,
    p_ref,
    qp_ref,
    op_ref,
    dm_ref,
    wp_ref,
    dp_ref,
    c_ref,
    s1_ref,
    s2_ref,
    orow_ref,
    ocol_ref,
    len_ref,
    a_ref,
    qw_ref,
    n_ref,
    ow_ref,
    ho_ref,
    pk_ref,
    lse_ref,
    dmo_ref,
    ww_ref,
    dw_ref,
    mix_ref,
    xs,
    got,
    rot,
    opk,
    psend,
    precv,
    *sems,
):
    s, f, z, y = where_am_i()
    me = s * 4 + f
    greet_all(s, f)
    gather = SeqGather(x_ref, xs, *sems[:5])
    slices = ColGather(qp_ref, qw_ref, *sems[5:10])
    whole = WholeGather(op_ref, ow_ref, *sems[10:17])
    grads = SeqGather(dm_ref, dmo_ref, *sems[17:22])
    wide = ColGather(wp_ref, ww_ref, *sems[22:27])
    down = FsdpGather(dp_ref, dw_ref, *sems[27:30])
    swap = RowExchange(mix_ref, ho_ref, *sems[30:])

    def param(k):
        i = (me + k) % 32
        return remote(p_ref, got.at[me], psend.at[k], precv.at[k], dealer(i))

    @pl.loop(1, 32)
    def _(k):
        param(k).start()

    gather.start()
    slices.start()
    got[me] = p_ref[...]

    @pl.loop(1, 32)
    def _(k):
        param(k).wait_recv()

    for i in range(16):
        n_ref[:, i * 128 : i * 128 + 128] = got[2 * i] + got[2 * i + 1]
    step = 16

    def norm(b):
        gain, shift = n_ref[0:1], n_ref[1:2]

        @pl.loop(0, x_ref.shape[0] // step)
        def _(i):
            r = row_at(i, step)
            normed, _ = normalize(xs[b, r].astype(jnp.float32))
            a_ref[b, r] = (normed * gain + shift).astype(jnp.bfloat16)

    def shift_of():
        w = rot.shape[1] // 3
        parts = []
        for n in range(3):
            part = jnp.zeros((1, w), jnp.float32)
            for i in range(8):
                piece = n_ref[4 + n : 5 + n, i * w : i * w + w]
                part = part + jnp.where(s == i, piece, jnp.zeros_like(piece))
            parts.append(part)
        return jnp.concatenate(parts, 1)

    work = attend(
        a_ref,
        qw_ref,
        shift_of,
        (c_ref, s1_ref, s2_ref),
        orow_ref,
        ocol_ref,
        len_ref,
        mix_ref,
        pk_ref,
        lse_ref,
        rot,
        opk,
    )
    p = functools.partial

    def own():
        gather.own.wait()
        norm(s)

    first = [own]
    for i in range(3):
        first.append(p(gather.arrive, i + 1))
        first.append(lambda i=i: norm(gather.cross(i)))
        first.append(lambda i=i: norm(2 * gather.near(i + 1) + y))
    first.append(lambda: norm(gather.cross(3)))
    lead, rest = slices.steps(), wide.steps()
    for item in merged(first[:7], lead[:6]):
        item()
    grads.start()
    wide.start()
    for item in merged(first[7:], lead[6:]):
        item()
    whole.start()
    down.start()
    slices.finish()
    lines = whole.steps()
    side = [p(grads.arrive, 1)] + rest[:3] + [p(grads.arrive, 2)] + rest[3:7] + [p(grads.arrive, 3)]
    for item in merged(work, side, lines[:6]):
        item()
    swap.start()
    for item in merged(rest[7:], lines[6:]):
        item()
    down.step()
    for i in range(4):
        grads.cross(i)
    swap.finish()
    wide.finish()
    whole.finish()
    down.finish()
    grads.finish()
    gather.finish(False)

    @pl.loop(1, 32)
    def _(k):
        param(k).wait_send()


def forward(
    x, params, qkv_p, out_p, dm, wide_p, down_p, tables, orow, ocol, lengths, valid, collective
):
    rows, width = x.shape
    w3 = qkv_p.shape[2]
    w = w3 // 3
    group = 8 * rows
    heads = w // HEAD_DIM

    def out(shape, dtype=jnp.bfloat16):
        return jax.ShapeDtypeStruct(shape, dtype)

    return pl.pallas_call(
        forward_kernel,
        out_shape=(
            out((8, rows, width)),
            out((width, w3)),
            out((8, width), jnp.float32),
            out((32,) + out_p.shape),
            out((8, rows, w)),
            out((valid, w3)),
            out((heads, valid, 1), jnp.float32),
            out((8, rows, width)),
            out((width, wide_p.shape[2])),
            out((4,) + down_p.shape),
            out((8, rows, w)),
        ),
        in_specs=[VMEM_SPEC] * 12 + [SMEM_SPEC],
        out_specs=(VMEM_SPEC,) * 3
        + (ANY_SPEC,)
        + (VMEM_SPEC,) * 3
        + (ANY_SPEC,) * 3
        + (VMEM_SPEC,),
        scratch_shapes=[
            pltpu.VMEM((8, rows, width), jnp.bfloat16),
            pltpu.VMEM((32, 8, 128), jnp.float32),
            pltpu.VMEM((group, w3), jnp.bfloat16),
            pltpu.VMEM((valid, w), jnp.bfloat16),
            DMA((32,)),
            DMA((32,)),
        ]
        + SeqGather.scratch()
        + ColGather.scratch()
        + WholeGather.scratch()
        + SeqGather.scratch()
        + ColGather.scratch()
        + FsdpGather.scratch()
        + RowExchange.scratch(),
        compiler_params=comm_params(collective),
    )(x, params, qkv_p, out_p, dm, wide_p, down_p, *tables, orow, ocol, lengths)


def tall(rows, step=16):
    def wrap(fn):
        @pl.loop(0, rows // step)
        def _(i):
            fn(row_at(i, step))

    return wrap


def middle_kernel(
    ho_ref,
    ow_ref,
    x_ref,
    n_ref,
    ww_ref,
    dw_ref,
    dm_ref,
    attn_ref,
    res_ref,
    rg_ref,
    vec_ref,
    mp_ref,
    dg_ref,
    h_ref,
    big,
    cloc,
    c_ref,
    hid,
    act,
    part,
    second,
    load,
    *scratch,
):
    s, f, z, y = where_am_i()
    rows, width = x_ref.shape
    lf = dw_ref.shape[0]
    lw = ho_ref.shape[2]
    fetch = pltpu.make_async_copy(ow_ref, big, load)
    fetch.start()
    greet_columns(s, f)
    gather = SeqGather(cloc, c_ref, *scratch[:5])
    reduce = SeqReduce(part, second, *scratch[5:11])
    sums = ColSum(big, h_ref, *scratch[11:])
    gain, shift = n_ref[2:3], n_ref[3:4]
    fetch.wait()

    @pl.loop(0, width // 512)
    def _(j):
        cols = pl.ds(pl.multiple_of(j * 512, 512), 512)
        total = dot(ho_ref[0], big[0:lw, cols])
        for k in range(1, 8):
            total = total + dot(ho_ref[k], big[k * lw : k * lw + lw, cols])
        attn_ref[:, cols] = total
        res_ref[:, cols] = x_ref[:, cols].astype(jnp.float32) + total

    @tall(rows)
    def _(r):
        normed, _ = normalize(res_ref[r])
        cloc[r] = (normed * gain + shift).astype(jnp.bfloat16)

    gather.start()
    gather.own.wait()

    def block(b):
        at = pl.ds(pl.multiple_of(b * rows, rows), rows)
        wide = dot(c_ref[b], ww_ref[...])
        gate, upper = wide[:, :lf], wide[:, lf:]
        hidden, sigma = mlp_forward(gate, upper)
        hid[at] = hidden
        grad = dot(dm_ref[b], dw_ref[...], 1, 1)
        gate_act, up_act = mlp_backward(grad, gate, upper, sigma)
        act[at] = jnp.concatenate([gate_act, up_act], 1)
        part[b] = dot(act[at], ww_ref[...], 1, 1).astype(jnp.bfloat16)

    gather.each(block)
    reduce.start()

    def wide_grad(i):
        left = [c_ref[b, :, i * 256 : i * 256 + 256] for b in range(8)]
        left = jnp.concatenate(left, 0)
        big[i * 256 : i * 256 + 256, 0 : 2 * lf] = dot(left, act[...], 0, 0).astype(jnp.bfloat16)
        sums.send(i)

    def mlp_part(i):
        @pl.loop(2 * i, 2 * i + 2)
        def _(b):
            at = pl.ds(pl.multiple_of(b * rows, rows), rows)
            mp_ref[b] = dot(hid[at], dw_ref[...]).astype(jnp.bfloat16)

    def down_grad(i):
        cols = slice(i * 256, i * 256 + 256)
        right = jnp.concatenate([dm_ref[b, :, cols] for b in range(8)], 0)
        dg_ref[:, cols] = dot(hid[...], right, 0, 0).astype(jnp.bfloat16)

    p = functools.partial
    work = []
    for i in range(8):
        work.append(p(wide_grad, i))
        if i:
            work.append(p(sums.step, i - 1))
    work += [p(mlp_part, 0), p(sums.step, 7)] + [p(mlp_part, i) for i in (1, 2, 3)]
    work += [p(down_grad, i) for i in range(8)]
    later = reduce.steps()
    for item in merged(work, later[:6]):
        item()
    for item in merged([p(sums.total, i) for i in range(8)], later[6:]):
        item()
    vec_ref[...] = jnp.zeros_like(vec_ref)

    @tall(rows)
    def _(r):
        grad = second[r]
        normed, rstd = normalize(res_ref[r])
        inner, gain_part, shift_part = norm_back(grad, normed, rstd, gain)
        rg_ref[r] = dm_ref[s, r].astype(jnp.float32) + inner
        vec_ref[0:1] += gain_part[None]
        vec_ref[1:2] += shift_part[None]

    gather.finish(False)
    reduce.finish()
    sums.finish()


def middle(heads_out, out_w, x, norms, wide_w, down_w, dm, collective):
    rows, width = x.shape
    lf = down_w.shape[0]
    group = 8 * rows
    part = width // 32

    def out(shape, dtype=jnp.bfloat16):
        return jax.ShapeDtypeStruct(shape, dtype)

    def vm(shape, dtype=jnp.bfloat16):
        return pltpu.VMEM(shape, dtype)

    wide = (rows, width)
    return pl.pallas_call(
        middle_kernel,
        out_shape=(
            out(wide, jnp.float32),
            out(wide, jnp.float32),
            out(wide, jnp.float32),
            out((8, width), jnp.float32),
            out((8,) + wide),
            out((lf, width)),
            out((8, part, 2 * lf)),
        ),
        in_specs=[VMEM_SPEC, ANY_SPEC] + [VMEM_SPEC] * 5,
        out_specs=(VMEM_SPEC,) * 7,
        scratch_shapes=[
            vm((width, width)),
            vm(wide),
            vm((8,) + wide),
            vm((group, lf)),
            vm((group, 2 * lf)),
            vm((8,) + wide),
            vm(wide, jnp.float32),
            DMA,
        ]
        + SeqGather.scratch()
        + SeqReduce.scratch(rows, width)
        + ColSum.scratch(part, 2 * lf),
        compiler_params=comm_params(collective, 63),
    )(heads_out, out_w, x, norms, wide_w, down_w, dm)


def backward_kernel(
    rg_ref,
    or_ref,
    mix_ref,
    pk_ref,
    lse_ref,
    c_ref,
    s1_ref,
    s2_ref,
    orow_ref,
    ocol_ref,
    len_ref,
    attn_ref,
    res_ref,
    valid_ref,
    mp_ref,
    dg_ref,
    h_ref,
    g_ref,
    b_ref,
    lo_ref,
    sum_ref,
    gate_ref,
    up_ref,
    down_ref,
    out_ref,
    da,
    full,
    do_ref,
    og,
    mlp,
    got,
    dpk,
    dq,
    dk,
    dv,
    gpk,
    *scratch,
):
    s, f, z, y = where_am_i()
    rows, width = rg_ref.shape
    part, ff = gate_ref.shape
    lf = ff // 8
    greet_columns(s, f)
    gather = SeqGather(da, full, *scratch[:5])
    reduce = SeqReduce(mp_ref, mlp, *scratch[5:11])
    swap = RowExchange(h_ref, got, *scratch[11:14])
    down = FsdpReduce(dg_ref, down_ref, *scratch[14:18])
    outer_sum = FsdpReduce(og, out_ref, *scratch[18:])

    @tall(rows)
    def _(r):
        da[r] = rg_ref[r].astype(jnp.bfloat16)

    gather.start()
    down.start()
    gather.own.wait()
    down.step()

    def block(b):
        at = pl.ds(pl.multiple_of(b * rows, rows), rows)
        do_ref[at] = dot(full[b], or_ref[...], 1, 1).astype(jnp.bfloat16)

    gather.each(block)
    reduce.start()
    swap.start()

    def out_grad(i):
        cols = slice(i * 256, i * 256 + 256)
        right = jnp.concatenate([full[b, :, cols] for b in range(8)], 0)
        value = dot(mix_ref[...], right, 0, 0).astype(jnp.bfloat16)
        for k in range(4):
            og[k, :, cols] = value[k * part : k * part + part]

    p = functools.partial
    work = attend_back(
        pk_ref,
        do_ref,
        lse_ref,
        (c_ref, s1_ref, s2_ref),
        orow_ref,
        ocol_ref,
        len_ref,
        g_ref,
        b_ref,
        dpk,
        dq,
        dk,
        dv,
        gpk,
    )
    work += [p(out_grad, i) for i in range(8)] + [outer_sum.start, outer_sum.step, down.total]
    later = reduce.steps()
    for item in merged(work, later[:4]):
        item()
    for item in later[4:]:
        item()
    outer_sum.total()
    sum_ref[...] = jnp.zeros_like(sum_ref)

    @tall(rows)
    def _(r):
        m = mlp[r]
        result = res_ref[r] + m
        lo_ref[r] = result.astype(jnp.bfloat16)
        keep = valid_ref[r]
        for n, v in enumerate((result, attn_ref[r], m)):
            total = jnp.sum(jnp.sum(v * v, -1, keepdims=True) * keep, 0, keepdims=True)
            sum_ref[n : n + 1] += jnp.broadcast_to(total, (1, 128))

    swap.finish()
    for n, ref in enumerate((gate_ref, up_ref)):
        for i in range(8):
            ref[:, i * lf : i * lf + lf] = got[i, :, n * lf : n * lf + lf].astype(jnp.float32)
    gather.finish(False)
    reduce.finish()
    down.finish()
    outer_sum.finish()


def backward(
    rg, out_rows, mixed, pk, lse, tables, orow, ocol, lengths, attn, res, keep, mp, dg, h, collective
):
    rows, width = rg.shape
    group, w = mixed.shape
    valid = pk.shape[0]
    part = h.shape[1]
    ff = h.shape[2] * 4

    def out(shape, dtype=jnp.float32):
        return jax.ShapeDtypeStruct(shape, dtype)

    def vm(shape, dtype=jnp.bfloat16):
        return pltpu.VMEM(shape, dtype)

    return pl.pallas_call(
        backward_kernel,
        out_shape=(
            out((group, 3 * w), jnp.bfloat16),
            out((1, 3 * w)),
            out((rows, width), jnp.bfloat16),
            out((8, 128)),
            out((part, ff)),
            out((part, ff)),
            out(dg.shape[1:]),
            out((part, width)),
        ),
        in_specs=[VMEM_SPEC] * 10 + [SMEM_SPEC] + [VMEM_SPEC] * 6,
        out_specs=(VMEM_SPEC,) * 8,
        scratch_shapes=[
            vm((rows, width)),
            vm((8, rows, width)),
            vm((group, w)),
            vm((4, part, width)),
            vm((rows, width), jnp.float32),
            vm(h.shape),
            vm((valid, w)),
            vm((valid, w), jnp.float32),
            vm((valid, w), jnp.float32),
            vm((valid, w), jnp.float32),
            vm((valid, 3 * w)),
        ]
        + SeqGather.scratch()
        + SeqReduce.scratch(rows, width)
        + RowExchange.scratch()
        + FsdpReduce.scratch(*dg.shape[1:])
        + FsdpReduce.scratch(part, width),
        compiler_params=comm_params(collective, 60),
    )(rg, out_rows, mixed, pk, lse, *tables, orow, ocol, lengths, attn, res, keep, mp, dg, h)


def last_kernel(
    g_ref,
    b_ref,
    qw_ref,
    a_ref,
    x_ref,
    rg_ref,
    n_ref,
    vec_ref,
    sum_ref,
    ig_ref,
    qg_ref,
    total_ref,
    part,
    first,
    grad,
    h,
    got,
    msg,
    inbox,
    vec,
    msend,
    mrecv,
    *scratch,
):
    s, f, z, y = where_am_i()
    me = s * 4 + f
    rows, width = x_ref.shape
    w3 = g_ref.shape[1]
    w = w3 // 3
    pr = qg_ref.shape[0]
    greet_all(s, f)
    reduce = SeqReduce(part, first, *scratch[:6])
    sums = ColSum(grad, h, *scratch[6:12])
    swap = RowExchange(h, got, *scratch[12:])

    def block(b):
        at = pl.ds(pl.multiple_of(b * rows, rows), rows)
        part[b] = dot(g_ref[at], qw_ref[...], 1, 1).astype(jnp.bfloat16)

    for k in range(4):
        block(2 * reduce.order(k) + 1 - y)
        reduce.send(k)

    def own_block(k):
        block(2 * reduce.order(k) + y)

    def qkv_grad(i):
        left = [a_ref[b, :, i * 256 : i * 256 + 256] for b in range(8)]
        left = jnp.concatenate(left, 0)
        grad[i * 256 : i * 256 + 256] = dot(left, g_ref[...], 0, 0).astype(jnp.bfloat16)
        sums.send(i)

    p = functools.partial
    for k in range(4):
        own_block(k)
    work = []
    for i in range(8):
        work.append(p(qkv_grad, i))
        if i:
            work.append(p(sums.step, i - 1))
    work.append(p(sums.step, 7))

    def hand_over(k):
        sums.total(peer(s, k))
        if k:
            swap.piece(k).start()
        else:
            swap.mine.start()

    work += [p(hand_over, k) for k in reversed(range(8))]
    for item in merged(work, reduce.steps()):
        item()
    vec[0:2] = jnp.zeros((2, width), jnp.float32)
    vec[2:4] = vec_ref[0:2]
    gain = n_ref[0:1]

    @tall(rows)
    def _(r):
        normed, rstd = normalize(x_ref[r].astype(jnp.float32))
        inner, gain_part, shift_part = norm_back(first[r], normed, rstd, gain)
        ig_ref[r] = rg_ref[r] + inner
        vec[0:1] += gain_part[None]
        vec[1:2] += shift_part[None]

    lane = lax.broadcasted_iota(jnp.int32, (1, 128), 1)
    scalars = jnp.where(lane == 0, sum_ref[0:1], jnp.where(lane == 1, sum_ref[1:2], sum_ref[2:3]))
    for i in range(16):
        cols = slice(i * 128, i * 128 + 128)
        msg[i, 0:4] = vec[0:4, cols]
        msg[i, 4:5] = scalars
        at = (i % 2) * 128
        for n in range(3):
            piece = b_ref[0:1, n * w + at : n * w + at + 128]
            msg[i, 5 + n : 6 + n] = jnp.where(s == i // 2, piece, jnp.zeros_like(piece))

    def message(k):
        i = (me + k) % 32
        return remote(msg.at[i // 2], inbox.at[k], msend.at[k], mrecv.at[k], dealer(i))

    @pl.loop(1, 32)
    def _(k):
        message(k).start()

    swap.finish()
    for i in range(8):
        for n in range(3):
            at = n * width + i * w
            qg_ref[:, at : at + w] = got[i, :, n * w : n * w + w].astype(jnp.float32)
    reduce.finish()
    sums.finish()
    total_ref[...] = msg[me // 2]

    @pl.loop(1, 32)
    def _(k):
        message(k).wait_recv()
        total_ref[...] += inbox[k]

    @pl.loop(1, 32)
    def _(k):
        message(k).wait_send()


def last(g, b, qkv_w, a, x, rg, norms, vec, sums, collective):
    rows, width = x.shape
    w3 = g.shape[1]
    pr = width // 32

    def out(shape, dtype=jnp.float32):
        return jax.ShapeDtypeStruct(shape, dtype)

    def vm(shape, dtype=jnp.bfloat16):
        return pltpu.VMEM(shape, dtype)

    return pl.pallas_call(
        last_kernel,
        out_shape=(out((rows, width)), out((pr, 3 * width)), out((8, 128))),
        in_specs=[VMEM_SPEC] * 9,
        out_specs=(VMEM_SPEC,) * 3,
        scratch_shapes=[
            vm((8, rows, width)),
            vm((rows, width), jnp.float32),
            vm((width, w3)),
            vm((8, pr, w3)),
            vm((8, pr, w3)),
            vm((16, 8, 128), jnp.float32),
            vm((32, 8, 128), jnp.float32),
            vm((4, width), jnp.float32),
            DMA((32,)),
            DMA((32,)),
        ]
        + SeqReduce.scratch(rows, width)
        + ColSum.scratch(pr, w3)
        + RowExchange.scratch(),
        compiler_params=comm_params(collective, 56),
    )(g, b, qkv_w, a, x, rg, norms, vec, sums)


def rotary_tables(rel):
    half = ROT // 2
    d = jnp.arange(128, dtype=jnp.int32) % HEAD_DIM
    freq = 10000.0 ** (-2.0 * (d % half).astype(jnp.float32) / ROT)
    angle = rel[:, None] * freq[None, :]
    c, s = jnp.cos(angle), jnp.sin(angle)
    second = (d >= half) & (d < ROT)
    return (jnp.where(d < ROT, c, 1.0), jnp.where(d < half, -s, 0.0), jnp.where(second, s, 0.0))


def line_body(
    hidden_in,
    ln1_gain,
    ln1_bias,
    qkv_weight,
    qkv_bias,
    out_weight,
    ln2_gain,
    ln2_bias,
    gate_weight,
    up_weight,
    down_weight,
    seq_lengths,
    deal_order,
    out_grad,
):
    rows = hidden_in.shape[1]
    width = hidden_in.shape[2]
    nseq = lax.axis_size("seq")
    nfsdp = lax.axis_size("fsdp")
    lw = width // nseq
    part = qkv_weight.shape[0]
    ff = gate_weight.shape[1]
    lf = ff // nseq
    seq_at, fsdp_at = lax.axis_index("seq"), lax.axis_index("fsdp")
    order = deal_order[0]
    lengths = seq_lengths[0]
    group_rows = order.shape[0]
    valid_rows = group_rows * 5 // 8
    orow, ocol = order[None, :], order[:, None]
    local_pos = lax.dynamic_slice_in_dim(order, seq_at * rows, rows)
    valid = (local_pos < valid_rows).astype(jnp.float32)[:, None]
    dealt_seg, dealt_start = segment_of(order, lengths)
    dealt_tables = rotary_tables((order - dealt_start).astype(jnp.float32))
    packed_pos = jnp.arange(valid_rows, dtype=jnp.int32)
    packed_seg, packed_start = segment_of(packed_pos, lengths)
    packed_tables = rotary_tables((packed_pos - packed_start).astype(jnp.float32))

    def column_parts(weights):
        views = [w.reshape(part, nseq, -1) for w in weights]
        return jnp.concatenate(views, 2).transpose(1, 0, 2)

    params = jnp.stack([ln1_gain, ln1_bias, ln2_gain, ln2_bias, *qkv_bias])
    params = jnp.pad(params.astype(jnp.float32), ((0, 1), (0, 64)))
    params = jnp.where(fsdp_at % 2 == 0, params, jnp.roll(params, part, 1))
    qkv_parts = qkv_weight.reshape(part, 3, nseq, lw).transpose(2, 0, 1, 3).reshape(nseq, part, -1)
    first_in, qkv_w, norms, out_w, heads_out, packed, lse, mlp_grad, wide_w, down_w, mixed = forward(
        hidden_in[0],
        params,
        qkv_parts,
        out_weight,
        out_grad[0],
        column_parts([gate_weight, up_weight]),
        down_weight,
        dealt_tables,
        orow,
        ocol,
        seq_lengths,
        valid_rows,
        1,
    )
    out_rows = lax.dynamic_slice_in_dim(out_w, seq_at * nfsdp, nfsdp).reshape(lw, width)
    attn, resid, resid_grad, norm2_grads, mlp_part, down_part, wide_sum = middle(
        heads_out,
        out_w.reshape(width, width),
        hidden_in[0],
        norms,
        wide_w,
        down_w.reshape(lf, width),
        mlp_grad,
        3,
    )
    qkv_act, bias_sums, result, sums, gate_grad, up_grad, down_grad, out_grad_w = backward(
        resid_grad,
        out_rows,
        mixed.reshape(group_rows, lw),
        packed,
        lse,
        packed_tables,
        orow,
        ocol,
        seq_lengths,
        attn,
        resid,
        valid,
        mlp_part,
        down_part.reshape(nfsdp, -1, width),
        wide_sum,
        4,
    )
    input_grad, qkv_grad, total = last(
        qkv_act, bias_sums, qkv_w, first_in, hidden_in[0], resid_grad, norms, norm2_grads, sums, 5
    )
    count = valid_rows * nfsdp * width
    rms = jnp.sqrt(total[4, :3] / count)
    halves = lax.dynamic_slice_in_dim(total, (fsdp_at % 2) * part, part, 1)
    shards = halves[:4]
    qkv_bias_grad = halves[5:8]
    return (
        result[None],
        input_grad[None],
        shards[0],
        shards[1],
        qkv_grad,
        qkv_bias_grad,
        out_grad_w,
        shards[2],
        shards[3],
        gate_grad,
        up_grad,
        down_grad,
        rms,
    )


def solution(mesh):
    in_specs = (
        P("fsdp", "seq", None),
        P(("seq", "fsdp")),
        P(("seq", "fsdp")),
        P(("seq", "fsdp"), None),
        P(None, ("seq", "fsdp")),
        P(("seq", "fsdp"), None),
        P(("seq", "fsdp")),
        P(("seq", "fsdp")),
        P(("seq", "fsdp"), None),
        P(("seq", "fsdp"), None),
        P(("seq", "fsdp"), None),
        P("fsdp", None),
        P("fsdp", None),
        P("fsdp", "seq", None),
    )
    out_specs = (
        P("fsdp", "seq", None),
        P("fsdp", "seq", None),
        P(("seq", "fsdp")),
        P(("seq", "fsdp")),
        P(("seq", "fsdp"), None),
        P(None, ("seq", "fsdp")),
        P(("seq", "fsdp"), None),
        P(("seq", "fsdp")),
        P(("seq", "fsdp")),
        P(("seq", "fsdp"), None),
        P(("seq", "fsdp"), None),
        P(("seq", "fsdp"), None),
        P(),
    )
    line = dict(mesh.shape) == {"seq": 8, "fsdp": 4}
    return jax.shard_map(
        line_body if line else body,
        mesh=mesh,
        in_specs=in_specs,
        out_specs=out_specs,
        check_vma=False,
    )
```

```python
import functools

import jax
import jax.numpy as jnp
from jax import lax
from jax.experimental import pallas as pl
from jax.experimental.pallas import tpu as pltpu
from jax.sharding import PartitionSpec as P

HEAD_DIM = 64
ROT = 16


EPS = 1e-05


def normalize(values):
    center = values - jnp.mean(values, -1, keepdims=True)
    spread = jnp.mean(center * center, -1, keepdims=True)
    rstd = lax.rsqrt(spread + EPS)
    return (center * rstd, rstd)


def norm_back(grad, normed, rstd, gain):
    scaled = grad * gain
    inner = (
        scaled
        - jnp.mean(scaled, -1, keepdims=True)
        - normed * jnp.mean(scaled * normed, -1, keepdims=True)
    )
    return (rstd * inner, jnp.sum(grad * normed, 0), jnp.sum(grad, 0))


def segment_of(pos, lengths):
    nseg = lengths.shape[0]
    ends = jnp.cumsum(lengths)
    seg = jnp.sum((pos[:, None] >= ends[None, :]).astype(jnp.int32), 1)
    starts = jnp.concatenate([jnp.zeros((1,), jnp.int32), ends[:-1]])
    start = jnp.sum(
        jnp.where(seg[:, None] == jnp.arange(nseg, dtype=jnp.int32)[None, :], starts[None, :], 0), 1
    )
    start = jnp.where(seg < nseg, start, pos)
    return (seg, start)


def rotate(values, rel, sign):
    count = values.shape[0]
    view = values.reshape(count, -1, HEAD_DIM)
    half = ROT // 2
    freq = 10000.0 ** (-2.0 * jnp.arange(half, dtype=jnp.float32) / ROT)
    angle = rel[:, None] * freq[None, :]
    cosine = jnp.cos(angle)[:, None, :]
    sine = jnp.sin(angle)[:, None, :]
    first = view[..., :half]
    second = view[..., half:ROT]
    turned = jnp.concatenate(
        [
            first * cosine - sign * second * sine,
            second * cosine + sign * first * sine,
            view[..., ROT:],
        ],
        -1,
    )
    return turned.reshape(count, -1)


def outer(left, right):
    return lax.dot_general(
        left, right, (((0,), (0,)), ((), ())), preferred_element_type=jnp.float32
    )


def times(left, right):
    return jnp.dot(left, right, preferred_element_type=jnp.float32)


def times_transposed(left, right):
    return lax.dot_general(
        left, right, (((1,), (1,)), ((), ())), preferred_element_type=jnp.float32
    )


def mlp_forward(gate, upper):
    sigma = jax.nn.sigmoid(gate)
    return ((gate * sigma * upper).astype(jnp.bfloat16), sigma)


def mlp_backward(hidden_grad, gate, upper, sigma):
    up_act = (hidden_grad * gate * sigma).astype(jnp.bfloat16)
    gate_act = (hidden_grad * upper * sigma * (1.0 + gate * (1.0 - sigma))).astype(jnp.bfloat16)
    return (gate_act, up_act)


def body(
    hidden_in,
    ln1_gain,
    ln1_bias,
    qkv_weight,
    qkv_bias,
    out_weight,
    ln2_gain,
    ln2_bias,
    gate_weight,
    up_weight,
    down_weight,
    seq_lengths,
    deal_order,
    out_grad,
):
    rows = hidden_in.shape[1]
    width = hidden_in.shape[2]
    nseq = lax.axis_size("seq")
    nfsdp = lax.axis_size("fsdp")
    local_width = width // nseq
    part = qkv_weight.shape[0]
    ff = gate_weight.shape[1]
    local_ff = ff // nseq
    stream = hidden_in[0].astype(jnp.float32)
    cotangent = out_grad[0].astype(jnp.float32)
    order = deal_order[0]
    lengths = seq_lengths[0]
    nseg = lengths.shape[0]
    group_rows = order.shape[0]
    valid_rows = group_rows * 5 // 8
    longest = valid_rows * 4 // 5
    blk = min(512, group_rows)
    keys = min(group_rows, longest + blk)
    nblocks = group_rows // blk
    scale = HEAD_DIM ** (-0.5)
    local_pos = lax.dynamic_slice_in_dim(order, lax.axis_index("seq") * rows, rows)
    valid = (local_pos < valid_rows).astype(jnp.float32)[:, None]
    dealt_seg, dealt_start = segment_of(order, lengths)
    rel = (order - dealt_start).astype(jnp.float32)
    inverse = (
        jnp.zeros((group_rows,), jnp.int32).at[order].set(jnp.arange(group_rows, dtype=jnp.int32))
    )
    seg_p, start_p = segment_of(jnp.arange(group_rows, dtype=jnp.int32), lengths)

    def gather_rows(values):
        return lax.all_gather(values, "seq", axis=0, tiled=True)

    def scatter_rows(partial):
        return lax.psum_scatter(
            partial.astype(jnp.bfloat16), "seq", scatter_dimension=0, tiled=True
        ).astype(jnp.float32)

    def column_slice(weight, blocks):
        cols = weight.shape[1] // (blocks * nseq)
        view = weight.reshape(part, blocks, nseq, cols).transpose(2, 0, 1, 3)
        mine = lax.all_to_all(
            view.reshape(nseq * part, blocks * cols), "seq", split_axis=0, concat_axis=0, tiled=True
        )
        full = lax.all_gather(mine.reshape(nseq, part, blocks * cols), "fsdp", axis=1)
        return full.reshape(width, blocks * cols)

    def row_slice(weight):
        return lax.all_gather(weight, "fsdp", axis=0, tiled=True)

    def column_shard(grad, blocks):
        cols = grad.shape[1] // blocks
        view = grad.astype(jnp.bfloat16).reshape(nseq, nfsdp, part, blocks * cols)
        mine = lax.psum_scatter(view.transpose(1, 0, 2, 3), "fsdp", scatter_dimension=0)
        got = lax.all_to_all(
            mine.reshape(nseq * part, blocks * cols), "seq", split_axis=0, concat_axis=0, tiled=True
        )
        view = got.reshape(nseq, part, blocks, cols).transpose(1, 2, 0, 3)
        return view.reshape(part, -1).astype(jnp.float32)

    def row_shard(grad):
        return lax.psum_scatter(
            grad.astype(jnp.bfloat16), "fsdp", scatter_dimension=0, tiled=True
        ).astype(jnp.float32)

    def to_pack(values):
        heads_here = values.shape[1] // HEAD_DIM
        return values[inverse].reshape(group_rows, heads_here, HEAD_DIM)

    def window(index, packed):
        query_p, key_p, value_p = packed
        first = index * blk
        key_first = jnp.clip(jnp.minimum(start_p[first], group_rows - keys), 0, group_rows - keys)
        qpos = first + jnp.arange(blk, dtype=jnp.int32)
        kpos = key_first + jnp.arange(keys, dtype=jnp.int32)
        qseg = lax.dynamic_slice_in_dim(seg_p, first, blk)
        kseg = lax.dynamic_slice_in_dim(seg_p, key_first, keys)
        allowed = (qseg[:, None] == kseg[None, :]) & (qseg[:, None] < nseg) & (
            kpos[None, :] <= qpos[:, None]
        ) | (kpos[None, :] == qpos[:, None])
        qblock = lax.dynamic_slice_in_dim(query_p, first, blk)
        kblock = lax.dynamic_slice_in_dim(key_p, key_first, keys)
        vblock = lax.dynamic_slice_in_dim(value_p, key_first, keys)
        scores = (
            jnp.einsum("qhd,khd->hqk", qblock, kblock, preferred_element_type=jnp.float32) * scale
        )
        scores = jnp.where(allowed[None], scores, -1e30)
        return (first, key_first, qblock, kblock, vblock, scores)

    both = ("seq", "fsdp")
    norms = lax.all_gather(
        jnp.stack([ln1_gain, ln1_bias, ln2_gain, ln2_bias, *qkv_bias]), both, axis=1, tiled=True
    )
    gain1, shift1, gain2, shift2 = norms[:4].astype(jnp.float32)
    qkv_shift = lax.dynamic_slice_in_dim(
        norms[4:], lax.axis_index("seq") * local_width, local_width, 1
    )
    qkv_shift = qkv_shift.reshape(-1).astype(jnp.float32)

    normed1, rstd1 = normalize(stream)
    first_local = (normed1 * gain1 + shift1).astype(jnp.bfloat16)
    first_in = gather_rows(first_local)
    qkv_w = column_slice(qkv_weight, 3)
    qkv = times(first_in, qkv_w) + qkv_shift
    query = rotate(qkv[:, :local_width], rel, 1.0).astype(jnp.bfloat16)
    keyset = rotate(qkv[:, local_width : 2 * local_width], rel, 1.0).astype(jnp.bfloat16)
    valueset = qkv[:, 2 * local_width :].astype(jnp.bfloat16)
    packed = (to_pack(query), to_pack(keyset), to_pack(valueset))

    def attend_block(index):
        first, key_first, qblock, kblock, vblock, scores = window(index, packed)
        top = jnp.max(scores, -1, keepdims=True)
        expo = jnp.exp(scores - top)
        total = jnp.sum(expo, -1, keepdims=True)
        probs = (expo / total).astype(jnp.bfloat16)
        mixed = jnp.einsum("hqk,khd->qhd", probs, vblock, preferred_element_type=jnp.float32)
        return (mixed.astype(jnp.bfloat16), (top + jnp.log(total))[..., 0])

    mixed_all, lse_all = lax.map(attend_block, jnp.arange(nblocks, dtype=jnp.int32))
    mixed = mixed_all.reshape(group_rows, -1)[order]
    heads_out = lax.all_to_all(mixed, "seq", split_axis=0, concat_axis=1, tiled=True)
    out_w = lax.all_gather(out_weight, both, axis=0, tiled=True)
    out_rows = row_slice(out_weight)
    attn = times(heads_out, out_w)
    resid = stream + attn
    normed2, rstd2 = normalize(resid)
    second_in = gather_rows((normed2 * gain2 + shift2).astype(jnp.bfloat16))
    gate_w = column_slice(gate_weight, 1)
    up_w = column_slice(up_weight, 1)
    down_w = row_slice(down_weight)
    gate = times(second_in, gate_w)
    upper = times(second_in, up_w)
    hidden, sigma = mlp_forward(gate, upper)
    mlp = scatter_rows(times(hidden, down_w))
    result = resid + mlp

    mlp_grad = gather_rows(out_grad[0])
    hidden_grad = times_transposed(mlp_grad, down_w)
    gate_act, up_act = mlp_backward(hidden_grad, gate, upper, sigma)
    second_grad = scatter_rows(times_transposed(gate_act, gate_w) + times_transposed(up_act, up_w))
    down_grad = row_shard(outer(hidden, mlp_grad))
    gate_grad = column_shard(outer(second_in, gate_act), 1)
    up_grad = column_shard(outer(second_in, up_act), 1)
    resid_part, gain2_grad, shift2_grad = norm_back(second_grad, normed2, rstd2, gain2)
    resid_grad = cotangent + resid_part

    attn_grad = gather_rows(resid_grad.astype(jnp.bfloat16))
    out_grad_w = row_shard(outer(mixed, attn_grad))
    mixed_grad_p = to_pack(times_transposed(attn_grad, out_rows).astype(jnp.bfloat16))

    def back_block(index, carry):
        query_acc, key_acc, value_acc = carry
        first, key_first, qblock, kblock, vblock, scores = window(index, packed)
        probs = jnp.exp(scores - lse_all[index][:, :, None])
        dblock = lax.dynamic_slice_in_dim(mixed_grad_p, first, blk)
        value_part = jnp.einsum(
            "hqk,qhd->khd", probs.astype(jnp.bfloat16), dblock, preferred_element_type=jnp.float32
        )
        prob_grad = jnp.einsum("qhd,khd->hqk", dblock, vblock, preferred_element_type=jnp.float32)
        inner = jnp.sum(probs * prob_grad, -1, keepdims=True)
        score_grad = (probs * (prob_grad - inner)).astype(jnp.bfloat16)
        query_part = (
            jnp.einsum("hqk,khd->qhd", score_grad, kblock, preferred_element_type=jnp.float32)
            * scale
        )
        key_part = (
            jnp.einsum("hqk,qhd->khd", score_grad, qblock, preferred_element_type=jnp.float32)
            * scale
        )
        query_acc = lax.dynamic_update_slice_in_dim(query_acc, query_part, first, 0)
        key_old = lax.dynamic_slice_in_dim(key_acc, key_first, keys)
        key_acc = lax.dynamic_update_slice_in_dim(key_acc, key_old + key_part, key_first, 0)
        value_old = lax.dynamic_slice_in_dim(value_acc, key_first, keys)
        value_acc = lax.dynamic_update_slice_in_dim(value_acc, value_old + value_part, key_first, 0)
        return (query_acc, key_acc, value_acc)

    zeros = jnp.zeros(packed[0].shape, jnp.float32)
    query_acc, key_acc, value_acc = lax.fori_loop(0, nblocks, back_block, (zeros, zeros, zeros))

    def to_dealt(values):
        return values.astype(jnp.bfloat16).reshape(group_rows, -1)[order]

    qkv_act = jnp.concatenate(
        [
            rotate(to_dealt(query_acc).astype(jnp.float32), rel, -1.0).astype(jnp.bfloat16),
            rotate(to_dealt(key_acc).astype(jnp.float32), rel, -1.0).astype(jnp.bfloat16),
            to_dealt(value_acc),
        ],
        1,
    )
    first_grad = scatter_rows(times_transposed(qkv_act, qkv_w))
    qkv_grad = column_shard(outer(first_in, qkv_act), 3)
    qkv_bias_grad = lax.psum_scatter(
        jnp.sum(qkv_act.astype(jnp.float32), 0).reshape(3, nfsdp, -1),
        "fsdp",
        scatter_dimension=1,
    )
    input_part, gain1_grad, shift1_grad = norm_back(first_grad, normed1, rstd1, gain1)
    input_grad = resid_grad + input_part

    norm_grads = lax.psum(
        (
            gain1_grad,
            shift1_grad,
            gain2_grad,
            shift2_grad,
            jnp.sum(valid * result * result),
            jnp.sum(valid * attn * attn),
            jnp.sum(valid * mlp * mlp),
        ),
        both,
    )
    count = valid_rows * nfsdp * width
    rms = jnp.sqrt(jnp.stack(norm_grads[4:]) / count)
    mine = (lax.axis_index("seq") * nfsdp + lax.axis_index("fsdp")) * part
    norm_shards = [lax.dynamic_slice_in_dim(value, mine, part) for value in norm_grads[:4]]
    return (
        result.astype(jnp.bfloat16)[None],
        input_grad[None],
        norm_shards[0],
        norm_shards[1],
        qkv_grad,
        qkv_bias_grad,
        out_grad_w,
        norm_shards[2],
        norm_shards[3],
        gate_grad,
        up_grad,
        down_grad,
        rms,
    )


MESH = pl.DeviceIdType.MESH
QB = 128
NEG = -1e30
CH = 2
VMEM_SPEC = pl.BlockSpec(memory_space=pltpu.VMEM)
SMEM_SPEC = pl.BlockSpec(memory_space=pltpu.SMEM)
ANY_SPEC = pl.BlockSpec(memory_space=pl.ANY)
DMA = pltpu.SemaphoreType.DMA


def comm_params(collective, limit=48):
    return pltpu.CompilerParams(
        collective_id=collective, has_side_effects=True, vmem_limit_bytes=limit << 20
    )


def where_am_i():
    s = lax.axis_index("seq")
    f = lax.axis_index("fsdp")
    return s, f, s // 2, s % 2


def remote(src, dst, send, recv, device):
    return pltpu.make_async_remote_copy(
        src, dst, send, recv, device_id=device, device_id_type=MESH
    )


def flip(v, bit):
    return v + bit * (1 - 2 * ((v // bit) % 2))


def peer(s, k):
    for bit in (1, 2, 4):
        if k & bit:
            s = flip(s, bit)
    return s


def dealer(i):
    return (i // 4, i % 4)


def greet_all(s, f):
    bar = pltpu.get_barrier_semaphore()
    me = s * 4 + f

    @pl.loop(1, 32)
    def _(k):
        pl.semaphore_signal(bar, inc=1, device_id=dealer((me + k) % 32), device_id_type=MESH)

    pl.semaphore_wait(bar, 31)


def greet_line(s, f, z, y):
    bar = pltpu.get_barrier_semaphore()
    pl.semaphore_signal(bar, inc=1, device_id=(flip(s, 1), f), device_id_type=MESH)

    @pl.when(z > 0)
    def _():
        pl.semaphore_signal(bar, inc=1, device_id=(s - 2, f), device_id_type=MESH)

    @pl.when(z < 3)
    def _():
        pl.semaphore_signal(bar, inc=1, device_id=(s + 2, f), device_id_type=MESH)

    edge = jnp.where((z == 0) | (z == 3), 1, 0)
    pl.semaphore_wait(bar, 3 - edge)


def greet_columns(s, f):
    bar = pltpu.get_barrier_semaphore()
    for k in range(1, 8):
        pl.semaphore_signal(bar, inc=1, device_id=(peer(s, k), f), device_id_type=MESH)
    pl.semaphore_signal(bar, inc=1, device_id=(s, flip(f, 1)), device_id_type=MESH)
    pl.semaphore_signal(bar, inc=1, device_id=(s, flip(f, 2)), device_id_type=MESH)
    pl.semaphore_wait(bar, 9)


def adder(dst, srcs, step=16):
    @pl.loop(0, dst.shape[0] // step)
    def _(i):
        r = pl.ds(pl.multiple_of(i * step, step), step)
        total = srcs[0][r].astype(jnp.float32)
        for v in srcs[1:]:
            total = total + v[r].astype(jnp.float32)
        dst[r] = total.astype(dst.dtype)


class SeqGather:
    @staticmethod
    def scratch():
        return [DMA, DMA((8,)), DMA((4,)), DMA((4,)), DMA((4,))]

    def __init__(self, x, o, own, recv, sy, su, sd):
        self.x, self.o, self.recv, self.sy, self.su, self.sd = x, o, recv, sy, su, sd
        self.s, self.f, self.z, self.y = where_am_i()
        self.other = flip(self.s, 1)
        self.own = pltpu.make_async_copy(x, o.at[self.s], own)

    def at(self, zb):
        return 2 * zb + self.y

    def ysend(self, zb, src):
        b = self.at(zb)
        return remote(src, self.o.at[b], self.sy.at[zb], self.recv.at[b], (self.other, self.f))

    def usend(self, zb, src):
        b = self.at(zb)
        return remote(src, self.o.at[b], self.su.at[zb], self.recv.at[b], (self.s + 2, self.f))

    def dsend(self, zb, src):
        b = self.at(zb)
        return remote(src, self.o.at[b], self.sd.at[zb], self.recv.at[b], (self.s - 2, self.f))

    def arrived(self, b):
        o = self.o.at[b]
        return remote(o, o, self.sy.at[0], self.recv.at[b], (self.other, self.f))

    def start(self):
        @pl.when(self.z < 3)
        def _():
            self.usend(self.z, self.x).start()

        @pl.when(self.z > 0)
        def _():
            self.dsend(self.z, self.x).start()

        self.ysend(self.z, self.x).start()
        self.own.start()

    def near(self, i):
        low = jnp.where(self.z < 2, self.z, 3 - self.z)
        base = jnp.where(low == 0, i, jnp.where(i < 2, 1 - i, i))
        return jnp.where(self.z < 2, base, 3 - base)

    def arrive(self, i):
        zb = self.near(i)
        b = self.at(zb)
        self.arrived(b).wait_recv()

        @pl.when((zb < self.z) & (self.z < 3))
        def _():
            self.usend(zb, self.o.at[b]).start()

        @pl.when((zb > self.z) & (self.z > 0))
        def _():
            self.dsend(zb, self.o.at[b]).start()

        self.ysend(zb, self.o.at[b]).start()
        return b

    def column(self, i):
        b = self.at(self.near(i))
        return b

    def cross(self, i):
        b = 2 * self.near(i) + 1 - self.y
        self.arrived(b).wait_recv()
        return b

    def steps(self):
        return [functools.partial(self.arrive, i) for i in (1, 2, 3)]

    def each(self, use):
        @pl.loop(0, 8)
        def _(j):
            i = (j + 1) // 2
            column = (j == 0) | ((j % 2 == 1) & (j < 7))

            @pl.when(j == 1)
            def _():
                self.arrive(1)
                self.arrive(2)

            @pl.when(j == 4)
            def _():
                self.arrive(3)

            other = jnp.where(j == 7, 3, j // 2 - 1)

            @pl.when(jnp.logical_not(column))
            def _():
                self.cross(other)

            zb = self.near(jnp.where(column, i, other))
            use(2 * zb + jnp.where(column, self.y, 1 - self.y))

    def finish(self, own=True):
        if own:
            self.own.wait()
        for zb in range(4):
            self.ysend(zb, self.x).wait_send()

            @pl.when((self.z < 3) & (zb <= self.z))
            def _():
                self.usend(zb, self.x).wait_send()

            @pl.when((self.z > 0) & (zb >= self.z))
            def _():
                self.dsend(zb, self.x).wait_send()


class SeqReduce:
    @staticmethod
    def scratch(rows, w):
        big = [pltpu.VMEM((n, rows, w), jnp.bfloat16) for n in (4, 5)]
        return big + [DMA((4, CH)), DMA((5, CH)), DMA((4, CH)), DMA((4, CH))]

    def __init__(self, p, o, ybuf, got, ry, rl, sy, sl):
        self.p, self.o, self.ybuf, self.got = p, o, ybuf, got
        self.ry, self.rl, self.sy, self.sl = ry, rl, sy, sl
        self.s, self.f, self.z, self.y = where_am_i()
        self.other = flip(self.s, 1)
        self.ch = p.shape[1] // CH

    def order(self, k):
        a, b, c, d = [3, 2, 1, 0][k], [3, 0, 2, 1][k], [0, 3, 1, 2][k], [0, 1, 2, 3][k]
        z = self.z
        return jnp.where(z == 0, a, jnp.where(z == 1, b, jnp.where(z == 2, c, d)))

    def rows(self, c):
        return pl.ds(c * self.ch, self.ch)

    def ysend(self, zb, c):
        r = self.rows(c)
        src = self.p.at[2 * zb + 1 - self.y, r]
        dst = self.ybuf.at[zb, r]
        return remote(src, dst, self.sy.at[zb, c], self.ry.at[zb, c], (self.other, self.f))

    def usend(self, zb, c):
        r = self.rows(c)
        src, dst = self.ybuf.at[zb, r], self.got.at[zb, r]
        return remote(src, dst, self.sl.at[zb, c], self.rl.at[zb, c], (self.s + 2, self.f))

    def dsend(self, zb, c):
        r = self.rows(c)
        slot = jnp.where(zb == self.z - 1, 4, zb)
        src, dst = self.ybuf.at[zb, r], self.got.at[slot, r]
        return remote(src, dst, self.sl.at[zb, c], self.rl.at[slot, c], (self.s - 2, self.f))

    def landed(self, slot, c):
        v = self.got.at[slot, self.rows(c)]
        return remote(v, v, self.sl.at[0, c], self.rl.at[slot, c], (self.other, self.f))

    def send(self, k):
        for c in range(CH):
            self.ysend(self.order(k), c).start()

    def start(self):
        for k in range(4):
            self.send(k)

    def step(self, k, c):
        z, zb, r = self.z, self.order(k), self.rows(c)
        self.ysend(zb, c).wait_recv()
        a, b = self.p.at[2 * zb + self.y, r], self.ybuf.at[zb, r]
        u, d = self.got.at[zb, r], self.got.at[4, r]
        alone = ((zb > z) & (z == 0)) | ((zb < z) & (z == 3))

        @pl.when(alone)
        def _():
            adder(b, [a, b])

        @pl.when((zb != z) & jnp.logical_not(alone))
        def _():
            self.landed(zb, c).wait_recv()
            adder(b, [a, b, u])

        @pl.when(zb > z)
        def _():
            self.usend(zb, c).start()

        @pl.when(zb < z)
        def _():
            self.dsend(zb, c).start()

        @pl.when(zb == z)
        def _():
            o = self.o.at[r]

            @pl.when(z == 0)
            def _():
                self.landed(4, c).wait_recv()
                adder(o, [a, b, d])

            @pl.when(z == 3)
            def _():
                self.landed(zb, c).wait_recv()
                adder(o, [a, b, u])

            @pl.when((z > 0) & (z < 3))
            def _():
                self.landed(zb, c).wait_recv()
                self.landed(4, c).wait_recv()
                adder(o, [a, b, u, d])

    def steps(self):
        return [functools.partial(self.step, k, c) for k in range(4) for c in range(CH)]

    def finish(self):
        for zb in range(4):
            for c in range(CH):
                self.ysend(zb, c).wait_send()

                @pl.when(zb != self.z)
                def _():
                    self.usend(zb, c).wait_send()


class ColGather:
    @staticmethod
    def scratch():
        return [DMA, DMA((8, 4)), DMA((8,)), DMA((8, 2)), DMA((8,))]

    def __init__(self, x, o, own, recv, direct, core, xs):
        self.x, self.o, self.own, self.recv = x, o, own, recv
        self.direct, self.core, self.xs = direct, core, xs
        self.s, self.f, _, _ = where_am_i()
        self.fc, self.fx = flip(self.f, 1), flip(self.f, 2)
        self.fd = flip(self.fc, 2)
        self.mine = pltpu.make_async_copy(x.at[self.s], self.piece(self.s, self.f), own)

    def piece(self, t, ff):
        r = self.x.shape[1]
        return self.o.at[pl.ds(pl.multiple_of((t * 4 + ff) * r, r), r)]

    def send_direct(self, k):
        s, f, t = self.s, self.f, peer(self.s, k)
        return remote(self.x.at[t], self.piece(s, f), self.direct.at[k], self.recv.at[s, f], (t, f))

    def send_core(self, k, which, src):
        t, ff = peer(self.s, k), self.f if which == 0 else self.fx
        dst = self.piece(t, ff)
        return remote(src, dst, self.core.at[k, which], self.recv.at[t, ff], (self.s, self.fc))

    def send_x(self, k, src):
        t = peer(self.s, k)
        dst = self.piece(t, self.f)
        return remote(src, dst, self.xs.at[k], self.recv.at[t, self.f], (self.s, self.fx))

    def arrived(self, k, ff):
        t = peer(self.s, k)
        o = self.piece(t, ff)
        return remote(o, o, self.own, self.recv.at[t, ff], (self.s, self.fc))

    def start(self):
        for k in reversed(range(1, 8)):
            self.send_direct(k).start()
        self.send_x(0, self.x.at[self.s]).start()
        self.send_core(0, 0, self.x.at[self.s]).start()
        self.mine.start()

    def step(self, k):
        t = peer(self.s, k)
        self.arrived(k, self.f).wait_recv()
        self.send_x(k, self.piece(t, self.f)).start()
        self.send_core(k, 0, self.piece(t, self.f)).start()

    def xstep(self, k):
        t = peer(self.s, k)
        self.arrived(k, self.fx).wait_recv()
        self.send_core(k, 1, self.piece(t, self.fx)).start()

    def steps(self):
        first = [functools.partial(self.step, k) for k in reversed(range(1, 8))]
        then = [functools.partial(self.xstep, k) for k in (0, 7, 6, 5, 4, 3, 2, 1)]
        return first + then

    def complete(self):
        self.mine.wait()
        for k in range(8):
            self.arrived(k, self.fc).wait_recv()
            self.arrived(k, self.fd).wait_recv()

    def finish(self):
        for k in range(8):
            if k:
                self.send_direct(k).wait_send()
            self.send_x(k, self.x.at[0]).wait_send()
            self.send_core(k, 0, self.x.at[0]).wait_send()
            self.send_core(k, 1, self.x.at[0]).wait_send()


class ColSum:
    @staticmethod
    def scratch(r, c):
        def v(*lead):
            return pltpu.VMEM(lead + (8, r, c), jnp.bfloat16)

        return [v(2), v(), DMA((2, 8)), DMA((2, 8)), DMA((8,)), DMA((8,))]

    def __init__(self, g, h, cb, xb, cs, cr, xs, xr):
        self.g, self.h, self.cb, self.xb = g, h, cb, xb
        self.cs, self.cr, self.xs, self.xr = cs, cr, xs, xr
        self.s, self.f, _, _ = where_am_i()
        self.fc, self.fx = flip(self.f, 1), flip(self.f, 2)
        self.fd = flip(self.fc, 2)
        self.r, self.c = h.shape[1:]

    def piece(self, i, ff):
        at = pl.multiple_of((i * 4 + ff) * self.r, self.r)
        return self.g.at[pl.ds(at, self.r), pl.ds(0, self.c)]

    def core(self, w, i):
        src = self.piece(i, self.fd if w == 0 else self.fc)
        dst = self.cb.at[w, i]
        return remote(src, dst, self.cs.at[w, i], self.cr.at[w, i], (self.s, self.fc))

    def xsend(self, i):
        src, dst = self.cb.at[0, i], self.xb.at[i]
        return remote(src, dst, self.xs.at[i], self.xr.at[i], (self.s, self.fx))

    def send(self, i):
        self.core(0, i).start()
        self.core(1, i).start()

    def step(self, i):
        self.core(0, i).wait_recv()
        adder(self.cb.at[0, i], [self.piece(i, self.fx), self.cb.at[0, i]])
        self.xsend(i).start()

    def total(self, i):
        self.core(1, i).wait_recv()
        self.xsend(i).wait_recv()
        adder(self.h.at[i], [self.piece(i, self.f), self.cb.at[1, i], self.xb.at[i]])

    def finish(self):
        for i in range(8):
            self.core(0, i).wait_send()
            self.core(1, i).wait_send()
            self.xsend(i).wait_send()


class FsdpReduce:
    @staticmethod
    def scratch(r, c):
        return [pltpu.VMEM((2, r, c), jnp.bfloat16), pltpu.VMEM((r, c), jnp.bfloat16), DMA((3,)), DMA((3,))]

    def __init__(self, g, o, cb, xb, send, recv):
        self.g, self.o, self.cb, self.xb = g, o, cb, xb
        self.s, self.f, _, _ = where_am_i()
        f = self.f
        self.fx = flip(f, 2)
        fc = flip(f, 1)
        core = (self.s, fc)
        self.far = remote(g.at[flip(fc, 2)], cb.at[0], send.at[0], recv.at[0], core)
        self.near = remote(g.at[fc], cb.at[1], send.at[1], recv.at[1], core)
        self.over = remote(cb.at[0], xb, send.at[2], recv.at[2], (self.s, self.fx))

    def start(self):
        self.far.start()
        self.near.start()

    def step(self):
        self.far.wait_recv()
        adder(self.cb.at[0], [self.g.at[self.fx], self.cb.at[0]])
        self.over.start()

    def total(self):
        self.near.wait_recv()
        self.over.wait_recv()
        adder(self.o, [self.g.at[self.f], self.cb.at[1], self.xb])

    def finish(self):
        self.far.wait_send()
        self.near.wait_send()
        self.over.wait_send()


class FsdpGather:
    @staticmethod
    def scratch():
        return [DMA, DMA((4,)), DMA((3,))]

    def __init__(self, x, o, own, recv, send):
        self.x, self.o, self.own, self.recv, self.send = x, o, own, recv, send
        self.s, self.f, _, _ = where_am_i()
        self.fc, self.fx = flip(self.f, 1), flip(self.f, 2)
        self.fd = flip(self.fc, 2)
        self.mine = pltpu.make_async_copy(x, o.at[self.f], own)

    def pass_on(self, n, src, ff, to):
        return remote(src, self.o.at[ff], self.send.at[n], self.recv.at[ff], (self.s, to))

    def arrived(self, ff):
        o = self.o.at[ff]
        return remote(o, o, self.own, self.recv.at[ff], (self.s, self.fc))

    def start(self):
        self.pass_on(0, self.x, self.f, self.fx).start()
        self.pass_on(1, self.x, self.f, self.fc).start()
        self.mine.start()

    def step(self):
        self.arrived(self.fx).wait_recv()
        self.pass_on(2, self.o.at[self.fx], self.fx, self.fc).start()

    def finish(self):
        self.mine.wait()
        self.arrived(self.fc).wait_recv()
        self.arrived(self.fd).wait_recv()
        for n in range(3):
            self.pass_on(n, self.x, self.f, self.fc).wait_send()


class WholeGather:
    @staticmethod
    def scratch():
        return [DMA, DMA((32,)), DMA((4,)), DMA((4,)), DMA((4,)), DMA((4, 2)), DMA((4, 2, 2))]

    def __init__(self, x, o, own, recv, su, sd, sy, sx, sc):
        self.x, self.o, self.own, self.recv = x, o, own, recv
        self.su, self.sd, self.sy, self.sx, self.sc = su, sd, sy, sx, sc
        self.s, self.f, self.z, self.y = where_am_i()
        self.fc, self.fx = flip(self.f, 1), flip(self.f, 2)
        self.fd = flip(self.fc, 2)
        self.me = self.s * 4 + self.f
        self.mine = pltpu.make_async_copy(x, o.at[self.me], own)

    def at(self, zb, yy, ff):
        return (2 * zb + (self.y if yy == 0 else 1 - self.y)) * 4 + ff

    def src(self, b, first):
        return self.x if first else self.o.at[b]

    def up(self, zb, first=False):
        b = self.at(zb, 0, self.f)
        to = (self.s + 2, self.f)
        return remote(self.src(b, first), self.o.at[b], self.su.at[zb], self.recv.at[b], to)

    def down(self, zb, first=False):
        b = self.at(zb, 0, self.f)
        to = (self.s - 2, self.f)
        return remote(self.src(b, first), self.o.at[b], self.sd.at[zb], self.recv.at[b], to)

    def over_y(self, zb, first=False):
        b = self.at(zb, 0, self.f)
        to = (flip(self.s, 1), self.f)
        return remote(self.src(b, first), self.o.at[b], self.sy.at[zb], self.recv.at[b], to)

    def over_x(self, zb, yy, first=False):
        b = self.at(zb, yy, self.f)
        to = (self.s, self.fx)
        return remote(self.src(b, first), self.o.at[b], self.sx.at[zb, yy], self.recv.at[b], to)

    def over_core(self, zb, yy, xx, first=False):
        b = self.at(zb, yy, self.f if xx == 0 else self.fx)
        to = (self.s, self.fc)
        return remote(self.src(b, first), self.o.at[b], self.sc.at[zb, yy, xx], self.recv.at[b], to)

    def arrived(self, b):
        o = self.o.at[b]
        return remote(o, o, self.own, self.recv.at[b], (self.s, self.fc))

    def start(self):
        z = self.z

        @pl.when(z < 3)
        def _():
            self.up(z, True).start()

        @pl.when(z > 0)
        def _():
            self.down(z, True).start()

        self.over_y(z, True).start()
        self.over_x(z, 0, True).start()
        self.over_core(z, 0, 0, True).start()
        self.mine.start()

    def line(self, sign, t):
        zb = self.z + sign * t

        @pl.when((zb >= 0) & (zb <= 3))
        def _():
            self.arrived(self.at(zb, 0, self.f)).wait_recv()
            if sign < 0:

                @pl.when(self.z < 3)
                def _():
                    self.up(zb).start()

            else:

                @pl.when(self.z > 0)
                def _():
                    self.down(zb).start()

            self.over_y(zb).start()
            self.over_x(zb, 0).start()
            self.over_core(zb, 0, 0).start()

    def column(self, sign, t):
        zb = self.z + sign * t

        @pl.when((zb >= 0) & (zb <= 3))
        def _():
            self.arrived(self.at(zb, 1, self.f)).wait_recv()
            self.over_x(zb, 1).start()
            self.over_core(zb, 1, 0).start()

    def side(self, sign, t, yy):
        zb = self.z + sign * t

        @pl.when((zb >= 0) & (zb <= 3))
        def _():
            self.arrived(self.at(zb, yy, self.fx)).wait_recv()
            self.over_core(zb, yy, 1).start()

    def steps(self):
        p = functools.partial
        out = []
        for t in range(4):
            for sign in (-1, 1) if t else (1,):
                if t:
                    out.append(p(self.line, sign, t))
        for t in range(4):
            for sign in (-1, 1) if t else (1,):
                out.append(p(self.column, sign, t))
                out.append(p(self.side, sign, t, 0))
        for t in range(4):
            for sign in (-1, 1) if t else (1,):
                out.append(p(self.side, sign, t, 1))
        return out

    def finish(self):
        self.mine.wait()
        for zb in range(4):
            for yy in range(2):
                self.arrived(self.at(zb, yy, self.fc)).wait_recv()
                self.arrived(self.at(zb, yy, self.fd)).wait_recv()
        for zb in range(4):
            self.over_y(zb).wait_send()

            @pl.when((self.z < 3) & (zb <= self.z))
            def _():
                self.up(zb).wait_send()

            @pl.when((self.z > 0) & (zb >= self.z))
            def _():
                self.down(zb).wait_send()

            for yy in range(2):
                self.over_x(zb, yy).wait_send()
                for xx in range(2):
                    self.over_core(zb, yy, xx).wait_send()


class RowExchange:
    @staticmethod
    def scratch():
        return [DMA, DMA((8,)), DMA((8,))]

    def __init__(self, x, o, own, send, recv):
        self.x, self.o, self.send, self.recv = x, o, send, recv
        self.s, self.f, _, _ = where_am_i()
        self.mine = pltpu.make_async_copy(x.at[self.s], o.at[self.s], own)

    def piece(self, k):
        t = peer(self.s, k)
        dst = self.o.at[self.s]
        return remote(self.x.at[t], dst, self.send.at[k], self.recv.at[k], (t, self.f))

    def start(self):
        for k in reversed(range(1, 8)):
            self.piece(k).start()
        self.mine.start()

    def finish(self):
        self.mine.wait()
        for k in reversed(range(1, 8)):
            self.piece(k).wait_recv()
            self.piece(k).wait_send()


def idle():
    pass


def perform(plan, queues):
    left = {name: list(items) for name, items in queues.items()}
    for name in "".join(plan):
        left[name].pop(0)()
    assert not any(left.values())


FORWARD_PLAN = (
    "nFngnWggssswwVnsnswwssvswsvsnsnssvsvwsnvDwwwcwcc",
    "wcfvccvwvdvdcwwcwwvcwcwcccvcccwdwvwwwcwwcXvvvww",
)
MIDDLE_PLAN = ("raaarmrmleeetaaateraeamllteletelhhthlthhhllhmthtz",)
BACKWARD_PLAN = ("FbrggXbfbbgbrZbbttborcqctcocotccrooctoooOtccpcccctPtz",)
LAST_PLAN = ("daddeawdahtaeeaaahatewwttheteetehhhwhttzhZ",)


def merged(*lists):
    keyed = []
    for n, items in enumerate(lists):
        keyed += [((i + 0.5) / len(items), n, item) for i, item in enumerate(items)]
    return [item for _, _, item in sorted(keyed, key=lambda v: v[:2])]


def dot(a, b, ca=1, cb=0):
    return lax.dot_general(a, b, (((ca,), (cb,)), ((), ())), preferred_element_type=jnp.float32)


def starts_of(pos, lengths_ref, nseg):
    start = jnp.zeros_like(pos)
    end = 0
    for i in range(nseg - 1):
        end = end + lengths_ref[0, i]
        start = jnp.where(pos >= end, end, start)
    return start


def head_lanes(h):
    lane = lax.broadcasted_iota(jnp.int32, (1, 128), 1)
    return (lane // HEAD_DIM) == h


def turn(x, c, s1, s2, sign):
    half = ROT // 2
    return x * c + (pltpu.roll(x, 128 - half, 1) * s1 + pltpu.roll(x, half, 1) * s2) * sign


def block_mask(qb, lengths_ref):
    keys = (qb + 1) * QB
    row = qb * QB + lax.broadcasted_iota(jnp.int32, (QB, 1), 0)
    col = lax.broadcasted_iota(jnp.int32, (1, keys), 1)
    return (col >= starts_of(row, lengths_ref, lengths_ref.shape[1])) & (col <= row)


def row_at(i, step=QB):
    return pl.ds(pl.multiple_of(i * step, step), step)


def picks(orow_ref, i):
    p = lax.broadcasted_iota(jnp.int32, (QB, 1), 0) + i * QB == orow_ref[...]
    return jnp.where(p, 1.0, 0.0).astype(jnp.bfloat16)


def puts(oc, valid):
    p = oc == lax.broadcasted_iota(jnp.int32, (1, valid), 1)
    return jnp.where(p, 1.0, 0.0).astype(jnp.bfloat16)


def attend(
    a_ref, w_ref, shift_of, tables, orow_ref, ocol_ref, len_ref, o_ref, pk_ref, lse_ref, rot, opk
):
    rows, w3 = rot.shape
    w = w3 // 3
    valid = pk_ref.shape[0]
    scale = HEAD_DIM**-0.5
    c_ref, s1_ref, s2_ref = tables

    def project(lo, hi):
        shift = shift_of()

        @pl.loop(lo, hi)
        def _(i):
            r = row_at(i, 256)
            c, s1, s2 = c_ref[r], s1_ref[r], s2_ref[r]
            left = jnp.concatenate([a_ref[2 * i], a_ref[2 * i + 1]], 0)
            qkv = dot(left, w_ref[...]) + shift
            for t in range(w3 // 128):
                cols = slice(t * 128, t * 128 + 128)
                x = qkv[:, cols]
                if t < 2 * w // 128:
                    x = turn(x, c, s1, s2, 1.0)
                rot[r, cols] = x.astype(jnp.bfloat16)

    def pack(lo, hi):
        @pl.loop(lo, hi)
        def _(i):
            pk_ref[row_at(i)] = dot(picks(orow_ref, i), rot[...]).astype(jnp.bfloat16)

    def block(qb, t):
        keys = (qb + 1) * QB
        rq = slice(qb * QB, qb * QB + QB)
        ct = slice(t * 128, t * 128 + 128)
        mask = block_mask(qb, len_ref)
        q = pk_ref[rq, ct]
        k = pk_ref[0:keys, w + t * 128 : w + t * 128 + 128]
        v = pk_ref[0:keys, 2 * w + t * 128 : 2 * w + t * 128 + 128]
        total = None
        for h in range(2):
            qh = jnp.where(head_lanes(h), q, jnp.zeros_like(q))
            scores = jnp.where(mask, dot(qh, k, 1, 1) * scale, NEG)
            top = jnp.max(scores, -1, keepdims=True)
            expo = jnp.exp(scores - top)
            norm = jnp.sum(expo, -1, keepdims=True)
            probs = (expo / norm).astype(jnp.bfloat16)
            lse_ref[2 * t + h, rq] = top + jnp.log(norm)
            out = dot(probs, v)
            total = out if h == 0 else jnp.where(head_lanes(1), out, total)
        opk[rq, ct] = total.astype(jnp.bfloat16)

    def unpack(lo, hi):
        per = o_ref.shape[1]

        @pl.loop(lo, hi)
        def _(i):
            r = row_at(i, per)
            oc = ocol_ref[r]
            back = dot(puts(oc, valid), opk[...])
            pad = rot[r, 2 * w :].astype(jnp.float32)
            o_ref[i] = jnp.where(oc >= valid, pad, back).astype(jnp.bfloat16)

    blocks = [
        functools.partial(block, qb, t) for qb in range(valid // QB) for t in range(w // 128)
    ]
    p = functools.partial
    steps, half, blks = rows // 256, valid // QB // 2, rows // o_ref.shape[1]
    head = [p(project, 0, steps // 2), p(project, steps // 2, steps)]
    head += [p(pack, 0, half), p(pack, half, valid // QB)]
    return head + blocks + [p(unpack, 0, blks // 2), p(unpack, blks // 2, blks)]


def attend_back(
    pk_ref, do_ref, lse_ref, tables, orow_ref, ocol_ref, len_ref, g_ref, b_ref, dpk, dq, dk, dv, gpk
):
    rows, w = do_ref.shape
    valid = pk_ref.shape[0]
    scale = HEAD_DIM**-0.5
    c_ref, s1_ref, s2_ref = tables

    def pack():
        @pl.loop(0, valid // QB)
        def _(i):
            r = row_at(i)
            dpk[r] = dot(picks(orow_ref, i), do_ref[...]).astype(jnp.bfloat16)
            dk[r] = jnp.zeros((QB, w), jnp.float32)
            dv[r] = jnp.zeros((QB, w), jnp.float32)

    def block(qb, t):
        keys = (qb + 1) * QB
        rq = slice(qb * QB, qb * QB + QB)
        ct = slice(t * 128, t * 128 + 128)
        mask = block_mask(qb, len_ref)
        q, d = pk_ref[rq, ct], dpk[rq, ct]
        k = pk_ref[0:keys, w + t * 128 : w + t * 128 + 128]
        v = pk_ref[0:keys, 2 * w + t * 128 : 2 * w + t * 128 + 128]
        total = None
        for h in range(2):
            hl = head_lanes(h)
            qh = jnp.where(hl, q, jnp.zeros_like(q))
            dh = jnp.where(hl, d, jnp.zeros_like(d))
            scores = jnp.where(mask, dot(qh, k, 1, 1) * scale, NEG)
            p = jnp.exp(scores - lse_ref[2 * t + h, rq])
            dp = dot(dh, v, 1, 1)
            inner = jnp.sum(p * dp, -1, keepdims=True)
            ds = (p * (dp - inner)).astype(jnp.bfloat16)
            dv[0:keys, ct] += dot(p.astype(jnp.bfloat16), dh, 0, 0)
            dk[0:keys, ct] += dot(ds, qh, 0, 0)
            part = dot(ds, k)
            total = part if h == 0 else jnp.where(head_lanes(1), part, total)
        dq[rq, ct] = total

    def rotary():
        @pl.loop(0, valid // QB)
        def _(i):
            r = row_at(i)
            c, s1, s2 = c_ref[r], s1_ref[r], s2_ref[r]
            for t in range(w // 128):
                ct = slice(t * 128, t * 128 + 128)
                for j, src in ((0, dq), (1, dk)):
                    x = (src[r, ct] * scale).astype(jnp.bfloat16).astype(jnp.float32)
                    at = j * w + t * 128
                    gpk[r, at : at + 128] = turn(x, c, s1, s2, -1.0).astype(jnp.bfloat16)
                at = 2 * w + t * 128
                gpk[r, at : at + 128] = dv[r, ct].astype(jnp.bfloat16)

    def unpack():
        b_ref[...] = jnp.zeros_like(b_ref)

        @pl.loop(0, rows // QB)
        def _(i):
            r = row_at(i)
            oc = ocol_ref[r]
            back = dot(puts(oc, valid), gpk[...])
            pad = jnp.where(oc >= valid, do_ref[r].astype(jnp.float32), 0.0)
            back = jnp.concatenate([back[:, : 2 * w], back[:, 2 * w :] + pad], 1)
            g_ref[r] = back.astype(jnp.bfloat16)
            b_ref[...] += jnp.sum(back, 0, keepdims=True)

    blocks = [
        functools.partial(block, qb, t) for qb in range(valid // QB) for t in range(w // 128)
    ]
    return [pack] + blocks + [rotary, unpack]


def forward_kernel(
    x_ref,
    p_ref,
    qp_ref,
    op_ref,
    dm_ref,
    wp_ref,
    dp_ref,
    c_ref,
    s1_ref,
    s2_ref,
    orow_ref,
    ocol_ref,
    len_ref,
    a_ref,
    qw_ref,
    n_ref,
    ow_ref,
    ho_ref,
    pk_ref,
    lse_ref,
    dmo_ref,
    ww_ref,
    dw_ref,
    mix_ref,
    xs,
    got,
    rot,
    opk,
    psend,
    precv,
    *sems,
):
    s, f, z, y = where_am_i()
    me = s * 4 + f
    greet_all(s, f)
    gather = SeqGather(x_ref, xs, *sems[:5])
    slices = ColGather(qp_ref, qw_ref, *sems[5:10])
    whole = WholeGather(op_ref, ow_ref, *sems[10:17])
    grads = SeqGather(dm_ref, dmo_ref, *sems[17:22])
    wide = ColGather(wp_ref, ww_ref, *sems[22:27])
    down = FsdpGather(dp_ref, dw_ref, *sems[27:30])
    swap = RowExchange(mix_ref, ho_ref, *sems[30:])

    def param(k):
        i = (me + k) % 32
        return remote(p_ref, got.at[me], psend.at[k], precv.at[k], dealer(i))

    @pl.loop(1, 32)
    def _(k):
        param(k).start()

    gather.start()
    slices.start()
    got[me] = p_ref[...]

    @pl.loop(1, 32)
    def _(k):
        param(k).wait_recv()

    for i in range(16):
        n_ref[:, i * 128 : i * 128 + 128] = got[2 * i] + got[2 * i + 1]
    step = 16

    def norm(b):
        gain, shift = n_ref[0:1], n_ref[1:2]

        @pl.loop(0, x_ref.shape[0] // step)
        def _(i):
            r = row_at(i, step)
            normed, _ = normalize(xs[b, r].astype(jnp.float32))
            a_ref[b, r] = (normed * gain + shift).astype(jnp.bfloat16)

    def shift_of():
        w = rot.shape[1] // 3
        parts = []
        for n in range(3):
            part = jnp.zeros((1, w), jnp.float32)
            for i in range(8):
                piece = n_ref[4 + n : 5 + n, i * w : i * w + w]
                part = part + jnp.where(s == i, piece, jnp.zeros_like(piece))
            parts.append(part)
        return jnp.concatenate(parts, 1)

    work = attend(
        a_ref,
        qw_ref,
        shift_of,
        (c_ref, s1_ref, s2_ref),
        orow_ref,
        ocol_ref,
        len_ref,
        mix_ref,
        pk_ref,
        lse_ref,
        rot,
        opk,
    )
    p = functools.partial

    def own():
        gather.own.wait()
        norm(s)

    norms = [own]
    for i in range(4):
        norms.append(lambda i=i: norm(gather.cross(i)))
        if i < 3:
            norms.append(lambda i=i: norm(2 * gather.near(i + 1) + y))
    work = [slices.complete, work[0], idle, work[1], idle] + work[2:]
    queues = dict(
        g=gather.steps(),
        n=norms,
        s=slices.steps(),
        d=grads.steps(),
        v=wide.steps(),
        w=whole.steps(),
        f=[down.step],
        c=work,
        D=[grads.start],
        V=[wide.start],
        W=[whole.start],
        F=[down.start],
        X=[swap.start],
    )
    work[0:2] = [lambda first=work[0], then=work[1]: (first(), then())]
    perform(FORWARD_PLAN, queues)
    for i in range(4):
        grads.cross(i)
    swap.finish()
    wide.complete()
    for task in (slices, wide, whole, down, grads):
        task.finish()
    gather.finish(False)

    @pl.loop(1, 32)
    def _(k):
        param(k).wait_send()


def forward(
    x, params, qkv_p, out_p, dm, wide_p, down_p, tables, orow, ocol, lengths, valid, collective
):
    rows, width = x.shape
    w3 = qkv_p.shape[2]
    w = w3 // 3
    group = 8 * rows
    heads = w // HEAD_DIM

    def out(shape, dtype=jnp.bfloat16):
        return jax.ShapeDtypeStruct(shape, dtype)

    return pl.pallas_call(
        forward_kernel,
        out_shape=(
            out((8, rows, width)),
            out((width, w3)),
            out((8, width), jnp.float32),
            out((32,) + out_p.shape),
            out((8, rows, w)),
            out((valid, w3)),
            out((heads, valid, 1), jnp.float32),
            out((8, rows, width)),
            out((width, wide_p.shape[2])),
            out((4,) + down_p.shape),
            out((8, rows, w)),
        ),
        in_specs=[VMEM_SPEC] * 12 + [SMEM_SPEC],
        out_specs=(VMEM_SPEC,) * 3
        + (ANY_SPEC,)
        + (VMEM_SPEC,) * 3
        + (ANY_SPEC,) * 3
        + (VMEM_SPEC,),
        scratch_shapes=[
            pltpu.VMEM((8, rows, width), jnp.bfloat16),
            pltpu.VMEM((32, 8, 128), jnp.float32),
            pltpu.VMEM((group, w3), jnp.bfloat16),
            pltpu.VMEM((valid, w), jnp.bfloat16),
            DMA((32,)),
            DMA((32,)),
        ]
        + SeqGather.scratch()
        + ColGather.scratch()
        + WholeGather.scratch()
        + SeqGather.scratch()
        + ColGather.scratch()
        + FsdpGather.scratch()
        + RowExchange.scratch(),
        compiler_params=comm_params(collective),
    )(x, params, qkv_p, out_p, dm, wide_p, down_p, *tables, orow, ocol, lengths)


def tall(rows, step=16):
    def wrap(fn):
        @pl.loop(0, rows // step)
        def _(i):
            fn(row_at(i, step))

    return wrap


def middle_kernel(
    ho_ref,
    ow_ref,
    x_ref,
    n_ref,
    ww_ref,
    dw_ref,
    dm_ref,
    attn_ref,
    res_ref,
    rg_ref,
    vec_ref,
    mp_ref,
    dg_ref,
    h_ref,
    big,
    cloc,
    c_ref,
    hid,
    act,
    part,
    second,
    load,
    *scratch,
):
    s, f, z, y = where_am_i()
    rows, width = x_ref.shape
    lf = dw_ref.shape[0]
    lw = ho_ref.shape[2]
    fetch = pltpu.make_async_copy(ow_ref, big, load)
    fetch.start()
    greet_columns(s, f)
    gather = SeqGather(cloc, c_ref, *scratch[:5])
    reduce = SeqReduce(part, second, *scratch[5:11])
    sums = ColSum(big, h_ref, *scratch[11:])
    gain, shift = n_ref[2:3], n_ref[3:4]
    fetch.wait()

    @pl.loop(0, width // 512)
    def _(j):
        cols = pl.ds(pl.multiple_of(j * 512, 512), 512)
        total = dot(ho_ref[0], big[0:lw, cols])
        for k in range(1, 8):
            total = total + dot(ho_ref[k], big[k * lw : k * lw + lw, cols])
        attn_ref[:, cols] = total
        res_ref[:, cols] = x_ref[:, cols].astype(jnp.float32) + total

    @tall(rows)
    def _(r):
        normed, _ = normalize(res_ref[r])
        cloc[r] = (normed * gain + shift).astype(jnp.bfloat16)

    gather.start()
    gather.own.wait()

    def block(b):
        at = pl.ds(pl.multiple_of(b * rows, rows), rows)
        wide = dot(c_ref[b], ww_ref[...])
        gate, upper = wide[:, :lf], wide[:, lf:]
        hidden, sigma = mlp_forward(gate, upper)
        hid[at] = hidden
        grad = dot(dm_ref[b], dw_ref[...], 1, 1)
        gate_act, up_act = mlp_backward(grad, gate, upper, sigma)
        act[at] = jnp.concatenate([gate_act, up_act], 1)
        part[b] = dot(act[at], ww_ref[...], 1, 1).astype(jnp.bfloat16)

    gather.each(block)

    def wide_grad(i):
        left = [c_ref[b, :, i * 256 : i * 256 + 256] for b in range(8)]
        left = jnp.concatenate(left, 0)
        big[i * 256 : i * 256 + 256, 0 : 2 * lf] = dot(left, act[...], 0, 0).astype(jnp.bfloat16)
        sums.send(i)

    def mlp_part(i):
        @pl.loop(2 * i, 2 * i + 2)
        def _(b):
            at = pl.ds(pl.multiple_of(b * rows, rows), rows)
            mp_ref[b] = dot(hid[at], dw_ref[...]).astype(jnp.bfloat16)

    def down_grad(i):
        cols = slice(i * 256, i * 256 + 256)
        right = jnp.concatenate([dm_ref[b, :, cols] for b in range(8)], 0)
        dg_ref[:, cols] = dot(hid[...], right, 0, 0).astype(jnp.bfloat16)

    def norm_backward():
        vec_ref[...] = jnp.zeros_like(vec_ref)

        @tall(rows)
        def _(r):
            grad = second[r]
            normed, rstd = normalize(res_ref[r])
            inner, gain_part, shift_part = norm_back(grad, normed, rstd, gain)
            rg_ref[r] = dm_ref[s, r].astype(jnp.float32) + inner
            vec_ref[0:1] += gain_part[None]
            vec_ref[1:2] += shift_part[None]

    p = functools.partial
    each = range(8)
    queues = dict(
        r=[p(reduce.send, k) for k in range(4)],
        t=reduce.steps(),
        a=[p(wide_grad, i) for i in each],
        e=[p(sums.step, i) for i in each],
        h=[p(sums.total, i) for i in each],
        m=[p(mlp_part, i) for i in range(4)],
        l=[p(down_grad, i) for i in each],
        z=[norm_backward],
    )
    perform(MIDDLE_PLAN, queues)
    gather.finish(False)
    reduce.finish()
    sums.finish()


def middle(heads_out, out_w, x, norms, wide_w, down_w, dm, collective):
    rows, width = x.shape
    lf = down_w.shape[0]
    group = 8 * rows
    part = width // 32

    def out(shape, dtype=jnp.bfloat16):
        return jax.ShapeDtypeStruct(shape, dtype)

    def vm(shape, dtype=jnp.bfloat16):
        return pltpu.VMEM(shape, dtype)

    wide = (rows, width)
    return pl.pallas_call(
        middle_kernel,
        out_shape=(
            out(wide, jnp.float32),
            out(wide, jnp.float32),
            out(wide, jnp.float32),
            out((8, width), jnp.float32),
            out((8,) + wide),
            out((lf, width)),
            out((8, part, 2 * lf)),
        ),
        in_specs=[VMEM_SPEC, ANY_SPEC] + [VMEM_SPEC] * 5,
        out_specs=(VMEM_SPEC,) * 7,
        scratch_shapes=[
            vm((width, width)),
            vm(wide),
            vm((8,) + wide),
            vm((group, lf)),
            vm((group, 2 * lf)),
            vm((8,) + wide),
            vm(wide, jnp.float32),
            DMA,
        ]
        + SeqGather.scratch()
        + SeqReduce.scratch(rows, width)
        + ColSum.scratch(part, 2 * lf),
        compiler_params=comm_params(collective, 63),
    )(heads_out, out_w, x, norms, wide_w, down_w, dm)


def backward_kernel(
    rg_ref,
    or_ref,
    mix_ref,
    pk_ref,
    lse_ref,
    c_ref,
    s1_ref,
    s2_ref,
    orow_ref,
    ocol_ref,
    len_ref,
    attn_ref,
    res_ref,
    valid_ref,
    mp_ref,
    dg_ref,
    h_ref,
    g_ref,
    b_ref,
    lo_ref,
    sum_ref,
    gate_ref,
    up_ref,
    down_ref,
    out_ref,
    da,
    full,
    do_ref,
    og,
    mlp,
    got,
    dpk,
    dq,
    dk,
    dv,
    gpk,
    *scratch,
):
    s, f, z, y = where_am_i()
    rows, width = rg_ref.shape
    part, ff = gate_ref.shape
    lf = ff // 8
    greet_columns(s, f)
    gather = SeqGather(da, full, *scratch[:5])
    reduce = SeqReduce(mp_ref, mlp, *scratch[5:11])
    swap = RowExchange(h_ref, got, *scratch[11:14])
    down = FsdpReduce(dg_ref, down_ref, *scratch[14:18])
    outer_sum = FsdpReduce(og, out_ref, *scratch[18:])

    @tall(rows)
    def _(r):
        da[r] = rg_ref[r].astype(jnp.bfloat16)

    gather.start()

    def block(b):
        at = pl.ds(pl.multiple_of(b * rows, rows), rows)
        do_ref[at] = dot(full[b], or_ref[...], 1, 1).astype(jnp.bfloat16)

    def own_block():
        gather.own.wait()
        block(s)

    blocks = [own_block]
    for i in range(4):
        if i < 3:
            blocks.append(lambda i=i: block(gather.column(i + 1)))
        blocks.append(lambda i=i: block(gather.cross(i)))

    def out_grad(i):
        cols = slice(i * 256, i * 256 + 256)
        right = jnp.concatenate([full[b, :, cols] for b in range(8)], 0)
        value = dot(mix_ref[...], right, 0, 0).astype(jnp.bfloat16)
        for k in range(4):
            og[k, :, cols] = value[k * part : k * part + part]

    p = functools.partial
    work = attend_back(
        pk_ref,
        do_ref,
        lse_ref,
        (c_ref, s1_ref, s2_ref),
        orow_ref,
        ocol_ref,
        len_ref,
        g_ref,
        b_ref,
        dpk,
        dq,
        dk,
        dv,
        gpk,
    )
    def results():
        sum_ref[...] = jnp.zeros_like(sum_ref)

        @tall(rows)
        def _(r):
            m = mlp[r]
            result = res_ref[r] + m
            lo_ref[r] = result.astype(jnp.bfloat16)
            keep = valid_ref[r]
            for n, v in enumerate((result, attn_ref[r], m)):
                total = jnp.sum(jnp.sum(v * v, -1, keepdims=True) * keep, 0, keepdims=True)
                sum_ref[n : n + 1] += jnp.broadcast_to(total, (1, 128))

    def spread():
        swap.finish()
        for n, ref in enumerate((gate_ref, up_ref)):
            for i in range(8):
                value = got[i, :, n * lf : n * lf + lf]
                ref[:, i * lf : i * lf + lf] = value.astype(jnp.float32)

    queues = dict(
        F=[down.start],
        f=[down.step],
        q=[down.total],
        b=blocks,
        g=gather.steps(),
        r=[p(reduce.send, k) for k in range(4)],
        t=reduce.steps(),
        X=[swap.start],
        Z=[spread],
        c=work,
        o=[p(out_grad, i) for i in range(8)],
        O=[outer_sum.start],
        p=[outer_sum.step],
        P=[outer_sum.total],
        z=[results],
    )
    perform(BACKWARD_PLAN, queues)
    gather.finish(False)
    reduce.finish()
    down.finish()
    outer_sum.finish()


def backward(
    rg, out_rows, mixed, pk, lse, tables, orow, ocol, lengths, attn, res, keep, mp, dg, h, collective
):
    rows, width = rg.shape
    group, w = mixed.shape
    valid = pk.shape[0]
    part = h.shape[1]
    ff = h.shape[2] * 4

    def out(shape, dtype=jnp.float32):
        return jax.ShapeDtypeStruct(shape, dtype)

    def vm(shape, dtype=jnp.bfloat16):
        return pltpu.VMEM(shape, dtype)

    return pl.pallas_call(
        backward_kernel,
        out_shape=(
            out((group, 3 * w), jnp.bfloat16),
            out((1, 3 * w)),
            out((rows, width), jnp.bfloat16),
            out((8, 128)),
            out((part, ff)),
            out((part, ff)),
            out(dg.shape[1:]),
            out((part, width)),
        ),
        in_specs=[VMEM_SPEC] * 10 + [SMEM_SPEC] + [VMEM_SPEC] * 6,
        out_specs=(VMEM_SPEC,) * 8,
        scratch_shapes=[
            vm((rows, width)),
            vm((8, rows, width)),
            vm((group, w)),
            vm((4, part, width)),
            vm((rows, width), jnp.float32),
            vm(h.shape),
            vm((valid, w)),
            vm((valid, w), jnp.float32),
            vm((valid, w), jnp.float32),
            vm((valid, w), jnp.float32),
            vm((valid, 3 * w)),
        ]
        + SeqGather.scratch()
        + SeqReduce.scratch(rows, width)
        + RowExchange.scratch()
        + FsdpReduce.scratch(*dg.shape[1:])
        + FsdpReduce.scratch(part, width),
        compiler_params=comm_params(collective, 60),
    )(rg, out_rows, mixed, pk, lse, *tables, orow, ocol, lengths, attn, res, keep, mp, dg, h)


def last_kernel(
    g_ref,
    b_ref,
    qw_ref,
    a_ref,
    x_ref,
    rg_ref,
    n_ref,
    vec_ref,
    sum_ref,
    ig_ref,
    qg_ref,
    total_ref,
    part,
    first,
    grad,
    h,
    got,
    msg,
    inbox,
    vec,
    msend,
    mrecv,
    *scratch,
):
    s, f, z, y = where_am_i()
    me = s * 4 + f
    rows, width = x_ref.shape
    w3 = g_ref.shape[1]
    w = w3 // 3
    pr = qg_ref.shape[0]
    greet_all(s, f)
    reduce = SeqReduce(part, first, *scratch[:6])
    sums = ColSum(grad, h, *scratch[6:12])
    swap = RowExchange(h, got, *scratch[12:])

    def block(b):
        at = pl.ds(pl.multiple_of(b * rows, rows), rows)
        part[b] = dot(g_ref[at], qw_ref[...], 1, 1).astype(jnp.bfloat16)

    def far_block(k):
        block(2 * reduce.order(k) + 1 - y)
        reduce.send(k)

    def own_block(k):
        block(2 * reduce.order(k) + y)

    def qkv_grad(k):
        i = peer(s, k)
        at = pl.ds(pl.multiple_of(i * 256, 256), 256)
        left = jnp.concatenate([a_ref[b, :, at] for b in range(8)], 0)
        grad[at] = dot(left, g_ref[...], 0, 0).astype(jnp.bfloat16)
        sums.send(i)

    def hand_over(k):
        sums.total(peer(s, k))
        if k:
            swap.piece(k).start()
        else:
            swap.mine.start()

    def message(k):
        i = (me + k) % 32
        return remote(msg.at[i // 2], inbox.at[k], msend.at[k], mrecv.at[k], dealer(i))

    def norm_backward():
        vec[0:2] = jnp.zeros((2, width), jnp.float32)
        vec[2:4] = vec_ref[0:2]
        gain = n_ref[0:1]

        @tall(rows)
        def _(r):
            normed, rstd = normalize(x_ref[r].astype(jnp.float32))
            inner, gain_part, shift_part = norm_back(first[r], normed, rstd, gain)
            ig_ref[r] = rg_ref[r] + inner
            vec[0:1] += gain_part[None]
            vec[1:2] += shift_part[None]

        lane = lax.broadcasted_iota(jnp.int32, (1, 128), 1)
        scalars = jnp.where(lane == 0, sum_ref[0:1], jnp.where(lane == 1, sum_ref[1:2], sum_ref[2:3]))
        for i in range(16):
            cols = slice(i * 128, i * 128 + 128)
            msg[i, 0:4] = vec[0:4, cols]
            msg[i, 4:5] = scalars
            at = (i % 2) * 128
            for n in range(3):
                piece = b_ref[0:1, n * w + at : n * w + at + 128]
                msg[i, 5 + n : 6 + n] = jnp.where(s == i // 2, piece, jnp.zeros_like(piece))

        @pl.loop(1, 32)
        def _(k):
            message(k).start()

    def spread():
        swap.finish()
        for i in range(8):
            for n in range(3):
                at = n * width + i * w
                qg_ref[:, at : at + w] = got[i, :, n * w : n * w + w].astype(jnp.float32)

    p = functools.partial
    ks = [7, 6, 5, 4, 3, 2, 1, 0]
    queues = dict(
        d=[p(far_block, k) for k in range(4)],
        w=[p(own_block, k) for k in range(4)],
        t=reduce.steps(),
        a=[p(qkv_grad, k) for k in ks],
        e=[lambda k=k: sums.step(peer(s, k)) for k in ks],
        h=[p(hand_over, k) for k in ks],
        z=[norm_backward],
        Z=[spread],
    )
    perform(LAST_PLAN, queues)
    reduce.finish()
    sums.finish()
    total_ref[...] = msg[me // 2]

    @pl.loop(1, 32)
    def _(k):
        message(k).wait_recv()
        total_ref[...] += inbox[k]

    @pl.loop(1, 32)
    def _(k):
        message(k).wait_send()


def last(g, b, qkv_w, a, x, rg, norms, vec, sums, collective):
    rows, width = x.shape
    w3 = g.shape[1]
    pr = width // 32

    def out(shape, dtype=jnp.float32):
        return jax.ShapeDtypeStruct(shape, dtype)

    def vm(shape, dtype=jnp.bfloat16):
        return pltpu.VMEM(shape, dtype)

    return pl.pallas_call(
        last_kernel,
        out_shape=(out((rows, width)), out((pr, 3 * width)), out((8, 128))),
        in_specs=[VMEM_SPEC] * 9,
        out_specs=(VMEM_SPEC,) * 3,
        scratch_shapes=[
            vm((8, rows, width)),
            vm((rows, width), jnp.float32),
            vm((width, w3)),
            vm((8, pr, w3)),
            vm((8, pr, w3)),
            vm((16, 8, 128), jnp.float32),
            vm((32, 8, 128), jnp.float32),
            vm((4, width), jnp.float32),
            DMA((32,)),
            DMA((32,)),
        ]
        + SeqReduce.scratch(rows, width)
        + ColSum.scratch(pr, w3)
        + RowExchange.scratch(),
        compiler_params=comm_params(collective, 56),
    )(g, b, qkv_w, a, x, rg, norms, vec, sums)


def rotary_tables(rel):
    half = ROT // 2
    d = jnp.arange(128, dtype=jnp.int32) % HEAD_DIM
    freq = 10000.0 ** (-2.0 * (d % half).astype(jnp.float32) / ROT)
    angle = rel[:, None] * freq[None, :]
    c, s = jnp.cos(angle), jnp.sin(angle)
    second = (d >= half) & (d < ROT)
    return (jnp.where(d < ROT, c, 1.0), jnp.where(d < half, -s, 0.0), jnp.where(second, s, 0.0))


def line_body(
    hidden_in,
    ln1_gain,
    ln1_bias,
    qkv_weight,
    qkv_bias,
    out_weight,
    ln2_gain,
    ln2_bias,
    gate_weight,
    up_weight,
    down_weight,
    seq_lengths,
    deal_order,
    out_grad,
):
    rows = hidden_in.shape[1]
    width = hidden_in.shape[2]
    nseq = lax.axis_size("seq")
    nfsdp = lax.axis_size("fsdp")
    lw = width // nseq
    part = qkv_weight.shape[0]
    ff = gate_weight.shape[1]
    lf = ff // nseq
    seq_at, fsdp_at = lax.axis_index("seq"), lax.axis_index("fsdp")
    order = deal_order[0]
    lengths = seq_lengths[0]
    group_rows = order.shape[0]
    valid_rows = group_rows * 5 // 8
    orow, ocol = order[None, :], order[:, None]
    local_pos = lax.dynamic_slice_in_dim(order, seq_at * rows, rows)
    valid = (local_pos < valid_rows).astype(jnp.float32)[:, None]
    dealt_seg, dealt_start = segment_of(order, lengths)
    dealt_tables = rotary_tables((order - dealt_start).astype(jnp.float32))
    packed_pos = jnp.arange(valid_rows, dtype=jnp.int32)
    packed_seg, packed_start = segment_of(packed_pos, lengths)
    packed_tables = rotary_tables((packed_pos - packed_start).astype(jnp.float32))

    def column_parts(weights):
        views = [w.reshape(part, nseq, -1) for w in weights]
        return jnp.concatenate(views, 2).transpose(1, 0, 2)

    params = jnp.stack([ln1_gain, ln1_bias, ln2_gain, ln2_bias, *qkv_bias])
    params = jnp.pad(params.astype(jnp.float32), ((0, 1), (0, 64)))
    params = jnp.where(fsdp_at % 2 == 0, params, jnp.roll(params, part, 1))
    qkv_parts = qkv_weight.reshape(part, 3, nseq, lw).transpose(2, 0, 1, 3).reshape(nseq, part, -1)
    first_in, qkv_w, norms, out_w, heads_out, packed, lse, mlp_grad, wide_w, down_w, mixed = forward(
        hidden_in[0],
        params,
        qkv_parts,
        out_weight,
        out_grad[0],
        column_parts([gate_weight, up_weight]),
        down_weight,
        dealt_tables,
        orow,
        ocol,
        seq_lengths,
        valid_rows,
        1,
    )
    out_rows = lax.dynamic_slice_in_dim(out_w, seq_at * nfsdp, nfsdp).reshape(lw, width)
    attn, resid, resid_grad, norm2_grads, mlp_part, down_part, wide_sum = middle(
        heads_out,
        out_w.reshape(width, width),
        hidden_in[0],
        norms,
        wide_w,
        down_w.reshape(lf, width),
        mlp_grad,
        3,
    )
    qkv_act, bias_sums, result, sums, gate_grad, up_grad, down_grad, out_grad_w = backward(
        resid_grad,
        out_rows,
        mixed.reshape(group_rows, lw),
        packed,
        lse,
        packed_tables,
        orow,
        ocol,
        seq_lengths,
        attn,
        resid,
        valid,
        mlp_part,
        down_part.reshape(nfsdp, -1, width),
        wide_sum,
        4,
    )
    input_grad, qkv_grad, total = last(
        qkv_act, bias_sums, qkv_w, first_in, hidden_in[0], resid_grad, norms, norm2_grads, sums, 5
    )
    count = valid_rows * nfsdp * width
    rms = jnp.sqrt(total[4, :3] / count)
    halves = lax.dynamic_slice_in_dim(total, (fsdp_at % 2) * part, part, 1)
    shards = halves[:4]
    qkv_bias_grad = halves[5:8]
    return (
        result[None],
        input_grad[None],
        shards[0],
        shards[1],
        qkv_grad,
        qkv_bias_grad,
        out_grad_w,
        shards[2],
        shards[3],
        gate_grad,
        up_grad,
        down_grad,
        rms,
    )


def solution(mesh):
    in_specs = (
        P("fsdp", "seq", None),
        P(("seq", "fsdp")),
        P(("seq", "fsdp")),
        P(("seq", "fsdp"), None),
        P(None, ("seq", "fsdp")),
        P(("seq", "fsdp"), None),
        P(("seq", "fsdp")),
        P(("seq", "fsdp")),
        P(("seq", "fsdp"), None),
        P(("seq", "fsdp"), None),
        P(("seq", "fsdp"), None),
        P("fsdp", None),
        P("fsdp", None),
        P("fsdp", "seq", None),
    )
    out_specs = (
        P("fsdp", "seq", None),
        P("fsdp", "seq", None),
        P(("seq", "fsdp")),
        P(("seq", "fsdp")),
        P(("seq", "fsdp"), None),
        P(None, ("seq", "fsdp")),
        P(("seq", "fsdp"), None),
        P(("seq", "fsdp")),
        P(("seq", "fsdp")),
        P(("seq", "fsdp"), None),
        P(("seq", "fsdp"), None),
        P(("seq", "fsdp"), None),
        P(),
    )
    line = dict(mesh.shape) == {"seq": 8, "fsdp": 4}
    return jax.shard_map(
        line_body if line else body,
        mesh=mesh,
        in_specs=in_specs,
        out_specs=out_specs,
        check_vma=False,
    )
```

```python
import functools

import jax
import jax.numpy as jnp
from jax import lax
from jax.experimental import pallas as pl
from jax.experimental.pallas import tpu as pltpu
from jax.sharding import PartitionSpec as P

HEAD_DIM = 64
ROT = 16


EPS = 1e-05


def normalize(values):
    center = values - jnp.mean(values, -1, keepdims=True)
    spread = jnp.mean(center * center, -1, keepdims=True)
    rstd = lax.rsqrt(spread + EPS)
    return (center * rstd, rstd)


def norm_back(grad, normed, rstd, gain):
    scaled = grad * gain
    inner = (
        scaled
        - jnp.mean(scaled, -1, keepdims=True)
        - normed * jnp.mean(scaled * normed, -1, keepdims=True)
    )
    return (rstd * inner, jnp.sum(grad * normed, 0), jnp.sum(grad, 0))


def segment_of(pos, lengths):
    nseg = lengths.shape[0]
    ends = jnp.cumsum(lengths)
    seg = jnp.sum((pos[:, None] >= ends[None, :]).astype(jnp.int32), 1)
    starts = jnp.concatenate([jnp.zeros((1,), jnp.int32), ends[:-1]])
    start = jnp.sum(
        jnp.where(seg[:, None] == jnp.arange(nseg, dtype=jnp.int32)[None, :], starts[None, :], 0), 1
    )
    start = jnp.where(seg < nseg, start, pos)
    return (seg, start)


def rotate(values, rel, sign):
    count = values.shape[0]
    view = values.reshape(count, -1, HEAD_DIM)
    half = ROT // 2
    freq = 10000.0 ** (-2.0 * jnp.arange(half, dtype=jnp.float32) / ROT)
    angle = rel[:, None] * freq[None, :]
    cosine = jnp.cos(angle)[:, None, :]
    sine = jnp.sin(angle)[:, None, :]
    first = view[..., :half]
    second = view[..., half:ROT]
    turned = jnp.concatenate(
        [
            first * cosine - sign * second * sine,
            second * cosine + sign * first * sine,
            view[..., ROT:],
        ],
        -1,
    )
    return turned.reshape(count, -1)


def outer(left, right):
    return lax.dot_general(
        left, right, (((0,), (0,)), ((), ())), preferred_element_type=jnp.float32
    )


def times(left, right):
    return jnp.dot(left, right, preferred_element_type=jnp.float32)


def times_transposed(left, right):
    return lax.dot_general(
        left, right, (((1,), (1,)), ((), ())), preferred_element_type=jnp.float32
    )


def mlp_forward(gate, upper):
    sigma = jax.nn.sigmoid(gate)
    return ((gate * sigma * upper).astype(jnp.bfloat16), sigma)


def mlp_backward(hidden_grad, gate, upper, sigma):
    up_act = (hidden_grad * gate * sigma).astype(jnp.bfloat16)
    gate_act = (hidden_grad * upper * sigma * (1.0 + gate * (1.0 - sigma))).astype(jnp.bfloat16)
    return (gate_act, up_act)


def body(
    hidden_in,
    ln1_gain,
    ln1_bias,
    qkv_weight,
    qkv_bias,
    out_weight,
    ln2_gain,
    ln2_bias,
    gate_weight,
    up_weight,
    down_weight,
    seq_lengths,
    deal_order,
    out_grad,
):
    rows = hidden_in.shape[1]
    width = hidden_in.shape[2]
    nseq = lax.axis_size("seq")
    nfsdp = lax.axis_size("fsdp")
    local_width = width // nseq
    part = qkv_weight.shape[0]
    ff = gate_weight.shape[1]
    local_ff = ff // nseq
    stream = hidden_in[0].astype(jnp.float32)
    cotangent = out_grad[0].astype(jnp.float32)
    order = deal_order[0]
    lengths = seq_lengths[0]
    nseg = lengths.shape[0]
    group_rows = order.shape[0]
    valid_rows = group_rows * 5 // 8
    longest = valid_rows * 4 // 5
    blk = min(512, group_rows)
    keys = min(group_rows, longest + blk)
    nblocks = group_rows // blk
    scale = HEAD_DIM ** (-0.5)
    local_pos = lax.dynamic_slice_in_dim(order, lax.axis_index("seq") * rows, rows)
    valid = (local_pos < valid_rows).astype(jnp.float32)[:, None]
    dealt_seg, dealt_start = segment_of(order, lengths)
    rel = (order - dealt_start).astype(jnp.float32)
    inverse = (
        jnp.zeros((group_rows,), jnp.int32).at[order].set(jnp.arange(group_rows, dtype=jnp.int32))
    )
    seg_p, start_p = segment_of(jnp.arange(group_rows, dtype=jnp.int32), lengths)

    def gather_rows(values):
        return lax.all_gather(values, "seq", axis=0, tiled=True)

    def scatter_rows(partial):
        return lax.psum_scatter(
            partial.astype(jnp.bfloat16), "seq", scatter_dimension=0, tiled=True
        ).astype(jnp.float32)

    def column_slice(weight, blocks):
        cols = weight.shape[1] // (blocks * nseq)
        view = weight.reshape(part, blocks, nseq, cols).transpose(2, 0, 1, 3)
        mine = lax.all_to_all(
            view.reshape(nseq * part, blocks * cols), "seq", split_axis=0, concat_axis=0, tiled=True
        )
        full = lax.all_gather(mine.reshape(nseq, part, blocks * cols), "fsdp", axis=1)
        return full.reshape(width, blocks * cols)

    def row_slice(weight):
        return lax.all_gather(weight, "fsdp", axis=0, tiled=True)

    def column_shard(grad, blocks):
        cols = grad.shape[1] // blocks
        view = grad.astype(jnp.bfloat16).reshape(nseq, nfsdp, part, blocks * cols)
        mine = lax.psum_scatter(view.transpose(1, 0, 2, 3), "fsdp", scatter_dimension=0)
        got = lax.all_to_all(
            mine.reshape(nseq * part, blocks * cols), "seq", split_axis=0, concat_axis=0, tiled=True
        )
        view = got.reshape(nseq, part, blocks, cols).transpose(1, 2, 0, 3)
        return view.reshape(part, -1).astype(jnp.float32)

    def row_shard(grad):
        return lax.psum_scatter(
            grad.astype(jnp.bfloat16), "fsdp", scatter_dimension=0, tiled=True
        ).astype(jnp.float32)

    def to_pack(values):
        heads_here = values.shape[1] // HEAD_DIM
        return values[inverse].reshape(group_rows, heads_here, HEAD_DIM)

    def window(index, packed):
        query_p, key_p, value_p = packed
        first = index * blk
        key_first = jnp.clip(jnp.minimum(start_p[first], group_rows - keys), 0, group_rows - keys)
        qpos = first + jnp.arange(blk, dtype=jnp.int32)
        kpos = key_first + jnp.arange(keys, dtype=jnp.int32)
        qseg = lax.dynamic_slice_in_dim(seg_p, first, blk)
        kseg = lax.dynamic_slice_in_dim(seg_p, key_first, keys)
        allowed = (qseg[:, None] == kseg[None, :]) & (qseg[:, None] < nseg) & (
            kpos[None, :] <= qpos[:, None]
        ) | (kpos[None, :] == qpos[:, None])
        qblock = lax.dynamic_slice_in_dim(query_p, first, blk)
        kblock = lax.dynamic_slice_in_dim(key_p, key_first, keys)
        vblock = lax.dynamic_slice_in_dim(value_p, key_first, keys)
        scores = (
            jnp.einsum("qhd,khd->hqk", qblock, kblock, preferred_element_type=jnp.float32) * scale
        )
        scores = jnp.where(allowed[None], scores, -1e30)
        return (first, key_first, qblock, kblock, vblock, scores)

    both = ("seq", "fsdp")
    norms = lax.all_gather(
        jnp.stack([ln1_gain, ln1_bias, ln2_gain, ln2_bias, *qkv_bias]), both, axis=1, tiled=True
    )
    gain1, shift1, gain2, shift2 = norms[:4].astype(jnp.float32)
    qkv_shift = lax.dynamic_slice_in_dim(
        norms[4:], lax.axis_index("seq") * local_width, local_width, 1
    )
    qkv_shift = qkv_shift.reshape(-1).astype(jnp.float32)

    normed1, rstd1 = normalize(stream)
    first_local = (normed1 * gain1 + shift1).astype(jnp.bfloat16)
    first_in = gather_rows(first_local)
    qkv_w = column_slice(qkv_weight, 3)
    qkv = times(first_in, qkv_w) + qkv_shift
    query = rotate(qkv[:, :local_width], rel, 1.0).astype(jnp.bfloat16)
    keyset = rotate(qkv[:, local_width : 2 * local_width], rel, 1.0).astype(jnp.bfloat16)
    valueset = qkv[:, 2 * local_width :].astype(jnp.bfloat16)
    packed = (to_pack(query), to_pack(keyset), to_pack(valueset))

    def attend_block(index):
        first, key_first, qblock, kblock, vblock, scores = window(index, packed)
        top = jnp.max(scores, -1, keepdims=True)
        expo = jnp.exp(scores - top)
        total = jnp.sum(expo, -1, keepdims=True)
        probs = (expo / total).astype(jnp.bfloat16)
        mixed = jnp.einsum("hqk,khd->qhd", probs, vblock, preferred_element_type=jnp.float32)
        return (mixed.astype(jnp.bfloat16), (top + jnp.log(total))[..., 0])

    mixed_all, lse_all = lax.map(attend_block, jnp.arange(nblocks, dtype=jnp.int32))
    mixed = mixed_all.reshape(group_rows, -1)[order]
    heads_out = lax.all_to_all(mixed, "seq", split_axis=0, concat_axis=1, tiled=True)
    out_w = lax.all_gather(out_weight, both, axis=0, tiled=True)
    out_rows = row_slice(out_weight)
    attn = times(heads_out, out_w)
    resid = stream + attn
    normed2, rstd2 = normalize(resid)
    second_in = gather_rows((normed2 * gain2 + shift2).astype(jnp.bfloat16))
    gate_w = column_slice(gate_weight, 1)
    up_w = column_slice(up_weight, 1)
    down_w = row_slice(down_weight)
    gate = times(second_in, gate_w)
    upper = times(second_in, up_w)
    hidden, sigma = mlp_forward(gate, upper)
    mlp = scatter_rows(times(hidden, down_w))
    result = resid + mlp

    mlp_grad = gather_rows(out_grad[0])
    hidden_grad = times_transposed(mlp_grad, down_w)
    gate_act, up_act = mlp_backward(hidden_grad, gate, upper, sigma)
    second_grad = scatter_rows(times_transposed(gate_act, gate_w) + times_transposed(up_act, up_w))
    down_grad = row_shard(outer(hidden, mlp_grad))
    gate_grad = column_shard(outer(second_in, gate_act), 1)
    up_grad = column_shard(outer(second_in, up_act), 1)
    resid_part, gain2_grad, shift2_grad = norm_back(second_grad, normed2, rstd2, gain2)
    resid_grad = cotangent + resid_part

    attn_grad = gather_rows(resid_grad.astype(jnp.bfloat16))
    out_grad_w = row_shard(outer(mixed, attn_grad))
    mixed_grad_p = to_pack(times_transposed(attn_grad, out_rows).astype(jnp.bfloat16))

    def back_block(index, carry):
        query_acc, key_acc, value_acc = carry
        first, key_first, qblock, kblock, vblock, scores = window(index, packed)
        probs = jnp.exp(scores - lse_all[index][:, :, None])
        dblock = lax.dynamic_slice_in_dim(mixed_grad_p, first, blk)
        value_part = jnp.einsum(
            "hqk,qhd->khd", probs.astype(jnp.bfloat16), dblock, preferred_element_type=jnp.float32
        )
        prob_grad = jnp.einsum("qhd,khd->hqk", dblock, vblock, preferred_element_type=jnp.float32)
        inner = jnp.sum(probs * prob_grad, -1, keepdims=True)
        score_grad = (probs * (prob_grad - inner)).astype(jnp.bfloat16)
        query_part = (
            jnp.einsum("hqk,khd->qhd", score_grad, kblock, preferred_element_type=jnp.float32)
            * scale
        )
        key_part = (
            jnp.einsum("hqk,qhd->khd", score_grad, qblock, preferred_element_type=jnp.float32)
            * scale
        )
        query_acc = lax.dynamic_update_slice_in_dim(query_acc, query_part, first, 0)
        key_old = lax.dynamic_slice_in_dim(key_acc, key_first, keys)
        key_acc = lax.dynamic_update_slice_in_dim(key_acc, key_old + key_part, key_first, 0)
        value_old = lax.dynamic_slice_in_dim(value_acc, key_first, keys)
        value_acc = lax.dynamic_update_slice_in_dim(value_acc, value_old + value_part, key_first, 0)
        return (query_acc, key_acc, value_acc)

    zeros = jnp.zeros(packed[0].shape, jnp.float32)
    query_acc, key_acc, value_acc = lax.fori_loop(0, nblocks, back_block, (zeros, zeros, zeros))

    def to_dealt(values):
        return values.astype(jnp.bfloat16).reshape(group_rows, -1)[order]

    qkv_act = jnp.concatenate(
        [
            rotate(to_dealt(query_acc).astype(jnp.float32), rel, -1.0).astype(jnp.bfloat16),
            rotate(to_dealt(key_acc).astype(jnp.float32), rel, -1.0).astype(jnp.bfloat16),
            to_dealt(value_acc),
        ],
        1,
    )
    first_grad = scatter_rows(times_transposed(qkv_act, qkv_w))
    qkv_grad = column_shard(outer(first_in, qkv_act), 3)
    qkv_bias_grad = lax.psum_scatter(
        jnp.sum(qkv_act.astype(jnp.float32), 0).reshape(3, nfsdp, -1),
        "fsdp",
        scatter_dimension=1,
    )
    input_part, gain1_grad, shift1_grad = norm_back(first_grad, normed1, rstd1, gain1)
    input_grad = resid_grad + input_part

    norm_grads = lax.psum(
        (
            gain1_grad,
            shift1_grad,
            gain2_grad,
            shift2_grad,
            jnp.sum(valid * result * result),
            jnp.sum(valid * attn * attn),
            jnp.sum(valid * mlp * mlp),
        ),
        both,
    )
    count = valid_rows * nfsdp * width
    rms = jnp.sqrt(jnp.stack(norm_grads[4:]) / count)
    mine = (lax.axis_index("seq") * nfsdp + lax.axis_index("fsdp")) * part
    norm_shards = [lax.dynamic_slice_in_dim(value, mine, part) for value in norm_grads[:4]]
    return (
        result.astype(jnp.bfloat16)[None],
        input_grad[None],
        norm_shards[0],
        norm_shards[1],
        qkv_grad,
        qkv_bias_grad,
        out_grad_w,
        norm_shards[2],
        norm_shards[3],
        gate_grad,
        up_grad,
        down_grad,
        rms,
    )


MESH = pl.DeviceIdType.MESH
QB = 128
NEG = -1e30
CH = 2
VMEM_SPEC = pl.BlockSpec(memory_space=pltpu.VMEM)
SMEM_SPEC = pl.BlockSpec(memory_space=pltpu.SMEM)
ANY_SPEC = pl.BlockSpec(memory_space=pl.ANY)
HBM_SPEC = pl.BlockSpec(memory_space=pltpu.HBM)
DMA = pltpu.SemaphoreType.DMA


def comm_params(collective, limit=63):
    return pltpu.CompilerParams(
        collective_id=collective, has_side_effects=True, vmem_limit_bytes=limit << 20
    )


def where_am_i():
    s = lax.axis_index("seq")
    f = lax.axis_index("fsdp")
    return s, f, s // 2, s % 2


def remote(src, dst, send, recv, device):
    return pltpu.make_async_remote_copy(
        src, dst, send, recv, device_id=device, device_id_type=MESH
    )


def flip(v, bit):
    return v + bit * (1 - 2 * ((v // bit) % 2))


def peer(s, k):
    for bit in (1, 2, 4):
        if k & bit:
            s = flip(s, bit)
    return s


def dealer(i):
    return (i // 4, i % 4)


def greet_all(s, f):
    bar = pltpu.get_barrier_semaphore()
    me = s * 4 + f

    @pl.loop(1, 32)
    def _(k):
        pl.semaphore_signal(bar, inc=1, device_id=dealer((me + k) % 32), device_id_type=MESH)

    pl.semaphore_wait(bar, 31)


def greet_line(s, f, z, y):
    bar = pltpu.get_barrier_semaphore()
    pl.semaphore_signal(bar, inc=1, device_id=(flip(s, 1), f), device_id_type=MESH)

    @pl.when(z > 0)
    def _():
        pl.semaphore_signal(bar, inc=1, device_id=(s - 2, f), device_id_type=MESH)

    @pl.when(z < 3)
    def _():
        pl.semaphore_signal(bar, inc=1, device_id=(s + 2, f), device_id_type=MESH)

    edge = jnp.where((z == 0) | (z == 3), 1, 0)
    pl.semaphore_wait(bar, 3 - edge)


def greet_columns(s, f):
    bar = pltpu.get_barrier_semaphore()
    for k in range(1, 8):
        pl.semaphore_signal(bar, inc=1, device_id=(peer(s, k), f), device_id_type=MESH)
    pl.semaphore_signal(bar, inc=1, device_id=(s, flip(f, 1)), device_id_type=MESH)
    pl.semaphore_signal(bar, inc=1, device_id=(s, flip(f, 2)), device_id_type=MESH)
    pl.semaphore_wait(bar, 9)


def adder(dst, srcs, step=16):
    @pl.loop(0, dst.shape[0] // step)
    def _(i):
        r = pl.ds(pl.multiple_of(i * step, step), step)
        total = srcs[0][r].astype(jnp.float32)
        for v in srcs[1:]:
            total = total + v[r].astype(jnp.float32)
        dst[r] = total.astype(dst.dtype)


class SeqGather:
    @staticmethod
    def scratch(parts=1):
        return [DMA, DMA((8, parts)), DMA((4, parts)), DMA((4, parts)), DMA((4, parts))]

    def __init__(self, x, o, own, recv, sy, su, sd):
        self.x, self.o, self.recv, self.sy, self.su, self.sd = x, o, recv, sy, su, sd
        self.s, self.f, self.z, self.y = where_am_i()
        self.parts = recv.shape[1]
        self.other = flip(self.s, 1)
        self.own = pltpu.make_async_copy(x, o.at[self.s], own)

    def rows(self, c):
        n = self.x.shape[0] // self.parts
        return pl.ds(c * n, n)

    def at(self, zb):
        return 2 * zb + self.y

    def copy(self, zb, c, own, sems, to):
        b, r = self.at(zb), self.rows(c)
        src = self.x.at[r] if own else self.o.at[b, r]
        return remote(src, self.o.at[b, r], sems.at[zb, c], self.recv.at[b, c], (to, self.f))

    def ysend(self, zb, c, own=False):
        return self.copy(zb, c, own, self.sy, self.other)

    def usend(self, zb, c, own=False):
        return self.copy(zb, c, own, self.su, self.s + 2)

    def dsend(self, zb, c, own=False):
        return self.copy(zb, c, own, self.sd, self.s - 2)

    def arrived(self, b, c):
        o = self.o.at[b, self.rows(c)]
        return remote(o, o, self.sy.at[0, c], self.recv.at[b, c], (self.other, self.f))

    def start(self):
        for c in range(self.parts):

            @pl.when(self.z < 3)
            def _():
                self.usend(self.z, c, True).start()

            @pl.when(self.z > 0)
            def _():
                self.dsend(self.z, c, True).start()

            self.ysend(self.z, c, True).start()
        self.own.start()

    def near(self, i):
        low = jnp.where(self.z < 2, self.z, 3 - self.z)
        base = jnp.where(low == 0, i, jnp.where(i < 2, 1 - i, i))
        return jnp.where(self.z < 2, base, 3 - base)

    def arrive(self, i, c=0):
        zb = self.near(i)
        self.arrived(self.at(zb), c).wait_recv()

        @pl.when((zb < self.z) & (self.z < 3))
        def _():
            self.usend(zb, c).start()

        @pl.when((zb > self.z) & (self.z > 0))
        def _():
            self.dsend(zb, c).start()

        self.ysend(zb, c).start()

    def column(self, i):
        return self.at(self.near(i))

    def cross(self, i):
        b = 2 * self.near(i) + 1 - self.y
        for c in range(self.parts):
            self.arrived(b, c).wait_recv()
        return b

    def steps(self):
        return [functools.partial(self.arrive, i, c) for i in (1, 2, 3) for c in range(self.parts)]

    def each(self, use, counts):
        left = self.steps()

        @pl.loop(0, 8)
        def _(j):
            i = (j + 1) // 2
            column = (j == 0) | ((j % 2 == 1) & (j < 7))
            for n, count in enumerate(counts):
                now = [left.pop(0) for _ in range(count)]
                if now:

                    @pl.when(j == n)
                    def _():
                        for item in now:
                            item()

            other = jnp.where(j == 7, 3, j // 2 - 1)

            @pl.when(jnp.logical_not(column))
            def _():
                self.cross(other)

            zb = self.near(jnp.where(column, i, other))
            use(2 * zb + jnp.where(column, self.y, 1 - self.y))

    def finish(self, own=True):
        if own:
            self.own.wait()
        for c in range(self.parts):
            for zb in range(4):
                self.ysend(zb, c).wait_send()

                @pl.when((self.z < 3) & (zb <= self.z))
                def _():
                    self.usend(zb, c).wait_send()

                @pl.when((self.z > 0) & (zb >= self.z))
                def _():
                    self.dsend(zb, c).wait_send()


class SeqReduce:
    @staticmethod
    def scratch(rows, w):
        big = [pltpu.VMEM((n, rows, w), jnp.bfloat16) for n in (4, 5)]
        return big + [DMA((4, CH)), DMA((5, CH)), DMA((4, CH)), DMA((4, CH))]

    def __init__(self, p, o, ybuf, got, ry, rl, sy, sl):
        self.p, self.o, self.ybuf, self.got = p, o, ybuf, got
        self.ry, self.rl, self.sy, self.sl = ry, rl, sy, sl
        self.s, self.f, self.z, self.y = where_am_i()
        self.other = flip(self.s, 1)
        self.ch = p.shape[1] // CH

    def order(self, k):
        a, b, c, d = [3, 2, 1, 0][k], [3, 0, 2, 1][k], [0, 3, 1, 2][k], [0, 1, 2, 3][k]
        z = self.z
        return jnp.where(z == 0, a, jnp.where(z == 1, b, jnp.where(z == 2, c, d)))

    def rows(self, c):
        return pl.ds(c * self.ch, self.ch)

    def ysend(self, zb, c):
        r = self.rows(c)
        src = self.p.at[2 * zb + 1 - self.y, r]
        dst = self.ybuf.at[zb, r]
        return remote(src, dst, self.sy.at[zb, c], self.ry.at[zb, c], (self.other, self.f))

    def usend(self, zb, c):
        r = self.rows(c)
        src, dst = self.ybuf.at[zb, r], self.got.at[zb, r]
        return remote(src, dst, self.sl.at[zb, c], self.rl.at[zb, c], (self.s + 2, self.f))

    def dsend(self, zb, c):
        r = self.rows(c)
        slot = jnp.where(zb == self.z - 1, 4, zb)
        src, dst = self.ybuf.at[zb, r], self.got.at[slot, r]
        return remote(src, dst, self.sl.at[zb, c], self.rl.at[slot, c], (self.s - 2, self.f))

    def landed(self, slot, c):
        v = self.got.at[slot, self.rows(c)]
        return remote(v, v, self.sl.at[0, c], self.rl.at[slot, c], (self.other, self.f))

    def send(self, k):
        for c in range(CH):
            self.ysend(self.order(k), c).start()

    def start(self):
        for k in range(4):
            self.send(k)

    def step(self, k, c):
        z, zb, r = self.z, self.order(k), self.rows(c)
        self.ysend(zb, c).wait_recv()
        a, b = self.p.at[2 * zb + self.y, r], self.ybuf.at[zb, r]
        u, d = self.got.at[zb, r], self.got.at[4, r]
        alone = ((zb > z) & (z == 0)) | ((zb < z) & (z == 3))

        @pl.when(alone)
        def _():
            adder(b, [a, b])

        @pl.when((zb != z) & jnp.logical_not(alone))
        def _():
            self.landed(zb, c).wait_recv()
            adder(b, [a, b, u])

        @pl.when(zb > z)
        def _():
            self.usend(zb, c).start()

        @pl.when(zb < z)
        def _():
            self.dsend(zb, c).start()

        @pl.when(zb == z)
        def _():
            o = self.o.at[r]

            @pl.when(z == 0)
            def _():
                self.landed(4, c).wait_recv()
                adder(o, [a, b, d])

            @pl.when(z == 3)
            def _():
                self.landed(zb, c).wait_recv()
                adder(o, [a, b, u])

            @pl.when((z > 0) & (z < 3))
            def _():
                self.landed(zb, c).wait_recv()
                self.landed(4, c).wait_recv()
                adder(o, [a, b, u, d])

    def steps(self):
        return [functools.partial(self.step, k, c) for k in range(4) for c in range(CH)]

    def finish(self):
        for zb in range(4):
            for c in range(CH):
                self.ysend(zb, c).wait_send()

                @pl.when(zb != self.z)
                def _():
                    self.usend(zb, c).wait_send()


class ColGather:
    @staticmethod
    def scratch():
        return [DMA, DMA((8, 4)), DMA((8,)), DMA((8, 2)), DMA((8,))]

    def __init__(self, x, o, own, recv, direct, core, xs):
        self.x, self.o, self.own, self.recv = x, o, own, recv
        self.direct, self.core, self.xs = direct, core, xs
        self.s, self.f, _, _ = where_am_i()
        self.fc, self.fx = flip(self.f, 1), flip(self.f, 2)
        self.fd = flip(self.fc, 2)
        self.mine = pltpu.make_async_copy(x.at[self.s], self.piece(self.s, self.f), own)

    def piece(self, t, ff):
        r = self.x.shape[1]
        return self.o.at[pl.ds(pl.multiple_of((t * 4 + ff) * r, r), r)]

    def send_direct(self, k):
        s, f, t = self.s, self.f, peer(self.s, k)
        return remote(self.x.at[t], self.piece(s, f), self.direct.at[k], self.recv.at[s, f], (t, f))

    def send_core(self, k, which, src):
        t, ff = peer(self.s, k), self.f if which == 0 else self.fx
        dst = self.piece(t, ff)
        return remote(src, dst, self.core.at[k, which], self.recv.at[t, ff], (self.s, self.fc))

    def send_x(self, k, src):
        t = peer(self.s, k)
        dst = self.piece(t, self.f)
        return remote(src, dst, self.xs.at[k], self.recv.at[t, self.f], (self.s, self.fx))

    def arrived(self, k, ff):
        t = peer(self.s, k)
        o = self.piece(t, ff)
        return remote(o, o, self.own, self.recv.at[t, ff], (self.s, self.fc))

    def start(self):
        for k in reversed(range(1, 8)):
            self.send_direct(k).start()
        self.send_x(0, self.x.at[self.s]).start()
        self.send_core(0, 0, self.x.at[self.s]).start()
        self.mine.start()

    def step(self, k):
        t = peer(self.s, k)
        self.arrived(k, self.f).wait_recv()
        self.send_x(k, self.piece(t, self.f)).start()
        self.send_core(k, 0, self.piece(t, self.f)).start()

    def xstep(self, k):
        t = peer(self.s, k)
        self.arrived(k, self.fx).wait_recv()
        self.send_core(k, 1, self.piece(t, self.fx)).start()

    def steps(self):
        first = [functools.partial(self.step, k) for k in reversed(range(1, 8))]
        then = [functools.partial(self.xstep, k) for k in (0, 7, 6, 5, 4, 3, 2, 1)]
        return first + then

    def complete(self):
        self.mine.wait()
        for k in range(8):
            self.arrived(k, self.fc).wait_recv()
            self.arrived(k, self.fd).wait_recv()

    def finish(self):
        for k in range(8):
            if k:
                self.send_direct(k).wait_send()
            self.send_x(k, self.x.at[0]).wait_send()
            self.send_core(k, 0, self.x.at[0]).wait_send()
            self.send_core(k, 1, self.x.at[0]).wait_send()


class ColSum:
    @staticmethod
    def scratch(r, c):
        def v(*lead):
            return pltpu.VMEM(lead + (8, r, c), jnp.bfloat16)

        return [v(2), v(), DMA((2, 8)), DMA((2, 8)), DMA((8,)), DMA((8,))]

    def __init__(self, g, h, cb, xb, cs, cr, xs, xr):
        self.g, self.h, self.cb, self.xb = g, h, cb, xb
        self.cs, self.cr, self.xs, self.xr = cs, cr, xs, xr
        self.s, self.f, _, _ = where_am_i()
        self.fc, self.fx = flip(self.f, 1), flip(self.f, 2)
        self.fd = flip(self.fc, 2)
        self.r, self.c = h.shape[1:]

    def piece(self, i, ff):
        at = pl.multiple_of((i * 4 + ff) * self.r, self.r)
        return self.g.at[pl.ds(at, self.r), pl.ds(0, self.c)]

    def core(self, w, i):
        src = self.piece(i, self.fd if w == 0 else self.fc)
        dst = self.cb.at[w, i]
        return remote(src, dst, self.cs.at[w, i], self.cr.at[w, i], (self.s, self.fc))

    def xsend(self, i):
        src, dst = self.cb.at[0, i], self.xb.at[i]
        return remote(src, dst, self.xs.at[i], self.xr.at[i], (self.s, self.fx))

    def send(self, i):
        self.core(0, i).start()
        self.core(1, i).start()

    def step(self, i):
        self.core(0, i).wait_recv()
        adder(self.cb.at[0, i], [self.piece(i, self.fx), self.cb.at[0, i]])
        self.xsend(i).start()

    def total(self, i):
        self.core(1, i).wait_recv()
        self.xsend(i).wait_recv()
        adder(self.h.at[i], [self.piece(i, self.f), self.cb.at[1, i], self.xb.at[i]])

    def finish(self):
        for i in range(8):
            self.core(0, i).wait_send()
            self.core(1, i).wait_send()
            self.xsend(i).wait_send()


class FsdpReduce:
    @staticmethod
    def scratch(r, c):
        return [pltpu.VMEM((2, r, c), jnp.bfloat16), pltpu.VMEM((r, c), jnp.bfloat16), DMA((3,)), DMA((3,))]

    def __init__(self, g, o, cb, xb, send, recv):
        self.g, self.o, self.cb, self.xb = g, o, cb, xb
        self.s, self.f, _, _ = where_am_i()
        f = self.f
        self.fx = flip(f, 2)
        fc = flip(f, 1)
        core = (self.s, fc)
        self.far = remote(g.at[flip(fc, 2)], cb.at[0], send.at[0], recv.at[0], core)
        self.near = remote(g.at[fc], cb.at[1], send.at[1], recv.at[1], core)
        self.over = remote(cb.at[0], xb, send.at[2], recv.at[2], (self.s, self.fx))

    def start(self):
        self.far.start()
        self.near.start()

    def step(self):
        self.far.wait_recv()
        adder(self.cb.at[0], [self.g.at[self.fx], self.cb.at[0]])
        self.over.start()

    def total(self):
        self.near.wait_recv()
        self.over.wait_recv()
        adder(self.o, [self.g.at[self.f], self.cb.at[1], self.xb])

    def finish(self):
        self.far.wait_send()
        self.near.wait_send()
        self.over.wait_send()


class FsdpGather:
    @staticmethod
    def scratch():
        return [DMA, DMA((4,)), DMA((3,))]

    def __init__(self, x, o, own, recv, send):
        self.x, self.o, self.own, self.recv, self.send = x, o, own, recv, send
        self.s, self.f, _, _ = where_am_i()
        self.fc, self.fx = flip(self.f, 1), flip(self.f, 2)
        self.fd = flip(self.fc, 2)
        self.mine = pltpu.make_async_copy(x, o.at[self.f], own)

    def pass_on(self, n, src, ff, to):
        return remote(src, self.o.at[ff], self.send.at[n], self.recv.at[ff], (self.s, to))

    def arrived(self, ff):
        o = self.o.at[ff]
        return remote(o, o, self.own, self.recv.at[ff], (self.s, self.fc))

    def start(self):
        self.pass_on(0, self.x, self.f, self.fx).start()
        self.pass_on(1, self.x, self.f, self.fc).start()
        self.mine.start()

    def step(self):
        self.arrived(self.fx).wait_recv()
        self.pass_on(2, self.o.at[self.fx], self.fx, self.fc).start()

    def finish(self):
        self.mine.wait()
        self.arrived(self.fc).wait_recv()
        self.arrived(self.fd).wait_recv()
        for n in range(3):
            self.pass_on(n, self.x, self.f, self.fc).wait_send()


class WholeGather:
    @staticmethod
    def scratch():
        return [DMA, DMA((32,)), DMA((4,)), DMA((4,)), DMA((4,)), DMA((4, 2)), DMA((4, 2, 2))]

    def __init__(self, x, o, own, recv, su, sd, sy, sx, sc):
        self.x, self.o, self.own, self.recv = x, o, own, recv
        self.su, self.sd, self.sy, self.sx, self.sc = su, sd, sy, sx, sc
        self.s, self.f, self.z, self.y = where_am_i()
        self.fc, self.fx = flip(self.f, 1), flip(self.f, 2)
        self.fd = flip(self.fc, 2)
        self.me = self.s * 4 + self.f
        self.mine = pltpu.make_async_copy(x, o.at[self.me], own)

    def at(self, zb, yy, ff):
        return (2 * zb + (self.y if yy == 0 else 1 - self.y)) * 4 + ff

    def src(self, b, first):
        return self.x if first else self.o.at[b]

    def up(self, zb, first=False):
        b = self.at(zb, 0, self.f)
        to = (self.s + 2, self.f)
        return remote(self.src(b, first), self.o.at[b], self.su.at[zb], self.recv.at[b], to)

    def down(self, zb, first=False):
        b = self.at(zb, 0, self.f)
        to = (self.s - 2, self.f)
        return remote(self.src(b, first), self.o.at[b], self.sd.at[zb], self.recv.at[b], to)

    def over_y(self, zb, first=False):
        b = self.at(zb, 0, self.f)
        to = (flip(self.s, 1), self.f)
        return remote(self.src(b, first), self.o.at[b], self.sy.at[zb], self.recv.at[b], to)

    def over_x(self, zb, yy, first=False):
        b = self.at(zb, yy, self.f)
        to = (self.s, self.fx)
        return remote(self.src(b, first), self.o.at[b], self.sx.at[zb, yy], self.recv.at[b], to)

    def over_core(self, zb, yy, xx, first=False):
        b = self.at(zb, yy, self.f if xx == 0 else self.fx)
        to = (self.s, self.fc)
        return remote(self.src(b, first), self.o.at[b], self.sc.at[zb, yy, xx], self.recv.at[b], to)

    def arrived(self, b):
        o = self.o.at[b]
        return remote(o, o, self.own, self.recv.at[b], (self.s, self.fc))

    def start(self):
        z = self.z

        @pl.when(z < 3)
        def _():
            self.up(z, True).start()

        @pl.when(z > 0)
        def _():
            self.down(z, True).start()

        self.over_y(z, True).start()
        self.over_x(z, 0, True).start()
        self.over_core(z, 0, 0, True).start()
        self.mine.start()

    def line(self, sign, t):
        zb = self.z + sign * t

        @pl.when((zb >= 0) & (zb <= 3))
        def _():
            self.arrived(self.at(zb, 0, self.f)).wait_recv()
            if sign < 0:

                @pl.when(self.z < 3)
                def _():
                    self.up(zb).start()

            else:

                @pl.when(self.z > 0)
                def _():
                    self.down(zb).start()

            self.over_y(zb).start()
            self.over_x(zb, 0).start()
            self.over_core(zb, 0, 0).start()

    def column(self, sign, t):
        zb = self.z + sign * t

        @pl.when((zb >= 0) & (zb <= 3))
        def _():
            self.arrived(self.at(zb, 1, self.f)).wait_recv()
            self.over_x(zb, 1).start()
            self.over_core(zb, 1, 0).start()

    def side(self, sign, t, yy):
        zb = self.z + sign * t

        @pl.when((zb >= 0) & (zb <= 3))
        def _():
            self.arrived(self.at(zb, yy, self.fx)).wait_recv()
            self.over_core(zb, yy, 1).start()

    def steps(self):
        p = functools.partial
        out = []
        for t in range(4):
            for sign in (-1, 1) if t else (1,):
                if t:
                    out.append(p(self.line, sign, t))
        for t in range(4):
            for sign in (-1, 1) if t else (1,):
                out.append(p(self.column, sign, t))
                out.append(p(self.side, sign, t, 0))
        for t in range(4):
            for sign in (-1, 1) if t else (1,):
                out.append(p(self.side, sign, t, 1))
        return out

    def finish(self):
        self.mine.wait()
        for zb in range(4):
            for yy in range(2):
                self.arrived(self.at(zb, yy, self.fc)).wait_recv()
                self.arrived(self.at(zb, yy, self.fd)).wait_recv()
        for zb in range(4):
            self.over_y(zb).wait_send()

            @pl.when((self.z < 3) & (zb <= self.z))
            def _():
                self.up(zb).wait_send()

            @pl.when((self.z > 0) & (zb >= self.z))
            def _():
                self.down(zb).wait_send()

            for yy in range(2):
                self.over_x(zb, yy).wait_send()
                for xx in range(2):
                    self.over_core(zb, yy, xx).wait_send()


class RowExchange:
    @staticmethod
    def scratch():
        return [DMA, DMA((8,)), DMA((8,))]

    def __init__(self, x, o, own, send, recv):
        self.x, self.o, self.send, self.recv = x, o, send, recv
        self.s, self.f, _, _ = where_am_i()
        self.mine = pltpu.make_async_copy(x.at[self.s], o.at[self.s], own)

    def piece(self, k):
        t = peer(self.s, k)
        dst = self.o.at[self.s]
        return remote(self.x.at[t], dst, self.send.at[k], self.recv.at[k], (t, self.f))

    def start(self):
        for k in reversed(range(1, 8)):
            self.piece(k).start()
        self.mine.start()

    def finish(self):
        self.mine.wait()
        for k in reversed(range(1, 8)):
            self.piece(k).wait_recv()
            self.piece(k).wait_send()


def idle():
    pass


def fetch(refs, sems):
    copies = [pltpu.make_async_copy(a, b, sems.at[i]) for i, (a, b) in enumerate(refs)]
    for copy in copies:
        copy.start()
    return copies


def rotary_rows(pos, lengths_ref, freq):
    half = ROT // 2
    d = lax.broadcasted_iota(jnp.int32, (1, 128), 1) % HEAD_DIM
    rel = pos - starts_of(pos, lengths_ref, lengths_ref.shape[1])
    angle = rel.astype(jnp.float32) * freq
    c, s = jnp.cos(angle), jnp.sin(angle)
    second = (d >= half) & (d < ROT)
    return jnp.where(d < ROT, c, 1.0), jnp.where(d < half, -s, 0.0), jnp.where(second, s, 0.0)


def perform(plan, queues):
    left = {name: list(items) for name, items in queues.items()}
    for name in "".join(plan):
        left[name].pop(0)()
    assert not any(left.values())


FORWARD_PLAN = (
    "nFngnWggssswwVnsnswwssvswsvsnsnssvsvwsnvDwwwcwcc",
    "wcfvccvwvdvdcwwcwwvcwcwcccvcccwdwvwwwcwwcXvvvww",
)
MIDDLE_ARRIVALS = (1, 2, 0, 1, 1, 1)
MIDDLE_PLAN = ("ramaarteeraatelalmmetalteretlemmalltlehhthllhhhhtzhh",)
BACKWARD_PLAN = ("bFggrgbbXgbgbgrbfbrtZtbcrotccoocotocootocqOcccptccccPttz",)
LAST_PLAN = ("daddeawdahtaeeaaahatewwttheteetehhhwhttzhZ",)


def merged(*lists):
    keyed = []
    for n, items in enumerate(lists):
        keyed += [((i + 0.5) / len(items), n, item) for i, item in enumerate(items)]
    return [item for _, _, item in sorted(keyed, key=lambda v: v[:2])]


def dot(a, b, ca=1, cb=0):
    return lax.dot_general(a, b, (((ca,), (cb,)), ((), ())), preferred_element_type=jnp.float32)


def starts_of(pos, lengths_ref, nseg):
    start = jnp.zeros_like(pos)
    end = 0
    for i in range(nseg - 1):
        end = end + lengths_ref[0, i]
        start = jnp.where(pos >= end, end, start)
    return start


def head_lanes(h):
    lane = lax.broadcasted_iota(jnp.int32, (1, 128), 1)
    return (lane // HEAD_DIM) == h


def turn(x, c, s1, s2, sign):
    half = ROT // 2
    return x * c + (pltpu.roll(x, 128 - half, 1) * s1 + pltpu.roll(x, half, 1) * s2) * sign


def block_mask(qb, lengths_ref):
    keys = (qb + 1) * QB
    row = qb * QB + lax.broadcasted_iota(jnp.int32, (QB, 1), 0)
    col = lax.broadcasted_iota(jnp.int32, (1, keys), 1)
    return (col >= starts_of(row, lengths_ref, lengths_ref.shape[1])) & (col <= row)


def row_at(i, step=QB):
    return pl.ds(pl.multiple_of(i * step, step), step)


def picks(orow_ref, i):
    p = lax.broadcasted_iota(jnp.int32, (QB, 1), 0) + i * QB == orow_ref[...]
    return jnp.where(p, 1.0, 0.0).astype(jnp.bfloat16)


def puts(oc, valid):
    p = oc == lax.broadcasted_iota(jnp.int32, (1, valid), 1)
    return jnp.where(p, 1.0, 0.0).astype(jnp.bfloat16)


def attend(
    a_ref, w_ref, shift_of, tables, orow_ref, ocol_ref, len_ref, o_ref, pk_ref, lse_ref, rot, opk
):
    rows, w3 = rot.shape
    w = w3 // 3
    valid = pk_ref.shape[0]
    scale = HEAD_DIM**-0.5
    freq_ref = tables

    def project(lo, hi):
        shift = shift_of()

        @pl.loop(lo, hi)
        def _(i):
            r = row_at(i, 256)
            c, s1, s2 = rotary_rows(ocol_ref[r], len_ref, freq_ref[...])
            left = jnp.concatenate([a_ref[2 * i], a_ref[2 * i + 1]], 0)
            qkv = dot(left, w_ref[...]) + shift
            for t in range(w3 // 128):
                cols = slice(t * 128, t * 128 + 128)
                x = qkv[:, cols]
                if t < 2 * w // 128:
                    x = turn(x, c, s1, s2, 1.0)
                rot[r, cols] = x.astype(jnp.bfloat16)

    def pack(lo, hi):
        @pl.loop(lo, hi)
        def _(i):
            pk_ref[row_at(i)] = dot(picks(orow_ref, i), rot[...]).astype(jnp.bfloat16)

    def block(qb, t):
        keys = (qb + 1) * QB
        rq = slice(qb * QB, qb * QB + QB)
        ct = slice(t * 128, t * 128 + 128)
        mask = block_mask(qb, len_ref)
        q = pk_ref[rq, ct]
        k = pk_ref[0:keys, w + t * 128 : w + t * 128 + 128]
        v = pk_ref[0:keys, 2 * w + t * 128 : 2 * w + t * 128 + 128]
        total = None
        for h in range(2):
            qh = jnp.where(head_lanes(h), q, jnp.zeros_like(q))
            scores = jnp.where(mask, dot(qh, k, 1, 1) * scale, NEG)
            top = jnp.max(scores, -1, keepdims=True)
            expo = jnp.exp(scores - top)
            norm = jnp.sum(expo, -1, keepdims=True)
            probs = (expo / norm).astype(jnp.bfloat16)
            lse_ref[2 * t + h, rq] = top + jnp.log(norm)
            out = dot(probs, v)
            total = out if h == 0 else jnp.where(head_lanes(1), out, total)
        opk[rq, ct] = total.astype(jnp.bfloat16)

    def unpack(lo, hi):
        per = o_ref.shape[1]

        @pl.loop(lo, hi)
        def _(i):
            r = row_at(i, per)
            oc = ocol_ref[r]
            back = dot(puts(oc, valid), opk[...])
            pad = rot[r, 2 * w :].astype(jnp.float32)
            o_ref[i] = jnp.where(oc >= valid, pad, back).astype(jnp.bfloat16)

    blocks = [
        functools.partial(block, qb, t) for qb in range(valid // QB) for t in range(w // 128)
    ]
    p = functools.partial
    steps, half, blks = rows // 256, valid // QB // 2, rows // o_ref.shape[1]
    head = [p(project, 0, steps // 2), p(project, steps // 2, steps)]
    head += [p(pack, 0, half), p(pack, half, valid // QB)]
    return head + blocks + [p(unpack, 0, blks // 2), p(unpack, blks // 2, blks)]


def attend_back(
    pk_ref, do_ref, lse_ref, tables, orow_ref, ocol_ref, len_ref, g_ref, b_ref, dpk, dq, dk, dv, gpk
):
    rows, w = do_ref.shape
    valid = pk_ref.shape[0]
    scale = HEAD_DIM**-0.5
    freq_ref = tables

    def pack():
        @pl.loop(0, valid // QB)
        def _(i):
            r = row_at(i)
            dpk[r] = dot(picks(orow_ref, i), do_ref[...]).astype(jnp.bfloat16)
            dk[r] = jnp.zeros((QB, w), jnp.float32)
            dv[r] = jnp.zeros((QB, w), jnp.float32)

    def block(qb, t):
        keys = (qb + 1) * QB
        rq = slice(qb * QB, qb * QB + QB)
        ct = slice(t * 128, t * 128 + 128)
        mask = block_mask(qb, len_ref)
        q, d = pk_ref[rq, ct], dpk[rq, ct]
        k = pk_ref[0:keys, w + t * 128 : w + t * 128 + 128]
        v = pk_ref[0:keys, 2 * w + t * 128 : 2 * w + t * 128 + 128]
        total = None
        for h in range(2):
            hl = head_lanes(h)
            qh = jnp.where(hl, q, jnp.zeros_like(q))
            dh = jnp.where(hl, d, jnp.zeros_like(d))
            scores = jnp.where(mask, dot(qh, k, 1, 1) * scale, NEG)
            p = jnp.exp(scores - lse_ref[2 * t + h, rq])
            dp = dot(dh, v, 1, 1)
            inner = jnp.sum(p * dp, -1, keepdims=True)
            ds = (p * (dp - inner)).astype(jnp.bfloat16)
            dv[0:keys, ct] += dot(p.astype(jnp.bfloat16), dh, 0, 0)
            dk[0:keys, ct] += dot(ds, qh, 0, 0)
            part = dot(ds, k)
            total = part if h == 0 else jnp.where(head_lanes(1), part, total)
        dq[rq, ct] = total

    def rotary():
        @pl.loop(0, valid // QB)
        def _(i):
            r = row_at(i)
            pos = lax.broadcasted_iota(jnp.int32, (QB, 1), 0) + i * QB
            c, s1, s2 = rotary_rows(pos, len_ref, freq_ref[...])
            for t in range(w // 128):
                ct = slice(t * 128, t * 128 + 128)
                for j, src in ((0, dq), (1, dk)):
                    x = (src[r, ct] * scale).astype(jnp.bfloat16).astype(jnp.float32)
                    at = j * w + t * 128
                    gpk[r, at : at + 128] = turn(x, c, s1, s2, -1.0).astype(jnp.bfloat16)
                at = 2 * w + t * 128
                gpk[r, at : at + 128] = dv[r, ct].astype(jnp.bfloat16)

    def unpack():
        b_ref[...] = jnp.zeros_like(b_ref)

        @pl.loop(0, rows // QB)
        def _(i):
            r = row_at(i)
            oc = ocol_ref[r]
            back = dot(puts(oc, valid), gpk[...])
            pad = jnp.where(oc >= valid, do_ref[r].astype(jnp.float32), 0.0)
            back = jnp.concatenate([back[:, : 2 * w], back[:, 2 * w :] + pad], 1)
            g_ref[r] = back.astype(jnp.bfloat16)
            b_ref[...] += jnp.sum(back, 0, keepdims=True)

    blocks = [
        functools.partial(block, qb, t) for qb in range(valid // QB) for t in range(w // 128)
    ]
    return [pack] + blocks + [rotary, unpack]


def forward_kernel(
    x_hbm,
    p_ref,
    qkv_ref,
    op_hbm,
    dm_hbm,
    gate_hbm,
    up_hbm,
    dp_hbm,
    freq_ref,
    orow_ref,
    ocol_ref,
    len_ref,
    a_ref,
    qw_ref,
    n_ref,
    ow_ref,
    ho_ref,
    pk_ref,
    lse_ref,
    dmo_ref,
    ww_ref,
    dw_ref,
    mix_ref,
    x_ref,
    op_ref,
    dm_ref,
    gate_ref,
    up_ref,
    dp_ref,
    xs,
    got,
    rot,
    opk,
    qp_ref,
    wp_ref,
    load,
    psend,
    precv,
    *sems,
):
    s, f, z, y = where_am_i()
    me = s * 4 + f
    w = rot.shape[1] // 3
    lf = wp_ref.shape[2] // 2

    def piece_of(i):
        t, n = i // 3, i % 3
        at = n * x_ref.shape[1] + t * w
        return qkv_ref.at[:, at : at + w], qp_ref.at[t, :, n * w : n * w + w]

    operands = [(x_hbm, x_ref)] + [piece_of(i) for i in range(24)]
    operands += [(op_hbm, op_ref), (dm_hbm, dm_ref), (dp_hbm, dp_ref)]
    operands += [(gate_hbm, gate_ref), (up_hbm, up_ref)]
    loads = fetch(operands, load)
    greet_all(s, f)
    gather = SeqGather(x_ref, xs, *sems[:5])
    slices = ColGather(qp_ref, qw_ref, *sems[5:10])
    whole = WholeGather(op_ref, ow_ref, *sems[10:17])
    grads = SeqGather(dm_ref, dmo_ref, *sems[17:22])
    wide = ColGather(wp_ref, ww_ref, *sems[22:27])
    down = FsdpGather(dp_ref, dw_ref, *sems[27:30])
    swap = RowExchange(mix_ref, ho_ref, *sems[30:])

    def param(k):
        i = (me + k) % 32
        return remote(p_ref, got.at[me], psend.at[k], precv.at[k], dealer(i))

    @pl.loop(1, 32)
    def _(k):
        param(k).start()

    loads[0].wait()
    gather.start()
    for copy in loads[1:]:
        copy.wait()
    slices.start()
    got[me] = p_ref[...]

    @pl.loop(1, 32)
    def _(k):
        param(k).wait_recv()

    for i in range(16):
        n_ref[:, i * 128 : i * 128 + 128] = got[2 * i] + got[2 * i + 1]
    step = 16

    def norm(b):
        gain, shift = n_ref[0:1], n_ref[1:2]

        @pl.loop(0, x_ref.shape[0] // step)
        def _(i):
            r = row_at(i, step)
            normed, _ = normalize(xs[b, r].astype(jnp.float32))
            a_ref[b, r] = (normed * gain + shift).astype(jnp.bfloat16)

    def shift_of():
        parts = []
        for n in range(3):
            part = jnp.zeros((1, w), jnp.float32)
            for i in range(8):
                piece = n_ref[4 + n : 5 + n, i * w : i * w + w]
                part = part + jnp.where(s == i, piece, jnp.zeros_like(piece))
            parts.append(part)
        return jnp.concatenate(parts, 1)

    work = attend(
        a_ref,
        qw_ref,
        shift_of,
        freq_ref,
        orow_ref,
        ocol_ref,
        len_ref,
        mix_ref,
        pk_ref,
        lse_ref,
        rot,
        opk,
    )
    p = functools.partial

    def own():
        gather.own.wait()
        norm(s)

    def wide_start():
        for i in range(8):
            at = slice(i * lf, i * lf + lf)
            wp_ref[i, :, 0:lf] = gate_ref[:, at]
            wp_ref[i, :, lf : 2 * lf] = up_ref[:, at]
        wide.start()

    norms = [own]
    for i in range(4):
        norms.append(lambda i=i: norm(gather.cross(i)))
        if i < 3:
            norms.append(lambda i=i: norm(2 * gather.near(i + 1) + y))
    work = [slices.complete, work[0], idle, work[1], idle] + work[2:]
    queues = dict(
        g=gather.steps(),
        n=norms,
        s=slices.steps(),
        d=grads.steps(),
        v=wide.steps(),
        w=whole.steps(),
        f=[down.step],
        c=work,
        D=[grads.start],
        V=[wide_start],
        W=[whole.start],
        F=[down.start],
        X=[swap.start],
    )
    work[0:2] = [lambda first=work[0], then=work[1]: (first(), then())]
    perform(FORWARD_PLAN, queues)
    for i in range(4):
        grads.cross(i)
    swap.finish()
    wide.complete()
    for task in (slices, wide, whole, down, grads):
        task.finish()
    gather.finish(False)

    @pl.loop(1, 32)
    def _(k):
        param(k).wait_send()


def forward(
    x, params, qkv, out_p, dm, gate, up, down_p, freq, orow, ocol, lengths, valid, collective
):
    rows, width = x.shape
    w3 = qkv.shape[1] // 8
    part, wide = gate.shape[0], gate.shape[1] // 4
    w = w3 // 3
    group = 8 * rows
    heads = w // HEAD_DIM

    def out(shape, dtype=jnp.bfloat16):
        return jax.ShapeDtypeStruct(shape, dtype)

    return pl.pallas_call(
        forward_kernel,
        out_shape=(
            out((8, rows, width)),
            out((width, w3)),
            out((8, width), jnp.float32),
            out((32,) + out_p.shape),
            out((8, rows, w)),
            out((valid, w3)),
            out((heads, valid, 1), jnp.float32),
            out((8, rows, width)),
            out((width, wide)),
            out((4,) + down_p.shape),
            out((8, rows, w)),
        ),
        in_specs=[HBM_SPEC, VMEM_SPEC] + [HBM_SPEC] * 6 + [VMEM_SPEC] * 3 + [SMEM_SPEC],
        out_specs=(VMEM_SPEC,) * 3
        + (ANY_SPEC,)
        + (VMEM_SPEC,) * 3
        + (ANY_SPEC,) * 3
        + (VMEM_SPEC,),
        scratch_shapes=[pltpu.VMEM(v.shape, v.dtype) for v in (x, out_p, dm, gate, up, down_p)]
        + [
            pltpu.VMEM((8, rows, width), jnp.bfloat16),
            pltpu.VMEM((32, 8, 128), jnp.float32),
            pltpu.VMEM((group, w3), jnp.bfloat16),
            pltpu.VMEM((valid, w), jnp.bfloat16),
            pltpu.VMEM((8, part, w3), jnp.bfloat16),
            pltpu.VMEM((8, part, wide), jnp.bfloat16),
            DMA((30,)),
            DMA((32,)),
            DMA((32,)),
        ]
        + SeqGather.scratch()
        + ColGather.scratch()
        + WholeGather.scratch()
        + SeqGather.scratch()
        + ColGather.scratch()
        + FsdpGather.scratch()
        + RowExchange.scratch(),
        compiler_params=comm_params(collective),
    )(x, params, qkv, out_p, dm, gate, up, down_p, freq, orow, ocol, lengths)


def tall(rows, step=16):
    def wrap(fn):
        @pl.loop(0, rows // step)
        def _(i):
            fn(row_at(i, step))

    return wrap


def middle_kernel(
    ho_hbm,
    ow_ref,
    x_hbm,
    n_ref,
    ww_hbm,
    dw_hbm,
    dm_hbm,
    attn_hbm,
    res_hbm,
    rg_ref,
    vec_ref,
    mp_hbm,
    dg_hbm,
    h_hbm,
    ho_ref,
    x_ref,
    ww_ref,
    dw_ref,
    dm_ref,
    attn_ref,
    res_ref,
    mp_ref,
    dg_ref,
    h_ref,
    big,
    cloc,
    c_ref,
    hid,
    act,
    part,
    second,
    load,
    store,
    *scratch,
):
    s, f, z, y = where_am_i()
    rows, width = x_ref.shape
    lf = dw_ref.shape[0]
    lw = ho_ref.shape[2]
    first = [(ho_hbm, ho_ref), (x_hbm, x_ref), (ow_ref, big)]
    loads = fetch(first + [(ww_hbm, ww_ref), (dw_hbm, dw_ref), (dm_hbm, dm_ref)], load)
    greet_columns(s, f)
    gather = SeqGather(cloc, c_ref, *scratch[:5])
    reduce = SeqReduce(part, second, *scratch[5:11])
    sums = ColSum(big, h_ref, *scratch[11:])
    gain, shift = n_ref[2:3], n_ref[3:4]
    for copy in loads[:3]:
        copy.wait()

    @pl.loop(0, width // 512)
    def _(j):
        cols = pl.ds(pl.multiple_of(j * 512, 512), 512)
        total = dot(ho_ref[0], big[0:lw, cols])
        for k in range(1, 8):
            total = total + dot(ho_ref[k], big[k * lw : k * lw + lw, cols])
        attn_ref[:, cols] = total
        res_ref[:, cols] = x_ref[:, cols].astype(jnp.float32) + total

    @tall(rows)
    def _(r):
        normed, _ = normalize(res_ref[r])
        cloc[r] = (normed * gain + shift).astype(jnp.bfloat16)

    gather.start()
    stores = fetch([(attn_ref, attn_hbm), (res_ref, res_hbm)], store)
    gather.own.wait()
    for copy in loads[3:]:
        copy.wait()

    def block(b):
        at = pl.ds(pl.multiple_of(b * rows, rows), rows)
        wide = dot(c_ref[b], ww_ref[...])
        gate, upper = wide[:, :lf], wide[:, lf:]
        hidden, sigma = mlp_forward(gate, upper)
        hid[at] = hidden
        grad = dot(dm_ref[b], dw_ref[...], 1, 1)
        gate_act, up_act = mlp_backward(grad, gate, upper, sigma)
        act[at] = jnp.concatenate([gate_act, up_act], 1)
        part[b] = dot(act[at], ww_ref[...], 1, 1).astype(jnp.bfloat16)

    gather.each(block, MIDDLE_ARRIVALS)

    def wide_grad(i):
        left = [c_ref[b, :, i * 256 : i * 256 + 256] for b in range(8)]
        left = jnp.concatenate(left, 0)
        big[i * 256 : i * 256 + 256, 0 : 2 * lf] = dot(left, act[...], 0, 0).astype(jnp.bfloat16)
        sums.send(i)

    def mlp_part(i):
        @pl.loop(2 * i, 2 * i + 2)
        def _(b):
            at = pl.ds(pl.multiple_of(b * rows, rows), rows)
            mp_ref[b] = dot(hid[at], dw_ref[...]).astype(jnp.bfloat16)

    def down_grad(i):
        cols = slice(i * 256, i * 256 + 256)
        right = jnp.concatenate([dm_ref[b, :, cols] for b in range(8)], 0)
        dg_ref[:, cols] = dot(hid[...], right, 0, 0).astype(jnp.bfloat16)

    def norm_backward():
        vec_ref[...] = jnp.zeros_like(vec_ref)

        @tall(rows)
        def _(r):
            grad = second[r]
            normed, rstd = normalize(res_ref[r])
            inner, gain_part, shift_part = norm_back(grad, normed, rstd, gain)
            rg_ref[r] = dm_ref[s, r].astype(jnp.float32) + inner
            vec_ref[0:1] += gain_part[None]
            vec_ref[1:2] += shift_part[None]

    p = functools.partial
    each = range(8)
    queues = dict(
        r=[p(reduce.send, k) for k in range(4)],
        t=reduce.steps(),
        a=[p(wide_grad, i) for i in each],
        e=[p(sums.step, i) for i in each],
        h=[p(sums.total, i) for i in each],
        m=[p(mlp_part, i) for i in range(4)],
        l=[p(down_grad, i) for i in each],
        z=[norm_backward],
    )
    out_copies = [
        pltpu.make_async_copy(mp_ref, mp_hbm, store.at[2]),
        pltpu.make_async_copy(dg_ref, dg_hbm, store.at[3]),
        pltpu.make_async_copy(h_ref, h_hbm, store.at[4]),
    ]
    for name, copy in zip("mlh", out_copies):
        queues[name].append(copy.start)
    perform(MIDDLE_PLAN, queues)
    for copy in stores + out_copies:
        copy.wait()
    gather.finish(False)
    reduce.finish()
    sums.finish()


def middle(heads_out, out_w, x, norms, wide_w, down_w, dm, collective):
    rows, width = x.shape
    lf = down_w.shape[0]
    group = 8 * rows
    part = width // 32

    def out(shape, dtype=jnp.bfloat16):
        return jax.ShapeDtypeStruct(shape, dtype)

    def vm(shape, dtype=jnp.bfloat16):
        return pltpu.VMEM(shape, dtype)

    wide = (rows, width)
    return pl.pallas_call(
        middle_kernel,
        out_shape=(
            out(wide, jnp.float32),
            out(wide, jnp.float32),
            out(wide, jnp.float32),
            out((8, width), jnp.float32),
            out((8,) + wide),
            out((lf, width)),
            out((8, part, 2 * lf)),
        ),
        in_specs=[HBM_SPEC] * 3 + [VMEM_SPEC] + [HBM_SPEC] * 3,
        out_specs=(ANY_SPEC,) * 2 + (VMEM_SPEC,) * 2 + (ANY_SPEC,) * 3,
        scratch_shapes=[
            vm(heads_out.shape),
            vm(wide),
            vm(wide_w.shape),
            vm(down_w.shape),
            vm(dm.shape),
            vm(wide, jnp.float32),
            vm(wide, jnp.float32),
            vm((8,) + wide),
            vm((lf, width)),
            vm((8, part, 2 * lf)),
            vm((width, width)),
            vm(wide),
            vm((8,) + wide),
            vm((group, lf)),
            vm((group, 2 * lf)),
            vm((8,) + wide),
            vm(wide, jnp.float32),
            DMA((6,)),
            DMA((5,)),
        ]
        + SeqGather.scratch(2)
        + SeqReduce.scratch(rows, width)
        + ColSum.scratch(part, 2 * lf),
        compiler_params=comm_params(collective),
    )(heads_out, out_w, x, norms, wide_w, down_w, dm)


def backward_kernel(
    rg_ref,
    freq_ref,
    orow_ref,
    ocol_ref,
    len_ref,
    ow_hbm,
    mix_hbm,
    pk_hbm,
    lse_hbm,
    attn_hbm,
    res_hbm,
    mp_hbm,
    dg_hbm,
    h_hbm,
    g_ref,
    b_ref,
    lo_ref,
    sum_ref,
    got,
    down_hbm,
    out_ref,
    or_ref,
    mix_ref,
    pk_ref,
    lse_ref,
    attn_ref,
    res_ref,
    mp_ref,
    dg_ref,
    h_ref,
    down_ref,
    da,
    full,
    do_ref,
    og,
    mlp,
    dpk,
    dq,
    dk,
    dv,
    gpk,
    load,
    store,
    *scratch,
):
    s, f, z, y = where_am_i()
    rows, width = rg_ref.shape
    part = out_ref.shape[0]
    valid = pk_ref.shape[0]
    loads = fetch(
        [
            (ow_hbm.at[pl.ds(pl.multiple_of(s * 4, 4), 4)], or_ref),
            (dg_hbm, dg_ref),
            (mp_hbm, mp_ref),
            (h_hbm, h_ref),
            (pk_hbm, pk_ref),
            (lse_hbm, lse_ref),
            (mix_hbm, mix_ref),
            (attn_hbm, attn_ref),
            (res_hbm, res_ref),
        ],
        load,
    )
    greet_columns(s, f)
    gather = SeqGather(da, full, *scratch[:5])
    reduce = SeqReduce(mp_ref, mlp, *scratch[5:11])
    swap = RowExchange(h_ref, got, *scratch[11:14])
    down = FsdpReduce(dg_ref, down_ref, *scratch[14:18])
    outer_sum = FsdpReduce(og, out_ref, *scratch[18:])

    @tall(rows)
    def _(r):
        da[r] = rg_ref[r].astype(jnp.bfloat16)

    gather.start()

    def block(b):
        at = pl.ds(pl.multiple_of(b * rows, rows), rows)
        out_rows = jnp.concatenate([or_ref[k] for k in range(4)], 0)
        do_ref[at] = dot(full[b], out_rows, 1, 1).astype(jnp.bfloat16)

    def own_block():
        gather.own.wait()
        loads[0].wait()
        block(s)

    def before(copies, then):
        def run():
            for copy in copies:
                copy.wait()
            then()

        return run

    out_copies = [pltpu.make_async_copy(down_ref, down_hbm, store)]

    def down_total():
        down.total()
        out_copies[0].start()

    blocks = [own_block]
    for i in range(4):
        if i < 3:
            blocks.append(lambda i=i: block(gather.column(i + 1)))
        blocks.append(lambda i=i: block(gather.cross(i)))

    def out_grad(i):
        cols = slice(i * 256, i * 256 + 256)
        right = jnp.concatenate([full[b, :, cols] for b in range(8)], 0)
        value = dot(mix_ref[...], right, 0, 0).astype(jnp.bfloat16)
        for k in range(4):
            og[k, :, cols] = value[k * part : k * part + part]

    p = functools.partial
    work = attend_back(
        pk_ref,
        do_ref,
        lse_ref,
        freq_ref,
        orow_ref,
        ocol_ref,
        len_ref,
        g_ref,
        b_ref,
        dpk,
        dq,
        dk,
        dv,
        gpk,
    )
    def results():
        sum_ref[...] = jnp.zeros_like(sum_ref)

        step = 16

        @pl.loop(0, rows // step)
        def _(i):
            r = row_at(i, step)
            m = mlp[r]
            result = res_ref[r] + m
            lo_ref[r] = result.astype(jnp.bfloat16)
            pos = ocol_ref[pl.ds(pl.multiple_of(s * rows + i * step, step), step)]
            keep = jnp.where(pos < valid, 1.0, 0.0)
            for n, v in enumerate((result, attn_ref[r], m)):
                total = jnp.sum(jnp.sum(v * v, -1, keepdims=True) * keep, 0, keepdims=True)
                sum_ref[n : n + 1] += jnp.broadcast_to(total, (1, 128))

    sends = [p(reduce.send, k) for k in range(4)]
    outs = [p(out_grad, i) for i in range(8)]
    queues = dict(
        F=[before(loads[1:2], down.start)],
        f=[down.step],
        q=[down_total],
        b=blocks,
        g=gather.steps(),
        r=[before(loads[2:3], sends[0])] + sends[1:],
        t=reduce.steps(),
        X=[before(loads[3:4], swap.start)],
        Z=[swap.finish],
        c=[before(loads[4:6], work[0])] + work[1:],
        o=[before(loads[6:7], outs[0])] + outs[1:],
        O=[outer_sum.start],
        p=[outer_sum.step],
        P=[outer_sum.total],
        z=[before(loads[7:9], results)],
    )
    perform(BACKWARD_PLAN, queues)
    gather.finish(False)
    reduce.finish()
    down.finish()
    outer_sum.finish()
    for copy in out_copies:
        copy.wait()


def backward(
    rg, freq, orow, ocol, lengths, out_w, mixed, pk, lse, attn, res, mp, dg, h, collective
):
    rows, width = rg.shape
    group, w = mixed.shape
    valid = pk.shape[0]
    part = h.shape[1]

    def out(shape, dtype=jnp.float32):
        return jax.ShapeDtypeStruct(shape, dtype)

    def vm(shape, dtype=jnp.bfloat16):
        return pltpu.VMEM(shape, dtype)

    return pl.pallas_call(
        backward_kernel,
        out_shape=(
            out((group, 3 * w), jnp.bfloat16),
            out((1, 3 * w)),
            out((rows, width), jnp.bfloat16),
            out((8, 128)),
            out(h.shape, jnp.bfloat16),
            out(dg.shape[1:]),
            out((part, width)),
        ),
        in_specs=[VMEM_SPEC] * 4 + [SMEM_SPEC] + [HBM_SPEC] * 9,
        out_specs=(VMEM_SPEC,) * 4 + (ANY_SPEC,) * 2 + (VMEM_SPEC,),
        scratch_shapes=[
            vm((4, part, width)),
            vm(mixed.shape),
            vm(pk.shape),
            vm(lse.shape, jnp.float32),
            vm(attn.shape, jnp.float32),
            vm(res.shape, jnp.float32),
            vm(mp.shape),
            vm(dg.shape),
            vm(h.shape),
            vm(dg.shape[1:], jnp.float32),
            vm((rows, width)),
            vm((8, rows, width)),
            vm((group, w)),
            vm((4, part, width)),
            vm((rows, width), jnp.float32),
            vm((valid, w)),
            vm((valid, w), jnp.float32),
            vm((valid, w), jnp.float32),
            vm((valid, w), jnp.float32),
            vm((valid, 3 * w)),
            DMA((9,)),
            DMA,
        ]
        + SeqGather.scratch(2)
        + SeqReduce.scratch(rows, width)
        + RowExchange.scratch()
        + FsdpReduce.scratch(*dg.shape[1:])
        + FsdpReduce.scratch(part, width),
        compiler_params=comm_params(collective),
    )(rg, freq, orow, ocol, lengths, out_w, mixed, pk, lse, attn, res, mp, dg, h)


def last_kernel(
    g_ref,
    b_ref,
    n_ref,
    vec_ref,
    sum_ref,
    qw_hbm,
    a_hbm,
    x_hbm,
    rg_hbm,
    ig_ref,
    got,
    total_ref,
    qw_ref,
    a_ref,
    x_ref,
    rg_ref,
    load,
    part,
    first,
    grad,
    h,
    msg,
    inbox,
    vec,
    msend,
    mrecv,
    *scratch,
):
    s, f, z, y = where_am_i()
    me = s * 4 + f
    rows, width = x_ref.shape
    w3 = g_ref.shape[1]
    w = w3 // 3
    loads = fetch([(qw_hbm, qw_ref), (a_hbm, a_ref), (x_hbm, x_ref), (rg_hbm, rg_ref)], load)
    greet_all(s, f)
    loads[0].wait()
    reduce = SeqReduce(part, first, *scratch[:6])
    sums = ColSum(grad, h, *scratch[6:12])
    swap = RowExchange(h, got, *scratch[12:])

    def block(b):
        at = pl.ds(pl.multiple_of(b * rows, rows), rows)
        part[b] = dot(g_ref[at], qw_ref[...], 1, 1).astype(jnp.bfloat16)

    def far_block(k):
        block(2 * reduce.order(k) + 1 - y)
        reduce.send(k)

    def own_block(k):
        block(2 * reduce.order(k) + y)

    def qkv_grad(k):
        if k == 7:
            loads[1].wait()
        i = peer(s, k)
        at = pl.ds(pl.multiple_of(i * 256, 256), 256)
        left = jnp.concatenate([a_ref[b, :, at] for b in range(8)], 0)
        grad[at] = dot(left, g_ref[...], 0, 0).astype(jnp.bfloat16)
        sums.send(i)

    def hand_over(k):
        sums.total(peer(s, k))
        if k:
            swap.piece(k).start()
        else:
            swap.mine.start()

    def message(k):
        i = (me + k) % 32
        return remote(msg.at[i // 2], inbox.at[k], msend.at[k], mrecv.at[k], dealer(i))

    def norm_backward():
        vec[0:2] = jnp.zeros((2, width), jnp.float32)
        vec[2:4] = vec_ref[0:2]
        gain = n_ref[0:1]
        loads[2].wait()
        loads[3].wait()

        @tall(rows)
        def _(r):
            normed, rstd = normalize(x_ref[r].astype(jnp.float32))
            inner, gain_part, shift_part = norm_back(first[r], normed, rstd, gain)
            ig_ref[r] = rg_ref[r] + inner
            vec[0:1] += gain_part[None]
            vec[1:2] += shift_part[None]

        lane = lax.broadcasted_iota(jnp.int32, (1, 128), 1)
        scalars = jnp.where(lane == 0, sum_ref[0:1], jnp.where(lane == 1, sum_ref[1:2], sum_ref[2:3]))
        for i in range(16):
            cols = slice(i * 128, i * 128 + 128)
            msg[i, 0:4] = vec[0:4, cols]
            msg[i, 4:5] = scalars
            at = (i % 2) * 128
            for n in range(3):
                piece = b_ref[0:1, n * w + at : n * w + at + 128]
                msg[i, 5 + n : 6 + n] = jnp.where(s == i // 2, piece, jnp.zeros_like(piece))

        @pl.loop(1, 32)
        def _(k):
            message(k).start()

    p = functools.partial
    ks = [7, 6, 5, 4, 3, 2, 1, 0]
    queues = dict(
        d=[p(far_block, k) for k in range(4)],
        w=[p(own_block, k) for k in range(4)],
        t=reduce.steps(),
        a=[p(qkv_grad, k) for k in ks],
        e=[lambda k=k: sums.step(peer(s, k)) for k in ks],
        h=[p(hand_over, k) for k in ks],
        z=[norm_backward],
        Z=[swap.finish],
    )
    perform(LAST_PLAN, queues)
    reduce.finish()
    sums.finish()
    total_ref[...] = msg[me // 2]

    @pl.loop(1, 32)
    def _(k):
        message(k).wait_recv()
        total_ref[...] += inbox[k]

    @pl.loop(1, 32)
    def _(k):
        message(k).wait_send()


def last(g, b, qkv_w, a, x, rg, norms, vec, sums, collective):
    rows, width = x.shape
    w3 = g.shape[1]
    pr = width // 32

    def out(shape, dtype=jnp.float32):
        return jax.ShapeDtypeStruct(shape, dtype)

    def vm(shape, dtype=jnp.bfloat16):
        return pltpu.VMEM(shape, dtype)

    return pl.pallas_call(
        last_kernel,
        out_shape=(out((rows, width)), out((8, pr, w3), jnp.bfloat16), out((8, 128))),
        in_specs=[VMEM_SPEC] * 5 + [HBM_SPEC] * 4,
        out_specs=(VMEM_SPEC, ANY_SPEC, VMEM_SPEC),
        scratch_shapes=[
            vm(qkv_w.shape),
            vm(a.shape),
            vm(x.shape),
            vm(rg.shape, jnp.float32),
            DMA((4,)),
            vm((8, rows, width)),
            vm((rows, width), jnp.float32),
            vm((width, w3)),
            vm((8, pr, w3)),
            vm((16, 8, 128), jnp.float32),
            vm((32, 8, 128), jnp.float32),
            vm((4, width), jnp.float32),
            DMA((32,)),
            DMA((32,)),
        ]
        + SeqReduce.scratch(rows, width)
        + ColSum.scratch(pr, w3)
        + RowExchange.scratch(),
        compiler_params=comm_params(collective),
    )(g, b, norms, vec, sums, qkv_w, a, x, rg)


def results_kernel(*refs):
    same, pieces, outs = refs[:4], refs[4:6], refs[6:13]
    bufs, wide, qkv, spread, load, store = refs[13:17], refs[17], refs[18], refs[19:22], refs[22], refs[23]
    moves = list(zip(same, bufs)) + [(pieces[0], wide), (pieces[1], qkv)]
    loads = fetch(moves, load)
    stores = [pltpu.make_async_copy(bufs[i], outs[i], store.at[i]) for i in range(4)]
    stores += [pltpu.make_async_copy(spread[i], outs[4 + i], store.at[4 + i]) for i in range(3)]
    for i in range(4):
        loads[i].wait()
        stores[i].start()
    loads[4].wait()
    lf = wide.shape[2] // 2
    for n in range(2):
        for i in range(8):
            value = wide[i, :, n * lf : n * lf + lf]
            spread[n][:, i * lf : i * lf + lf] = value.astype(jnp.float32)
        stores[4 + n].start()
    loads[5].wait()
    w = qkv.shape[2] // 3
    for i in range(8):
        for n in range(3):
            at = (n * 8 + i) * w
            spread[2][:, at : at + w] = qkv[i, :, n * w : n * w + w].astype(jnp.float32)
    stores[6].start()
    for copy in stores:
        copy.wait()


def results(same, wide, qkv):
    part = wide.shape[1]
    spread = [(part, 4 * wide.shape[2])] * 2 + [(part, 8 * qkv.shape[2])]
    return pl.pallas_call(
        results_kernel,
        out_shape=[jax.ShapeDtypeStruct(v.shape, v.dtype) for v in same]
        + [jax.ShapeDtypeStruct(v, jnp.float32) for v in spread],
        in_specs=[HBM_SPEC] * 6,
        out_specs=[ANY_SPEC] * 7,
        scratch_shapes=[pltpu.VMEM(v.shape, v.dtype) for v in (*same, wide, qkv)]
        + [pltpu.VMEM(v, jnp.float32) for v in spread]
        + [DMA((6,)), DMA((7,))],
        compiler_params=pltpu.CompilerParams(vmem_limit_bytes=63 << 20),
    )(*same, wide, qkv)


def line_body(
    hidden_in,
    ln1_gain,
    ln1_bias,
    qkv_weight,
    qkv_bias,
    out_weight,
    ln2_gain,
    ln2_bias,
    gate_weight,
    up_weight,
    down_weight,
    seq_lengths,
    deal_order,
    out_grad,
):
    rows = hidden_in.shape[1]
    width = hidden_in.shape[2]
    nseq = lax.axis_size("seq")
    nfsdp = lax.axis_size("fsdp")
    lw = width // nseq
    part = qkv_weight.shape[0]
    ff = gate_weight.shape[1]
    lf = ff // nseq
    seq_at, fsdp_at = lax.axis_index("seq"), lax.axis_index("fsdp")
    order = deal_order[0]
    group_rows = order.shape[0]
    valid_rows = group_rows * 5 // 8
    orow, ocol = order[None, :], order[:, None]
    lane = jnp.arange(128, dtype=jnp.int32) % HEAD_DIM % (ROT // 2)
    freq = 10000.0 ** (-2.0 * lane.astype(jnp.float32) / ROT)
    freq = freq[None, :]
    params = jnp.stack([ln1_gain, ln1_bias, ln2_gain, ln2_bias, *qkv_bias])
    params = jnp.pad(params.astype(jnp.float32), ((0, 1), (0, 64)))
    params = jnp.where(fsdp_at % 2 == 0, params, jnp.roll(params, part, 1))
    first_in, qkv_w, norms, out_w, heads_out, packed, lse, mlp_grad, wide_w, down_w, mixed = forward(
        hidden_in[0],
        params,
        qkv_weight,
        out_weight,
        out_grad[0],
        gate_weight,
        up_weight,
        down_weight,
        freq,
        orow,
        ocol,
        seq_lengths,
        valid_rows,
        1,
    )
    attn, resid, resid_grad, norm2_grads, mlp_part, down_part, wide_sum = middle(
        heads_out,
        out_w.reshape(width, width),
        hidden_in[0],
        norms,
        wide_w,
        down_w.reshape(lf, width),
        mlp_grad,
        3,
    )
    qkv_act, bias_sums, result, sums, wide_pieces, down_grad, out_grad_w = backward(
        resid_grad,
        freq,
        orow,
        ocol,
        seq_lengths,
        out_w,
        mixed.reshape(group_rows, lw),
        packed,
        lse,
        attn,
        resid,
        mlp_part,
        down_part.reshape(nfsdp, -1, width),
        wide_sum,
        4,
    )
    input_grad, qkv_pieces, total = last(
        qkv_act, bias_sums, qkv_w, first_in, hidden_in[0], resid_grad, norms, norm2_grads, sums, 5
    )
    result, input_grad, down_grad, out_grad_w, gate_grad, up_grad, qkv_grad = results(
        (result, input_grad, down_grad, out_grad_w), wide_pieces, qkv_pieces
    )
    count = valid_rows * nfsdp * width
    rms = jnp.sqrt(total[4, :3] / count)
    halves = lax.dynamic_slice_in_dim(total, (fsdp_at % 2) * part, part, 1)
    shards = halves[:4]
    qkv_bias_grad = halves[5:8]
    return (
        result[None],
        input_grad[None],
        shards[0],
        shards[1],
        qkv_grad,
        qkv_bias_grad,
        out_grad_w,
        shards[2],
        shards[3],
        gate_grad,
        up_grad,
        down_grad,
        rms,
    )


def solution(mesh):
    in_specs = (
        P("fsdp", "seq", None),
        P(("seq", "fsdp")),
        P(("seq", "fsdp")),
        P(("seq", "fsdp"), None),
        P(None, ("seq", "fsdp")),
        P(("seq", "fsdp"), None),
        P(("seq", "fsdp")),
        P(("seq", "fsdp")),
        P(("seq", "fsdp"), None),
        P(("seq", "fsdp"), None),
        P(("seq", "fsdp"), None),
        P("fsdp", None),
        P("fsdp", None),
        P("fsdp", "seq", None),
    )
    out_specs = (
        P("fsdp", "seq", None),
        P("fsdp", "seq", None),
        P(("seq", "fsdp")),
        P(("seq", "fsdp")),
        P(("seq", "fsdp"), None),
        P(None, ("seq", "fsdp")),
        P(("seq", "fsdp"), None),
        P(("seq", "fsdp")),
        P(("seq", "fsdp")),
        P(("seq", "fsdp"), None),
        P(("seq", "fsdp"), None),
        P(("seq", "fsdp"), None),
        P(),
    )
    line = dict(mesh.shape) == {"seq": 8, "fsdp": 4}
    return jax.shard_map(
        line_body if line else body,
        mesh=mesh,
        in_specs=in_specs,
        out_specs=out_specs,
        check_vma=False,
    )
```

```python
import functools

import jax
import jax.numpy as jnp
from jax import lax
from jax.experimental import pallas as pl
from jax.experimental.pallas import tpu as pltpu
from jax.sharding import PartitionSpec as P

HEAD_DIM = 64
ROT = 16


EPS = 1e-05


def normalize(values):
    center = values - jnp.mean(values, -1, keepdims=True)
    spread = jnp.mean(center * center, -1, keepdims=True)
    rstd = lax.rsqrt(spread + EPS)
    return (center * rstd, rstd)


def norm_back(grad, normed, rstd, gain):
    scaled = grad * gain
    inner = (
        scaled
        - jnp.mean(scaled, -1, keepdims=True)
        - normed * jnp.mean(scaled * normed, -1, keepdims=True)
    )
    return (rstd * inner, jnp.sum(grad * normed, 0), jnp.sum(grad, 0))


def segment_of(pos, lengths):
    nseg = lengths.shape[0]
    ends = jnp.cumsum(lengths)
    seg = jnp.sum((pos[:, None] >= ends[None, :]).astype(jnp.int32), 1)
    starts = jnp.concatenate([jnp.zeros((1,), jnp.int32), ends[:-1]])
    start = jnp.sum(
        jnp.where(seg[:, None] == jnp.arange(nseg, dtype=jnp.int32)[None, :], starts[None, :], 0), 1
    )
    start = jnp.where(seg < nseg, start, pos)
    return (seg, start)


def rotate(values, rel, sign):
    count = values.shape[0]
    view = values.reshape(count, -1, HEAD_DIM)
    half = ROT // 2
    freq = 10000.0 ** (-2.0 * jnp.arange(half, dtype=jnp.float32) / ROT)
    angle = rel[:, None] * freq[None, :]
    cosine = jnp.cos(angle)[:, None, :]
    sine = jnp.sin(angle)[:, None, :]
    first = view[..., :half]
    second = view[..., half:ROT]
    turned = jnp.concatenate(
        [
            first * cosine - sign * second * sine,
            second * cosine + sign * first * sine,
            view[..., ROT:],
        ],
        -1,
    )
    return turned.reshape(count, -1)


def outer(left, right):
    return lax.dot_general(
        left, right, (((0,), (0,)), ((), ())), preferred_element_type=jnp.float32
    )


def times(left, right):
    return jnp.dot(left, right, preferred_element_type=jnp.float32)


def times_transposed(left, right):
    return lax.dot_general(
        left, right, (((1,), (1,)), ((), ())), preferred_element_type=jnp.float32
    )


def mlp_forward(gate, upper):
    sigma = jax.nn.sigmoid(gate)
    return ((gate * sigma * upper).astype(jnp.bfloat16), sigma)


def mlp_backward(hidden_grad, gate, upper, sigma):
    up_act = (hidden_grad * gate * sigma).astype(jnp.bfloat16)
    gate_act = (hidden_grad * upper * sigma * (1.0 + gate * (1.0 - sigma))).astype(jnp.bfloat16)
    return (gate_act, up_act)


def body(
    hidden_in,
    ln1_gain,
    ln1_bias,
    qkv_weight,
    qkv_bias,
    out_weight,
    ln2_gain,
    ln2_bias,
    gate_weight,
    up_weight,
    down_weight,
    seq_lengths,
    deal_order,
    out_grad,
):
    rows = hidden_in.shape[1]
    width = hidden_in.shape[2]
    nseq = lax.axis_size("seq")
    nfsdp = lax.axis_size("fsdp")
    local_width = width // nseq
    part = qkv_weight.shape[0]
    ff = gate_weight.shape[1]
    local_ff = ff // nseq
    stream = hidden_in[0].astype(jnp.float32)
    cotangent = out_grad[0].astype(jnp.float32)
    order = deal_order[0]
    lengths = seq_lengths[0]
    nseg = lengths.shape[0]
    group_rows = order.shape[0]
    valid_rows = group_rows * 5 // 8
    longest = valid_rows * 4 // 5
    blk = min(512, group_rows)
    keys = min(group_rows, longest + blk)
    nblocks = group_rows // blk
    scale = HEAD_DIM ** (-0.5)
    local_pos = lax.dynamic_slice_in_dim(order, lax.axis_index("seq") * rows, rows)
    valid = (local_pos < valid_rows).astype(jnp.float32)[:, None]
    dealt_seg, dealt_start = segment_of(order, lengths)
    rel = (order - dealt_start).astype(jnp.float32)
    inverse = (
        jnp.zeros((group_rows,), jnp.int32).at[order].set(jnp.arange(group_rows, dtype=jnp.int32))
    )
    seg_p, start_p = segment_of(jnp.arange(group_rows, dtype=jnp.int32), lengths)

    def gather_rows(values):
        return lax.all_gather(values, "seq", axis=0, tiled=True)

    def scatter_rows(partial):
        return lax.psum_scatter(
            partial.astype(jnp.bfloat16), "seq", scatter_dimension=0, tiled=True
        ).astype(jnp.float32)

    def column_slice(weight, blocks):
        cols = weight.shape[1] // (blocks * nseq)
        view = weight.reshape(part, blocks, nseq, cols).transpose(2, 0, 1, 3)
        mine = lax.all_to_all(
            view.reshape(nseq * part, blocks * cols), "seq", split_axis=0, concat_axis=0, tiled=True
        )
        full = lax.all_gather(mine.reshape(nseq, part, blocks * cols), "fsdp", axis=1)
        return full.reshape(width, blocks * cols)

    def row_slice(weight):
        return lax.all_gather(weight, "fsdp", axis=0, tiled=True)

    def column_shard(grad, blocks):
        cols = grad.shape[1] // blocks
        view = grad.astype(jnp.bfloat16).reshape(nseq, nfsdp, part, blocks * cols)
        mine = lax.psum_scatter(view.transpose(1, 0, 2, 3), "fsdp", scatter_dimension=0)
        got = lax.all_to_all(
            mine.reshape(nseq * part, blocks * cols), "seq", split_axis=0, concat_axis=0, tiled=True
        )
        view = got.reshape(nseq, part, blocks, cols).transpose(1, 2, 0, 3)
        return view.reshape(part, -1).astype(jnp.float32)

    def row_shard(grad):
        return lax.psum_scatter(
            grad.astype(jnp.bfloat16), "fsdp", scatter_dimension=0, tiled=True
        ).astype(jnp.float32)

    def to_pack(values):
        heads_here = values.shape[1] // HEAD_DIM
        return values[inverse].reshape(group_rows, heads_here, HEAD_DIM)

    def window(index, packed):
        query_p, key_p, value_p = packed
        first = index * blk
        key_first = jnp.clip(jnp.minimum(start_p[first], group_rows - keys), 0, group_rows - keys)
        qpos = first + jnp.arange(blk, dtype=jnp.int32)
        kpos = key_first + jnp.arange(keys, dtype=jnp.int32)
        qseg = lax.dynamic_slice_in_dim(seg_p, first, blk)
        kseg = lax.dynamic_slice_in_dim(seg_p, key_first, keys)
        allowed = (qseg[:, None] == kseg[None, :]) & (qseg[:, None] < nseg) & (
            kpos[None, :] <= qpos[:, None]
        ) | (kpos[None, :] == qpos[:, None])
        qblock = lax.dynamic_slice_in_dim(query_p, first, blk)
        kblock = lax.dynamic_slice_in_dim(key_p, key_first, keys)
        vblock = lax.dynamic_slice_in_dim(value_p, key_first, keys)
        scores = (
            jnp.einsum("qhd,khd->hqk", qblock, kblock, preferred_element_type=jnp.float32) * scale
        )
        scores = jnp.where(allowed[None], scores, -1e30)
        return (first, key_first, qblock, kblock, vblock, scores)

    both = ("seq", "fsdp")
    norms = lax.all_gather(
        jnp.stack([ln1_gain, ln1_bias, ln2_gain, ln2_bias, *qkv_bias]), both, axis=1, tiled=True
    )
    gain1, shift1, gain2, shift2 = norms[:4].astype(jnp.float32)
    qkv_shift = lax.dynamic_slice_in_dim(
        norms[4:], lax.axis_index("seq") * local_width, local_width, 1
    )
    qkv_shift = qkv_shift.reshape(-1).astype(jnp.float32)

    normed1, rstd1 = normalize(stream)
    first_local = (normed1 * gain1 + shift1).astype(jnp.bfloat16)
    first_in = gather_rows(first_local)
    qkv_w = column_slice(qkv_weight, 3)
    qkv = times(first_in, qkv_w) + qkv_shift
    query = rotate(qkv[:, :local_width], rel, 1.0).astype(jnp.bfloat16)
    keyset = rotate(qkv[:, local_width : 2 * local_width], rel, 1.0).astype(jnp.bfloat16)
    valueset = qkv[:, 2 * local_width :].astype(jnp.bfloat16)
    packed = (to_pack(query), to_pack(keyset), to_pack(valueset))

    def attend_block(index):
        first, key_first, qblock, kblock, vblock, scores = window(index, packed)
        top = jnp.max(scores, -1, keepdims=True)
        expo = jnp.exp(scores - top)
        total = jnp.sum(expo, -1, keepdims=True)
        probs = (expo / total).astype(jnp.bfloat16)
        mixed = jnp.einsum("hqk,khd->qhd", probs, vblock, preferred_element_type=jnp.float32)
        return (mixed.astype(jnp.bfloat16), (top + jnp.log(total))[..., 0])

    mixed_all, lse_all = lax.map(attend_block, jnp.arange(nblocks, dtype=jnp.int32))
    mixed = mixed_all.reshape(group_rows, -1)[order]
    heads_out = lax.all_to_all(mixed, "seq", split_axis=0, concat_axis=1, tiled=True)
    out_w = lax.all_gather(out_weight, both, axis=0, tiled=True)
    out_rows = row_slice(out_weight)
    attn = times(heads_out, out_w)
    resid = stream + attn
    normed2, rstd2 = normalize(resid)
    second_in = gather_rows((normed2 * gain2 + shift2).astype(jnp.bfloat16))
    gate_w = column_slice(gate_weight, 1)
    up_w = column_slice(up_weight, 1)
    down_w = row_slice(down_weight)
    gate = times(second_in, gate_w)
    upper = times(second_in, up_w)
    hidden, sigma = mlp_forward(gate, upper)
    mlp = scatter_rows(times(hidden, down_w))
    result = resid + mlp

    mlp_grad = gather_rows(out_grad[0])
    hidden_grad = times_transposed(mlp_grad, down_w)
    gate_act, up_act = mlp_backward(hidden_grad, gate, upper, sigma)
    second_grad = scatter_rows(times_transposed(gate_act, gate_w) + times_transposed(up_act, up_w))
    down_grad = row_shard(outer(hidden, mlp_grad))
    gate_grad = column_shard(outer(second_in, gate_act), 1)
    up_grad = column_shard(outer(second_in, up_act), 1)
    resid_part, gain2_grad, shift2_grad = norm_back(second_grad, normed2, rstd2, gain2)
    resid_grad = cotangent + resid_part

    attn_grad = gather_rows(resid_grad.astype(jnp.bfloat16))
    out_grad_w = row_shard(outer(mixed, attn_grad))
    mixed_grad_p = to_pack(times_transposed(attn_grad, out_rows).astype(jnp.bfloat16))

    def back_block(index, carry):
        query_acc, key_acc, value_acc = carry
        first, key_first, qblock, kblock, vblock, scores = window(index, packed)
        probs = jnp.exp(scores - lse_all[index][:, :, None])
        dblock = lax.dynamic_slice_in_dim(mixed_grad_p, first, blk)
        value_part = jnp.einsum(
            "hqk,qhd->khd", probs.astype(jnp.bfloat16), dblock, preferred_element_type=jnp.float32
        )
        prob_grad = jnp.einsum("qhd,khd->hqk", dblock, vblock, preferred_element_type=jnp.float32)
        inner = jnp.sum(probs * prob_grad, -1, keepdims=True)
        score_grad = (probs * (prob_grad - inner)).astype(jnp.bfloat16)
        query_part = (
            jnp.einsum("hqk,khd->qhd", score_grad, kblock, preferred_element_type=jnp.float32)
            * scale
        )
        key_part = (
            jnp.einsum("hqk,qhd->khd", score_grad, qblock, preferred_element_type=jnp.float32)
            * scale
        )
        query_acc = lax.dynamic_update_slice_in_dim(query_acc, query_part, first, 0)
        key_old = lax.dynamic_slice_in_dim(key_acc, key_first, keys)
        key_acc = lax.dynamic_update_slice_in_dim(key_acc, key_old + key_part, key_first, 0)
        value_old = lax.dynamic_slice_in_dim(value_acc, key_first, keys)
        value_acc = lax.dynamic_update_slice_in_dim(value_acc, value_old + value_part, key_first, 0)
        return (query_acc, key_acc, value_acc)

    zeros = jnp.zeros(packed[0].shape, jnp.float32)
    query_acc, key_acc, value_acc = lax.fori_loop(0, nblocks, back_block, (zeros, zeros, zeros))

    def to_dealt(values):
        return values.astype(jnp.bfloat16).reshape(group_rows, -1)[order]

    qkv_act = jnp.concatenate(
        [
            rotate(to_dealt(query_acc).astype(jnp.float32), rel, -1.0).astype(jnp.bfloat16),
            rotate(to_dealt(key_acc).astype(jnp.float32), rel, -1.0).astype(jnp.bfloat16),
            to_dealt(value_acc),
        ],
        1,
    )
    first_grad = scatter_rows(times_transposed(qkv_act, qkv_w))
    qkv_grad = column_shard(outer(first_in, qkv_act), 3)
    qkv_bias_grad = lax.psum_scatter(
        jnp.sum(qkv_act.astype(jnp.float32), 0).reshape(3, nfsdp, -1),
        "fsdp",
        scatter_dimension=1,
    )
    input_part, gain1_grad, shift1_grad = norm_back(first_grad, normed1, rstd1, gain1)
    input_grad = resid_grad + input_part

    norm_grads = lax.psum(
        (
            gain1_grad,
            shift1_grad,
            gain2_grad,
            shift2_grad,
            jnp.sum(valid * result * result),
            jnp.sum(valid * attn * attn),
            jnp.sum(valid * mlp * mlp),
        ),
        both,
    )
    count = valid_rows * nfsdp * width
    rms = jnp.sqrt(jnp.stack(norm_grads[4:]) / count)
    mine = (lax.axis_index("seq") * nfsdp + lax.axis_index("fsdp")) * part
    norm_shards = [lax.dynamic_slice_in_dim(value, mine, part) for value in norm_grads[:4]]
    return (
        result.astype(jnp.bfloat16)[None],
        input_grad[None],
        norm_shards[0],
        norm_shards[1],
        qkv_grad,
        qkv_bias_grad,
        out_grad_w,
        norm_shards[2],
        norm_shards[3],
        gate_grad,
        up_grad,
        down_grad,
        rms,
    )


MESH = pl.DeviceIdType.MESH
QB = 128
NEG = -1e30
CH = 2
VMEM_SPEC = pl.BlockSpec(memory_space=pltpu.VMEM)
SMEM_SPEC = pl.BlockSpec(memory_space=pltpu.SMEM)
ANY_SPEC = pl.BlockSpec(memory_space=pl.ANY)
HBM_SPEC = pl.BlockSpec(memory_space=pltpu.HBM)
DMA = pltpu.SemaphoreType.DMA


def comm_params(collective, limit=63):
    return pltpu.CompilerParams(
        collective_id=collective, has_side_effects=True, vmem_limit_bytes=limit << 20
    )


def where_am_i():
    s = lax.axis_index("seq")
    f = lax.axis_index("fsdp")
    return s, f, s // 2, s % 2


def remote(src, dst, send, recv, device):
    return pltpu.make_async_remote_copy(
        src, dst, send, recv, device_id=device, device_id_type=MESH
    )


def flip(v, bit):
    return v + bit * (1 - 2 * ((v // bit) % 2))


def peer(s, k):
    for bit in (1, 2, 4):
        if k & bit:
            s = flip(s, bit)
    return s


def peer_at(s, k):
    for bit in (1, 2, 4):
        s = s + ((k // bit) % 2) * bit * (1 - 2 * ((s // bit) % 2))
    return s


def dealer(i):
    return (i // 4, i % 4)


def greet_all(s, f):
    bar = pltpu.get_barrier_semaphore()
    me = s * 4 + f

    @pl.loop(1, 32)
    def _(k):
        pl.semaphore_signal(bar, inc=1, device_id=dealer((me + k) % 32), device_id_type=MESH)

    pl.semaphore_wait(bar, 31)


def greet_line(s, f, z, y):
    bar = pltpu.get_barrier_semaphore()
    pl.semaphore_signal(bar, inc=1, device_id=(flip(s, 1), f), device_id_type=MESH)

    @pl.when(z > 0)
    def _():
        pl.semaphore_signal(bar, inc=1, device_id=(s - 2, f), device_id_type=MESH)

    @pl.when(z < 3)
    def _():
        pl.semaphore_signal(bar, inc=1, device_id=(s + 2, f), device_id_type=MESH)

    edge = jnp.where((z == 0) | (z == 3), 1, 0)
    pl.semaphore_wait(bar, 3 - edge)


def greet_columns(s, f):
    bar = pltpu.get_barrier_semaphore()
    for k in range(1, 8):
        pl.semaphore_signal(bar, inc=1, device_id=(peer(s, k), f), device_id_type=MESH)
    pl.semaphore_signal(bar, inc=1, device_id=(s, flip(f, 1)), device_id_type=MESH)
    pl.semaphore_signal(bar, inc=1, device_id=(s, flip(f, 2)), device_id_type=MESH)
    pl.semaphore_wait(bar, 9)


def adder(dst, srcs, step=16):
    @pl.loop(0, dst.shape[0] // step)
    def _(i):
        r = pl.ds(pl.multiple_of(i * step, step), step)
        total = srcs[0][r].astype(jnp.float32)
        for v in srcs[1:]:
            total = total + v[r].astype(jnp.float32)
        dst[r] = total.astype(dst.dtype)


class SeqGather:
    @staticmethod
    def scratch(parts=1):
        return [DMA, DMA((8, parts)), DMA((4, parts)), DMA((4, parts)), DMA((4, parts))]

    def __init__(self, x, o, own, recv, sy, su, sd):
        self.x, self.o, self.recv, self.sy, self.su, self.sd = x, o, recv, sy, su, sd
        self.s, self.f, self.z, self.y = where_am_i()
        self.parts = recv.shape[1]
        self.other = flip(self.s, 1)
        self.own = pltpu.make_async_copy(x, o.at[self.s], own)

    def rows(self, c):
        n = self.x.shape[0] // self.parts
        return pl.ds(c * n, n)

    def at(self, zb):
        return 2 * zb + self.y

    def copy(self, zb, c, own, sems, to):
        b, r = self.at(zb), self.rows(c)
        src = self.x.at[r] if own else self.o.at[b, r]
        return remote(src, self.o.at[b, r], sems.at[zb, c], self.recv.at[b, c], (to, self.f))

    def ysend(self, zb, c, own=False):
        return self.copy(zb, c, own, self.sy, self.other)

    def usend(self, zb, c, own=False):
        return self.copy(zb, c, own, self.su, self.s + 2)

    def dsend(self, zb, c, own=False):
        return self.copy(zb, c, own, self.sd, self.s - 2)

    def arrived(self, b, c):
        o = self.o.at[b, self.rows(c)]
        return remote(o, o, self.sy.at[0, c], self.recv.at[b, c], (self.other, self.f))

    def start(self):
        for c in range(self.parts):

            @pl.when(self.z < 3)
            def _():
                self.usend(self.z, c, True).start()

            @pl.when(self.z > 0)
            def _():
                self.dsend(self.z, c, True).start()

            self.ysend(self.z, c, True).start()
        self.own.start()

    def near(self, i):
        low = jnp.where(self.z < 2, self.z, 3 - self.z)
        base = jnp.where(low == 0, i, jnp.where(i < 2, 1 - i, i))
        return jnp.where(self.z < 2, base, 3 - base)

    def arrive(self, i, c=0):
        zb = self.near(i)
        self.arrived(self.at(zb), c).wait_recv()

        @pl.when((zb < self.z) & (self.z < 3))
        def _():
            self.usend(zb, c).start()

        @pl.when((zb > self.z) & (self.z > 0))
        def _():
            self.dsend(zb, c).start()

        self.ysend(zb, c).start()

    def column(self, i):
        return self.at(self.near(i))

    def cross(self, i):
        b = 2 * self.near(i) + 1 - self.y
        for c in range(self.parts):
            self.arrived(b, c).wait_recv()
        return b

    def steps(self):
        return [functools.partial(self.arrive, i, c) for i in (1, 2, 3) for c in range(self.parts)]

    def turn(self, j):
        i = (j + 1) // 2
        column = (j == 0) | ((j % 2 == 1) & (j < 7))
        other = jnp.where(j == 7, 3, j // 2 - 1)

        @pl.when(jnp.logical_not(column))
        def _():
            self.cross(other)

        zb = self.near(jnp.where(column, i, other))
        return 2 * zb + jnp.where(column, self.y, 1 - self.y)

    def finish(self, own=True):
        if own:
            self.own.wait()
        for c in range(self.parts):
            for zb in range(4):
                self.ysend(zb, c).wait_send()

                @pl.when((self.z < 3) & (zb <= self.z))
                def _():
                    self.usend(zb, c).wait_send()

                @pl.when((self.z > 0) & (zb >= self.z))
                def _():
                    self.dsend(zb, c).wait_send()


class SeqReduce:
    @staticmethod
    def scratch(rows, w):
        big = [pltpu.VMEM((n, rows, w), jnp.bfloat16) for n in (4, 5)]
        return big + [DMA((4, CH)), DMA((5, CH)), DMA((4, CH)), DMA((4, CH))]

    def __init__(self, p, o, ybuf, got, ry, rl, sy, sl):
        self.p, self.o, self.ybuf, self.got = p, o, ybuf, got
        self.ry, self.rl, self.sy, self.sl = ry, rl, sy, sl
        self.s, self.f, self.z, self.y = where_am_i()
        self.other = flip(self.s, 1)
        self.ch = p.shape[1] // CH

    def order(self, k):
        low = jnp.where(self.z < 2, self.z, 3 - self.z)
        inner = jnp.where(k == 0, 3, jnp.where(k == 1, 0, jnp.where(k == 2, 2, 1)))
        base = jnp.where(low == 0, 3 - k, inner)
        return jnp.where(self.z < 2, base, 3 - base)

    def rows(self, c):
        return pl.ds(c * self.ch, self.ch)

    def ysend(self, zb, c):
        r = self.rows(c)
        src = self.p.at[2 * zb + 1 - self.y, r]
        dst = self.ybuf.at[zb, r]
        return remote(src, dst, self.sy.at[zb, c], self.ry.at[zb, c], (self.other, self.f))

    def usend(self, zb, c):
        r = self.rows(c)
        src, dst = self.ybuf.at[zb, r], self.got.at[zb, r]
        return remote(src, dst, self.sl.at[zb, c], self.rl.at[zb, c], (self.s + 2, self.f))

    def dsend(self, zb, c):
        r = self.rows(c)
        slot = jnp.where(zb == self.z - 1, 4, zb)
        src, dst = self.ybuf.at[zb, r], self.got.at[slot, r]
        return remote(src, dst, self.sl.at[zb, c], self.rl.at[slot, c], (self.s - 2, self.f))

    def landed(self, slot, c):
        v = self.got.at[slot, self.rows(c)]
        return remote(v, v, self.sl.at[0, c], self.rl.at[slot, c], (self.other, self.f))

    def send(self, k):
        for c in range(CH):
            self.ysend(self.order(k), c).start()

    def start(self):
        for k in range(4):
            self.send(k)

    def step(self, k, c):
        z, zb, r = self.z, self.order(k), self.rows(c)
        self.ysend(zb, c).wait_recv()
        a, b = self.p.at[2 * zb + self.y, r], self.ybuf.at[zb, r]
        u, d = self.got.at[zb, r], self.got.at[4, r]
        alone = ((zb > z) & (z == 0)) | ((zb < z) & (z == 3))

        @pl.when(alone)
        def _():
            adder(b, [a, b])

        @pl.when((zb != z) & jnp.logical_not(alone))
        def _():
            self.landed(zb, c).wait_recv()
            adder(b, [a, b, u])

        @pl.when(zb > z)
        def _():
            self.usend(zb, c).start()

        @pl.when(zb < z)
        def _():
            self.dsend(zb, c).start()

        @pl.when(zb == z)
        def _():
            o = self.o.at[r]

            @pl.when(z == 0)
            def _():
                self.landed(4, c).wait_recv()
                adder(o, [a, b, d])

            @pl.when(z == 3)
            def _():
                self.landed(zb, c).wait_recv()
                adder(o, [a, b, u])

            @pl.when((z > 0) & (z < 3))
            def _():
                self.landed(zb, c).wait_recv()
                self.landed(4, c).wait_recv()
                adder(o, [a, b, u, d])

    def steps(self):
        return [functools.partial(self.step, k, c) for k in range(4) for c in range(CH)]

    def finish(self):
        for zb in range(4):
            for c in range(CH):
                self.ysend(zb, c).wait_send()

                @pl.when(zb != self.z)
                def _():
                    self.usend(zb, c).wait_send()


class ColGather:
    @staticmethod
    def scratch():
        return [DMA, DMA((8, 4)), DMA((8,)), DMA((8, 2)), DMA((8,))]

    def __init__(self, x, o, own, recv, direct, core, xs):
        self.x, self.o, self.own, self.recv = x, o, own, recv
        self.direct, self.core, self.xs = direct, core, xs
        self.s, self.f, _, _ = where_am_i()
        self.fc, self.fx = flip(self.f, 1), flip(self.f, 2)
        self.fd = flip(self.fc, 2)
        self.mine = pltpu.make_async_copy(x.at[self.s], self.piece(self.s, self.f), own)

    def piece(self, t, ff):
        r = self.x.shape[1]
        return self.o.at[pl.ds(pl.multiple_of((t * 4 + ff) * r, r), r)]

    def send_direct(self, k):
        s, f, t = self.s, self.f, peer(self.s, k)
        return remote(self.x.at[t], self.piece(s, f), self.direct.at[k], self.recv.at[s, f], (t, f))

    def send_core(self, k, which, src):
        t, ff = peer(self.s, k), self.f if which == 0 else self.fx
        dst = self.piece(t, ff)
        return remote(src, dst, self.core.at[k, which], self.recv.at[t, ff], (self.s, self.fc))

    def send_x(self, k, src):
        t = peer(self.s, k)
        dst = self.piece(t, self.f)
        return remote(src, dst, self.xs.at[k], self.recv.at[t, self.f], (self.s, self.fx))

    def arrived(self, k, ff):
        t = peer(self.s, k)
        o = self.piece(t, ff)
        return remote(o, o, self.own, self.recv.at[t, ff], (self.s, self.fc))

    def start(self):
        for k in reversed(range(1, 8)):
            self.send_direct(k).start()
        self.send_x(0, self.x.at[self.s]).start()
        self.send_core(0, 0, self.x.at[self.s]).start()
        self.mine.start()

    def step(self, k):
        t = peer(self.s, k)
        self.arrived(k, self.f).wait_recv()
        self.send_x(k, self.piece(t, self.f)).start()
        self.send_core(k, 0, self.piece(t, self.f)).start()

    def xstep(self, k):
        t = peer(self.s, k)
        self.arrived(k, self.fx).wait_recv()
        self.send_core(k, 1, self.piece(t, self.fx)).start()

    def steps(self):
        first = [functools.partial(self.step, k) for k in reversed(range(1, 8))]
        then = [functools.partial(self.xstep, k) for k in (0, 7, 6, 5, 4, 3, 2, 1)]
        return first + then

    def complete(self):
        self.mine.wait()
        for k in range(8):
            self.arrived(k, self.fc).wait_recv()
            self.arrived(k, self.fd).wait_recv()

    def finish(self):
        for k in range(8):
            if k:
                self.send_direct(k).wait_send()
            self.send_x(k, self.x.at[0]).wait_send()
            self.send_core(k, 0, self.x.at[0]).wait_send()
            self.send_core(k, 1, self.x.at[0]).wait_send()


class ColSum:
    @staticmethod
    def scratch(r, c):
        def v(*lead):
            return pltpu.VMEM(lead + (8, r, c), jnp.bfloat16)

        return [v(2), v(), DMA((2, 8)), DMA((2, 8)), DMA((8,)), DMA((8,))]

    def __init__(self, g, h, cb, xb, cs, cr, xs, xr):
        self.g, self.h, self.cb, self.xb = g, h, cb, xb
        self.cs, self.cr, self.xs, self.xr = cs, cr, xs, xr
        self.s, self.f, _, _ = where_am_i()
        self.fc, self.fx = flip(self.f, 1), flip(self.f, 2)
        self.fd = flip(self.fc, 2)
        self.r, self.c = h.shape[1:]

    def piece(self, i, ff):
        at = pl.multiple_of((i * 4 + ff) * self.r, self.r)
        return self.g.at[pl.ds(at, self.r), pl.ds(0, self.c)]

    def core(self, w, i):
        src = self.piece(i, self.fd if w == 0 else self.fc)
        dst = self.cb.at[w, i]
        return remote(src, dst, self.cs.at[w, i], self.cr.at[w, i], (self.s, self.fc))

    def xsend(self, i):
        src, dst = self.cb.at[0, i], self.xb.at[i]
        return remote(src, dst, self.xs.at[i], self.xr.at[i], (self.s, self.fx))

    def send(self, i):
        self.core(0, i).start()
        self.core(1, i).start()

    def step(self, i):
        self.core(0, i).wait_recv()
        adder(self.cb.at[0, i], [self.piece(i, self.fx), self.cb.at[0, i]])
        self.xsend(i).start()

    def total(self, i):
        self.core(1, i).wait_recv()
        self.xsend(i).wait_recv()
        adder(self.h.at[i], [self.piece(i, self.f), self.cb.at[1, i], self.xb.at[i]])

    def finish(self):
        for i in range(8):
            self.core(0, i).wait_send()
            self.core(1, i).wait_send()
            self.xsend(i).wait_send()


class FsdpReduce:
    @staticmethod
    def scratch(r, c):
        return [pltpu.VMEM((2, r, c), jnp.bfloat16), pltpu.VMEM((r, c), jnp.bfloat16), DMA((3,)), DMA((3,))]

    def __init__(self, g, o, cb, xb, send, recv):
        self.g, self.o, self.cb, self.xb = g, o, cb, xb
        self.s, self.f, _, _ = where_am_i()
        f = self.f
        self.fx = flip(f, 2)
        fc = flip(f, 1)
        core = (self.s, fc)
        self.far = remote(g.at[flip(fc, 2)], cb.at[0], send.at[0], recv.at[0], core)
        self.near = remote(g.at[fc], cb.at[1], send.at[1], recv.at[1], core)
        self.over = remote(cb.at[0], xb, send.at[2], recv.at[2], (self.s, self.fx))

    def start(self):
        self.far.start()
        self.near.start()

    def step(self):
        self.far.wait_recv()
        adder(self.cb.at[0], [self.g.at[self.fx], self.cb.at[0]])
        self.over.start()

    def total(self):
        self.near.wait_recv()
        self.over.wait_recv()
        adder(self.o, [self.g.at[self.f], self.cb.at[1], self.xb])

    def finish(self):
        self.far.wait_send()
        self.near.wait_send()
        self.over.wait_send()


class FsdpGather:
    @staticmethod
    def scratch():
        return [DMA, DMA((4,)), DMA((3,))]

    def __init__(self, x, o, own, recv, send):
        self.x, self.o, self.own, self.recv, self.send = x, o, own, recv, send
        self.s, self.f, _, _ = where_am_i()
        self.fc, self.fx = flip(self.f, 1), flip(self.f, 2)
        self.fd = flip(self.fc, 2)
        self.mine = pltpu.make_async_copy(x, o.at[self.f], own)

    def pass_on(self, n, src, ff, to):
        return remote(src, self.o.at[ff], self.send.at[n], self.recv.at[ff], (self.s, to))

    def arrived(self, ff):
        o = self.o.at[ff]
        return remote(o, o, self.own, self.recv.at[ff], (self.s, self.fc))

    def start(self):
        self.pass_on(0, self.x, self.f, self.fx).start()
        self.pass_on(1, self.x, self.f, self.fc).start()
        self.mine.start()

    def step(self):
        self.arrived(self.fx).wait_recv()
        self.pass_on(2, self.o.at[self.fx], self.fx, self.fc).start()

    def finish(self):
        self.mine.wait()
        self.arrived(self.fc).wait_recv()
        self.arrived(self.fd).wait_recv()
        for n in range(3):
            self.pass_on(n, self.x, self.f, self.fc).wait_send()


class WholeGather:
    @staticmethod
    def scratch():
        return [DMA, DMA((32,)), DMA((4,)), DMA((4,)), DMA((4,)), DMA((4, 2)), DMA((4, 2, 2))]

    def __init__(self, x, o, own, recv, su, sd, sy, sx, sc):
        self.x, self.o, self.own, self.recv = x, o, own, recv
        self.su, self.sd, self.sy, self.sx, self.sc = su, sd, sy, sx, sc
        self.s, self.f, self.z, self.y = where_am_i()
        self.fc, self.fx = flip(self.f, 1), flip(self.f, 2)
        self.fd = flip(self.fc, 2)
        self.me = self.s * 4 + self.f
        self.mine = pltpu.make_async_copy(x, o.at[self.me], own)

    def at(self, zb, yy, ff):
        return (2 * zb + (self.y if yy == 0 else 1 - self.y)) * 4 + ff

    def src(self, b, first):
        return self.x if first else self.o.at[b]

    def up(self, zb, first=False):
        b = self.at(zb, 0, self.f)
        to = (self.s + 2, self.f)
        return remote(self.src(b, first), self.o.at[b], self.su.at[zb], self.recv.at[b], to)

    def down(self, zb, first=False):
        b = self.at(zb, 0, self.f)
        to = (self.s - 2, self.f)
        return remote(self.src(b, first), self.o.at[b], self.sd.at[zb], self.recv.at[b], to)

    def over_y(self, zb, first=False):
        b = self.at(zb, 0, self.f)
        to = (flip(self.s, 1), self.f)
        return remote(self.src(b, first), self.o.at[b], self.sy.at[zb], self.recv.at[b], to)

    def over_x(self, zb, yy, first=False):
        b = self.at(zb, yy, self.f)
        to = (self.s, self.fx)
        return remote(self.src(b, first), self.o.at[b], self.sx.at[zb, yy], self.recv.at[b], to)

    def over_core(self, zb, yy, xx, first=False):
        b = self.at(zb, yy, self.f if xx == 0 else self.fx)
        to = (self.s, self.fc)
        return remote(self.src(b, first), self.o.at[b], self.sc.at[zb, yy, xx], self.recv.at[b], to)

    def arrived(self, b):
        o = self.o.at[b]
        return remote(o, o, self.own, self.recv.at[b], (self.s, self.fc))

    def start(self):
        z = self.z

        @pl.when(z < 3)
        def _():
            self.up(z, True).start()

        @pl.when(z > 0)
        def _():
            self.down(z, True).start()

        self.over_y(z, True).start()
        self.over_x(z, 0, True).start()
        self.over_core(z, 0, 0, True).start()
        self.mine.start()

    def line(self, sign, t):
        zb = self.z + sign * t

        @pl.when((zb >= 0) & (zb <= 3))
        def _():
            self.arrived(self.at(zb, 0, self.f)).wait_recv()
            if sign < 0:

                @pl.when(self.z < 3)
                def _():
                    self.up(zb).start()

            else:

                @pl.when(self.z > 0)
                def _():
                    self.down(zb).start()

            self.over_y(zb).start()
            self.over_x(zb, 0).start()
            self.over_core(zb, 0, 0).start()

    def column(self, sign, t):
        zb = self.z + sign * t

        @pl.when((zb >= 0) & (zb <= 3))
        def _():
            self.arrived(self.at(zb, 1, self.f)).wait_recv()
            self.over_x(zb, 1).start()
            self.over_core(zb, 1, 0).start()

    def side(self, sign, t, yy):
        zb = self.z + sign * t

        @pl.when((zb >= 0) & (zb <= 3))
        def _():
            self.arrived(self.at(zb, yy, self.fx)).wait_recv()
            self.over_core(zb, yy, 1).start()

    def steps(self):
        p = functools.partial
        out = []
        for t in range(4):
            for sign in (-1, 1) if t else (1,):
                if t:
                    out.append(p(self.line, sign, t))
        for t in range(4):
            for sign in (-1, 1) if t else (1,):
                out.append(p(self.column, sign, t))
                out.append(p(self.side, sign, t, 0))
        for t in range(4):
            for sign in (-1, 1) if t else (1,):
                out.append(p(self.side, sign, t, 1))
        return out

    def finish(self):
        self.mine.wait()
        for zb in range(4):
            for yy in range(2):
                self.arrived(self.at(zb, yy, self.fc)).wait_recv()
                self.arrived(self.at(zb, yy, self.fd)).wait_recv()
        for zb in range(4):
            self.over_y(zb).wait_send()

            @pl.when((self.z < 3) & (zb <= self.z))
            def _():
                self.up(zb).wait_send()

            @pl.when((self.z > 0) & (zb >= self.z))
            def _():
                self.down(zb).wait_send()

            for yy in range(2):
                self.over_x(zb, yy).wait_send()
                for xx in range(2):
                    self.over_core(zb, yy, xx).wait_send()


class RowExchange:
    @staticmethod
    def scratch():
        return [DMA, DMA((8,)), DMA((8,))]

    def __init__(self, x, o, own, send, recv):
        self.x, self.o, self.send, self.recv = x, o, send, recv
        self.s, self.f, _, _ = where_am_i()
        self.mine = pltpu.make_async_copy(x.at[self.s], o.at[self.s], own)

    def piece(self, k):
        t = peer(self.s, k)
        dst = self.o.at[self.s]
        return remote(self.x.at[t], dst, self.send.at[k], self.recv.at[k], (t, self.f))

    def start(self):
        for k in reversed(range(1, 8)):
            self.piece(k).start()
        self.mine.start()

    def finish(self):
        self.mine.wait()
        for k in reversed(range(1, 8)):
            self.piece(k).wait_recv()
            self.piece(k).wait_send()


def idle():
    pass


def looped(plan, name, work, queues):
    count = plan.count(name)
    groups = plan.split(name)
    left = {k: list(v) for k, v in queues.items()}

    def between(now, group):
        items = [left[k].pop(0) for k in group]
        if items:

            @pl.when(now)
            def _():
                for item in items:
                    item()

    @pl.loop(0, count)
    def _(i):
        for n in range(count):
            between(i == n, groups[n])
        work(i)

    for k in groups[count]:
        left[k].pop(0)()
    return left


def fetch(refs, sems):
    copies = [pltpu.make_async_copy(a, b, sems.at[i]) for i, (a, b) in enumerate(refs)]
    for copy in copies:
        copy.start()
    return copies


def rotary_rows(pos, lengths_ref, freq):
    half = ROT // 2
    d = lax.broadcasted_iota(jnp.int32, (1, 128), 1) % HEAD_DIM
    rel = pos - starts_of(pos, lengths_ref, lengths_ref.shape[1])
    angle = rel.astype(jnp.float32) * freq
    c, s = jnp.cos(angle), jnp.sin(angle)
    second = (d >= half) & (d < ROT)
    return jnp.where(d < ROT, c, 1.0), jnp.where(d < half, -s, 0.0), jnp.where(second, s, 0.0)


def perform(plan, queues):
    left = {name: list(items) for name, items in queues.items()}
    for name in "".join(plan):
        left[name].pop(0)()
    assert not any(left.values())


FORWARD_PLAN = (
    "nFngnWggssswwVnsnswwssvswsvsnsnssvsvwsnvDwwwcwcc",
    "wcfvccvwvdvdcwwcwwvcwcwcccvcccwdwvwwwcwwcXvvvww",
)
MIDDLE_PLAN = (
    "gbggbbgbgbgbbb",
    "raaaraeateaeearea",
    "mertmeemm",
    "Mlltllhtthhlltlthhl",
    "LhhhHtz",
)
BACKWARD_PLAN = ("bFggrgbbXgbgbgrbfbrtZtb", "crotccoocotocootocqOcccptccccPttz")
LAST_PLAN = ("ataaeeathtaheatttehehetaa", "eehthhzhZ")


def dot(a, b, ca=1, cb=0):
    return lax.dot_general(a, b, (((ca,), (cb,)), ((), ())), preferred_element_type=jnp.float32)


def starts_of(pos, lengths_ref, nseg):
    start = jnp.zeros_like(pos)
    end = 0
    for i in range(nseg - 1):
        end = end + lengths_ref[0, i]
        start = jnp.where(pos >= end, end, start)
    return start


def head_lanes(h):
    lane = lax.broadcasted_iota(jnp.int32, (1, 128), 1)
    return (lane // HEAD_DIM) == h


def turn(x, c, s1, s2, sign):
    half = ROT // 2
    return x * c + (pltpu.roll(x, 128 - half, 1) * s1 + pltpu.roll(x, half, 1) * s2) * sign


def block_mask(qb, lengths_ref):
    keys = (qb + 1) * QB
    row = qb * QB + lax.broadcasted_iota(jnp.int32, (QB, 1), 0)
    col = lax.broadcasted_iota(jnp.int32, (1, keys), 1)
    return (col >= starts_of(row, lengths_ref, lengths_ref.shape[1])) & (col <= row)


def row_at(i, step=QB):
    return pl.ds(pl.multiple_of(i * step, step), step)


def picks(orow_ref, i):
    p = lax.broadcasted_iota(jnp.int32, (QB, 1), 0) + i * QB == orow_ref[...]
    return jnp.where(p, 1.0, 0.0).astype(jnp.bfloat16)


def puts(oc, valid):
    p = oc == lax.broadcasted_iota(jnp.int32, (1, valid), 1)
    return jnp.where(p, 1.0, 0.0).astype(jnp.bfloat16)


def attend(
    a_ref, w_ref, shift_of, tables, orow_ref, ocol_ref, len_ref, o_ref, pk_ref, lse_ref, rot, opk
):
    rows, w3 = rot.shape
    w = w3 // 3
    valid = pk_ref.shape[0]
    scale = HEAD_DIM**-0.5
    freq_ref = tables

    def project(lo, hi):
        shift = shift_of()

        @pl.loop(lo, hi)
        def _(i):
            r = row_at(i, 256)
            c, s1, s2 = rotary_rows(ocol_ref[r], len_ref, freq_ref[...])
            left = jnp.concatenate([a_ref[2 * i], a_ref[2 * i + 1]], 0)
            qkv = dot(left, w_ref[...]) + shift
            for t in range(w3 // 128):
                cols = slice(t * 128, t * 128 + 128)
                x = qkv[:, cols]
                if t < 2 * w // 128:
                    x = turn(x, c, s1, s2, 1.0)
                rot[r, cols] = x.astype(jnp.bfloat16)

    def pack(lo, hi):
        @pl.loop(lo, hi)
        def _(i):
            pk_ref[row_at(i)] = dot(picks(orow_ref, i), rot[...]).astype(jnp.bfloat16)

    def block(qb, t):
        keys = (qb + 1) * QB
        rq = slice(qb * QB, qb * QB + QB)
        ct = slice(t * 128, t * 128 + 128)
        mask = block_mask(qb, len_ref)
        q = pk_ref[rq, ct]
        k = pk_ref[0:keys, w + t * 128 : w + t * 128 + 128]
        v = pk_ref[0:keys, 2 * w + t * 128 : 2 * w + t * 128 + 128]
        total = None
        for h in range(2):
            qh = jnp.where(head_lanes(h), q, jnp.zeros_like(q))
            scores = jnp.where(mask, dot(qh, k, 1, 1) * scale, NEG)
            top = jnp.max(scores, -1, keepdims=True)
            expo = jnp.exp(scores - top)
            norm = jnp.sum(expo, -1, keepdims=True)
            probs = (expo / norm).astype(jnp.bfloat16)
            lse_ref[2 * t + h, rq] = top + jnp.log(norm)
            out = dot(probs, v)
            total = out if h == 0 else jnp.where(head_lanes(1), out, total)
        opk[rq, ct] = total.astype(jnp.bfloat16)

    def unpack(lo, hi):
        per = o_ref.shape[1]

        @pl.loop(lo, hi)
        def _(i):
            r = row_at(i, per)
            oc = ocol_ref[r]
            back = dot(puts(oc, valid), opk[...])
            pad = rot[r, 2 * w :].astype(jnp.float32)
            o_ref[i] = jnp.where(oc >= valid, pad, back).astype(jnp.bfloat16)

    blocks = [
        functools.partial(block, qb, t) for qb in range(valid // QB) for t in range(w // 128)
    ]
    p = functools.partial
    steps, half, blks = rows // 256, valid // QB // 2, rows // o_ref.shape[1]
    head = [p(project, 0, steps // 2), p(project, steps // 2, steps)]
    head += [p(pack, 0, half), p(pack, half, valid // QB)]
    return head + blocks + [p(unpack, 0, blks // 2), p(unpack, blks // 2, blks)]


def attend_back(
    pk_ref, do_ref, lse_ref, tables, orow_ref, ocol_ref, len_ref, g_ref, b_ref, dpk, dq, dk, dv, gpk
):
    rows, w = do_ref.shape
    valid = pk_ref.shape[0]
    scale = HEAD_DIM**-0.5
    freq_ref = tables

    def pack():
        @pl.loop(0, valid // QB)
        def _(i):
            r = row_at(i)
            dpk[r] = dot(picks(orow_ref, i), do_ref[...]).astype(jnp.bfloat16)
            dk[r] = jnp.zeros((QB, w), jnp.float32)
            dv[r] = jnp.zeros((QB, w), jnp.float32)

    def block(qb, t):
        keys = (qb + 1) * QB
        rq = slice(qb * QB, qb * QB + QB)
        ct = slice(t * 128, t * 128 + 128)
        mask = block_mask(qb, len_ref)
        q, d = pk_ref[rq, ct], dpk[rq, ct]
        k = pk_ref[0:keys, w + t * 128 : w + t * 128 + 128]
        v = pk_ref[0:keys, 2 * w + t * 128 : 2 * w + t * 128 + 128]
        total = None
        for h in range(2):
            hl = head_lanes(h)
            qh = jnp.where(hl, q, jnp.zeros_like(q))
            dh = jnp.where(hl, d, jnp.zeros_like(d))
            scores = jnp.where(mask, dot(qh, k, 1, 1) * scale, NEG)
            p = jnp.exp(scores - lse_ref[2 * t + h, rq])
            dp = dot(dh, v, 1, 1)
            inner = jnp.sum(p * dp, -1, keepdims=True)
            ds = (p * (dp - inner)).astype(jnp.bfloat16)
            dv[0:keys, ct] += dot(p.astype(jnp.bfloat16), dh, 0, 0)
            dk[0:keys, ct] += dot(ds, qh, 0, 0)
            part = dot(ds, k)
            total = part if h == 0 else jnp.where(head_lanes(1), part, total)
        dq[rq, ct] = total

    def rotary():
        @pl.loop(0, valid // QB)
        def _(i):
            r = row_at(i)
            pos = lax.broadcasted_iota(jnp.int32, (QB, 1), 0) + i * QB
            c, s1, s2 = rotary_rows(pos, len_ref, freq_ref[...])
            for t in range(w // 128):
                ct = slice(t * 128, t * 128 + 128)
                for j, src in ((0, dq), (1, dk)):
                    x = (src[r, ct] * scale).astype(jnp.bfloat16).astype(jnp.float32)
                    at = j * w + t * 128
                    gpk[r, at : at + 128] = turn(x, c, s1, s2, -1.0).astype(jnp.bfloat16)
                at = 2 * w + t * 128
                gpk[r, at : at + 128] = dv[r, ct].astype(jnp.bfloat16)

    def unpack():
        b_ref[...] = jnp.zeros_like(b_ref)

        @pl.loop(0, rows // QB)
        def _(i):
            r = row_at(i)
            oc = ocol_ref[r]
            back = dot(puts(oc, valid), gpk[...])
            pad = jnp.where(oc >= valid, do_ref[r].astype(jnp.float32), 0.0)
            back = jnp.concatenate([back[:, : 2 * w], back[:, 2 * w :] + pad], 1)
            g_ref[r] = back.astype(jnp.bfloat16)
            b_ref[...] += jnp.sum(back, 0, keepdims=True)

    blocks = [
        functools.partial(block, qb, t) for qb in range(valid // QB) for t in range(w // 128)
    ]
    return [pack] + blocks + [rotary, unpack]


def forward_kernel(
    x_hbm,
    p_ref,
    qkv_ref,
    op_hbm,
    dm_hbm,
    gate_hbm,
    up_hbm,
    dp_hbm,
    freq_ref,
    orow_ref,
    ocol_ref,
    len_ref,
    a_ref,
    qw_ref,
    n_ref,
    ow_ref,
    ho_ref,
    pk_ref,
    lse_ref,
    dmo_ref,
    ww_ref,
    dw_ref,
    mix_ref,
    x_ref,
    op_ref,
    dm_ref,
    gate_ref,
    up_ref,
    dp_ref,
    xs,
    got,
    rot,
    opk,
    qp_ref,
    wp_ref,
    load,
    psend,
    precv,
    *sems,
):
    s, f, z, y = where_am_i()
    me = s * 4 + f
    w = rot.shape[1] // 3
    lf = wp_ref.shape[2] // 2

    def piece_of(i):
        t, n = i // 3, i % 3
        at = n * x_ref.shape[1] + t * w
        return qkv_ref.at[:, at : at + w], qp_ref.at[t, :, n * w : n * w + w]

    operands = [(x_hbm, x_ref)] + [piece_of(i) for i in range(24)]
    operands += [(op_hbm, op_ref), (dm_hbm, dm_ref), (dp_hbm, dp_ref)]
    operands += [(gate_hbm, gate_ref), (up_hbm, up_ref)]
    loads = fetch(operands, load)
    greet_all(s, f)
    gather = SeqGather(x_ref, xs, *sems[:5])
    slices = ColGather(qp_ref, qw_ref, *sems[5:10])
    whole = WholeGather(op_ref, ow_ref, *sems[10:17])
    grads = SeqGather(dm_ref, dmo_ref, *sems[17:22])
    wide = ColGather(wp_ref, ww_ref, *sems[22:27])
    down = FsdpGather(dp_ref, dw_ref, *sems[27:30])
    swap = RowExchange(mix_ref, ho_ref, *sems[30:])

    def param(k):
        i = (me + k) % 32
        return remote(p_ref, got.at[me], psend.at[k], precv.at[k], dealer(i))

    @pl.loop(1, 32)
    def _(k):
        param(k).start()

    loads[0].wait()
    gather.start()
    for copy in loads[1:]:
        copy.wait()
    slices.start()
    got[me] = p_ref[...]

    @pl.loop(1, 32)
    def _(k):
        param(k).wait_recv()

    for i in range(16):
        n_ref[:, i * 128 : i * 128 + 128] = got[2 * i] + got[2 * i + 1]
    step = 16

    def norm(b):
        gain, shift = n_ref[0:1], n_ref[1:2]

        @pl.loop(0, x_ref.shape[0] // step)
        def _(i):
            r = row_at(i, step)
            normed, _ = normalize(xs[b, r].astype(jnp.float32))
            a_ref[b, r] = (normed * gain + shift).astype(jnp.bfloat16)

    def shift_of():
        parts = []
        for n in range(3):
            part = jnp.zeros((1, w), jnp.float32)
            for i in range(8):
                piece = n_ref[4 + n : 5 + n, i * w : i * w + w]
                part = part + jnp.where(s == i, piece, jnp.zeros_like(piece))
            parts.append(part)
        return jnp.concatenate(parts, 1)

    work = attend(
        a_ref,
        qw_ref,
        shift_of,
        freq_ref,
        orow_ref,
        ocol_ref,
        len_ref,
        mix_ref,
        pk_ref,
        lse_ref,
        rot,
        opk,
    )
    p = functools.partial

    def own():
        gather.own.wait()
        norm(s)

    def wide_start():
        for i in range(8):
            at = slice(i * lf, i * lf + lf)
            wp_ref[i, :, 0:lf] = gate_ref[:, at]
            wp_ref[i, :, lf : 2 * lf] = up_ref[:, at]
        wide.start()

    norms = [own]
    for i in range(4):
        norms.append(lambda i=i: norm(gather.cross(i)))
        if i < 3:
            norms.append(lambda i=i: norm(2 * gather.near(i + 1) + y))
    work = [slices.complete, work[0], idle, work[1], idle] + work[2:]
    queues = dict(
        g=gather.steps(),
        n=norms,
        s=slices.steps(),
        d=grads.steps(),
        v=wide.steps(),
        w=whole.steps(),
        f=[down.step],
        c=work,
        D=[grads.start],
        V=[wide_start],
        W=[whole.start],
        F=[down.start],
        X=[swap.start],
    )
    work[0:2] = [lambda first=work[0], then=work[1]: (first(), then())]
    perform(FORWARD_PLAN, queues)
    for i in range(4):
        grads.cross(i)
    swap.finish()
    wide.complete()
    for task in (slices, wide, whole, down, grads):
        task.finish()
    gather.finish(False)

    @pl.loop(1, 32)
    def _(k):
        param(k).wait_send()


def forward(
    x, params, qkv, out_p, dm, gate, up, down_p, freq, orow, ocol, lengths, valid, collective
):
    rows, width = x.shape
    w3 = qkv.shape[1] // 8
    part, wide = gate.shape[0], gate.shape[1] // 4
    w = w3 // 3
    group = 8 * rows
    heads = w // HEAD_DIM

    def out(shape, dtype=jnp.bfloat16):
        return jax.ShapeDtypeStruct(shape, dtype)

    return pl.pallas_call(
        forward_kernel,
        out_shape=(
            out((8, rows, width)),
            out((width, w3)),
            out((8, width), jnp.float32),
            out((32,) + out_p.shape),
            out((8, rows, w)),
            out((valid, w3)),
            out((heads, valid, 1), jnp.float32),
            out((8, rows, width)),
            out((width, wide)),
            out((4,) + down_p.shape),
            out((8, rows, w)),
        ),
        in_specs=[HBM_SPEC, VMEM_SPEC] + [HBM_SPEC] * 6 + [VMEM_SPEC] * 3 + [SMEM_SPEC],
        out_specs=(VMEM_SPEC,) * 3
        + (ANY_SPEC,)
        + (VMEM_SPEC,) * 3
        + (ANY_SPEC,) * 3
        + (VMEM_SPEC,),
        scratch_shapes=[pltpu.VMEM(v.shape, v.dtype) for v in (x, out_p, dm, gate, up, down_p)]
        + [
            pltpu.VMEM((8, rows, width), jnp.bfloat16),
            pltpu.VMEM((32, 8, 128), jnp.float32),
            pltpu.VMEM((group, w3), jnp.bfloat16),
            pltpu.VMEM((valid, w), jnp.bfloat16),
            pltpu.VMEM((8, part, w3), jnp.bfloat16),
            pltpu.VMEM((8, part, wide), jnp.bfloat16),
            DMA((30,)),
            DMA((32,)),
            DMA((32,)),
        ]
        + SeqGather.scratch()
        + ColGather.scratch()
        + WholeGather.scratch()
        + SeqGather.scratch()
        + ColGather.scratch()
        + FsdpGather.scratch()
        + RowExchange.scratch(),
        compiler_params=comm_params(collective),
    )(x, params, qkv, out_p, dm, gate, up, down_p, freq, orow, ocol, lengths)


def tall(rows, step=16):
    def wrap(fn):
        @pl.loop(0, rows // step)
        def _(i):
            fn(row_at(i, step))

    return wrap


def middle_kernel(
    ho_hbm,
    ow_ref,
    x_hbm,
    n_ref,
    ww_hbm,
    dw_hbm,
    dm_hbm,
    attn_hbm,
    res_hbm,
    rg_ref,
    vec_ref,
    mp_hbm,
    dg_hbm,
    h_hbm,
    ho_ref,
    x_ref,
    ww_ref,
    dw_ref,
    dm_ref,
    attn_ref,
    res_ref,
    mp_ref,
    dg_ref,
    h_ref,
    big,
    cloc,
    c_ref,
    hid,
    act,
    part,
    second,
    load,
    store,
    *scratch,
):
    s, f, z, y = where_am_i()
    rows, width = x_ref.shape
    lf = dw_ref.shape[0]
    lw = ho_ref.shape[2]
    first = [(ho_hbm, ho_ref), (x_hbm, x_ref), (ow_ref, big)]
    loads = fetch(first + [(ww_hbm, ww_ref), (dw_hbm, dw_ref), (dm_hbm, dm_ref)], load)
    greet_columns(s, f)
    gather = SeqGather(cloc, c_ref, *scratch[:5])
    reduce = SeqReduce(part, second, *scratch[5:11])
    sums = ColSum(big, h_ref, *scratch[11:])
    gain, shift = n_ref[2:3], n_ref[3:4]
    for copy in loads[:3]:
        copy.wait()

    @pl.loop(0, width // 512)
    def _(j):
        cols = pl.ds(pl.multiple_of(j * 512, 512), 512)
        total = dot(ho_ref[0], big[0:lw, cols])
        for k in range(1, 8):
            total = total + dot(ho_ref[k], big[k * lw : k * lw + lw, cols])
        attn_ref[:, cols] = total
        res_ref[:, cols] = x_ref[:, cols].astype(jnp.float32) + total

    @tall(rows)
    def _(r):
        normed, _ = normalize(res_ref[r])
        cloc[r] = (normed * gain + shift).astype(jnp.bfloat16)

    gather.start()
    stores = fetch([(attn_ref, attn_hbm), (res_ref, res_hbm)], store)
    gather.own.wait()
    for copy in loads[3:]:
        copy.wait()

    def block(b):
        at = pl.ds(pl.multiple_of(b * rows, rows), rows)
        wide = dot(c_ref[b], ww_ref[...])
        gate, upper = wide[:, :lf], wide[:, lf:]
        hidden, sigma = mlp_forward(gate, upper)
        hid[at] = hidden
        grad = dot(dm_ref[b], dw_ref[...], 1, 1)
        gate_act, up_act = mlp_backward(grad, gate, upper, sigma)
        act[at] = jnp.concatenate([gate_act, up_act], 1)
        part[b] = dot(act[at], ww_ref[...], 1, 1).astype(jnp.bfloat16)

    def wide_grad(i):
        at = row_at(i, 256)
        left = jnp.concatenate([c_ref[b, :, at] for b in range(8)], 0)
        big[at, 0 : 2 * lf] = dot(left, act[...], 0, 0).astype(jnp.bfloat16)
        sums.send(i)

    def mlp_part(i):
        for k in range(2):
            b = 2 * i + k
            at = pl.ds(pl.multiple_of(b * rows, rows), rows)
            mp_ref[b] = dot(hid[at], dw_ref[...]).astype(jnp.bfloat16)

    def down_grad(i):
        cols = row_at(i, 256)
        right = jnp.concatenate([dm_ref[b, :, cols] for b in range(8)], 0)
        dg_ref[:, cols] = dot(hid[...], right, 0, 0).astype(jnp.bfloat16)

    def norm_backward():
        vec_ref[...] = jnp.zeros_like(vec_ref)

        @tall(rows)
        def _(r):
            grad = second[r]
            normed, rstd = normalize(res_ref[r])
            inner, gain_part, shift_part = norm_back(grad, normed, rstd, gain)
            rg_ref[r] = dm_ref[s, r].astype(jnp.float32) + inner
            vec_ref[0:1] += gain_part[None]
            vec_ref[1:2] += shift_part[None]

    p = functools.partial
    each = range(8)
    out_copies = [
        pltpu.make_async_copy(mp_ref, mp_hbm, store.at[2]),
        pltpu.make_async_copy(dg_ref, dg_hbm, store.at[3]),
        pltpu.make_async_copy(h_ref, h_hbm, store.at[4]),
    ]
    left = dict(
        g=gather.steps(),
        r=[p(reduce.send, k) for k in range(4)],
        t=reduce.steps(),
        e=[p(sums.step, i) for i in each],
        h=[p(sums.total, i) for i in each],
        z=[norm_backward],
        M=[out_copies[0].start],
        L=[out_copies[1].start],
        H=[out_copies[2].start],
    )
    left = looped(MIDDLE_PLAN[0], "b", lambda j: block(gather.turn(j)), left)
    left = looped(MIDDLE_PLAN[1], "a", wide_grad, left)
    left = looped(MIDDLE_PLAN[2], "m", mlp_part, left)
    left = looped(MIDDLE_PLAN[3], "l", down_grad, left)
    perform(MIDDLE_PLAN[4], left)
    for copy in stores + out_copies:
        copy.wait()
    gather.finish(False)
    reduce.finish()
    sums.finish()


def middle(heads_out, out_w, x, norms, wide_w, down_w, dm, collective):
    rows, width = x.shape
    lf = down_w.shape[0]
    group = 8 * rows
    part = width // 32

    def out(shape, dtype=jnp.bfloat16):
        return jax.ShapeDtypeStruct(shape, dtype)

    def vm(shape, dtype=jnp.bfloat16):
        return pltpu.VMEM(shape, dtype)

    wide = (rows, width)
    return pl.pallas_call(
        middle_kernel,
        out_shape=(
            out(wide, jnp.float32),
            out(wide, jnp.float32),
            out(wide, jnp.float32),
            out((8, width), jnp.float32),
            out((8,) + wide),
            out((lf, width)),
            out((8, part, 2 * lf)),
        ),
        in_specs=[HBM_SPEC] * 3 + [VMEM_SPEC] + [HBM_SPEC] * 3,
        out_specs=(ANY_SPEC,) * 2 + (VMEM_SPEC,) * 2 + (ANY_SPEC,) * 3,
        scratch_shapes=[
            vm(heads_out.shape),
            vm(wide),
            vm(wide_w.shape),
            vm(down_w.shape),
            vm(dm.shape),
            vm(wide, jnp.float32),
            vm(wide, jnp.float32),
            vm((8,) + wide),
            vm((lf, width)),
            vm((8, part, 2 * lf)),
            vm((width, width)),
            vm(wide),
            vm((8,) + wide),
            vm((group, lf)),
            vm((group, 2 * lf)),
            vm((8,) + wide),
            vm(wide, jnp.float32),
            DMA((6,)),
            DMA((5,)),
        ]
        + SeqGather.scratch(2)
        + SeqReduce.scratch(rows, width)
        + ColSum.scratch(part, 2 * lf),
        compiler_params=comm_params(collective),
    )(heads_out, out_w, x, norms, wide_w, down_w, dm)


def backward_kernel(
    rg_ref,
    freq_ref,
    orow_ref,
    ocol_ref,
    len_ref,
    ow_hbm,
    mix_hbm,
    pk_hbm,
    lse_hbm,
    attn_hbm,
    res_hbm,
    mp_hbm,
    dg_hbm,
    h_hbm,
    g_ref,
    b_ref,
    lo_ref,
    sum_ref,
    got,
    down_hbm,
    out_ref,
    or_ref,
    mix_ref,
    pk_ref,
    lse_ref,
    attn_ref,
    res_ref,
    mp_ref,
    dg_ref,
    h_ref,
    down_ref,
    da,
    full,
    do_ref,
    og,
    mlp,
    dpk,
    dq,
    dk,
    dv,
    gpk,
    load,
    store,
    *scratch,
):
    s, f, z, y = where_am_i()
    rows, width = rg_ref.shape
    part = out_ref.shape[0]
    valid = pk_ref.shape[0]
    loads = fetch(
        [
            (ow_hbm.at[pl.ds(pl.multiple_of(s * 4, 4), 4)], or_ref),
            (dg_hbm, dg_ref),
            (mp_hbm, mp_ref),
            (h_hbm, h_ref),
            (pk_hbm, pk_ref),
            (lse_hbm, lse_ref),
            (mix_hbm, mix_ref),
            (attn_hbm, attn_ref),
            (res_hbm, res_ref),
        ],
        load,
    )
    greet_columns(s, f)
    gather = SeqGather(da, full, *scratch[:5])
    reduce = SeqReduce(mp_ref, mlp, *scratch[5:11])
    swap = RowExchange(h_ref, got, *scratch[11:14])
    down = FsdpReduce(dg_ref, down_ref, *scratch[14:18])
    outer_sum = FsdpReduce(og, out_ref, *scratch[18:])

    @tall(rows)
    def _(r):
        da[r] = rg_ref[r].astype(jnp.bfloat16)

    gather.start()
    gather.own.wait()
    loads[0].wait()

    def block(b):
        at = pl.ds(pl.multiple_of(b * rows, rows), rows)
        out_rows = jnp.concatenate([or_ref[k] for k in range(4)], 0)
        do_ref[at] = dot(full[b], out_rows, 1, 1).astype(jnp.bfloat16)

    def before(copies, then):
        def run():
            for copy in copies:
                copy.wait()
            then()

        return run

    out_copies = [pltpu.make_async_copy(down_ref, down_hbm, store)]

    def down_total():
        down.total()
        out_copies[0].start()

    def out_grad(i):
        cols = slice(i * 256, i * 256 + 256)
        right = jnp.concatenate([full[b, :, cols] for b in range(8)], 0)
        value = dot(mix_ref[...], right, 0, 0).astype(jnp.bfloat16)
        for k in range(4):
            og[k, :, cols] = value[k * part : k * part + part]

    p = functools.partial
    work = attend_back(
        pk_ref,
        do_ref,
        lse_ref,
        freq_ref,
        orow_ref,
        ocol_ref,
        len_ref,
        g_ref,
        b_ref,
        dpk,
        dq,
        dk,
        dv,
        gpk,
    )
    def results():
        sum_ref[...] = jnp.zeros_like(sum_ref)

        step = 16

        @pl.loop(0, rows // step)
        def _(i):
            r = row_at(i, step)
            m = mlp[r]
            result = res_ref[r] + m
            lo_ref[r] = result.astype(jnp.bfloat16)
            pos = ocol_ref[pl.ds(pl.multiple_of(s * rows + i * step, step), step)]
            keep = jnp.where(pos < valid, 1.0, 0.0)
            for n, v in enumerate((result, attn_ref[r], m)):
                total = jnp.sum(jnp.sum(v * v, -1, keepdims=True) * keep, 0, keepdims=True)
                sum_ref[n : n + 1] += jnp.broadcast_to(total, (1, 128))

    sends = [p(reduce.send, k) for k in range(4)]
    outs = [p(out_grad, i) for i in range(8)]
    queues = dict(
        F=[before(loads[1:2], down.start)],
        f=[down.step],
        q=[down_total],
        g=gather.steps(),
        r=[before(loads[2:3], sends[0])] + sends[1:],
        t=reduce.steps(),
        X=[before(loads[3:4], swap.start)],
        Z=[swap.finish],
        c=[before(loads[4:6], work[0])] + work[1:],
        o=[before(loads[6:7], outs[0])] + outs[1:],
        O=[outer_sum.start],
        p=[outer_sum.step],
        P=[outer_sum.total],
        z=[before(loads[7:9], results)],
    )
    left = looped(BACKWARD_PLAN[0], "b", lambda j: block(gather.turn(j)), queues)
    perform(BACKWARD_PLAN[1], left)
    gather.finish(False)
    reduce.finish()
    down.finish()
    outer_sum.finish()
    for copy in out_copies:
        copy.wait()


def backward(
    rg, freq, orow, ocol, lengths, out_w, mixed, pk, lse, attn, res, mp, dg, h, collective
):
    rows, width = rg.shape
    group, w = mixed.shape
    valid = pk.shape[0]
    part = h.shape[1]

    def out(shape, dtype=jnp.float32):
        return jax.ShapeDtypeStruct(shape, dtype)

    def vm(shape, dtype=jnp.bfloat16):
        return pltpu.VMEM(shape, dtype)

    return pl.pallas_call(
        backward_kernel,
        out_shape=(
            out((group, 3 * w), jnp.bfloat16),
            out((1, 3 * w)),
            out((rows, width), jnp.bfloat16),
            out((8, 128)),
            out(h.shape, jnp.bfloat16),
            out(dg.shape[1:]),
            out((part, width)),
        ),
        in_specs=[VMEM_SPEC] * 4 + [SMEM_SPEC] + [HBM_SPEC] * 9,
        out_specs=(VMEM_SPEC,) * 4 + (ANY_SPEC,) * 2 + (VMEM_SPEC,),
        scratch_shapes=[
            vm((4, part, width)),
            vm(mixed.shape),
            vm(pk.shape),
            vm(lse.shape, jnp.float32),
            vm(attn.shape, jnp.float32),
            vm(res.shape, jnp.float32),
            vm(mp.shape),
            vm(dg.shape),
            vm(h.shape),
            vm(dg.shape[1:], jnp.float32),
            vm((rows, width)),
            vm((8, rows, width)),
            vm((group, w)),
            vm((4, part, width)),
            vm((rows, width), jnp.float32),
            vm((valid, w)),
            vm((valid, w), jnp.float32),
            vm((valid, w), jnp.float32),
            vm((valid, w), jnp.float32),
            vm((valid, 3 * w)),
            DMA((9,)),
            DMA,
        ]
        + SeqGather.scratch(2)
        + SeqReduce.scratch(rows, width)
        + RowExchange.scratch()
        + FsdpReduce.scratch(*dg.shape[1:])
        + FsdpReduce.scratch(part, width),
        compiler_params=comm_params(collective),
    )(rg, freq, orow, ocol, lengths, out_w, mixed, pk, lse, attn, res, mp, dg, h)


def last_kernel(
    g_ref,
    b_ref,
    n_ref,
    vec_ref,
    sum_ref,
    qw_hbm,
    a_hbm,
    x_hbm,
    rg_hbm,
    ig_ref,
    got,
    total_ref,
    qw_ref,
    a_ref,
    x_ref,
    rg_ref,
    load,
    part,
    first,
    grad,
    h,
    msg,
    inbox,
    vec,
    msend,
    mrecv,
    *scratch,
):
    s, f, z, y = where_am_i()
    me = s * 4 + f
    rows, width = x_ref.shape
    w3 = g_ref.shape[1]
    w = w3 // 3
    loads = fetch([(qw_hbm, qw_ref), (a_hbm, a_ref), (x_hbm, x_ref), (rg_hbm, rg_ref)], load)
    greet_all(s, f)
    loads[0].wait()
    reduce = SeqReduce(part, first, *scratch[:6])
    sums = ColSum(grad, h, *scratch[6:12])
    swap = RowExchange(h, got, *scratch[12:])

    def block(b):
        at = pl.ds(pl.multiple_of(b * rows, rows), rows)
        part[b] = dot(g_ref[at], qw_ref[...], 1, 1).astype(jnp.bfloat16)

    def block_at(j):
        far = j < 4
        zb = reduce.order(j % 4)
        block(2 * zb + jnp.where(far, 1 - y, y))

        @pl.when(far)
        def _():
            reduce.send(j)

    def qkv_grad(n):
        i = peer_at(s, 7 - n)
        at = row_at(i, 256)
        left = jnp.concatenate([a_ref[b, :, at] for b in range(8)], 0)
        grad[at] = dot(left, g_ref[...], 0, 0).astype(jnp.bfloat16)
        sums.send(i)

    def hand_over(k):
        sums.total(peer(s, k))
        if k:
            swap.piece(k).start()
        else:
            swap.mine.start()

    def message(k):
        i = (me + k) % 32
        return remote(msg.at[i // 2], inbox.at[k], msend.at[k], mrecv.at[k], dealer(i))

    def norm_backward():
        vec[0:2] = jnp.zeros((2, width), jnp.float32)
        vec[2:4] = vec_ref[0:2]
        gain = n_ref[0:1]
        loads[2].wait()
        loads[3].wait()

        @tall(rows)
        def _(r):
            normed, rstd = normalize(x_ref[r].astype(jnp.float32))
            inner, gain_part, shift_part = norm_back(first[r], normed, rstd, gain)
            ig_ref[r] = rg_ref[r] + inner
            vec[0:1] += gain_part[None]
            vec[1:2] += shift_part[None]

        lane = lax.broadcasted_iota(jnp.int32, (1, 128), 1)
        scalars = jnp.where(lane == 0, sum_ref[0:1], jnp.where(lane == 1, sum_ref[1:2], sum_ref[2:3]))
        for i in range(16):
            cols = slice(i * 128, i * 128 + 128)
            msg[i, 0:4] = vec[0:4, cols]
            msg[i, 4:5] = scalars
            at = (i % 2) * 128
            for n in range(3):
                piece = b_ref[0:1, n * w + at : n * w + at + 128]
                msg[i, 5 + n : 6 + n] = jnp.where(s == i // 2, piece, jnp.zeros_like(piece))

        @pl.loop(1, 32)
        def _(k):
            message(k).start()

    p = functools.partial
    ks = [7, 6, 5, 4, 3, 2, 1, 0]
    queues = dict(
        t=reduce.steps(),
        e=[lambda k=k: sums.step(peer(s, k)) for k in ks],
        h=[p(hand_over, k) for k in ks],
        z=[norm_backward],
        Z=[swap.finish],
    )
    pl.loop(0, 8)(block_at)
    loads[1].wait()
    left = looped(LAST_PLAN[0], "a", qkv_grad, queues)
    perform(LAST_PLAN[1], left)
    reduce.finish()
    sums.finish()
    total_ref[...] = msg[me // 2]

    @pl.loop(1, 32)
    def _(k):
        message(k).wait_recv()
        total_ref[...] += inbox[k]

    @pl.loop(1, 32)
    def _(k):
        message(k).wait_send()


def last(g, b, qkv_w, a, x, rg, norms, vec, sums, collective):
    rows, width = x.shape
    w3 = g.shape[1]
    pr = width // 32

    def out(shape, dtype=jnp.float32):
        return jax.ShapeDtypeStruct(shape, dtype)

    def vm(shape, dtype=jnp.bfloat16):
        return pltpu.VMEM(shape, dtype)

    return pl.pallas_call(
        last_kernel,
        out_shape=(out((rows, width)), out((8, pr, w3), jnp.bfloat16), out((8, 128))),
        in_specs=[VMEM_SPEC] * 5 + [HBM_SPEC] * 4,
        out_specs=(VMEM_SPEC, ANY_SPEC, VMEM_SPEC),
        scratch_shapes=[
            vm(qkv_w.shape),
            vm(a.shape),
            vm(x.shape),
            vm(rg.shape, jnp.float32),
            DMA((4,)),
            vm((8, rows, width)),
            vm((rows, width), jnp.float32),
            vm((width, w3)),
            vm((8, pr, w3)),
            vm((16, 8, 128), jnp.float32),
            vm((32, 8, 128), jnp.float32),
            vm((4, width), jnp.float32),
            DMA((32,)),
            DMA((32,)),
        ]
        + SeqReduce.scratch(rows, width)
        + ColSum.scratch(pr, w3)
        + RowExchange.scratch(),
        compiler_params=comm_params(collective),
    )(g, b, norms, vec, sums, qkv_w, a, x, rg)


def results_kernel(*refs):
    same, pieces, outs = refs[:4], refs[4:6], refs[6:13]
    bufs, wide, qkv, spread, load, store = refs[13:17], refs[17], refs[18], refs[19:22], refs[22], refs[23]
    moves = list(zip(same, bufs)) + [(pieces[0], wide), (pieces[1], qkv)]
    loads = fetch(moves, load)
    stores = [pltpu.make_async_copy(bufs[i], outs[i], store.at[i]) for i in range(4)]
    stores += [pltpu.make_async_copy(spread[i], outs[4 + i], store.at[4 + i]) for i in range(3)]
    for i in range(4):
        loads[i].wait()
        stores[i].start()
    loads[4].wait()
    lf = wide.shape[2] // 2
    for n in range(2):
        for i in range(8):
            value = wide[i, :, n * lf : n * lf + lf]
            spread[n][:, i * lf : i * lf + lf] = value.astype(jnp.float32)
        stores[4 + n].start()
    loads[5].wait()
    w = qkv.shape[2] // 3
    for i in range(8):
        for n in range(3):
            at = (n * 8 + i) * w
            spread[2][:, at : at + w] = qkv[i, :, n * w : n * w + w].astype(jnp.float32)
    stores[6].start()
    for copy in stores:
        copy.wait()


def results(same, wide, qkv):
    part = wide.shape[1]
    spread = [(part, 4 * wide.shape[2])] * 2 + [(part, 8 * qkv.shape[2])]
    return pl.pallas_call(
        results_kernel,
        out_shape=[jax.ShapeDtypeStruct(v.shape, v.dtype) for v in same]
        + [jax.ShapeDtypeStruct(v, jnp.float32) for v in spread],
        in_specs=[HBM_SPEC] * 6,
        out_specs=[ANY_SPEC] * 7,
        scratch_shapes=[pltpu.VMEM(v.shape, v.dtype) for v in (*same, wide, qkv)]
        + [pltpu.VMEM(v, jnp.float32) for v in spread]
        + [DMA((6,)), DMA((7,))],
        compiler_params=pltpu.CompilerParams(vmem_limit_bytes=63 << 20),
    )(*same, wide, qkv)


def line_body(
    hidden_in,
    ln1_gain,
    ln1_bias,
    qkv_weight,
    qkv_bias,
    out_weight,
    ln2_gain,
    ln2_bias,
    gate_weight,
    up_weight,
    down_weight,
    seq_lengths,
    deal_order,
    out_grad,
):
    rows = hidden_in.shape[1]
    width = hidden_in.shape[2]
    nseq = lax.axis_size("seq")
    nfsdp = lax.axis_size("fsdp")
    lw = width // nseq
    part = qkv_weight.shape[0]
    ff = gate_weight.shape[1]
    lf = ff // nseq
    seq_at, fsdp_at = lax.axis_index("seq"), lax.axis_index("fsdp")
    order = deal_order[0]
    group_rows = order.shape[0]
    valid_rows = group_rows * 5 // 8
    orow, ocol = order[None, :], order[:, None]
    lane = jnp.arange(128, dtype=jnp.int32) % HEAD_DIM % (ROT // 2)
    freq = 10000.0 ** (-2.0 * lane.astype(jnp.float32) / ROT)
    freq = freq[None, :]
    params = jnp.stack([ln1_gain, ln1_bias, ln2_gain, ln2_bias, *qkv_bias])
    params = jnp.pad(params.astype(jnp.float32), ((0, 1), (0, 64)))
    params = jnp.where(fsdp_at % 2 == 0, params, jnp.roll(params, part, 1))
    first_in, qkv_w, norms, out_w, heads_out, packed, lse, mlp_grad, wide_w, down_w, mixed = forward(
        hidden_in[0],
        params,
        qkv_weight,
        out_weight,
        out_grad[0],
        gate_weight,
        up_weight,
        down_weight,
        freq,
        orow,
        ocol,
        seq_lengths,
        valid_rows,
        1,
    )
    attn, resid, resid_grad, norm2_grads, mlp_part, down_part, wide_sum = middle(
        heads_out,
        out_w.reshape(width, width),
        hidden_in[0],
        norms,
        wide_w,
        down_w.reshape(lf, width),
        mlp_grad,
        3,
    )
    qkv_act, bias_sums, result, sums, wide_pieces, down_grad, out_grad_w = backward(
        resid_grad,
        freq,
        orow,
        ocol,
        seq_lengths,
        out_w,
        mixed.reshape(group_rows, lw),
        packed,
        lse,
        attn,
        resid,
        mlp_part,
        down_part.reshape(nfsdp, -1, width),
        wide_sum,
        4,
    )
    input_grad, qkv_pieces, total = last(
        qkv_act, bias_sums, qkv_w, first_in, hidden_in[0], resid_grad, norms, norm2_grads, sums, 5
    )
    result, input_grad, down_grad, out_grad_w, gate_grad, up_grad, qkv_grad = results(
        (result, input_grad, down_grad, out_grad_w), wide_pieces, qkv_pieces
    )
    count = valid_rows * nfsdp * width
    rms = jnp.sqrt(total[4, :3] / count)
    halves = lax.dynamic_slice_in_dim(total, (fsdp_at % 2) * part, part, 1)
    shards = halves[:4]
    qkv_bias_grad = halves[5:8]
    return (
        result[None],
        input_grad[None],
        shards[0],
        shards[1],
        qkv_grad,
        qkv_bias_grad,
        out_grad_w,
        shards[2],
        shards[3],
        gate_grad,
        up_grad,
        down_grad,
        rms,
    )


def solution(mesh):
    in_specs = (
        P("fsdp", "seq", None),
        P(("seq", "fsdp")),
        P(("seq", "fsdp")),
        P(("seq", "fsdp"), None),
        P(None, ("seq", "fsdp")),
        P(("seq", "fsdp"), None),
        P(("seq", "fsdp")),
        P(("seq", "fsdp")),
        P(("seq", "fsdp"), None),
        P(("seq", "fsdp"), None),
        P(("seq", "fsdp"), None),
        P("fsdp", None),
        P("fsdp", None),
        P("fsdp", "seq", None),
    )
    out_specs = (
        P("fsdp", "seq", None),
        P("fsdp", "seq", None),
        P(("seq", "fsdp")),
        P(("seq", "fsdp")),
        P(("seq", "fsdp"), None),
        P(None, ("seq", "fsdp")),
        P(("seq", "fsdp"), None),
        P(("seq", "fsdp")),
        P(("seq", "fsdp")),
        P(("seq", "fsdp"), None),
        P(("seq", "fsdp"), None),
        P(("seq", "fsdp"), None),
        P(),
    )
    line = dict(mesh.shape) == {"seq": 8, "fsdp": 4}
    return jax.shard_map(
        line_body if line else body,
        mesh=mesh,
        in_specs=in_specs,
        out_specs=out_specs,
        check_vma=False,
    )
```

```python
import functools

import jax
import jax.numpy as jnp
from jax import lax
from jax.experimental import pallas as pl
from jax.experimental.pallas import tpu as pltpu
from jax.sharding import PartitionSpec as P

HEAD_DIM = 64
ROT = 16


EPS = 1e-05


def normalize(values):
    center = values - jnp.mean(values, -1, keepdims=True)
    spread = jnp.mean(center * center, -1, keepdims=True)
    rstd = lax.rsqrt(spread + EPS)
    return (center * rstd, rstd)


def norm_back(grad, normed, rstd, gain):
    scaled = grad * gain
    inner = (
        scaled
        - jnp.mean(scaled, -1, keepdims=True)
        - normed * jnp.mean(scaled * normed, -1, keepdims=True)
    )
    return (rstd * inner, jnp.sum(grad * normed, 0), jnp.sum(grad, 0))


def segment_of(pos, lengths):
    nseg = lengths.shape[0]
    ends = jnp.cumsum(lengths)
    seg = jnp.sum((pos[:, None] >= ends[None, :]).astype(jnp.int32), 1)
    starts = jnp.concatenate([jnp.zeros((1,), jnp.int32), ends[:-1]])
    start = jnp.sum(
        jnp.where(seg[:, None] == jnp.arange(nseg, dtype=jnp.int32)[None, :], starts[None, :], 0), 1
    )
    start = jnp.where(seg < nseg, start, pos)
    return (seg, start)


def rotate(values, rel, sign):
    count = values.shape[0]
    view = values.reshape(count, -1, HEAD_DIM)
    half = ROT // 2
    freq = 10000.0 ** (-2.0 * jnp.arange(half, dtype=jnp.float32) / ROT)
    angle = rel[:, None] * freq[None, :]
    cosine = jnp.cos(angle)[:, None, :]
    sine = jnp.sin(angle)[:, None, :]
    first = view[..., :half]
    second = view[..., half:ROT]
    turned = jnp.concatenate(
        [
            first * cosine - sign * second * sine,
            second * cosine + sign * first * sine,
            view[..., ROT:],
        ],
        -1,
    )
    return turned.reshape(count, -1)


def outer(left, right):
    return lax.dot_general(
        left, right, (((0,), (0,)), ((), ())), preferred_element_type=jnp.float32
    )


def times(left, right):
    return jnp.dot(left, right, preferred_element_type=jnp.float32)


def times_transposed(left, right):
    return lax.dot_general(
        left, right, (((1,), (1,)), ((), ())), preferred_element_type=jnp.float32
    )


def mlp_forward(gate, upper):
    sigma = jax.nn.sigmoid(gate)
    return ((gate * sigma * upper).astype(jnp.bfloat16), sigma)


def mlp_backward(hidden_grad, gate, upper, sigma):
    up_act = (hidden_grad * gate * sigma).astype(jnp.bfloat16)
    gate_act = (hidden_grad * upper * sigma * (1.0 + gate * (1.0 - sigma))).astype(jnp.bfloat16)
    return (gate_act, up_act)


def body(
    hidden_in,
    ln1_gain,
    ln1_bias,
    qkv_weight,
    qkv_bias,
    out_weight,
    ln2_gain,
    ln2_bias,
    gate_weight,
    up_weight,
    down_weight,
    seq_lengths,
    deal_order,
    out_grad,
):
    rows = hidden_in.shape[1]
    width = hidden_in.shape[2]
    nseq = lax.axis_size("seq")
    nfsdp = lax.axis_size("fsdp")
    local_width = width // nseq
    part = qkv_weight.shape[0]
    ff = gate_weight.shape[1]
    local_ff = ff // nseq
    stream = hidden_in[0].astype(jnp.float32)
    cotangent = out_grad[0].astype(jnp.float32)
    order = deal_order[0]
    lengths = seq_lengths[0]
    nseg = lengths.shape[0]
    group_rows = order.shape[0]
    valid_rows = group_rows * 5 // 8
    longest = valid_rows * 4 // 5
    blk = min(512, group_rows)
    keys = min(group_rows, longest + blk)
    nblocks = group_rows // blk
    scale = HEAD_DIM ** (-0.5)
    local_pos = lax.dynamic_slice_in_dim(order, lax.axis_index("seq") * rows, rows)
    valid = (local_pos < valid_rows).astype(jnp.float32)[:, None]
    dealt_seg, dealt_start = segment_of(order, lengths)
    rel = (order - dealt_start).astype(jnp.float32)
    inverse = (
        jnp.zeros((group_rows,), jnp.int32).at[order].set(jnp.arange(group_rows, dtype=jnp.int32))
    )
    seg_p, start_p = segment_of(jnp.arange(group_rows, dtype=jnp.int32), lengths)

    def gather_rows(values):
        return lax.all_gather(values, "seq", axis=0, tiled=True)

    def scatter_rows(partial):
        return lax.psum_scatter(
            partial.astype(jnp.bfloat16), "seq", scatter_dimension=0, tiled=True
        ).astype(jnp.float32)

    def column_slice(weight, blocks):
        cols = weight.shape[1] // (blocks * nseq)
        view = weight.reshape(part, blocks, nseq, cols).transpose(2, 0, 1, 3)
        mine = lax.all_to_all(
            view.reshape(nseq * part, blocks * cols), "seq", split_axis=0, concat_axis=0, tiled=True
        )
        full = lax.all_gather(mine.reshape(nseq, part, blocks * cols), "fsdp", axis=1)
        return full.reshape(width, blocks * cols)

    def row_slice(weight):
        return lax.all_gather(weight, "fsdp", axis=0, tiled=True)

    def column_shard(grad, blocks):
        cols = grad.shape[1] // blocks
        view = grad.astype(jnp.bfloat16).reshape(nseq, nfsdp, part, blocks * cols)
        mine = lax.psum_scatter(view.transpose(1, 0, 2, 3), "fsdp", scatter_dimension=0)
        got = lax.all_to_all(
            mine.reshape(nseq * part, blocks * cols), "seq", split_axis=0, concat_axis=0, tiled=True
        )
        view = got.reshape(nseq, part, blocks, cols).transpose(1, 2, 0, 3)
        return view.reshape(part, -1).astype(jnp.float32)

    def row_shard(grad):
        return lax.psum_scatter(
            grad.astype(jnp.bfloat16), "fsdp", scatter_dimension=0, tiled=True
        ).astype(jnp.float32)

    def to_pack(values):
        heads_here = values.shape[1] // HEAD_DIM
        return values[inverse].reshape(group_rows, heads_here, HEAD_DIM)

    def window(index, packed):
        query_p, key_p, value_p = packed
        first = index * blk
        key_first = jnp.clip(jnp.minimum(start_p[first], group_rows - keys), 0, group_rows - keys)
        qpos = first + jnp.arange(blk, dtype=jnp.int32)
        kpos = key_first + jnp.arange(keys, dtype=jnp.int32)
        qseg = lax.dynamic_slice_in_dim(seg_p, first, blk)
        kseg = lax.dynamic_slice_in_dim(seg_p, key_first, keys)
        allowed = (qseg[:, None] == kseg[None, :]) & (qseg[:, None] < nseg) & (
            kpos[None, :] <= qpos[:, None]
        ) | (kpos[None, :] == qpos[:, None])
        qblock = lax.dynamic_slice_in_dim(query_p, first, blk)
        kblock = lax.dynamic_slice_in_dim(key_p, key_first, keys)
        vblock = lax.dynamic_slice_in_dim(value_p, key_first, keys)
        scores = (
            jnp.einsum("qhd,khd->hqk", qblock, kblock, preferred_element_type=jnp.float32) * scale
        )
        scores = jnp.where(allowed[None], scores, -1e30)
        return (first, key_first, qblock, kblock, vblock, scores)

    both = ("seq", "fsdp")
    norms = lax.all_gather(
        jnp.stack([ln1_gain, ln1_bias, ln2_gain, ln2_bias, *qkv_bias]), both, axis=1, tiled=True
    )
    gain1, shift1, gain2, shift2 = norms[:4].astype(jnp.float32)
    qkv_shift = lax.dynamic_slice_in_dim(
        norms[4:], lax.axis_index("seq") * local_width, local_width, 1
    )
    qkv_shift = qkv_shift.reshape(-1).astype(jnp.float32)

    normed1, rstd1 = normalize(stream)
    first_local = (normed1 * gain1 + shift1).astype(jnp.bfloat16)
    first_in = gather_rows(first_local)
    qkv_w = column_slice(qkv_weight, 3)
    qkv = times(first_in, qkv_w) + qkv_shift
    query = rotate(qkv[:, :local_width], rel, 1.0).astype(jnp.bfloat16)
    keyset = rotate(qkv[:, local_width : 2 * local_width], rel, 1.0).astype(jnp.bfloat16)
    valueset = qkv[:, 2 * local_width :].astype(jnp.bfloat16)
    packed = (to_pack(query), to_pack(keyset), to_pack(valueset))

    def attend_block(index):
        first, key_first, qblock, kblock, vblock, scores = window(index, packed)
        top = jnp.max(scores, -1, keepdims=True)
        expo = jnp.exp(scores - top)
        total = jnp.sum(expo, -1, keepdims=True)
        probs = (expo / total).astype(jnp.bfloat16)
        mixed = jnp.einsum("hqk,khd->qhd", probs, vblock, preferred_element_type=jnp.float32)
        return (mixed.astype(jnp.bfloat16), (top + jnp.log(total))[..., 0])

    mixed_all, lse_all = lax.map(attend_block, jnp.arange(nblocks, dtype=jnp.int32))
    mixed = mixed_all.reshape(group_rows, -1)[order]
    heads_out = lax.all_to_all(mixed, "seq", split_axis=0, concat_axis=1, tiled=True)
    out_w = lax.all_gather(out_weight, both, axis=0, tiled=True)
    out_rows = row_slice(out_weight)
    attn = times(heads_out, out_w)
    resid = stream + attn
    normed2, rstd2 = normalize(resid)
    second_in = gather_rows((normed2 * gain2 + shift2).astype(jnp.bfloat16))
    gate_w = column_slice(gate_weight, 1)
    up_w = column_slice(up_weight, 1)
    down_w = row_slice(down_weight)
    gate = times(second_in, gate_w)
    upper = times(second_in, up_w)
    hidden, sigma = mlp_forward(gate, upper)
    mlp = scatter_rows(times(hidden, down_w))
    result = resid + mlp

    mlp_grad = gather_rows(out_grad[0])
    hidden_grad = times_transposed(mlp_grad, down_w)
    gate_act, up_act = mlp_backward(hidden_grad, gate, upper, sigma)
    second_grad = scatter_rows(times_transposed(gate_act, gate_w) + times_transposed(up_act, up_w))
    down_grad = row_shard(outer(hidden, mlp_grad))
    gate_grad = column_shard(outer(second_in, gate_act), 1)
    up_grad = column_shard(outer(second_in, up_act), 1)
    resid_part, gain2_grad, shift2_grad = norm_back(second_grad, normed2, rstd2, gain2)
    resid_grad = cotangent + resid_part

    attn_grad = gather_rows(resid_grad.astype(jnp.bfloat16))
    out_grad_w = row_shard(outer(mixed, attn_grad))
    mixed_grad_p = to_pack(times_transposed(attn_grad, out_rows).astype(jnp.bfloat16))

    def back_block(index, carry):
        query_acc, key_acc, value_acc = carry
        first, key_first, qblock, kblock, vblock, scores = window(index, packed)
        probs = jnp.exp(scores - lse_all[index][:, :, None])
        dblock = lax.dynamic_slice_in_dim(mixed_grad_p, first, blk)
        value_part = jnp.einsum(
            "hqk,qhd->khd", probs.astype(jnp.bfloat16), dblock, preferred_element_type=jnp.float32
        )
        prob_grad = jnp.einsum("qhd,khd->hqk", dblock, vblock, preferred_element_type=jnp.float32)
        inner = jnp.sum(probs * prob_grad, -1, keepdims=True)
        score_grad = (probs * (prob_grad - inner)).astype(jnp.bfloat16)
        query_part = (
            jnp.einsum("hqk,khd->qhd", score_grad, kblock, preferred_element_type=jnp.float32)
            * scale
        )
        key_part = (
            jnp.einsum("hqk,qhd->khd", score_grad, qblock, preferred_element_type=jnp.float32)
            * scale
        )
        query_acc = lax.dynamic_update_slice_in_dim(query_acc, query_part, first, 0)
        key_old = lax.dynamic_slice_in_dim(key_acc, key_first, keys)
        key_acc = lax.dynamic_update_slice_in_dim(key_acc, key_old + key_part, key_first, 0)
        value_old = lax.dynamic_slice_in_dim(value_acc, key_first, keys)
        value_acc = lax.dynamic_update_slice_in_dim(value_acc, value_old + value_part, key_first, 0)
        return (query_acc, key_acc, value_acc)

    zeros = jnp.zeros(packed[0].shape, jnp.float32)
    query_acc, key_acc, value_acc = lax.fori_loop(0, nblocks, back_block, (zeros, zeros, zeros))

    def to_dealt(values):
        return values.astype(jnp.bfloat16).reshape(group_rows, -1)[order]

    qkv_act = jnp.concatenate(
        [
            rotate(to_dealt(query_acc).astype(jnp.float32), rel, -1.0).astype(jnp.bfloat16),
            rotate(to_dealt(key_acc).astype(jnp.float32), rel, -1.0).astype(jnp.bfloat16),
            to_dealt(value_acc),
        ],
        1,
    )
    first_grad = scatter_rows(times_transposed(qkv_act, qkv_w))
    qkv_grad = column_shard(outer(first_in, qkv_act), 3)
    qkv_bias_grad = lax.psum_scatter(
        jnp.sum(qkv_act.astype(jnp.float32), 0).reshape(3, nfsdp, -1),
        "fsdp",
        scatter_dimension=1,
    )
    input_part, gain1_grad, shift1_grad = norm_back(first_grad, normed1, rstd1, gain1)
    input_grad = resid_grad + input_part

    norm_grads = lax.psum(
        (
            gain1_grad,
            shift1_grad,
            gain2_grad,
            shift2_grad,
            jnp.sum(valid * result * result),
            jnp.sum(valid * attn * attn),
            jnp.sum(valid * mlp * mlp),
        ),
        both,
    )
    count = valid_rows * nfsdp * width
    rms = jnp.sqrt(jnp.stack(norm_grads[4:]) / count)
    mine = (lax.axis_index("seq") * nfsdp + lax.axis_index("fsdp")) * part
    norm_shards = [lax.dynamic_slice_in_dim(value, mine, part) for value in norm_grads[:4]]
    return (
        result.astype(jnp.bfloat16)[None],
        input_grad[None],
        norm_shards[0],
        norm_shards[1],
        qkv_grad,
        qkv_bias_grad,
        out_grad_w,
        norm_shards[2],
        norm_shards[3],
        gate_grad,
        up_grad,
        down_grad,
        rms,
    )


MESH = pl.DeviceIdType.MESH
QB = 128
NEG = -1e30
CH = 2
VMEM_SPEC = pl.BlockSpec(memory_space=pltpu.VMEM)
SMEM_SPEC = pl.BlockSpec(memory_space=pltpu.SMEM)
ANY_SPEC = pl.BlockSpec(memory_space=pl.ANY)
HBM_SPEC = pl.BlockSpec(memory_space=pltpu.HBM)
DMA = pltpu.SemaphoreType.DMA


def comm_params(collective, limit=63):
    return pltpu.CompilerParams(
        collective_id=collective, has_side_effects=True, vmem_limit_bytes=limit << 20
    )


def where_am_i():
    s = lax.axis_index("seq")
    f = lax.axis_index("fsdp")
    return s, f, s // 2, s % 2


def remote(src, dst, send, recv, device):
    return pltpu.make_async_remote_copy(
        src, dst, send, recv, device_id=device, device_id_type=MESH
    )


def flip(v, bit):
    return v + bit * (1 - 2 * ((v // bit) % 2))


def peer(s, k):
    for bit in (1, 2, 4):
        if k & bit:
            s = flip(s, bit)
    return s


def peer_at(s, k):
    for bit in (1, 2, 4):
        s = s + ((k // bit) % 2) * bit * (1 - 2 * ((s // bit) % 2))
    return s


def dealer(i):
    return (i // 4, i % 4)


def greet_all(s, f):
    bar = pltpu.get_barrier_semaphore()
    me = s * 4 + f

    @pl.loop(1, 32)
    def _(k):
        pl.semaphore_signal(bar, inc=1, device_id=dealer((me + k) % 32), device_id_type=MESH)

    pl.semaphore_wait(bar, 31)


def greet_line(s, f, z, y):
    bar = pltpu.get_barrier_semaphore()
    pl.semaphore_signal(bar, inc=1, device_id=(flip(s, 1), f), device_id_type=MESH)

    @pl.when(z > 0)
    def _():
        pl.semaphore_signal(bar, inc=1, device_id=(s - 2, f), device_id_type=MESH)

    @pl.when(z < 3)
    def _():
        pl.semaphore_signal(bar, inc=1, device_id=(s + 2, f), device_id_type=MESH)

    edge = jnp.where((z == 0) | (z == 3), 1, 0)
    pl.semaphore_wait(bar, 3 - edge)


def greet_columns(s, f):
    bar = pltpu.get_barrier_semaphore()
    for k in range(1, 8):
        pl.semaphore_signal(bar, inc=1, device_id=(peer(s, k), f), device_id_type=MESH)
    pl.semaphore_signal(bar, inc=1, device_id=(s, flip(f, 1)), device_id_type=MESH)
    pl.semaphore_signal(bar, inc=1, device_id=(s, flip(f, 2)), device_id_type=MESH)
    pl.semaphore_wait(bar, 9)


def adder(dst, srcs, step=16):
    @pl.loop(0, dst.shape[0] // step)
    def _(i):
        r = pl.ds(pl.multiple_of(i * step, step), step)
        total = srcs[0][r].astype(jnp.float32)
        for v in srcs[1:]:
            total = total + v[r].astype(jnp.float32)
        dst[r] = total.astype(dst.dtype)


class SeqGather:
    @staticmethod
    def scratch(parts=1):
        return [DMA, DMA((8, parts)), DMA((4, parts)), DMA((4, parts)), DMA((4, parts))]

    def __init__(self, x, o, own, recv, sy, su, sd):
        self.x, self.o, self.recv, self.sy, self.su, self.sd = x, o, recv, sy, su, sd
        self.s, self.f, self.z, self.y = where_am_i()
        self.parts = recv.shape[1]
        self.other = flip(self.s, 1)
        self.own = pltpu.make_async_copy(x, o.at[self.s], own)

    def rows(self, c):
        n = self.x.shape[0] // self.parts
        return pl.ds(c * n, n)

    def at(self, zb):
        return 2 * zb + self.y

    def copy(self, zb, c, own, sems, to):
        b, r = self.at(zb), self.rows(c)
        src = self.x.at[r] if own else self.o.at[b, r]
        return remote(src, self.o.at[b, r], sems.at[zb, c], self.recv.at[b, c], (to, self.f))

    def ysend(self, zb, c, own=False):
        return self.copy(zb, c, own, self.sy, self.other)

    def usend(self, zb, c, own=False):
        return self.copy(zb, c, own, self.su, self.s + 2)

    def dsend(self, zb, c, own=False):
        return self.copy(zb, c, own, self.sd, self.s - 2)

    def arrived(self, b, c):
        o = self.o.at[b, self.rows(c)]
        return remote(o, o, self.sy.at[0, c], self.recv.at[b, c], (self.other, self.f))

    def start(self):
        for c in range(self.parts):

            @pl.when(self.z < 3)
            def _():
                self.usend(self.z, c, True).start()

            @pl.when(self.z > 0)
            def _():
                self.dsend(self.z, c, True).start()

            self.ysend(self.z, c, True).start()
        self.own.start()

    def near(self, i):
        low = jnp.where(self.z < 2, self.z, 3 - self.z)
        base = jnp.where(low == 0, i, jnp.where(i < 2, 1 - i, i))
        return jnp.where(self.z < 2, base, 3 - base)

    def arrive(self, i, c=0):
        zb = self.near(i)
        self.arrived(self.at(zb), c).wait_recv()

        @pl.when((zb < self.z) & (self.z < 3))
        def _():
            self.usend(zb, c).start()

        @pl.when((zb > self.z) & (self.z > 0))
        def _():
            self.dsend(zb, c).start()

        self.ysend(zb, c).start()

    def column(self, i):
        return self.at(self.near(i))

    def cross(self, i):
        b = 2 * self.near(i) + 1 - self.y
        for c in range(self.parts):
            self.arrived(b, c).wait_recv()
        return b

    def steps(self):
        return [functools.partial(self.arrive, i, c) for i in (1, 2, 3) for c in range(self.parts)]

    def turn(self, j):
        i = (j + 1) // 2
        column = (j == 0) | ((j % 2 == 1) & (j < 7))
        other = jnp.where(j == 7, 3, j // 2 - 1)

        @pl.when(jnp.logical_not(column))
        def _():
            self.cross(other)

        zb = self.near(jnp.where(column, i, other))
        return 2 * zb + jnp.where(column, self.y, 1 - self.y)

    def finish(self, own=True):
        if own:
            self.own.wait()
        for c in range(self.parts):
            for zb in range(4):
                self.ysend(zb, c).wait_send()

                @pl.when((self.z < 3) & (zb <= self.z))
                def _():
                    self.usend(zb, c).wait_send()

                @pl.when((self.z > 0) & (zb >= self.z))
                def _():
                    self.dsend(zb, c).wait_send()


class SeqReduce:
    @staticmethod
    def scratch(rows, w):
        big = [pltpu.VMEM((n, rows, w), jnp.bfloat16) for n in (4, 5)]
        return big + [DMA((4, CH)), DMA((5, CH)), DMA((4, CH)), DMA((4, CH))]

    def __init__(self, p, o, ybuf, got, ry, rl, sy, sl):
        self.p, self.o, self.ybuf, self.got = p, o, ybuf, got
        self.ry, self.rl, self.sy, self.sl = ry, rl, sy, sl
        self.s, self.f, self.z, self.y = where_am_i()
        self.other = flip(self.s, 1)
        self.ch = p.shape[1] // CH

    def order(self, k):
        low = jnp.where(self.z < 2, self.z, 3 - self.z)
        inner = jnp.where(k == 0, 3, jnp.where(k == 1, 0, jnp.where(k == 2, 2, 1)))
        base = jnp.where(low == 0, 3 - k, inner)
        return jnp.where(self.z < 2, base, 3 - base)

    def rows(self, c):
        return pl.ds(c * self.ch, self.ch)

    def ysend(self, zb, c):
        r = self.rows(c)
        src = self.p.at[2 * zb + 1 - self.y, r]
        dst = self.ybuf.at[zb, r]
        return remote(src, dst, self.sy.at[zb, c], self.ry.at[zb, c], (self.other, self.f))

    def usend(self, zb, c):
        r = self.rows(c)
        src, dst = self.ybuf.at[zb, r], self.got.at[zb, r]
        return remote(src, dst, self.sl.at[zb, c], self.rl.at[zb, c], (self.s + 2, self.f))

    def dsend(self, zb, c):
        r = self.rows(c)
        slot = jnp.where(zb == self.z - 1, 4, zb)
        src, dst = self.ybuf.at[zb, r], self.got.at[slot, r]
        return remote(src, dst, self.sl.at[zb, c], self.rl.at[slot, c], (self.s - 2, self.f))

    def landed(self, slot, c):
        v = self.got.at[slot, self.rows(c)]
        return remote(v, v, self.sl.at[0, c], self.rl.at[slot, c], (self.other, self.f))

    def send(self, k):
        for c in range(CH):
            self.ysend(self.order(k), c).start()

    def start(self):
        for k in range(4):
            self.send(k)

    def step(self, k, c):
        z, zb, r = self.z, self.order(k), self.rows(c)
        self.ysend(zb, c).wait_recv()
        a, b = self.p.at[2 * zb + self.y, r], self.ybuf.at[zb, r]
        u, d = self.got.at[zb, r], self.got.at[4, r]
        alone = ((zb > z) & (z == 0)) | ((zb < z) & (z == 3))

        @pl.when(alone)
        def _():
            adder(b, [a, b])

        @pl.when((zb != z) & jnp.logical_not(alone))
        def _():
            self.landed(zb, c).wait_recv()
            adder(b, [a, b, u])

        @pl.when(zb > z)
        def _():
            self.usend(zb, c).start()

        @pl.when(zb < z)
        def _():
            self.dsend(zb, c).start()

        @pl.when(zb == z)
        def _():
            o = self.o.at[r]

            @pl.when(z == 0)
            def _():
                self.landed(4, c).wait_recv()
                adder(o, [a, b, d])

            @pl.when(z == 3)
            def _():
                self.landed(zb, c).wait_recv()
                adder(o, [a, b, u])

            @pl.when((z > 0) & (z < 3))
            def _():
                self.landed(zb, c).wait_recv()
                self.landed(4, c).wait_recv()
                adder(o, [a, b, u, d])

    def steps(self):
        return [functools.partial(self.step, k, c) for k in range(4) for c in range(CH)]

    def finish(self):
        for zb in range(4):
            for c in range(CH):
                self.ysend(zb, c).wait_send()

                @pl.when(zb != self.z)
                def _():
                    self.usend(zb, c).wait_send()


class ColGather:
    @staticmethod
    def scratch():
        return [DMA, DMA((8, 4)), DMA((8,)), DMA((8, 2)), DMA((8,))]

    def __init__(self, x, o, own, recv, direct, core, xs):
        self.x, self.o, self.own, self.recv = x, o, own, recv
        self.direct, self.core, self.xs = direct, core, xs
        self.s, self.f, _, _ = where_am_i()
        self.fc, self.fx = flip(self.f, 1), flip(self.f, 2)
        self.fd = flip(self.fc, 2)
        self.mine = pltpu.make_async_copy(x.at[self.s], self.piece(self.s, self.f), own)

    def piece(self, t, ff):
        r = self.x.shape[1]
        return self.o.at[pl.ds(pl.multiple_of((t * 4 + ff) * r, r), r)]

    def send_direct(self, k):
        s, f, t = self.s, self.f, peer(self.s, k)
        return remote(self.x.at[t], self.piece(s, f), self.direct.at[k], self.recv.at[s, f], (t, f))

    def send_core(self, k, which, src):
        t, ff = peer(self.s, k), self.f if which == 0 else self.fx
        dst = self.piece(t, ff)
        return remote(src, dst, self.core.at[k, which], self.recv.at[t, ff], (self.s, self.fc))

    def send_x(self, k, src):
        t = peer(self.s, k)
        dst = self.piece(t, self.f)
        return remote(src, dst, self.xs.at[k], self.recv.at[t, self.f], (self.s, self.fx))

    def arrived(self, k, ff):
        t = peer(self.s, k)
        o = self.piece(t, ff)
        return remote(o, o, self.own, self.recv.at[t, ff], (self.s, self.fc))

    def start(self):
        for k in reversed(range(1, 8)):
            self.send_direct(k).start()
        self.send_x(0, self.x.at[self.s]).start()
        self.send_core(0, 0, self.x.at[self.s]).start()
        self.mine.start()

    def step(self, k):
        t = peer(self.s, k)
        self.arrived(k, self.f).wait_recv()
        self.send_x(k, self.piece(t, self.f)).start()
        self.send_core(k, 0, self.piece(t, self.f)).start()

    def xstep(self, k):
        t = peer(self.s, k)
        self.arrived(k, self.fx).wait_recv()
        self.send_core(k, 1, self.piece(t, self.fx)).start()

    def steps(self):
        first = [functools.partial(self.step, k) for k in reversed(range(1, 8))]
        then = [functools.partial(self.xstep, k) for k in (0, 7, 6, 5, 4, 3, 2, 1)]
        return first + then

    def complete(self):
        self.mine.wait()
        for k in range(8):
            self.arrived(k, self.fc).wait_recv()
            self.arrived(k, self.fd).wait_recv()

    def finish(self):
        for k in range(8):
            if k:
                self.send_direct(k).wait_send()
            self.send_x(k, self.x.at[0]).wait_send()
            self.send_core(k, 0, self.x.at[0]).wait_send()
            self.send_core(k, 1, self.x.at[0]).wait_send()


class ColSum:
    @staticmethod
    def scratch(r, c):
        def v(*lead):
            return pltpu.VMEM(lead + (8, r, c), jnp.bfloat16)

        return [v(2), v(), DMA((2, 8)), DMA((2, 8)), DMA((8,)), DMA((8,))]

    def __init__(self, g, h, cb, xb, cs, cr, xs, xr):
        self.g, self.h, self.cb, self.xb = g, h, cb, xb
        self.cs, self.cr, self.xs, self.xr = cs, cr, xs, xr
        self.s, self.f, _, _ = where_am_i()
        self.fc, self.fx = flip(self.f, 1), flip(self.f, 2)
        self.fd = flip(self.fc, 2)
        self.r, self.c = h.shape[1:]

    def piece(self, i, ff):
        at = pl.multiple_of((i * 4 + ff) * self.r, self.r)
        return self.g.at[pl.ds(at, self.r), pl.ds(0, self.c)]

    def core(self, w, i):
        src = self.piece(i, self.fd if w == 0 else self.fc)
        dst = self.cb.at[w, i]
        return remote(src, dst, self.cs.at[w, i], self.cr.at[w, i], (self.s, self.fc))

    def xsend(self, i):
        src, dst = self.cb.at[0, i], self.xb.at[i]
        return remote(src, dst, self.xs.at[i], self.xr.at[i], (self.s, self.fx))

    def send(self, i):
        self.core(0, i).start()
        self.core(1, i).start()

    def step(self, i):
        self.core(0, i).wait_recv()
        adder(self.cb.at[0, i], [self.piece(i, self.fx), self.cb.at[0, i]])
        self.xsend(i).start()

    def total(self, i):
        self.core(1, i).wait_recv()
        self.xsend(i).wait_recv()
        adder(self.h.at[i], [self.piece(i, self.f), self.cb.at[1, i], self.xb.at[i]])

    def finish(self):
        for i in range(8):
            self.core(0, i).wait_send()
            self.core(1, i).wait_send()
            self.xsend(i).wait_send()


class FsdpReduce:
    @staticmethod
    def scratch(r, c):
        return [pltpu.VMEM((2, r, c), jnp.bfloat16), pltpu.VMEM((r, c), jnp.bfloat16), DMA((3,)), DMA((3,))]

    def __init__(self, g, o, cb, xb, send, recv):
        self.g, self.o, self.cb, self.xb = g, o, cb, xb
        self.s, self.f, _, _ = where_am_i()
        f = self.f
        self.fx = flip(f, 2)
        fc = flip(f, 1)
        core = (self.s, fc)
        self.far = remote(g.at[flip(fc, 2)], cb.at[0], send.at[0], recv.at[0], core)
        self.near = remote(g.at[fc], cb.at[1], send.at[1], recv.at[1], core)
        self.over = remote(cb.at[0], xb, send.at[2], recv.at[2], (self.s, self.fx))

    def start(self):
        self.far.start()
        self.near.start()

    def step(self):
        self.far.wait_recv()
        adder(self.cb.at[0], [self.g.at[self.fx], self.cb.at[0]])
        self.over.start()

    def total(self):
        self.near.wait_recv()
        self.over.wait_recv()
        adder(self.o, [self.g.at[self.f], self.cb.at[1], self.xb])

    def finish(self):
        self.far.wait_send()
        self.near.wait_send()
        self.over.wait_send()


class FsdpGather:
    @staticmethod
    def scratch():
        return [DMA, DMA((4,)), DMA((3,))]

    def __init__(self, x, o, own, recv, send):
        self.x, self.o, self.own, self.recv, self.send = x, o, own, recv, send
        self.s, self.f, _, _ = where_am_i()
        self.fc, self.fx = flip(self.f, 1), flip(self.f, 2)
        self.fd = flip(self.fc, 2)
        self.mine = pltpu.make_async_copy(x, o.at[self.f], own)

    def pass_on(self, n, src, ff, to):
        return remote(src, self.o.at[ff], self.send.at[n], self.recv.at[ff], (self.s, to))

    def arrived(self, ff):
        o = self.o.at[ff]
        return remote(o, o, self.own, self.recv.at[ff], (self.s, self.fc))

    def start(self):
        self.pass_on(0, self.x, self.f, self.fx).start()
        self.pass_on(1, self.x, self.f, self.fc).start()
        self.mine.start()

    def step(self):
        self.arrived(self.fx).wait_recv()
        self.pass_on(2, self.o.at[self.fx], self.fx, self.fc).start()

    def complete(self):
        self.mine.wait()
        self.arrived(self.fc).wait_recv()
        self.arrived(self.fd).wait_recv()

    def finish(self):
        for n in range(3):
            self.pass_on(n, self.x, self.f, self.fc).wait_send()


class WholeGather:
    @staticmethod
    def scratch():
        return [DMA, DMA((32,)), DMA((4,)), DMA((4,)), DMA((4,)), DMA((4, 2)), DMA((4, 2, 2))]

    def __init__(self, x, o, own, recv, su, sd, sy, sx, sc):
        self.x, self.o, self.own, self.recv = x, o, own, recv
        self.su, self.sd, self.sy, self.sx, self.sc = su, sd, sy, sx, sc
        self.s, self.f, self.z, self.y = where_am_i()
        self.fc, self.fx = flip(self.f, 1), flip(self.f, 2)
        self.fd = flip(self.fc, 2)
        self.me = self.s * 4 + self.f
        self.mine = pltpu.make_async_copy(x, o.at[self.me], own)

    def at(self, zb, yy, ff):
        return (2 * zb + (self.y if yy == 0 else 1 - self.y)) * 4 + ff

    def src(self, b, first):
        return self.x if first else self.o.at[b]

    def up(self, zb, first=False):
        b = self.at(zb, 0, self.f)
        to = (self.s + 2, self.f)
        return remote(self.src(b, first), self.o.at[b], self.su.at[zb], self.recv.at[b], to)

    def down(self, zb, first=False):
        b = self.at(zb, 0, self.f)
        to = (self.s - 2, self.f)
        return remote(self.src(b, first), self.o.at[b], self.sd.at[zb], self.recv.at[b], to)

    def over_y(self, zb, first=False):
        b = self.at(zb, 0, self.f)
        to = (flip(self.s, 1), self.f)
        return remote(self.src(b, first), self.o.at[b], self.sy.at[zb], self.recv.at[b], to)

    def over_x(self, zb, yy, first=False):
        b = self.at(zb, yy, self.f)
        to = (self.s, self.fx)
        return remote(self.src(b, first), self.o.at[b], self.sx.at[zb, yy], self.recv.at[b], to)

    def over_core(self, zb, yy, xx, first=False):
        b = self.at(zb, yy, self.f if xx == 0 else self.fx)
        to = (self.s, self.fc)
        return remote(self.src(b, first), self.o.at[b], self.sc.at[zb, yy, xx], self.recv.at[b], to)

    def arrived(self, b):
        o = self.o.at[b]
        return remote(o, o, self.own, self.recv.at[b], (self.s, self.fc))

    def start(self):
        z = self.z

        @pl.when(z < 3)
        def _():
            self.up(z, True).start()

        @pl.when(z > 0)
        def _():
            self.down(z, True).start()

        self.over_y(z, True).start()
        self.over_x(z, 0, True).start()
        self.over_core(z, 0, 0, True).start()
        self.mine.start()

    def line(self, sign, t):
        zb = self.z + sign * t

        @pl.when((zb >= 0) & (zb <= 3))
        def _():
            self.arrived(self.at(zb, 0, self.f)).wait_recv()
            if sign < 0:

                @pl.when(self.z < 3)
                def _():
                    self.up(zb).start()

            else:

                @pl.when(self.z > 0)
                def _():
                    self.down(zb).start()

            self.over_y(zb).start()
            self.over_x(zb, 0).start()
            self.over_core(zb, 0, 0).start()

    def column(self, sign, t):
        zb = self.z + sign * t

        @pl.when((zb >= 0) & (zb <= 3))
        def _():
            self.arrived(self.at(zb, 1, self.f)).wait_recv()
            self.over_x(zb, 1).start()
            self.over_core(zb, 1, 0).start()

    def side(self, sign, t, yy):
        zb = self.z + sign * t

        @pl.when((zb >= 0) & (zb <= 3))
        def _():
            self.arrived(self.at(zb, yy, self.fx)).wait_recv()
            self.over_core(zb, yy, 1).start()

    def steps(self):
        p = functools.partial
        out = []
        for t in range(4):
            for sign in (-1, 1) if t else (1,):
                if t:
                    out.append(p(self.line, sign, t))
        for t in range(4):
            for sign in (-1, 1) if t else (1,):
                out.append(p(self.column, sign, t))
                out.append(p(self.side, sign, t, 0))
        for t in range(4):
            for sign in (-1, 1) if t else (1,):
                out.append(p(self.side, sign, t, 1))
        return out

    def complete(self):
        self.mine.wait()
        for zb in range(4):
            for yy in range(2):
                self.arrived(self.at(zb, yy, self.fc)).wait_recv()
                self.arrived(self.at(zb, yy, self.fd)).wait_recv()

    def finish(self):
        for zb in range(4):
            self.over_y(zb).wait_send()

            @pl.when((self.z < 3) & (zb <= self.z))
            def _():
                self.up(zb).wait_send()

            @pl.when((self.z > 0) & (zb >= self.z))
            def _():
                self.down(zb).wait_send()

            for yy in range(2):
                self.over_x(zb, yy).wait_send()
                for xx in range(2):
                    self.over_core(zb, yy, xx).wait_send()


class RowExchange:
    @staticmethod
    def scratch():
        return [DMA, DMA((8,)), DMA((8,))]

    def __init__(self, x, o, own, send, recv):
        self.x, self.o, self.send, self.recv = x, o, send, recv
        self.s, self.f, _, _ = where_am_i()
        self.mine = pltpu.make_async_copy(x.at[self.s], o.at[self.s], own)

    def piece(self, k):
        t = peer(self.s, k)
        dst = self.o.at[self.s]
        return remote(self.x.at[t], dst, self.send.at[k], self.recv.at[k], (t, self.f))

    def start(self):
        for k in reversed(range(1, 8)):
            self.piece(k).start()
        self.mine.start()

    def finish(self):
        self.mine.wait()
        for k in reversed(range(1, 8)):
            self.piece(k).wait_recv()
            self.piece(k).wait_send()


def idle():
    pass


def looped(plan, name, work, queues):
    count = plan.count(name)
    groups = plan.split(name)
    left = {k: list(v) for k, v in queues.items()}

    def between(now, group):
        items = [left[k].pop(0) for k in group]
        if items:

            @pl.when(now)
            def _():
                for item in items:
                    item()

    @pl.loop(0, count)
    def _(i):
        for n in range(count):
            between(i == n, groups[n])
        work(i)

    for k in groups[count]:
        left[k].pop(0)()
    return left


def fetch(refs, sems):
    copies = [pltpu.make_async_copy(a, b, sems.at[i]) for i, (a, b) in enumerate(refs)]
    for copy in copies:
        copy.start()
    return copies


def rotary_rows(pos, lengths_ref, freq):
    half = ROT // 2
    d = lax.broadcasted_iota(jnp.int32, (1, 128), 1) % HEAD_DIM
    rel = pos - starts_of(pos, lengths_ref, lengths_ref.shape[1])
    angle = rel.astype(jnp.float32) * freq
    c, s = jnp.cos(angle), jnp.sin(angle)
    second = (d >= half) & (d < ROT)
    return jnp.where(d < ROT, c, 1.0), jnp.where(d < half, -s, 0.0), jnp.where(second, s, 0.0)


def perform(plan, queues):
    left = {name: list(items) for name, items in queues.items()}
    for name in "".join(plan):
        left[name].pop(0)()
    return left


FORWARD_PLAN = (
    "FnggsnWsgswwsDswwnnsssVswsswsws",
    "nswwnsnnccwwccccvdvwcccwccwwcdv",
    "vwwwfcccwwwccwwcvXwwwvvdvvvwvvY",
    "PPvvvPP",
    "Q",
)
MIDDLE_PLAN = (
    "gbggbbgbgbgbbb",
    "raaaraeateaeearea",
    "mertmeemm",
    "Mlltllhtthhlltlthhl",
    "LhhhHtz",
)
BACKWARD_PLAN = ("bFggrgbbXgbgbgrbfbrtZtb", "crotccoocotocootocqOcccptccccPttz")
LAST_PLAN = ("ataaeeathtaheatttehehetaa", "eehthhzhZ")


def dot(a, b, ca=1, cb=0):
    return lax.dot_general(a, b, (((ca,), (cb,)), ((), ())), preferred_element_type=jnp.float32)


def starts_of(pos, lengths_ref, nseg):
    start = jnp.zeros_like(pos)
    end = 0
    for i in range(nseg - 1):
        end = end + lengths_ref[0, i]
        start = jnp.where(pos >= end, end, start)
    return start


def head_lanes(h):
    lane = lax.broadcasted_iota(jnp.int32, (1, 128), 1)
    return (lane // HEAD_DIM) == h


def turn(x, c, s1, s2, sign):
    half = ROT // 2
    return x * c + (pltpu.roll(x, 128 - half, 1) * s1 + pltpu.roll(x, half, 1) * s2) * sign


def block_mask(qb, lengths_ref):
    keys = (qb + 1) * QB
    row = qb * QB + lax.broadcasted_iota(jnp.int32, (QB, 1), 0)
    col = lax.broadcasted_iota(jnp.int32, (1, keys), 1)
    return (col >= starts_of(row, lengths_ref, lengths_ref.shape[1])) & (col <= row)


def row_at(i, step=QB):
    return pl.ds(pl.multiple_of(i * step, step), step)


def picks(orow_ref, i):
    p = lax.broadcasted_iota(jnp.int32, (QB, 1), 0) + i * QB == orow_ref[...]
    return jnp.where(p, 1.0, 0.0).astype(jnp.bfloat16)


def puts(oc, valid):
    p = oc == lax.broadcasted_iota(jnp.int32, (1, valid), 1)
    return jnp.where(p, 1.0, 0.0).astype(jnp.bfloat16)


def attend(
    a_ref, w_ref, shift_of, tables, orow_ref, ocol_ref, len_ref, o_ref, pk_ref, lse_ref, rot, opk
):
    rows, w3 = rot.shape
    w = w3 // 3
    valid = pk_ref.shape[0]
    scale = HEAD_DIM**-0.5
    freq_ref = tables

    def project(lo, hi):
        shift = shift_of()

        @pl.loop(lo, hi)
        def _(i):
            r = row_at(i, 256)
            c, s1, s2 = rotary_rows(ocol_ref[r], len_ref, freq_ref[...])
            left = jnp.concatenate([a_ref[2 * i], a_ref[2 * i + 1]], 0)
            qkv = dot(left, w_ref[...]) + shift
            for t in range(w3 // 128):
                cols = slice(t * 128, t * 128 + 128)
                x = qkv[:, cols]
                if t < 2 * w // 128:
                    x = turn(x, c, s1, s2, 1.0)
                rot[r, cols] = x.astype(jnp.bfloat16)

    def pack(lo, hi):
        @pl.loop(lo, hi)
        def _(i):
            pk_ref[row_at(i)] = dot(picks(orow_ref, i), rot[...]).astype(jnp.bfloat16)

    def block(qb, t):
        keys = (qb + 1) * QB
        rq = slice(qb * QB, qb * QB + QB)
        ct = slice(t * 128, t * 128 + 128)
        mask = block_mask(qb, len_ref)
        q = pk_ref[rq, ct]
        k = pk_ref[0:keys, w + t * 128 : w + t * 128 + 128]
        v = pk_ref[0:keys, 2 * w + t * 128 : 2 * w + t * 128 + 128]
        total = None
        for h in range(2):
            qh = jnp.where(head_lanes(h), q, jnp.zeros_like(q))
            scores = jnp.where(mask, dot(qh, k, 1, 1) * scale, NEG)
            top = jnp.max(scores, -1, keepdims=True)
            expo = jnp.exp(scores - top)
            norm = jnp.sum(expo, -1, keepdims=True)
            probs = (expo / norm).astype(jnp.bfloat16)
            lse_ref[2 * t + h, rq] = top + jnp.log(norm)
            out = dot(probs, v)
            total = out if h == 0 else jnp.where(head_lanes(1), out, total)
        opk[rq, ct] = total.astype(jnp.bfloat16)

    def unpack(lo, hi):
        per = o_ref.shape[1]

        @pl.loop(lo, hi)
        def _(i):
            r = row_at(i, per)
            oc = ocol_ref[r]
            back = dot(puts(oc, valid), opk[...])
            pad = rot[r, 2 * w :].astype(jnp.float32)
            o_ref[i] = jnp.where(oc >= valid, pad, back).astype(jnp.bfloat16)

    blocks = [
        functools.partial(block, qb, t) for qb in range(valid // QB) for t in range(w // 128)
    ]
    p = functools.partial
    steps, half, blks = rows // 256, valid // QB // 2, rows // o_ref.shape[1]
    head = [p(project, 0, steps // 2), p(project, steps // 2, steps)]
    head += [p(pack, 0, half), p(pack, half, valid // QB)]
    return head + blocks + [p(unpack, 0, blks // 2), p(unpack, blks // 2, blks)]


def attend_back(
    pk_ref, do_ref, lse_ref, tables, orow_ref, ocol_ref, len_ref, g_ref, b_ref, dpk, dq, dk, dv, gpk
):
    rows, w = do_ref.shape
    valid = pk_ref.shape[0]
    scale = HEAD_DIM**-0.5
    freq_ref = tables

    def pack():
        @pl.loop(0, valid // QB)
        def _(i):
            r = row_at(i)
            dpk[r] = dot(picks(orow_ref, i), do_ref[...]).astype(jnp.bfloat16)
            dk[r] = jnp.zeros((QB, w), jnp.float32)
            dv[r] = jnp.zeros((QB, w), jnp.float32)

    def block(qb, t):
        keys = (qb + 1) * QB
        rq = slice(qb * QB, qb * QB + QB)
        ct = slice(t * 128, t * 128 + 128)
        mask = block_mask(qb, len_ref)
        q, d = pk_ref[rq, ct], dpk[rq, ct]
        k = pk_ref[0:keys, w + t * 128 : w + t * 128 + 128]
        v = pk_ref[0:keys, 2 * w + t * 128 : 2 * w + t * 128 + 128]
        total = None
        for h in range(2):
            hl = head_lanes(h)
            qh = jnp.where(hl, q, jnp.zeros_like(q))
            dh = jnp.where(hl, d, jnp.zeros_like(d))
            scores = jnp.where(mask, dot(qh, k, 1, 1) * scale, NEG)
            p = jnp.exp(scores - lse_ref[2 * t + h, rq])
            dp = dot(dh, v, 1, 1)
            inner = jnp.sum(p * dp, -1, keepdims=True)
            ds = (p * (dp - inner)).astype(jnp.bfloat16)
            dv[0:keys, ct] += dot(p.astype(jnp.bfloat16), dh, 0, 0)
            dk[0:keys, ct] += dot(ds, qh, 0, 0)
            part = dot(ds, k)
            total = part if h == 0 else jnp.where(head_lanes(1), part, total)
        dq[rq, ct] = total

    def rotary():
        @pl.loop(0, valid // QB)
        def _(i):
            r = row_at(i)
            pos = lax.broadcasted_iota(jnp.int32, (QB, 1), 0) + i * QB
            c, s1, s2 = rotary_rows(pos, len_ref, freq_ref[...])
            for t in range(w // 128):
                ct = slice(t * 128, t * 128 + 128)
                for j, src in ((0, dq), (1, dk)):
                    x = (src[r, ct] * scale).astype(jnp.bfloat16).astype(jnp.float32)
                    at = j * w + t * 128
                    gpk[r, at : at + 128] = turn(x, c, s1, s2, -1.0).astype(jnp.bfloat16)
                at = 2 * w + t * 128
                gpk[r, at : at + 128] = dv[r, ct].astype(jnp.bfloat16)

    def unpack():
        b_ref[...] = jnp.zeros_like(b_ref)

        @pl.loop(0, rows // QB)
        def _(i):
            r = row_at(i)
            oc = ocol_ref[r]
            back = dot(puts(oc, valid), gpk[...])
            pad = jnp.where(oc >= valid, do_ref[r].astype(jnp.float32), 0.0)
            back = jnp.concatenate([back[:, : 2 * w], back[:, 2 * w :] + pad], 1)
            g_ref[r] = back.astype(jnp.bfloat16)
            b_ref[...] += jnp.sum(back, 0, keepdims=True)

    blocks = [
        functools.partial(block, qb, t) for qb in range(valid // QB) for t in range(w // 128)
    ]
    return [pack] + blocks + [rotary, unpack]


def forward_kernel(
    x_hbm,
    p_ref,
    qkv_ref,
    op_hbm,
    dm_hbm,
    gate_hbm,
    up_hbm,
    dp_hbm,
    freq_ref,
    orow_ref,
    ocol_ref,
    len_ref,
    a_hbm,
    qw_hbm,
    n_ref,
    or_hbm,
    pk_hbm,
    lse_hbm,
    dmo_ref,
    ww_ref,
    dw_ref,
    mix_hbm,
    attn_ref,
    res_ref,
    second_ref,
    a_ref,
    qw_ref,
    ow_ref,
    ho_ref,
    pk_ref,
    lse_ref,
    mix_ref,
    x_ref,
    op_ref,
    dm_ref,
    gate_ref,
    up_ref,
    dp_ref,
    xs,
    got,
    rot,
    opk,
    qp_ref,
    wp_ref,
    load,
    store,
    psend,
    precv,
    *sems,
):
    s, f, z, y = where_am_i()
    me = s * 4 + f
    w = rot.shape[1] // 3
    lf = wp_ref.shape[2] // 2
    rows, width = x_ref.shape

    def piece_of(i):
        t, n = i // 3, i % 3
        at = n * x_ref.shape[1] + t * w
        return qkv_ref.at[:, at : at + w], qp_ref.at[t, :, n * w : n * w + w]

    operands = [(x_hbm, x_ref)] + [piece_of(i) for i in range(24)]
    operands += [(op_hbm, op_ref), (dm_hbm, dm_ref), (dp_hbm, dp_ref)]
    operands += [(gate_hbm, gate_ref), (up_hbm, up_ref)]
    loads = fetch(operands, load)
    greet_all(s, f)
    gather = SeqGather(x_ref, xs, *sems[:5])
    slices = ColGather(qp_ref, qw_ref, *sems[5:10])
    whole = WholeGather(op_ref, ow_ref, *sems[10:17])
    grads = SeqGather(dm_ref, dmo_ref, *sems[17:22])
    wide = ColGather(wp_ref, ww_ref, *sems[22:27])
    down = FsdpGather(dp_ref, dw_ref, *sems[27:30])
    swap = RowExchange(mix_ref, ho_ref, *sems[30:])

    def param(k):
        i = (me + k) % 32
        return remote(p_ref, got.at[me], psend.at[k], precv.at[k], dealer(i))

    @pl.loop(1, 32)
    def _(k):
        param(k).start()

    loads[0].wait()
    gather.start()
    for copy in loads[1:]:
        copy.wait()
    slices.start()
    got[me] = p_ref[...]

    @pl.loop(1, 32)
    def _(k):
        param(k).wait_recv()

    for i in range(16):
        n_ref[:, i * 128 : i * 128 + 128] = got[2 * i] + got[2 * i + 1]
    step = 16

    def norm(b):
        gain, shift = n_ref[0:1], n_ref[1:2]

        @pl.loop(0, x_ref.shape[0] // step)
        def _(i):
            r = row_at(i, step)
            normed, _ = normalize(xs[b, r].astype(jnp.float32))
            a_ref[b, r] = (normed * gain + shift).astype(jnp.bfloat16)

    def shift_of():
        parts = []
        for n in range(3):
            part = jnp.zeros((1, w), jnp.float32)
            for i in range(8):
                piece = n_ref[4 + n : 5 + n, i * w : i * w + w]
                part = part + jnp.where(s == i, piece, jnp.zeros_like(piece))
            parts.append(part)
        return jnp.concatenate(parts, 1)

    work = attend(
        a_ref,
        qw_ref,
        shift_of,
        freq_ref,
        orow_ref,
        ocol_ref,
        len_ref,
        mix_ref,
        pk_ref,
        lse_ref,
        rot,
        opk,
    )
    p = functools.partial

    def own():
        gather.own.wait()
        norm(s)

    def wide_start():
        for i in range(8):
            at = slice(i * lf, i * lf + lf)
            wp_ref[i, :, 0:lf] = gate_ref[:, at]
            wp_ref[i, :, lf : 2 * lf] = up_ref[:, at]
        wide.start()

    saved = [(a_ref, a_hbm), (qw_ref, qw_hbm), (pk_ref, pk_hbm), (lse_ref, lse_hbm)]
    saved.append((mix_ref, mix_hbm))
    stores = [pltpu.make_async_copy(u, v, store.at[i]) for i, (u, v) in enumerate(saved)]
    here = pl.ds(pl.multiple_of(s * 4, 4), 4)
    stores.append(pltpu.make_async_copy(ow_ref.at[here], or_hbm, store.at[5]))

    def swap_start():
        swap.start()
        for copy in stores[:5]:
            copy.start()

    def mixed_ready():
        swap.finish()
        whole.complete()
        stores[5].start()

    def project_out(j):
        cols = row_at(j, 512)
        total = jnp.zeros((rows, 512), jnp.float32)
        for k in range(8):
            right = jnp.concatenate([ow_ref[4 * k + q, :, cols] for q in range(4)], 0)
            total = total + dot(ho_ref[k], right)
        attn_ref[:, cols] = total
        res_ref[:, cols] = x_ref[:, cols].astype(jnp.float32) + total

    def second_norm():
        gain, shift = n_ref[2:3], n_ref[3:4]

        @tall(rows)
        def _(r):
            normed, _ = normalize(res_ref[r])
            second_ref[r] = (normed * gain + shift).astype(jnp.bfloat16)

    norms = [own]
    for i in range(4):
        norms.append(lambda i=i: norm(gather.cross(i)))
        if i < 3:
            norms.append(lambda i=i: norm(2 * gather.near(i + 1) + y))
    work = [slices.complete, work[0], idle, work[1], idle] + work[2:]
    queues = dict(
        g=gather.steps(),
        n=norms,
        s=slices.steps(),
        d=grads.steps(),
        v=wide.steps(),
        w=whole.steps(),
        f=[down.step],
        c=work,
        D=[grads.start],
        V=[wide_start],
        W=[whole.start],
        F=[down.start],
        X=[swap_start],
        Y=[mixed_ready],
        Q=[second_norm],
    )
    work[0:2] = [lambda first=work[0], then=work[1]: (first(), then())]
    left = perform(FORWARD_PLAN[:3], queues)
    left = looped(FORWARD_PLAN[3], "P", project_out, left)
    perform(FORWARD_PLAN[4:], left)
    for i in range(4):
        grads.cross(i)
    wide.complete()
    down.complete()
    for task in (slices, wide, whole, down, grads):
        task.finish()
    gather.finish(False)

    for copy in stores:
        copy.wait()

    @pl.loop(1, 32)
    def _(k):
        param(k).wait_send()


def forward(
    x, params, qkv, out_p, dm, gate, up, down_p, freq, orow, ocol, lengths, valid, collective
):
    rows, width = x.shape
    w3 = qkv.shape[1] // 8
    part, wide = gate.shape[0], gate.shape[1] // 4
    w = w3 // 3
    group = 8 * rows
    heads = w // HEAD_DIM

    def out(shape, dtype=jnp.bfloat16):
        return jax.ShapeDtypeStruct(shape, dtype)

    return pl.pallas_call(
        forward_kernel,
        out_shape=(
            out((8, rows, width)),
            out((width, w3)),
            out((8, width), jnp.float32),
            out((4,) + out_p.shape),
            out((valid, w3)),
            out((heads, valid, 1), jnp.float32),
            out((8, rows, width)),
            out((width, wide)),
            out((4,) + down_p.shape),
            out((8, rows, w)),
            out((rows, width), jnp.float32),
            out((rows, width), jnp.float32),
            out((rows, width)),
        ),
        in_specs=[HBM_SPEC, VMEM_SPEC] + [HBM_SPEC] * 6 + [VMEM_SPEC] * 3 + [SMEM_SPEC],
        out_specs=(ANY_SPEC,) * 2 + (VMEM_SPEC,) + (ANY_SPEC,) * 7 + (VMEM_SPEC,) * 3,
        scratch_shapes=[
            pltpu.VMEM((8, rows, width), jnp.bfloat16),
            pltpu.VMEM((width, w3), jnp.bfloat16),
            pltpu.VMEM((32,) + out_p.shape, jnp.bfloat16),
            pltpu.VMEM((8, rows, w), jnp.bfloat16),
            pltpu.VMEM((valid, w3), jnp.bfloat16),
            pltpu.VMEM((heads, valid, 1), jnp.float32),
            pltpu.VMEM((8, rows, w), jnp.bfloat16),
        ]
        + [pltpu.VMEM(v.shape, v.dtype) for v in (x, out_p, dm, gate, up, down_p)]
        + [
            pltpu.VMEM((8, rows, width), jnp.bfloat16),
            pltpu.VMEM((32, 8, 128), jnp.float32),
            pltpu.VMEM((group, w3), jnp.bfloat16),
            pltpu.VMEM((valid, w), jnp.bfloat16),
            pltpu.VMEM((8, part, w3), jnp.bfloat16),
            pltpu.VMEM((8, part, wide), jnp.bfloat16),
            DMA((30,)),
            DMA((6,)),
            DMA((32,)),
            DMA((32,)),
        ]
        + SeqGather.scratch()
        + ColGather.scratch()
        + WholeGather.scratch()
        + SeqGather.scratch()
        + ColGather.scratch()
        + FsdpGather.scratch()
        + RowExchange.scratch(),
        compiler_params=comm_params(collective),
    )(x, params, qkv, out_p, dm, gate, up, down_p, freq, orow, ocol, lengths)


def tall(rows, step=16):
    def wrap(fn):
        @pl.loop(0, rows // step)
        def _(i):
            fn(row_at(i, step))

    return wrap


def middle_kernel(
    cloc,
    n_ref,
    ww_hbm,
    dw_hbm,
    dm_hbm,
    res_hbm,
    rg_ref,
    vec_ref,
    mp_hbm,
    dg_hbm,
    h_hbm,
    ww_ref,
    dw_ref,
    dm_ref,
    res_ref,
    mp_ref,
    dg_ref,
    h_ref,
    big,
    c_ref,
    hid,
    act,
    part,
    second,
    load,
    store,
    *scratch,
):
    s, f, z, y = where_am_i()
    rows, width = cloc.shape
    lf = dw_ref.shape[0]
    operands = [(ww_hbm, ww_ref), (dw_hbm, dw_ref), (dm_hbm, dm_ref), (res_hbm, res_ref)]
    loads = fetch(operands, load)
    greet_columns(s, f)
    gather = SeqGather(cloc, c_ref, *scratch[:5])
    reduce = SeqReduce(part, second, *scratch[5:11])
    sums = ColSum(big, h_ref, *scratch[11:])
    gain = n_ref[2:3]
    gather.start()
    gather.own.wait()
    for copy in loads:
        copy.wait()

    def block(b):
        at = pl.ds(pl.multiple_of(b * rows, rows), rows)
        wide = dot(c_ref[b], ww_ref[...])
        gate, upper = wide[:, :lf], wide[:, lf:]
        hidden, sigma = mlp_forward(gate, upper)
        hid[at] = hidden
        grad = dot(dm_ref[b], dw_ref[...], 1, 1)
        gate_act, up_act = mlp_backward(grad, gate, upper, sigma)
        act[at] = jnp.concatenate([gate_act, up_act], 1)
        part[b] = dot(act[at], ww_ref[...], 1, 1).astype(jnp.bfloat16)

    def wide_grad(i):
        at = row_at(i, 256)
        left = jnp.concatenate([c_ref[b, :, at] for b in range(8)], 0)
        big[at, 0 : 2 * lf] = dot(left, act[...], 0, 0).astype(jnp.bfloat16)
        sums.send(i)

    def mlp_part(i):
        for k in range(2):
            b = 2 * i + k
            at = pl.ds(pl.multiple_of(b * rows, rows), rows)
            mp_ref[b] = dot(hid[at], dw_ref[...]).astype(jnp.bfloat16)

    def down_grad(i):
        cols = row_at(i, 256)
        right = jnp.concatenate([dm_ref[b, :, cols] for b in range(8)], 0)
        dg_ref[:, cols] = dot(hid[...], right, 0, 0).astype(jnp.bfloat16)

    def norm_backward():
        vec_ref[...] = jnp.zeros_like(vec_ref)

        @tall(rows)
        def _(r):
            grad = second[r]
            normed, rstd = normalize(res_ref[r])
            inner, gain_part, shift_part = norm_back(grad, normed, rstd, gain)
            rg_ref[r] = dm_ref[s, r].astype(jnp.float32) + inner
            vec_ref[0:1] += gain_part[None]
            vec_ref[1:2] += shift_part[None]

    p = functools.partial
    each = range(8)
    out_copies = [
        pltpu.make_async_copy(mp_ref, mp_hbm, store.at[0]),
        pltpu.make_async_copy(dg_ref, dg_hbm, store.at[1]),
        pltpu.make_async_copy(h_ref, h_hbm, store.at[2]),
    ]
    left = dict(
        g=gather.steps(),
        r=[p(reduce.send, k) for k in range(4)],
        t=reduce.steps(),
        e=[p(sums.step, i) for i in each],
        h=[p(sums.total, i) for i in each],
        z=[norm_backward],
        M=[out_copies[0].start],
        L=[out_copies[1].start],
        H=[out_copies[2].start],
    )
    left = looped(MIDDLE_PLAN[0], "b", lambda j: block(gather.turn(j)), left)
    left = looped(MIDDLE_PLAN[1], "a", wide_grad, left)
    left = looped(MIDDLE_PLAN[2], "m", mlp_part, left)
    left = looped(MIDDLE_PLAN[3], "l", down_grad, left)
    perform(MIDDLE_PLAN[4], left)
    for copy in out_copies:
        copy.wait()
    gather.finish(False)
    reduce.finish()
    sums.finish()


def middle(second, norms, wide_w, down_w, dm, res, collective):
    rows, width = second.shape
    lf = down_w.shape[0]
    group = 8 * rows
    part = width // 32

    def out(shape, dtype=jnp.bfloat16):
        return jax.ShapeDtypeStruct(shape, dtype)

    def vm(shape, dtype=jnp.bfloat16):
        return pltpu.VMEM(shape, dtype)

    wide = (rows, width)
    return pl.pallas_call(
        middle_kernel,
        out_shape=(
            out(wide, jnp.float32),
            out((8, width), jnp.float32),
            out((8,) + wide),
            out((lf, width)),
            out((8, part, 2 * lf)),
        ),
        in_specs=[VMEM_SPEC] * 2 + [HBM_SPEC] * 4,
        out_specs=(VMEM_SPEC,) * 2 + (ANY_SPEC,) * 3,
        scratch_shapes=[
            vm(wide_w.shape),
            vm(down_w.shape),
            vm(dm.shape),
            vm(wide, jnp.float32),
            vm((8,) + wide),
            vm((lf, width)),
            vm((8, part, 2 * lf)),
            vm((width, 2 * lf)),
            vm((8,) + wide),
            vm((group, lf)),
            vm((group, 2 * lf)),
            vm((8,) + wide),
            vm(wide, jnp.float32),
            DMA((4,)),
            DMA((3,)),
        ]
        + SeqGather.scratch(2)
        + SeqReduce.scratch(rows, width)
        + ColSum.scratch(part, 2 * lf),
        compiler_params=comm_params(collective),
    )(second, norms, wide_w, down_w, dm, res)


def backward_kernel(
    rg_ref,
    freq_ref,
    orow_ref,
    ocol_ref,
    len_ref,
    ow_hbm,
    mix_hbm,
    pk_hbm,
    lse_hbm,
    attn_hbm,
    res_hbm,
    mp_hbm,
    dg_hbm,
    h_hbm,
    g_ref,
    b_ref,
    lo_ref,
    sum_ref,
    got,
    down_hbm,
    out_ref,
    or_ref,
    mix_ref,
    pk_ref,
    lse_ref,
    attn_ref,
    res_ref,
    mp_ref,
    dg_ref,
    h_ref,
    down_ref,
    da,
    full,
    do_ref,
    og,
    mlp,
    dpk,
    dq,
    dk,
    dv,
    gpk,
    load,
    store,
    *scratch,
):
    s, f, z, y = where_am_i()
    rows, width = rg_ref.shape
    part = out_ref.shape[0]
    valid = pk_ref.shape[0]
    loads = fetch(
        [
            (ow_hbm, or_ref),
            (dg_hbm, dg_ref),
            (mp_hbm, mp_ref),
            (h_hbm, h_ref),
            (pk_hbm, pk_ref),
            (lse_hbm, lse_ref),
            (mix_hbm, mix_ref),
            (attn_hbm, attn_ref),
            (res_hbm, res_ref),
        ],
        load,
    )
    greet_columns(s, f)
    gather = SeqGather(da, full, *scratch[:5])
    reduce = SeqReduce(mp_ref, mlp, *scratch[5:11])
    swap = RowExchange(h_ref, got, *scratch[11:14])
    down = FsdpReduce(dg_ref, down_ref, *scratch[14:18])
    outer_sum = FsdpReduce(og, out_ref, *scratch[18:])

    @tall(rows)
    def _(r):
        da[r] = rg_ref[r].astype(jnp.bfloat16)

    gather.start()
    gather.own.wait()
    loads[0].wait()

    def block(b):
        at = pl.ds(pl.multiple_of(b * rows, rows), rows)
        out_rows = jnp.concatenate([or_ref[k] for k in range(4)], 0)
        do_ref[at] = dot(full[b], out_rows, 1, 1).astype(jnp.bfloat16)

    def before(copies, then):
        def run():
            for copy in copies:
                copy.wait()
            then()

        return run

    out_copies = [pltpu.make_async_copy(down_ref, down_hbm, store)]

    def down_total():
        down.total()
        out_copies[0].start()

    def out_grad(i):
        cols = slice(i * 256, i * 256 + 256)
        right = jnp.concatenate([full[b, :, cols] for b in range(8)], 0)
        value = dot(mix_ref[...], right, 0, 0).astype(jnp.bfloat16)
        for k in range(4):
            og[k, :, cols] = value[k * part : k * part + part]

    p = functools.partial
    work = attend_back(
        pk_ref,
        do_ref,
        lse_ref,
        freq_ref,
        orow_ref,
        ocol_ref,
        len_ref,
        g_ref,
        b_ref,
        dpk,
        dq,
        dk,
        dv,
        gpk,
    )
    def results():
        sum_ref[...] = jnp.zeros_like(sum_ref)

        step = 16

        @pl.loop(0, rows // step)
        def _(i):
            r = row_at(i, step)
            m = mlp[r]
            result = res_ref[r] + m
            lo_ref[r] = result.astype(jnp.bfloat16)
            pos = ocol_ref[pl.ds(pl.multiple_of(s * rows + i * step, step), step)]
            keep = jnp.where(pos < valid, 1.0, 0.0)
            for n, v in enumerate((result, attn_ref[r], m)):
                total = jnp.sum(jnp.sum(v * v, -1, keepdims=True) * keep, 0, keepdims=True)
                sum_ref[n : n + 1] += jnp.broadcast_to(total, (1, 128))

    sends = [p(reduce.send, k) for k in range(4)]
    outs = [p(out_grad, i) for i in range(8)]
    queues = dict(
        F=[before(loads[1:2], down.start)],
        f=[down.step],
        q=[down_total],
        g=gather.steps(),
        r=[before(loads[2:3], sends[0])] + sends[1:],
        t=reduce.steps(),
        X=[before(loads[3:4], swap.start)],
        Z=[swap.finish],
        c=[before(loads[4:6], work[0])] + work[1:],
        o=[before(loads[6:7], outs[0])] + outs[1:],
        O=[outer_sum.start],
        p=[outer_sum.step],
        P=[outer_sum.total],
        z=[before(loads[7:9], results)],
    )
    left = looped(BACKWARD_PLAN[0], "b", lambda j: block(gather.turn(j)), queues)
    perform(BACKWARD_PLAN[1], left)
    gather.finish(False)
    reduce.finish()
    down.finish()
    outer_sum.finish()
    for copy in out_copies:
        copy.wait()


def backward(
    rg, freq, orow, ocol, lengths, out_w, mixed, pk, lse, attn, res, mp, dg, h, collective
):
    rows, width = rg.shape
    group, w = mixed.shape
    valid = pk.shape[0]
    part = h.shape[1]

    def out(shape, dtype=jnp.float32):
        return jax.ShapeDtypeStruct(shape, dtype)

    def vm(shape, dtype=jnp.bfloat16):
        return pltpu.VMEM(shape, dtype)

    return pl.pallas_call(
        backward_kernel,
        out_shape=(
            out((group, 3 * w), jnp.bfloat16),
            out((1, 3 * w)),
            out((rows, width), jnp.bfloat16),
            out((8, 128)),
            out(h.shape, jnp.bfloat16),
            out(dg.shape[1:]),
            out((part, width)),
        ),
        in_specs=[VMEM_SPEC] * 4 + [SMEM_SPEC] + [HBM_SPEC] * 9,
        out_specs=(VMEM_SPEC,) * 4 + (ANY_SPEC,) * 2 + (VMEM_SPEC,),
        scratch_shapes=[
            vm((4, part, width)),
            vm(mixed.shape),
            vm(pk.shape),
            vm(lse.shape, jnp.float32),
            vm(attn.shape, jnp.float32),
            vm(res.shape, jnp.float32),
            vm(mp.shape),
            vm(dg.shape),
            vm(h.shape),
            vm(dg.shape[1:], jnp.float32),
            vm((rows, width)),
            vm((8, rows, width)),
            vm((group, w)),
            vm((4, part, width)),
            vm((rows, width), jnp.float32),
            vm((valid, w)),
            vm((valid, w), jnp.float32),
            vm((valid, w), jnp.float32),
            vm((valid, w), jnp.float32),
            vm((valid, 3 * w)),
            DMA((9,)),
            DMA,
        ]
        + SeqGather.scratch(2)
        + SeqReduce.scratch(rows, width)
        + RowExchange.scratch()
        + FsdpReduce.scratch(*dg.shape[1:])
        + FsdpReduce.scratch(part, width),
        compiler_params=comm_params(collective),
    )(rg, freq, orow, ocol, lengths, out_w, mixed, pk, lse, attn, res, mp, dg, h)


def last_kernel(
    g_ref,
    b_ref,
    n_ref,
    vec_ref,
    sum_ref,
    qw_hbm,
    a_hbm,
    x_hbm,
    rg_hbm,
    ig_ref,
    got,
    total_ref,
    qw_ref,
    a_ref,
    x_ref,
    rg_ref,
    load,
    part,
    first,
    grad,
    h,
    msg,
    inbox,
    vec,
    msend,
    mrecv,
    *scratch,
):
    s, f, z, y = where_am_i()
    me = s * 4 + f
    rows, width = x_ref.shape
    w3 = g_ref.shape[1]
    w = w3 // 3
    loads = fetch([(qw_hbm, qw_ref), (a_hbm, a_ref), (x_hbm, x_ref), (rg_hbm, rg_ref)], load)
    greet_all(s, f)
    loads[0].wait()
    reduce = SeqReduce(part, first, *scratch[:6])
    sums = ColSum(grad, h, *scratch[6:12])
    swap = RowExchange(h, got, *scratch[12:])

    def block(b):
        at = pl.ds(pl.multiple_of(b * rows, rows), rows)
        part[b] = dot(g_ref[at], qw_ref[...], 1, 1).astype(jnp.bfloat16)

    def block_at(j):
        far = j < 4
        zb = reduce.order(j % 4)
        block(2 * zb + jnp.where(far, 1 - y, y))

        @pl.when(far)
        def _():
            reduce.send(j)

    def qkv_grad(n):
        i = peer_at(s, 7 - n)
        at = row_at(i, 256)
        left = jnp.concatenate([a_ref[b, :, at] for b in range(8)], 0)
        grad[at] = dot(left, g_ref[...], 0, 0).astype(jnp.bfloat16)
        sums.send(i)

    def hand_over(k):
        sums.total(peer(s, k))
        if k:
            swap.piece(k).start()
        else:
            swap.mine.start()

    def message(k):
        i = (me + k) % 32
        return remote(msg.at[i // 2], inbox.at[k], msend.at[k], mrecv.at[k], dealer(i))

    def norm_backward():
        vec[0:2] = jnp.zeros((2, width), jnp.float32)
        vec[2:4] = vec_ref[0:2]
        gain = n_ref[0:1]
        loads[2].wait()
        loads[3].wait()

        @tall(rows)
        def _(r):
            normed, rstd = normalize(x_ref[r].astype(jnp.float32))
            inner, gain_part, shift_part = norm_back(first[r], normed, rstd, gain)
            ig_ref[r] = rg_ref[r] + inner
            vec[0:1] += gain_part[None]
            vec[1:2] += shift_part[None]

        lane = lax.broadcasted_iota(jnp.int32, (1, 128), 1)
        scalars = jnp.where(lane == 0, sum_ref[0:1], jnp.where(lane == 1, sum_ref[1:2], sum_ref[2:3]))
        for i in range(16):
            cols = slice(i * 128, i * 128 + 128)
            msg[i, 0:4] = vec[0:4, cols]
            msg[i, 4:5] = scalars
            at = (i % 2) * 128
            for n in range(3):
                piece = b_ref[0:1, n * w + at : n * w + at + 128]
                msg[i, 5 + n : 6 + n] = jnp.where(s == i // 2, piece, jnp.zeros_like(piece))

        @pl.loop(1, 32)
        def _(k):
            message(k).start()

    p = functools.partial
    ks = [7, 6, 5, 4, 3, 2, 1, 0]
    queues = dict(
        t=reduce.steps(),
        e=[lambda k=k: sums.step(peer(s, k)) for k in ks],
        h=[p(hand_over, k) for k in ks],
        z=[norm_backward],
        Z=[swap.finish],
    )
    pl.loop(0, 8)(block_at)
    loads[1].wait()
    left = looped(LAST_PLAN[0], "a", qkv_grad, queues)
    perform(LAST_PLAN[1], left)
    reduce.finish()
    sums.finish()
    total_ref[...] = msg[me // 2]

    @pl.loop(1, 32)
    def _(k):
        message(k).wait_recv()
        total_ref[...] += inbox[k]

    @pl.loop(1, 32)
    def _(k):
        message(k).wait_send()


def last(g, b, qkv_w, a, x, rg, norms, vec, sums, collective):
    rows, width = x.shape
    w3 = g.shape[1]
    pr = width // 32

    def out(shape, dtype=jnp.float32):
        return jax.ShapeDtypeStruct(shape, dtype)

    def vm(shape, dtype=jnp.bfloat16):
        return pltpu.VMEM(shape, dtype)

    return pl.pallas_call(
        last_kernel,
        out_shape=(out((rows, width)), out((8, pr, w3), jnp.bfloat16), out((8, 128))),
        in_specs=[VMEM_SPEC] * 5 + [HBM_SPEC] * 4,
        out_specs=(VMEM_SPEC, ANY_SPEC, VMEM_SPEC),
        scratch_shapes=[
            vm(qkv_w.shape),
            vm(a.shape),
            vm(x.shape),
            vm(rg.shape, jnp.float32),
            DMA((4,)),
            vm((8, rows, width)),
            vm((rows, width), jnp.float32),
            vm((width, w3)),
            vm((8, pr, w3)),
            vm((16, 8, 128), jnp.float32),
            vm((32, 8, 128), jnp.float32),
            vm((4, width), jnp.float32),
            DMA((32,)),
            DMA((32,)),
        ]
        + SeqReduce.scratch(rows, width)
        + ColSum.scratch(pr, w3)
        + RowExchange.scratch(),
        compiler_params=comm_params(collective),
    )(g, b, norms, vec, sums, qkv_w, a, x, rg)


def results_kernel(*refs):
    same, pieces, outs = refs[:4], refs[4:6], refs[6:13]
    bufs, wide, qkv, spread, load, store = refs[13:17], refs[17], refs[18], refs[19:22], refs[22], refs[23]
    moves = list(zip(same, bufs)) + [(pieces[0], wide), (pieces[1], qkv)]
    loads = fetch(moves, load)
    stores = [pltpu.make_async_copy(bufs[i], outs[i], store.at[i]) for i in range(4)]
    stores += [pltpu.make_async_copy(spread[i], outs[4 + i], store.at[4 + i]) for i in range(3)]
    for i in range(4):
        loads[i].wait()
        stores[i].start()
    loads[4].wait()
    lf = wide.shape[2] // 2
    for n in range(2):
        for i in range(8):
            value = wide[i, :, n * lf : n * lf + lf]
            spread[n][:, i * lf : i * lf + lf] = value.astype(jnp.float32)
        stores[4 + n].start()
    loads[5].wait()
    w = qkv.shape[2] // 3
    for i in range(8):
        for n in range(3):
            at = (n * 8 + i) * w
            spread[2][:, at : at + w] = qkv[i, :, n * w : n * w + w].astype(jnp.float32)
    stores[6].start()
    for copy in stores:
        copy.wait()


def results(same, wide, qkv):
    part = wide.shape[1]
    spread = [(part, 4 * wide.shape[2])] * 2 + [(part, 8 * qkv.shape[2])]
    return pl.pallas_call(
        results_kernel,
        out_shape=[jax.ShapeDtypeStruct(v.shape, v.dtype) for v in same]
        + [jax.ShapeDtypeStruct(v, jnp.float32) for v in spread],
        in_specs=[HBM_SPEC] * 6,
        out_specs=[ANY_SPEC] * 7,
        scratch_shapes=[pltpu.VMEM(v.shape, v.dtype) for v in (*same, wide, qkv)]
        + [pltpu.VMEM(v, jnp.float32) for v in spread]
        + [DMA((6,)), DMA((7,))],
        compiler_params=pltpu.CompilerParams(vmem_limit_bytes=63 << 20),
    )(*same, wide, qkv)


def line_body(
    hidden_in,
    ln1_gain,
    ln1_bias,
    qkv_weight,
    qkv_bias,
    out_weight,
    ln2_gain,
    ln2_bias,
    gate_weight,
    up_weight,
    down_weight,
    seq_lengths,
    deal_order,
    out_grad,
):
    rows = hidden_in.shape[1]
    width = hidden_in.shape[2]
    nseq = lax.axis_size("seq")
    nfsdp = lax.axis_size("fsdp")
    lw = width // nseq
    part = qkv_weight.shape[0]
    ff = gate_weight.shape[1]
    lf = ff // nseq
    seq_at, fsdp_at = lax.axis_index("seq"), lax.axis_index("fsdp")
    order = deal_order[0]
    group_rows = order.shape[0]
    valid_rows = group_rows * 5 // 8
    orow, ocol = order[None, :], order[:, None]
    lane = jnp.arange(128, dtype=jnp.int32) % HEAD_DIM % (ROT // 2)
    freq = 10000.0 ** (-2.0 * lane.astype(jnp.float32) / ROT)
    freq = freq[None, :]
    params = jnp.stack([ln1_gain, ln1_bias, ln2_gain, ln2_bias, *qkv_bias])
    params = jnp.pad(params.astype(jnp.float32), ((0, 1), (0, 64)))
    params = jnp.where(fsdp_at % 2 == 0, params, jnp.roll(params, part, 1))
    (
        first_in,
        qkv_w,
        norms,
        out_rows,
        packed,
        lse,
        mlp_grad,
        wide_w,
        down_w,
        mixed,
        attn,
        resid,
        second,
    ) = forward(
        hidden_in[0],
        params,
        qkv_weight,
        out_weight,
        out_grad[0],
        gate_weight,
        up_weight,
        down_weight,
        freq,
        orow,
        ocol,
        seq_lengths,
        valid_rows,
        1,
    )
    resid_grad, norm2_grads, mlp_part, down_part, wide_sum = middle(
        second, norms, wide_w, down_w.reshape(lf, width), mlp_grad, resid, 3
    )
    qkv_act, bias_sums, result, sums, wide_pieces, down_grad, out_grad_w = backward(
        resid_grad,
        freq,
        orow,
        ocol,
        seq_lengths,
        out_rows,
        mixed.reshape(group_rows, lw),
        packed,
        lse,
        attn,
        resid,
        mlp_part,
        down_part.reshape(nfsdp, -1, width),
        wide_sum,
        4,
    )
    input_grad, qkv_pieces, total = last(
        qkv_act, bias_sums, qkv_w, first_in, hidden_in[0], resid_grad, norms, norm2_grads, sums, 5
    )
    result, input_grad, down_grad, out_grad_w, gate_grad, up_grad, qkv_grad = results(
        (result, input_grad, down_grad, out_grad_w), wide_pieces, qkv_pieces
    )
    count = valid_rows * nfsdp * width
    rms = jnp.sqrt(total[4, :3] / count)
    halves = lax.dynamic_slice_in_dim(total, (fsdp_at % 2) * part, part, 1)
    shards = halves[:4]
    qkv_bias_grad = halves[5:8]
    return (
        result[None],
        input_grad[None],
        shards[0],
        shards[1],
        qkv_grad,
        qkv_bias_grad,
        out_grad_w,
        shards[2],
        shards[3],
        gate_grad,
        up_grad,
        down_grad,
        rms,
    )


def solution(mesh):
    in_specs = (
        P("fsdp", "seq", None),
        P(("seq", "fsdp")),
        P(("seq", "fsdp")),
        P(("seq", "fsdp"), None),
        P(None, ("seq", "fsdp")),
        P(("seq", "fsdp"), None),
        P(("seq", "fsdp")),
        P(("seq", "fsdp")),
        P(("seq", "fsdp"), None),
        P(("seq", "fsdp"), None),
        P(("seq", "fsdp"), None),
        P("fsdp", None),
        P("fsdp", None),
        P("fsdp", "seq", None),
    )
    out_specs = (
        P("fsdp", "seq", None),
        P("fsdp", "seq", None),
        P(("seq", "fsdp")),
        P(("seq", "fsdp")),
        P(("seq", "fsdp"), None),
        P(None, ("seq", "fsdp")),
        P(("seq", "fsdp"), None),
        P(("seq", "fsdp")),
        P(("seq", "fsdp")),
        P(("seq", "fsdp"), None),
        P(("seq", "fsdp"), None),
        P(("seq", "fsdp"), None),
        P(),
    )
    line = dict(mesh.shape) == {"seq": 8, "fsdp": 4}
    return jax.shard_map(
        line_body if line else body,
        mesh=mesh,
        in_specs=in_specs,
        out_specs=out_specs,
        check_vma=False,
    )
```

```python
import functools

import jax
import jax.numpy as jnp
from jax import lax
from jax.experimental import pallas as pl
from jax.experimental.pallas import tpu as pltpu
from jax.sharding import PartitionSpec as P

HEAD_DIM = 64
ROT = 16


EPS = 1e-05


def normalize(values):
    center = values - jnp.mean(values, -1, keepdims=True)
    spread = jnp.mean(center * center, -1, keepdims=True)
    rstd = lax.rsqrt(spread + EPS)
    return (center * rstd, rstd)


def norm_back(grad, normed, rstd, gain):
    scaled = grad * gain
    inner = (
        scaled
        - jnp.mean(scaled, -1, keepdims=True)
        - normed * jnp.mean(scaled * normed, -1, keepdims=True)
    )
    return (rstd * inner, jnp.sum(grad * normed, 0), jnp.sum(grad, 0))


def segment_of(pos, lengths):
    nseg = lengths.shape[0]
    ends = jnp.cumsum(lengths)
    seg = jnp.sum((pos[:, None] >= ends[None, :]).astype(jnp.int32), 1)
    starts = jnp.concatenate([jnp.zeros((1,), jnp.int32), ends[:-1]])
    start = jnp.sum(
        jnp.where(seg[:, None] == jnp.arange(nseg, dtype=jnp.int32)[None, :], starts[None, :], 0), 1
    )
    start = jnp.where(seg < nseg, start, pos)
    return (seg, start)


def rotate(values, rel, sign):
    count = values.shape[0]
    view = values.reshape(count, -1, HEAD_DIM)
    half = ROT // 2
    freq = 10000.0 ** (-2.0 * jnp.arange(half, dtype=jnp.float32) / ROT)
    angle = rel[:, None] * freq[None, :]
    cosine = jnp.cos(angle)[:, None, :]
    sine = jnp.sin(angle)[:, None, :]
    first = view[..., :half]
    second = view[..., half:ROT]
    turned = jnp.concatenate(
        [
            first * cosine - sign * second * sine,
            second * cosine + sign * first * sine,
            view[..., ROT:],
        ],
        -1,
    )
    return turned.reshape(count, -1)


def outer(left, right):
    return lax.dot_general(
        left, right, (((0,), (0,)), ((), ())), preferred_element_type=jnp.float32
    )


def times(left, right):
    return jnp.dot(left, right, preferred_element_type=jnp.float32)


def times_transposed(left, right):
    return lax.dot_general(
        left, right, (((1,), (1,)), ((), ())), preferred_element_type=jnp.float32
    )


def mlp_forward(gate, upper):
    sigma = jax.nn.sigmoid(gate)
    return ((gate * sigma * upper).astype(jnp.bfloat16), sigma)


def mlp_backward(hidden_grad, gate, upper, sigma):
    up_act = (hidden_grad * gate * sigma).astype(jnp.bfloat16)
    gate_act = (hidden_grad * upper * sigma * (1.0 + gate * (1.0 - sigma))).astype(jnp.bfloat16)
    return (gate_act, up_act)


def body(
    hidden_in,
    ln1_gain,
    ln1_bias,
    qkv_weight,
    qkv_bias,
    out_weight,
    ln2_gain,
    ln2_bias,
    gate_weight,
    up_weight,
    down_weight,
    seq_lengths,
    deal_order,
    out_grad,
):
    rows = hidden_in.shape[1]
    width = hidden_in.shape[2]
    nseq = lax.axis_size("seq")
    nfsdp = lax.axis_size("fsdp")
    local_width = width // nseq
    part = qkv_weight.shape[0]
    ff = gate_weight.shape[1]
    local_ff = ff // nseq
    stream = hidden_in[0].astype(jnp.float32)
    cotangent = out_grad[0].astype(jnp.float32)
    order = deal_order[0]
    lengths = seq_lengths[0]
    nseg = lengths.shape[0]
    group_rows = order.shape[0]
    valid_rows = group_rows * 5 // 8
    longest = valid_rows * 4 // 5
    blk = min(512, group_rows)
    keys = min(group_rows, longest + blk)
    nblocks = group_rows // blk
    scale = HEAD_DIM ** (-0.5)
    local_pos = lax.dynamic_slice_in_dim(order, lax.axis_index("seq") * rows, rows)
    valid = (local_pos < valid_rows).astype(jnp.float32)[:, None]
    dealt_seg, dealt_start = segment_of(order, lengths)
    rel = (order - dealt_start).astype(jnp.float32)
    inverse = (
        jnp.zeros((group_rows,), jnp.int32).at[order].set(jnp.arange(group_rows, dtype=jnp.int32))
    )
    seg_p, start_p = segment_of(jnp.arange(group_rows, dtype=jnp.int32), lengths)

    def gather_rows(values):
        return lax.all_gather(values, "seq", axis=0, tiled=True)

    def scatter_rows(partial):
        return lax.psum_scatter(
            partial.astype(jnp.bfloat16), "seq", scatter_dimension=0, tiled=True
        ).astype(jnp.float32)

    def column_slice(weight, blocks):
        cols = weight.shape[1] // (blocks * nseq)
        view = weight.reshape(part, blocks, nseq, cols).transpose(2, 0, 1, 3)
        mine = lax.all_to_all(
            view.reshape(nseq * part, blocks * cols), "seq", split_axis=0, concat_axis=0, tiled=True
        )
        full = lax.all_gather(mine.reshape(nseq, part, blocks * cols), "fsdp", axis=1)
        return full.reshape(width, blocks * cols)

    def row_slice(weight):
        return lax.all_gather(weight, "fsdp", axis=0, tiled=True)

    def column_shard(grad, blocks):
        cols = grad.shape[1] // blocks
        view = grad.astype(jnp.bfloat16).reshape(nseq, nfsdp, part, blocks * cols)
        mine = lax.psum_scatter(view.transpose(1, 0, 2, 3), "fsdp", scatter_dimension=0)
        got = lax.all_to_all(
            mine.reshape(nseq * part, blocks * cols), "seq", split_axis=0, concat_axis=0, tiled=True
        )
        view = got.reshape(nseq, part, blocks, cols).transpose(1, 2, 0, 3)
        return view.reshape(part, -1).astype(jnp.float32)

    def row_shard(grad):
        return lax.psum_scatter(
            grad.astype(jnp.bfloat16), "fsdp", scatter_dimension=0, tiled=True
        ).astype(jnp.float32)

    def to_pack(values):
        heads_here = values.shape[1] // HEAD_DIM
        return values[inverse].reshape(group_rows, heads_here, HEAD_DIM)

    def window(index, packed):
        query_p, key_p, value_p = packed
        first = index * blk
        key_first = jnp.clip(jnp.minimum(start_p[first], group_rows - keys), 0, group_rows - keys)
        qpos = first + jnp.arange(blk, dtype=jnp.int32)
        kpos = key_first + jnp.arange(keys, dtype=jnp.int32)
        qseg = lax.dynamic_slice_in_dim(seg_p, first, blk)
        kseg = lax.dynamic_slice_in_dim(seg_p, key_first, keys)
        allowed = (qseg[:, None] == kseg[None, :]) & (qseg[:, None] < nseg) & (
            kpos[None, :] <= qpos[:, None]
        ) | (kpos[None, :] == qpos[:, None])
        qblock = lax.dynamic_slice_in_dim(query_p, first, blk)
        kblock = lax.dynamic_slice_in_dim(key_p, key_first, keys)
        vblock = lax.dynamic_slice_in_dim(value_p, key_first, keys)
        scores = (
            jnp.einsum("qhd,khd->hqk", qblock, kblock, preferred_element_type=jnp.float32) * scale
        )
        scores = jnp.where(allowed[None], scores, -1e30)
        return (first, key_first, qblock, kblock, vblock, scores)

    both = ("seq", "fsdp")
    norms = lax.all_gather(
        jnp.stack([ln1_gain, ln1_bias, ln2_gain, ln2_bias, *qkv_bias]), both, axis=1, tiled=True
    )
    gain1, shift1, gain2, shift2 = norms[:4].astype(jnp.float32)
    qkv_shift = lax.dynamic_slice_in_dim(
        norms[4:], lax.axis_index("seq") * local_width, local_width, 1
    )
    qkv_shift = qkv_shift.reshape(-1).astype(jnp.float32)

    normed1, rstd1 = normalize(stream)
    first_local = (normed1 * gain1 + shift1).astype(jnp.bfloat16)
    first_in = gather_rows(first_local)
    qkv_w = column_slice(qkv_weight, 3)
    qkv = times(first_in, qkv_w) + qkv_shift
    query = rotate(qkv[:, :local_width], rel, 1.0).astype(jnp.bfloat16)
    keyset = rotate(qkv[:, local_width : 2 * local_width], rel, 1.0).astype(jnp.bfloat16)
    valueset = qkv[:, 2 * local_width :].astype(jnp.bfloat16)
    packed = (to_pack(query), to_pack(keyset), to_pack(valueset))

    def attend_block(index):
        first, key_first, qblock, kblock, vblock, scores = window(index, packed)
        top = jnp.max(scores, -1, keepdims=True)
        expo = jnp.exp(scores - top)
        total = jnp.sum(expo, -1, keepdims=True)
        probs = (expo / total).astype(jnp.bfloat16)
        mixed = jnp.einsum("hqk,khd->qhd", probs, vblock, preferred_element_type=jnp.float32)
        return (mixed.astype(jnp.bfloat16), (top + jnp.log(total))[..., 0])

    mixed_all, lse_all = lax.map(attend_block, jnp.arange(nblocks, dtype=jnp.int32))
    mixed = mixed_all.reshape(group_rows, -1)[order]
    heads_out = lax.all_to_all(mixed, "seq", split_axis=0, concat_axis=1, tiled=True)
    out_w = lax.all_gather(out_weight, both, axis=0, tiled=True)
    out_rows = row_slice(out_weight)
    attn = times(heads_out, out_w)
    resid = stream + attn
    normed2, rstd2 = normalize(resid)
    second_in = gather_rows((normed2 * gain2 + shift2).astype(jnp.bfloat16))
    gate_w = column_slice(gate_weight, 1)
    up_w = column_slice(up_weight, 1)
    down_w = row_slice(down_weight)
    gate = times(second_in, gate_w)
    upper = times(second_in, up_w)
    hidden, sigma = mlp_forward(gate, upper)
    mlp = scatter_rows(times(hidden, down_w))
    result = resid + mlp

    mlp_grad = gather_rows(out_grad[0])
    hidden_grad = times_transposed(mlp_grad, down_w)
    gate_act, up_act = mlp_backward(hidden_grad, gate, upper, sigma)
    second_grad = scatter_rows(times_transposed(gate_act, gate_w) + times_transposed(up_act, up_w))
    down_grad = row_shard(outer(hidden, mlp_grad))
    gate_grad = column_shard(outer(second_in, gate_act), 1)
    up_grad = column_shard(outer(second_in, up_act), 1)
    resid_part, gain2_grad, shift2_grad = norm_back(second_grad, normed2, rstd2, gain2)
    resid_grad = cotangent + resid_part

    attn_grad = gather_rows(resid_grad.astype(jnp.bfloat16))
    out_grad_w = row_shard(outer(mixed, attn_grad))
    mixed_grad_p = to_pack(times_transposed(attn_grad, out_rows).astype(jnp.bfloat16))

    def back_block(index, carry):
        query_acc, key_acc, value_acc = carry
        first, key_first, qblock, kblock, vblock, scores = window(index, packed)
        probs = jnp.exp(scores - lse_all[index][:, :, None])
        dblock = lax.dynamic_slice_in_dim(mixed_grad_p, first, blk)
        value_part = jnp.einsum(
            "hqk,qhd->khd", probs.astype(jnp.bfloat16), dblock, preferred_element_type=jnp.float32
        )
        prob_grad = jnp.einsum("qhd,khd->hqk", dblock, vblock, preferred_element_type=jnp.float32)
        inner = jnp.sum(probs * prob_grad, -1, keepdims=True)
        score_grad = (probs * (prob_grad - inner)).astype(jnp.bfloat16)
        query_part = (
            jnp.einsum("hqk,khd->qhd", score_grad, kblock, preferred_element_type=jnp.float32)
            * scale
        )
        key_part = (
            jnp.einsum("hqk,qhd->khd", score_grad, qblock, preferred_element_type=jnp.float32)
            * scale
        )
        query_acc = lax.dynamic_update_slice_in_dim(query_acc, query_part, first, 0)
        key_old = lax.dynamic_slice_in_dim(key_acc, key_first, keys)
        key_acc = lax.dynamic_update_slice_in_dim(key_acc, key_old + key_part, key_first, 0)
        value_old = lax.dynamic_slice_in_dim(value_acc, key_first, keys)
        value_acc = lax.dynamic_update_slice_in_dim(value_acc, value_old + value_part, key_first, 0)
        return (query_acc, key_acc, value_acc)

    zeros = jnp.zeros(packed[0].shape, jnp.float32)
    query_acc, key_acc, value_acc = lax.fori_loop(0, nblocks, back_block, (zeros, zeros, zeros))

    def to_dealt(values):
        return values.astype(jnp.bfloat16).reshape(group_rows, -1)[order]

    qkv_act = jnp.concatenate(
        [
            rotate(to_dealt(query_acc).astype(jnp.float32), rel, -1.0).astype(jnp.bfloat16),
            rotate(to_dealt(key_acc).astype(jnp.float32), rel, -1.0).astype(jnp.bfloat16),
            to_dealt(value_acc),
        ],
        1,
    )
    first_grad = scatter_rows(times_transposed(qkv_act, qkv_w))
    qkv_grad = column_shard(outer(first_in, qkv_act), 3)
    qkv_bias_grad = lax.psum_scatter(
        jnp.sum(qkv_act.astype(jnp.float32), 0).reshape(3, nfsdp, -1),
        "fsdp",
        scatter_dimension=1,
    )
    input_part, gain1_grad, shift1_grad = norm_back(first_grad, normed1, rstd1, gain1)
    input_grad = resid_grad + input_part

    norm_grads = lax.psum(
        (
            gain1_grad,
            shift1_grad,
            gain2_grad,
            shift2_grad,
            jnp.sum(valid * result * result),
            jnp.sum(valid * attn * attn),
            jnp.sum(valid * mlp * mlp),
        ),
        both,
    )
    count = valid_rows * nfsdp * width
    rms = jnp.sqrt(jnp.stack(norm_grads[4:]) / count)
    mine = (lax.axis_index("seq") * nfsdp + lax.axis_index("fsdp")) * part
    norm_shards = [lax.dynamic_slice_in_dim(value, mine, part) for value in norm_grads[:4]]
    return (
        result.astype(jnp.bfloat16)[None],
        input_grad[None],
        norm_shards[0],
        norm_shards[1],
        qkv_grad,
        qkv_bias_grad,
        out_grad_w,
        norm_shards[2],
        norm_shards[3],
        gate_grad,
        up_grad,
        down_grad,
        rms,
    )


MESH = pl.DeviceIdType.MESH
QB = 128
NEG = -1e30
CH = 2
VMEM_SPEC = pl.BlockSpec(memory_space=pltpu.VMEM)
SMEM_SPEC = pl.BlockSpec(memory_space=pltpu.SMEM)
ANY_SPEC = pl.BlockSpec(memory_space=pl.ANY)
HBM_SPEC = pl.BlockSpec(memory_space=pltpu.HBM)
DMA = pltpu.SemaphoreType.DMA


def comm_params(collective, limit=63):
    return pltpu.CompilerParams(
        collective_id=collective, has_side_effects=True, vmem_limit_bytes=limit << 20
    )


def where_am_i():
    s = lax.axis_index("seq")
    f = lax.axis_index("fsdp")
    return s, f, s // 2, s % 2


def remote(src, dst, send, recv, device):
    return pltpu.make_async_remote_copy(
        src, dst, send, recv, device_id=device, device_id_type=MESH
    )


def flip(v, bit):
    return v + bit * (1 - 2 * ((v // bit) % 2))


def peer(s, k):
    for bit in (1, 2, 4):
        if k & bit:
            s = flip(s, bit)
    return s


def peer_at(s, k):
    for bit in (1, 2, 4):
        s = s + ((k // bit) % 2) * bit * (1 - 2 * ((s // bit) % 2))
    return s


def dealer(i):
    return (i // 4, i % 4)


def greet_all(s, f):
    bar = pltpu.get_barrier_semaphore()
    me = s * 4 + f

    @pl.loop(1, 32)
    def _(k):
        pl.semaphore_signal(bar, inc=1, device_id=dealer((me + k) % 32), device_id_type=MESH)

    pl.semaphore_wait(bar, 31)


def greet_line(s, f, z, y):
    bar = pltpu.get_barrier_semaphore()
    pl.semaphore_signal(bar, inc=1, device_id=(flip(s, 1), f), device_id_type=MESH)

    @pl.when(z > 0)
    def _():
        pl.semaphore_signal(bar, inc=1, device_id=(s - 2, f), device_id_type=MESH)

    @pl.when(z < 3)
    def _():
        pl.semaphore_signal(bar, inc=1, device_id=(s + 2, f), device_id_type=MESH)

    edge = jnp.where((z == 0) | (z == 3), 1, 0)
    pl.semaphore_wait(bar, 3 - edge)


def greet_columns(s, f):
    bar = pltpu.get_barrier_semaphore()
    for k in range(1, 8):
        pl.semaphore_signal(bar, inc=1, device_id=(peer(s, k), f), device_id_type=MESH)
    pl.semaphore_signal(bar, inc=1, device_id=(s, flip(f, 1)), device_id_type=MESH)
    pl.semaphore_signal(bar, inc=1, device_id=(s, flip(f, 2)), device_id_type=MESH)
    pl.semaphore_wait(bar, 9)


def adder(dst, srcs, step=16):
    @pl.loop(0, dst.shape[0] // step)
    def _(i):
        r = pl.ds(pl.multiple_of(i * step, step), step)
        total = srcs[0][r].astype(jnp.float32)
        for v in srcs[1:]:
            total = total + v[r].astype(jnp.float32)
        dst[r] = total.astype(dst.dtype)


class SeqGather:
    @staticmethod
    def scratch(parts=1):
        return [DMA, DMA((8, parts)), DMA((4, parts)), DMA((4, parts)), DMA((4, parts))]

    def __init__(self, x, o, own, recv, sy, su, sd):
        self.x, self.o, self.recv, self.sy, self.su, self.sd = x, o, recv, sy, su, sd
        self.s, self.f, self.z, self.y = where_am_i()
        self.parts = recv.shape[1]
        self.other = flip(self.s, 1)
        self.own = pltpu.make_async_copy(x, o.at[self.s], own)

    def rows(self, c):
        n = self.x.shape[0] // self.parts
        return pl.ds(c * n, n)

    def at(self, zb):
        return 2 * zb + self.y

    def copy(self, zb, c, own, sems, to):
        b, r = self.at(zb), self.rows(c)
        src = self.x.at[r] if own else self.o.at[b, r]
        return remote(src, self.o.at[b, r], sems.at[zb, c], self.recv.at[b, c], (to, self.f))

    def ysend(self, zb, c, own=False):
        return self.copy(zb, c, own, self.sy, self.other)

    def usend(self, zb, c, own=False):
        return self.copy(zb, c, own, self.su, self.s + 2)

    def dsend(self, zb, c, own=False):
        return self.copy(zb, c, own, self.sd, self.s - 2)

    def arrived(self, b, c):
        o = self.o.at[b, self.rows(c)]
        return remote(o, o, self.sy.at[0, c], self.recv.at[b, c], (self.other, self.f))

    def start(self):
        for c in range(self.parts):

            @pl.when(self.z < 3)
            def _():
                self.usend(self.z, c, True).start()

            @pl.when(self.z > 0)
            def _():
                self.dsend(self.z, c, True).start()

            self.ysend(self.z, c, True).start()
        self.own.start()

    def near(self, i):
        low = jnp.where(self.z < 2, self.z, 3 - self.z)
        base = jnp.where(low == 0, i, jnp.where(i < 2, 1 - i, i))
        return jnp.where(self.z < 2, base, 3 - base)

    def arrive(self, i, c=0):
        zb = self.near(i)
        self.arrived(self.at(zb), c).wait_recv()

        @pl.when((zb < self.z) & (self.z < 3))
        def _():
            self.usend(zb, c).start()

        @pl.when((zb > self.z) & (self.z > 0))
        def _():
            self.dsend(zb, c).start()

        self.ysend(zb, c).start()

    def column(self, i):
        return self.at(self.near(i))

    def cross(self, i):
        b = 2 * self.near(i) + 1 - self.y
        for c in range(self.parts):
            self.arrived(b, c).wait_recv()
        return b

    def steps(self):
        return [functools.partial(self.arrive, i, c) for i in (1, 2, 3) for c in range(self.parts)]

    def turn(self, j):
        i = (j + 1) // 2
        column = (j == 0) | ((j % 2 == 1) & (j < 7))
        other = jnp.where(j == 7, 3, j // 2 - 1)

        @pl.when(jnp.logical_not(column))
        def _():
            self.cross(other)

        zb = self.near(jnp.where(column, i, other))
        return 2 * zb + jnp.where(column, self.y, 1 - self.y)

    def finish(self, own=True):
        if own:
            self.own.wait()
        for c in range(self.parts):
            for zb in range(4):
                self.ysend(zb, c).wait_send()

                @pl.when((self.z < 3) & (zb <= self.z))
                def _():
                    self.usend(zb, c).wait_send()

                @pl.when((self.z > 0) & (zb >= self.z))
                def _():
                    self.dsend(zb, c).wait_send()


class EvenGather(SeqGather):
    @staticmethod
    def scratch():
        return SeqGather.scratch(2) + [DMA((2,))]

    def __init__(self, x, o, own, recv, sy, su, sd, side):
        super().__init__(x, o, own, recv, sy, su, sd)
        self.side_sems = side

    def arrive(self, i, c=0):
        zb = self.near(i)
        self.arrived(self.at(zb), c).wait_recv()

        @pl.when((zb < self.z) & (self.z < 3))
        def _():
            self.usend(zb, c).start()

        @pl.when((zb > self.z) & (self.z > 0))
        def _():
            self.dsend(zb, c).start()

        if c == 0:
            self.ysend(zb, c).start()
        else:

            @pl.when((zb == 1) | (zb == 2))
            def _():
                self.ysend(zb, c).start()

    def along(self, e):
        b, r = 2 * e + 1 - self.y, self.rows(1)
        v = self.o.at[b, r]
        to = self.s + 2 if e == 0 else self.s - 2
        return remote(v, v, self.side_sems.at[e // 3], self.recv.at[b, 1], (to, self.f))

    def pass_along(self, e):
        self.arrived(2 * e + 1 - self.y, 1).wait_recv()

        @pl.when(self.z != 3 - e)
        def _():
            self.along(e).start()

    def lead(self):
        for e in (0, 3):

            @pl.when(self.z == e)
            def _():
                self.pass_along(e)

    def follow(self):
        for first in (True, False):
            for e in (0, 3):
                closer = (self.z < 2) == (e == 0)

                @pl.when((self.z != e) & (closer == first))
                def _():
                    self.pass_along(e)

    def cross(self, i):
        zb = self.near(i)
        b = 2 * zb + 1 - self.y
        self.arrived(b, 0).wait_recv()

        @pl.when((zb == 1) | (zb == 2))
        def _():
            self.arrived(b, 1).wait_recv()

        return b

    def finish(self):
        for c in range(2):
            for zb in range(4):
                if c == 0 or zb in (1, 2):
                    self.ysend(zb, c).wait_send()
                else:

                    @pl.when(self.z == zb)
                    def _():
                        self.ysend(zb, c).wait_send()

                @pl.when((self.z < 3) & (zb <= self.z))
                def _():
                    self.usend(zb, c).wait_send()

                @pl.when((self.z > 0) & (zb >= self.z))
                def _():
                    self.dsend(zb, c).wait_send()

        for e in (0, 3):

            @pl.when(self.z != 3 - e)
            def _():
                self.along(e).wait_send()


class SeqReduce:
    @staticmethod
    def scratch(rows, w):
        big = [pltpu.VMEM((n, rows, w), jnp.bfloat16) for n in (4, 5)]
        return big + [DMA((4, CH)), DMA((5, CH)), DMA((4, CH)), DMA((4, CH))]

    def __init__(self, p, o, ybuf, got, ry, rl, sy, sl):
        self.p, self.o, self.ybuf, self.got = p, o, ybuf, got
        self.ry, self.rl, self.sy, self.sl = ry, rl, sy, sl
        self.s, self.f, self.z, self.y = where_am_i()
        self.other = flip(self.s, 1)
        self.ch = p.shape[1] // CH

    def order(self, k):
        low = jnp.where(self.z < 2, self.z, 3 - self.z)
        inner = jnp.where(k == 0, 3, jnp.where(k == 1, 0, jnp.where(k == 2, 2, 1)))
        base = jnp.where(low == 0, 3 - k, inner)
        return jnp.where(self.z < 2, base, 3 - base)

    def rows(self, c):
        return pl.ds(c * self.ch, self.ch)

    def ysend(self, zb, c):
        r = self.rows(c)
        src = self.p.at[2 * zb + 1 - self.y, r]
        dst = self.ybuf.at[zb, r]
        return remote(src, dst, self.sy.at[zb, c], self.ry.at[zb, c], (self.other, self.f))

    def usend(self, zb, c):
        r = self.rows(c)
        src, dst = self.ybuf.at[zb, r], self.got.at[zb, r]
        return remote(src, dst, self.sl.at[zb, c], self.rl.at[zb, c], (self.s + 2, self.f))

    def dsend(self, zb, c):
        r = self.rows(c)
        slot = jnp.where(zb == self.z - 1, 4, zb)
        src, dst = self.ybuf.at[zb, r], self.got.at[slot, r]
        return remote(src, dst, self.sl.at[zb, c], self.rl.at[slot, c], (self.s - 2, self.f))

    def landed(self, slot, c):
        v = self.got.at[slot, self.rows(c)]
        return remote(v, v, self.sl.at[0, c], self.rl.at[slot, c], (self.other, self.f))

    def send(self, k):
        for c in range(CH):
            self.ysend(self.order(k), c).start()

    def start(self):
        for k in range(4):
            self.send(k)

    def step(self, k, c):
        z, zb, r = self.z, self.order(k), self.rows(c)
        self.ysend(zb, c).wait_recv()
        a, b = self.p.at[2 * zb + self.y, r], self.ybuf.at[zb, r]
        u, d = self.got.at[zb, r], self.got.at[4, r]
        alone = ((zb > z) & (z == 0)) | ((zb < z) & (z == 3))

        @pl.when(alone)
        def _():
            adder(b, [a, b])

        @pl.when((zb != z) & jnp.logical_not(alone))
        def _():
            self.landed(zb, c).wait_recv()
            adder(b, [a, b, u])

        @pl.when(zb > z)
        def _():
            self.usend(zb, c).start()

        @pl.when(zb < z)
        def _():
            self.dsend(zb, c).start()

        @pl.when(zb == z)
        def _():
            o = self.o.at[r]

            @pl.when(z == 0)
            def _():
                self.landed(4, c).wait_recv()
                adder(o, [a, b, d])

            @pl.when(z == 3)
            def _():
                self.landed(zb, c).wait_recv()
                adder(o, [a, b, u])

            @pl.when((z > 0) & (z < 3))
            def _():
                self.landed(zb, c).wait_recv()
                self.landed(4, c).wait_recv()
                adder(o, [a, b, u, d])

    def steps(self):
        return [functools.partial(self.step, k, c) for k in range(4) for c in range(CH)]

    def finish(self):
        for zb in range(4):
            for c in range(CH):
                self.ysend(zb, c).wait_send()

                @pl.when(zb != self.z)
                def _():
                    self.usend(zb, c).wait_send()


class ColGather:
    @staticmethod
    def scratch():
        return [DMA, DMA((8, 4)), DMA((8,)), DMA((8, 2)), DMA((8,))]

    def __init__(self, x, o, own, recv, direct, core, xs):
        self.x, self.o, self.own, self.recv = x, o, own, recv
        self.direct, self.core, self.xs = direct, core, xs
        self.s, self.f, _, _ = where_am_i()
        self.fc, self.fx = flip(self.f, 1), flip(self.f, 2)
        self.fd = flip(self.fc, 2)
        self.mine = pltpu.make_async_copy(x.at[self.s], self.piece(self.s, self.f), own)

    def piece(self, t, ff):
        r = self.x.shape[1]
        return self.o.at[pl.ds(pl.multiple_of((t * 4 + ff) * r, r), r)]

    def send_direct(self, k):
        s, f, t = self.s, self.f, peer(self.s, k)
        return remote(self.x.at[t], self.piece(s, f), self.direct.at[k], self.recv.at[s, f], (t, f))

    def send_core(self, k, which, src):
        t, ff = peer(self.s, k), self.f if which == 0 else self.fx
        dst = self.piece(t, ff)
        return remote(src, dst, self.core.at[k, which], self.recv.at[t, ff], (self.s, self.fc))

    def send_x(self, k, src):
        t = peer(self.s, k)
        dst = self.piece(t, self.f)
        return remote(src, dst, self.xs.at[k], self.recv.at[t, self.f], (self.s, self.fx))

    def arrived(self, k, ff):
        t = peer(self.s, k)
        o = self.piece(t, ff)
        return remote(o, o, self.own, self.recv.at[t, ff], (self.s, self.fc))

    def start(self):
        for k in reversed(range(1, 8)):
            self.send_direct(k).start()
        self.send_x(0, self.x.at[self.s]).start()
        self.send_core(0, 0, self.x.at[self.s]).start()
        self.mine.start()

    def step(self, k):
        t = peer(self.s, k)
        self.arrived(k, self.f).wait_recv()
        self.send_x(k, self.piece(t, self.f)).start()
        self.send_core(k, 0, self.piece(t, self.f)).start()

    def xstep(self, k):
        t = peer(self.s, k)
        self.arrived(k, self.fx).wait_recv()
        self.send_core(k, 1, self.piece(t, self.fx)).start()

    def steps(self):
        first = [functools.partial(self.step, k) for k in reversed(range(1, 8))]
        then = [functools.partial(self.xstep, k) for k in (0, 7, 6, 5, 4, 3, 2, 1)]
        return first + then

    def complete(self):
        self.mine.wait()
        for k in range(8):
            self.arrived(k, self.fc).wait_recv()
            self.arrived(k, self.fd).wait_recv()

    def finish(self):
        for k in range(8):
            if k:
                self.send_direct(k).wait_send()
            self.send_x(k, self.x.at[0]).wait_send()
            self.send_core(k, 0, self.x.at[0]).wait_send()
            self.send_core(k, 1, self.x.at[0]).wait_send()


class ColSum:
    @staticmethod
    def scratch(r, c):
        def v(*lead):
            return pltpu.VMEM(lead + (8, r, c), jnp.bfloat16)

        return [v(2), v(), DMA((2, 8)), DMA((2, 8)), DMA((8,)), DMA((8,))]

    def __init__(self, g, h, cb, xb, cs, cr, xs, xr):
        self.g, self.h, self.cb, self.xb = g, h, cb, xb
        self.cs, self.cr, self.xs, self.xr = cs, cr, xs, xr
        self.s, self.f, _, _ = where_am_i()
        self.fc, self.fx = flip(self.f, 1), flip(self.f, 2)
        self.fd = flip(self.fc, 2)
        self.r, self.c = h.shape[1:]

    def piece(self, i, ff):
        at = pl.multiple_of((i * 4 + ff) * self.r, self.r)
        return self.g.at[pl.ds(at, self.r), pl.ds(0, self.c)]

    def core(self, w, i):
        src = self.piece(i, self.fd if w == 0 else self.fc)
        dst = self.cb.at[w, i]
        return remote(src, dst, self.cs.at[w, i], self.cr.at[w, i], (self.s, self.fc))

    def xsend(self, i):
        src, dst = self.cb.at[0, i], self.xb.at[i]
        return remote(src, dst, self.xs.at[i], self.xr.at[i], (self.s, self.fx))

    def send(self, i):
        self.core(0, i).start()
        self.core(1, i).start()

    def step(self, i):
        self.core(0, i).wait_recv()
        adder(self.cb.at[0, i], [self.piece(i, self.fx), self.cb.at[0, i]])
        self.xsend(i).start()

    def total(self, i):
        self.core(1, i).wait_recv()
        self.xsend(i).wait_recv()
        adder(self.h.at[i], [self.piece(i, self.f), self.cb.at[1, i], self.xb.at[i]])

    def finish(self):
        for i in range(8):
            self.core(0, i).wait_send()
            self.core(1, i).wait_send()
            self.xsend(i).wait_send()


class FsdpReduce:
    @staticmethod
    def scratch(r, c):
        return [pltpu.VMEM((2, r, c), jnp.bfloat16), pltpu.VMEM((r, c), jnp.bfloat16), DMA((3,)), DMA((3,))]

    def __init__(self, g, o, cb, xb, send, recv):
        self.g, self.o, self.cb, self.xb = g, o, cb, xb
        self.s, self.f, _, _ = where_am_i()
        f = self.f
        self.fx = flip(f, 2)
        fc = flip(f, 1)
        core = (self.s, fc)
        self.far = remote(g.at[flip(fc, 2)], cb.at[0], send.at[0], recv.at[0], core)
        self.near = remote(g.at[fc], cb.at[1], send.at[1], recv.at[1], core)
        self.over = remote(cb.at[0], xb, send.at[2], recv.at[2], (self.s, self.fx))

    def start(self):
        self.far.start()
        self.near.start()

    def step(self):
        self.far.wait_recv()
        adder(self.cb.at[0], [self.g.at[self.fx], self.cb.at[0]])
        self.over.start()

    def total(self):
        self.near.wait_recv()
        self.over.wait_recv()
        adder(self.o, [self.g.at[self.f], self.cb.at[1], self.xb])

    def finish(self):
        self.far.wait_send()
        self.near.wait_send()
        self.over.wait_send()


class FsdpGather:
    @staticmethod
    def scratch():
        return [DMA, DMA((4,)), DMA((3,))]

    def __init__(self, x, o, own, recv, send):
        self.x, self.o, self.own, self.recv, self.send = x, o, own, recv, send
        self.s, self.f, _, _ = where_am_i()
        self.fc, self.fx = flip(self.f, 1), flip(self.f, 2)
        self.fd = flip(self.fc, 2)
        self.mine = pltpu.make_async_copy(x, o.at[self.f], own)

    def pass_on(self, n, src, ff, to):
        return remote(src, self.o.at[ff], self.send.at[n], self.recv.at[ff], (self.s, to))

    def arrived(self, ff):
        o = self.o.at[ff]
        return remote(o, o, self.own, self.recv.at[ff], (self.s, self.fc))

    def start(self):
        self.pass_on(0, self.x, self.f, self.fx).start()
        self.pass_on(1, self.x, self.f, self.fc).start()
        self.mine.start()

    def step(self):
        self.arrived(self.fx).wait_recv()
        self.pass_on(2, self.o.at[self.fx], self.fx, self.fc).start()

    def complete(self):
        self.mine.wait()
        self.arrived(self.fc).wait_recv()
        self.arrived(self.fd).wait_recv()

    def finish(self):
        for n in range(3):
            self.pass_on(n, self.x, self.f, self.fc).wait_send()


class WholeGather:
    @staticmethod
    def scratch():
        return [DMA, DMA((32,)), DMA((4,)), DMA((4,)), DMA((4,)), DMA((4, 2)), DMA((4, 2, 2))]

    def __init__(self, x, o, own, recv, su, sd, sy, sx, sc):
        self.x, self.o, self.own, self.recv = x, o, own, recv
        self.su, self.sd, self.sy, self.sx, self.sc = su, sd, sy, sx, sc
        self.s, self.f, self.z, self.y = where_am_i()
        self.fc, self.fx = flip(self.f, 1), flip(self.f, 2)
        self.fd = flip(self.fc, 2)
        self.me = self.s * 4 + self.f
        self.mine = pltpu.make_async_copy(x, o.at[self.me], own)

    def at(self, zb, yy, ff):
        return (2 * zb + (self.y if yy == 0 else 1 - self.y)) * 4 + ff

    def src(self, b, first):
        return self.x if first else self.o.at[b]

    def up(self, zb, first=False):
        b = self.at(zb, 0, self.f)
        to = (self.s + 2, self.f)
        return remote(self.src(b, first), self.o.at[b], self.su.at[zb], self.recv.at[b], to)

    def down(self, zb, first=False):
        b = self.at(zb, 0, self.f)
        to = (self.s - 2, self.f)
        return remote(self.src(b, first), self.o.at[b], self.sd.at[zb], self.recv.at[b], to)

    def over_y(self, zb, first=False):
        b = self.at(zb, 0, self.f)
        to = (flip(self.s, 1), self.f)
        return remote(self.src(b, first), self.o.at[b], self.sy.at[zb], self.recv.at[b], to)

    def over_x(self, zb, yy, first=False):
        b = self.at(zb, yy, self.f)
        to = (self.s, self.fx)
        return remote(self.src(b, first), self.o.at[b], self.sx.at[zb, yy], self.recv.at[b], to)

    def over_core(self, zb, yy, xx, first=False):
        b = self.at(zb, yy, self.f if xx == 0 else self.fx)
        to = (self.s, self.fc)
        return remote(self.src(b, first), self.o.at[b], self.sc.at[zb, yy, xx], self.recv.at[b], to)

    def arrived(self, b):
        o = self.o.at[b]
        return remote(o, o, self.own, self.recv.at[b], (self.s, self.fc))

    def start(self):
        z = self.z

        @pl.when(z < 3)
        def _():
            self.up(z, True).start()

        @pl.when(z > 0)
        def _():
            self.down(z, True).start()

        self.over_y(z, True).start()
        self.over_x(z, 0, True).start()
        self.over_core(z, 0, 0, True).start()
        self.mine.start()

    def line(self, sign, t):
        zb = self.z + sign * t

        @pl.when((zb >= 0) & (zb <= 3))
        def _():
            self.arrived(self.at(zb, 0, self.f)).wait_recv()
            if sign < 0:

                @pl.when(self.z < 3)
                def _():
                    self.up(zb).start()

            else:

                @pl.when(self.z > 0)
                def _():
                    self.down(zb).start()

            self.over_y(zb).start()
            self.over_x(zb, 0).start()
            self.over_core(zb, 0, 0).start()

    def column(self, sign, t):
        zb = self.z + sign * t

        @pl.when((zb >= 0) & (zb <= 3))
        def _():
            self.arrived(self.at(zb, 1, self.f)).wait_recv()
            self.over_x(zb, 1).start()
            self.over_core(zb, 1, 0).start()

    def side(self, sign, t, yy):
        zb = self.z + sign * t

        @pl.when((zb >= 0) & (zb <= 3))
        def _():
            self.arrived(self.at(zb, yy, self.fx)).wait_recv()
            self.over_core(zb, yy, 1).start()

    def steps(self):
        p = functools.partial
        out = []
        for t in range(4):
            for sign in (-1, 1) if t else (1,):
                if t:
                    out.append(p(self.line, sign, t))
        for t in range(4):
            for sign in (-1, 1) if t else (1,):
                out.append(p(self.column, sign, t))
                out.append(p(self.side, sign, t, 0))
        for t in range(4):
            for sign in (-1, 1) if t else (1,):
                out.append(p(self.side, sign, t, 1))
        return out

    def complete(self):
        self.mine.wait()
        for zb in range(4):
            for yy in range(2):
                self.arrived(self.at(zb, yy, self.fc)).wait_recv()
                self.arrived(self.at(zb, yy, self.fd)).wait_recv()

    def finish(self):
        for zb in range(4):
            self.over_y(zb).wait_send()

            @pl.when((self.z < 3) & (zb <= self.z))
            def _():
                self.up(zb).wait_send()

            @pl.when((self.z > 0) & (zb >= self.z))
            def _():
                self.down(zb).wait_send()

            for yy in range(2):
                self.over_x(zb, yy).wait_send()
                for xx in range(2):
                    self.over_core(zb, yy, xx).wait_send()


class RowExchange:
    @staticmethod
    def scratch():
        return [DMA, DMA((8,)), DMA((8,))]

    def __init__(self, x, o, own, send, recv):
        self.x, self.o, self.send, self.recv = x, o, send, recv
        self.s, self.f, _, _ = where_am_i()
        self.mine = pltpu.make_async_copy(x.at[self.s], o.at[self.s], own)

    def piece(self, k):
        t = peer(self.s, k)
        dst = self.o.at[self.s]
        return remote(self.x.at[t], dst, self.send.at[k], self.recv.at[k], (t, self.f))

    def start(self):
        for k in reversed(range(1, 8)):
            self.piece(k).start()
        self.mine.start()

    def finish(self):
        self.mine.wait()
        for k in reversed(range(1, 8)):
            self.piece(k).wait_recv()
            self.piece(k).wait_send()


def idle():
    pass


def looped(plan, name, work, queues):
    count = plan.count(name)
    groups = plan.split(name)
    left = {k: list(v) for k, v in queues.items()}

    def between(now, group):
        items = [left[k].pop(0) for k in group]
        if items:

            @pl.when(now)
            def _():
                for item in items:
                    item()

    @pl.loop(0, count)
    def _(i):
        for n in range(count):
            between(i == n, groups[n])
        work(i)

    for k in groups[count]:
        left[k].pop(0)()
    return left


def fetch(refs, sems):
    copies = [pltpu.make_async_copy(a, b, sems.at[i]) for i, (a, b) in enumerate(refs)]
    for copy in copies:
        copy.start()
    return copies


def rotary_rows(pos, lengths_ref, freq):
    half = ROT // 2
    d = lax.broadcasted_iota(jnp.int32, (1, 128), 1) % HEAD_DIM
    rel = pos - starts_of(pos, lengths_ref, lengths_ref.shape[1])
    angle = rel.astype(jnp.float32) * freq
    c, s = jnp.cos(angle), jnp.sin(angle)
    second = (d >= half) & (d < ROT)
    return jnp.where(d < ROT, c, 1.0), jnp.where(d < half, -s, 0.0), jnp.where(second, s, 0.0)


def perform(plan, queues):
    left = {name: list(items) for name, items in queues.items()}
    for name in "".join(plan):
        left[name].pop(0)()
    return left


FORWARD_PLAN = (
    "FnggsnWsgswwsDswwnnsssVswsswsws",
    "nswwnsnnccwwccccvdvwcccwccwwcdv",
    "vwwwfcccwwwccwwcvXwwwvvdvvvwvvY",
    "PPvvvPP",
    "Q",
)
MIDDLE_PLAN = (
    "gbggbbgbgbgbbb",
    "raaaraeateaeearea",
    "mertmeemm",
    "Mlltllhtthhlltlthhl",
    "LhhhHtz",
)
BACKWARD_PLAN = ("bFggKrgbbXgbggSbrbfbrtZtb", "crotccoocotocootocqOcccptccccPttz")
LAST_PLAN = ("ataaeeathtaheatttehehetaa", "eehthhzhZ")


def dot(a, b, ca=1, cb=0):
    return lax.dot_general(a, b, (((ca,), (cb,)), ((), ())), preferred_element_type=jnp.float32)


def starts_of(pos, lengths_ref, nseg):
    start = jnp.zeros_like(pos)
    end = 0
    for i in range(nseg - 1):
        end = end + lengths_ref[0, i]
        start = jnp.where(pos >= end, end, start)
    return start


def head_lanes(h):
    lane = lax.broadcasted_iota(jnp.int32, (1, 128), 1)
    return (lane // HEAD_DIM) == h


def turn(x, c, s1, s2, sign):
    half = ROT // 2
    return x * c + (pltpu.roll(x, 128 - half, 1) * s1 + pltpu.roll(x, half, 1) * s2) * sign


def block_mask(qb, lengths_ref):
    keys = (qb + 1) * QB
    row = qb * QB + lax.broadcasted_iota(jnp.int32, (QB, 1), 0)
    col = lax.broadcasted_iota(jnp.int32, (1, keys), 1)
    return (col >= starts_of(row, lengths_ref, lengths_ref.shape[1])) & (col <= row)


def row_at(i, step=QB):
    return pl.ds(pl.multiple_of(i * step, step), step)


def picks(orow_ref, i):
    p = lax.broadcasted_iota(jnp.int32, (QB, 1), 0) + i * QB == orow_ref[...]
    return jnp.where(p, 1.0, 0.0).astype(jnp.bfloat16)


def puts(oc, valid):
    p = oc == lax.broadcasted_iota(jnp.int32, (1, valid), 1)
    return jnp.where(p, 1.0, 0.0).astype(jnp.bfloat16)


def attend(
    a_ref, w_ref, shift_of, tables, orow_ref, ocol_ref, len_ref, o_ref, pk_ref, lse_ref, rot, opk
):
    rows, w3 = rot.shape
    w = w3 // 3
    valid = pk_ref.shape[0]
    scale = HEAD_DIM**-0.5
    freq_ref = tables

    def project(lo, hi):
        shift = shift_of()

        @pl.loop(lo, hi)
        def _(i):
            r = row_at(i, 256)
            c, s1, s2 = rotary_rows(ocol_ref[r], len_ref, freq_ref[...])
            left = jnp.concatenate([a_ref[2 * i], a_ref[2 * i + 1]], 0)
            qkv = dot(left, w_ref[...]) + shift
            for t in range(w3 // 128):
                cols = slice(t * 128, t * 128 + 128)
                x = qkv[:, cols]
                if t < 2 * w // 128:
                    x = turn(x, c, s1, s2, 1.0)
                rot[r, cols] = x.astype(jnp.bfloat16)

    def pack(lo, hi):
        @pl.loop(lo, hi)
        def _(i):
            pk_ref[row_at(i)] = dot(picks(orow_ref, i), rot[...]).astype(jnp.bfloat16)

    def block(qb, t):
        keys = (qb + 1) * QB
        rq = slice(qb * QB, qb * QB + QB)
        ct = slice(t * 128, t * 128 + 128)
        mask = block_mask(qb, len_ref)
        q = pk_ref[rq, ct]
        k = pk_ref[0:keys, w + t * 128 : w + t * 128 + 128]
        v = pk_ref[0:keys, 2 * w + t * 128 : 2 * w + t * 128 + 128]
        total = None
        for h in range(2):
            qh = jnp.where(head_lanes(h), q, jnp.zeros_like(q))
            scores = jnp.where(mask, dot(qh, k, 1, 1) * scale, NEG)
            top = jnp.max(scores, -1, keepdims=True)
            expo = jnp.exp(scores - top)
            norm = jnp.sum(expo, -1, keepdims=True)
            probs = (expo / norm).astype(jnp.bfloat16)
            lse_ref[2 * t + h, rq] = top + jnp.log(norm)
            out = dot(probs, v)
            total = out if h == 0 else jnp.where(head_lanes(1), out, total)
        opk[rq, ct] = total.astype(jnp.bfloat16)

    def unpack(lo, hi):
        per = o_ref.shape[1]

        @pl.loop(lo, hi)
        def _(i):
            r = row_at(i, per)
            oc = ocol_ref[r]
            back = dot(puts(oc, valid), opk[...])
            pad = rot[r, 2 * w :].astype(jnp.float32)
            o_ref[i] = jnp.where(oc >= valid, pad, back).astype(jnp.bfloat16)

    blocks = [
        functools.partial(block, qb, t) for qb in range(valid // QB) for t in range(w // 128)
    ]
    p = functools.partial
    steps, half, blks = rows // 256, valid // QB // 2, rows // o_ref.shape[1]
    head = [p(project, 0, steps // 2), p(project, steps // 2, steps)]
    head += [p(pack, 0, half), p(pack, half, valid // QB)]
    return head + blocks + [p(unpack, 0, blks // 2), p(unpack, blks // 2, blks)]


def attend_back(
    pk_ref, do_ref, lse_ref, tables, orow_ref, ocol_ref, len_ref, g_ref, b_ref, dpk, dq, dk, dv, gpk
):
    rows, w = do_ref.shape
    valid = pk_ref.shape[0]
    scale = HEAD_DIM**-0.5
    freq_ref = tables

    def pack():
        @pl.loop(0, valid // QB)
        def _(i):
            r = row_at(i)
            dpk[r] = dot(picks(orow_ref, i), do_ref[...]).astype(jnp.bfloat16)
            dk[r] = jnp.zeros((QB, w), jnp.float32)
            dv[r] = jnp.zeros((QB, w), jnp.float32)

    def block(qb, t):
        keys = (qb + 1) * QB
        rq = slice(qb * QB, qb * QB + QB)
        ct = slice(t * 128, t * 128 + 128)
        mask = block_mask(qb, len_ref)
        q, d = pk_ref[rq, ct], dpk[rq, ct]
        k = pk_ref[0:keys, w + t * 128 : w + t * 128 + 128]
        v = pk_ref[0:keys, 2 * w + t * 128 : 2 * w + t * 128 + 128]
        total = None
        for h in range(2):
            hl = head_lanes(h)
            qh = jnp.where(hl, q, jnp.zeros_like(q))
            dh = jnp.where(hl, d, jnp.zeros_like(d))
            scores = jnp.where(mask, dot(qh, k, 1, 1) * scale, NEG)
            p = jnp.exp(scores - lse_ref[2 * t + h, rq])
            dp = dot(dh, v, 1, 1)
            inner = jnp.sum(p * dp, -1, keepdims=True)
            ds = (p * (dp - inner)).astype(jnp.bfloat16)
            dv[0:keys, ct] += dot(p.astype(jnp.bfloat16), dh, 0, 0)
            dk[0:keys, ct] += dot(ds, qh, 0, 0)
            part = dot(ds, k)
            total = part if h == 0 else jnp.where(head_lanes(1), part, total)
        dq[rq, ct] = total

    def rotary():
        @pl.loop(0, valid // QB)
        def _(i):
            r = row_at(i)
            pos = lax.broadcasted_iota(jnp.int32, (QB, 1), 0) + i * QB
            c, s1, s2 = rotary_rows(pos, len_ref, freq_ref[...])
            for t in range(w // 128):
                ct = slice(t * 128, t * 128 + 128)
                for j, src in ((0, dq), (1, dk)):
                    x = (src[r, ct] * scale).astype(jnp.bfloat16).astype(jnp.float32)
                    at = j * w + t * 128
                    gpk[r, at : at + 128] = turn(x, c, s1, s2, -1.0).astype(jnp.bfloat16)
                at = 2 * w + t * 128
                gpk[r, at : at + 128] = dv[r, ct].astype(jnp.bfloat16)

    def unpack():
        b_ref[...] = jnp.zeros_like(b_ref)

        @pl.loop(0, rows // QB)
        def _(i):
            r = row_at(i)
            oc = ocol_ref[r]
            back = dot(puts(oc, valid), gpk[...])
            pad = jnp.where(oc >= valid, do_ref[r].astype(jnp.float32), 0.0)
            back = jnp.concatenate([back[:, : 2 * w], back[:, 2 * w :] + pad], 1)
            g_ref[r] = back.astype(jnp.bfloat16)
            b_ref[...] += jnp.sum(back, 0, keepdims=True)

    blocks = [
        functools.partial(block, qb, t) for qb in range(valid // QB) for t in range(w // 128)
    ]
    return [pack] + blocks + [rotary, unpack]


def forward_kernel(
    x_hbm,
    p_ref,
    qkv_ref,
    op_hbm,
    dm_hbm,
    gate_hbm,
    up_hbm,
    dp_hbm,
    freq_ref,
    orow_ref,
    ocol_ref,
    len_ref,
    a_hbm,
    qw_hbm,
    n_ref,
    or_hbm,
    pk_hbm,
    lse_hbm,
    dmo_ref,
    ww_ref,
    dw_ref,
    mix_hbm,
    attn_ref,
    res_ref,
    second_ref,
    a_ref,
    qw_ref,
    ow_ref,
    ho_ref,
    pk_ref,
    lse_ref,
    mix_ref,
    x_ref,
    op_ref,
    dm_ref,
    gate_ref,
    up_ref,
    dp_ref,
    xs,
    got,
    rot,
    opk,
    qp_ref,
    wp_ref,
    load,
    store,
    psend,
    precv,
    *sems,
):
    s, f, z, y = where_am_i()
    me = s * 4 + f
    w = rot.shape[1] // 3
    lf = wp_ref.shape[2] // 2
    rows, width = x_ref.shape

    def piece_of(i):
        t, n = i // 3, i % 3
        at = n * x_ref.shape[1] + t * w
        return qkv_ref.at[:, at : at + w], qp_ref.at[t, :, n * w : n * w + w]

    operands = [(x_hbm, x_ref)] + [piece_of(i) for i in range(24)]
    operands += [(op_hbm, op_ref), (dm_hbm, dm_ref), (dp_hbm, dp_ref)]
    operands += [(gate_hbm, gate_ref), (up_hbm, up_ref)]
    loads = fetch(operands, load)
    greet_all(s, f)
    gather = SeqGather(x_ref, xs, *sems[:5])
    slices = ColGather(qp_ref, qw_ref, *sems[5:10])
    whole = WholeGather(op_ref, ow_ref, *sems[10:17])
    grads = SeqGather(dm_ref, dmo_ref, *sems[17:22])
    wide = ColGather(wp_ref, ww_ref, *sems[22:27])
    down = FsdpGather(dp_ref, dw_ref, *sems[27:30])
    swap = RowExchange(mix_ref, ho_ref, *sems[30:])

    def param(k):
        i = (me + k) % 32
        return remote(p_ref, got.at[me], psend.at[k], precv.at[k], dealer(i))

    @pl.loop(1, 32)
    def _(k):
        param(k).start()

    loads[0].wait()
    gather.start()
    for copy in loads[1:]:
        copy.wait()
    slices.start()
    got[me] = p_ref[...]

    @pl.loop(1, 32)
    def _(k):
        param(k).wait_recv()

    for i in range(16):
        n_ref[:, i * 128 : i * 128 + 128] = got[2 * i] + got[2 * i + 1]
    step = 16

    def norm(b):
        gain, shift = n_ref[0:1], n_ref[1:2]

        @pl.loop(0, x_ref.shape[0] // step)
        def _(i):
            r = row_at(i, step)
            normed, _ = normalize(xs[b, r].astype(jnp.float32))
            a_ref[b, r] = (normed * gain + shift).astype(jnp.bfloat16)

    def shift_of():
        parts = []
        for n in range(3):
            part = jnp.zeros((1, w), jnp.float32)
            for i in range(8):
                piece = n_ref[4 + n : 5 + n, i * w : i * w + w]
                part = part + jnp.where(s == i, piece, jnp.zeros_like(piece))
            parts.append(part)
        return jnp.concatenate(parts, 1)

    work = attend(
        a_ref,
        qw_ref,
        shift_of,
        freq_ref,
        orow_ref,
        ocol_ref,
        len_ref,
        mix_ref,
        pk_ref,
        lse_ref,
        rot,
        opk,
    )
    p = functools.partial

    def own():
        gather.own.wait()
        norm(s)

    def wide_start():
        for i in range(8):
            at = slice(i * lf, i * lf + lf)
            wp_ref[i, :, 0:lf] = gate_ref[:, at]
            wp_ref[i, :, lf : 2 * lf] = up_ref[:, at]
        wide.start()

    saved = [(a_ref, a_hbm), (qw_ref, qw_hbm), (pk_ref, pk_hbm), (lse_ref, lse_hbm)]
    saved.append((mix_ref, mix_hbm))
    stores = [pltpu.make_async_copy(u, v, store.at[i]) for i, (u, v) in enumerate(saved)]
    here = pl.ds(pl.multiple_of(s * 4, 4), 4)
    stores.append(pltpu.make_async_copy(ow_ref.at[here], or_hbm, store.at[5]))

    def swap_start():
        swap.start()
        for copy in stores[:5]:
            copy.start()

    def mixed_ready():
        swap.finish()
        whole.complete()
        stores[5].start()

    def project_out(j):
        cols = row_at(j, 512)
        total = jnp.zeros((rows, 512), jnp.float32)
        for k in range(8):
            right = jnp.concatenate([ow_ref[4 * k + q, :, cols] for q in range(4)], 0)
            total = total + dot(ho_ref[k], right)
        attn_ref[:, cols] = total
        res_ref[:, cols] = x_ref[:, cols].astype(jnp.float32) + total

    def second_norm():
        gain, shift = n_ref[2:3], n_ref[3:4]

        @tall(rows)
        def _(r):
            normed, _ = normalize(res_ref[r])
            second_ref[r] = (normed * gain + shift).astype(jnp.bfloat16)

    norms = [own]
    for i in range(4):
        norms.append(lambda i=i: norm(gather.cross(i)))
        if i < 3:
            norms.append(lambda i=i: norm(2 * gather.near(i + 1) + y))
    work = [slices.complete, work[0], idle, work[1], idle] + work[2:]
    queues = dict(
        g=gather.steps(),
        n=norms,
        s=slices.steps(),
        d=grads.steps(),
        v=wide.steps(),
        w=whole.steps(),
        f=[down.step],
        c=work,
        D=[grads.start],
        V=[wide_start],
        W=[whole.start],
        F=[down.start],
        X=[swap_start],
        Y=[mixed_ready],
        Q=[second_norm],
    )
    work[0:2] = [lambda first=work[0], then=work[1]: (first(), then())]
    left = perform(FORWARD_PLAN[:3], queues)
    left = looped(FORWARD_PLAN[3], "P", project_out, left)
    perform(FORWARD_PLAN[4:], left)
    for i in range(4):
        grads.cross(i)
    wide.complete()
    down.complete()
    for task in (slices, wide, whole, down, grads):
        task.finish()
    gather.finish(False)

    for copy in stores:
        copy.wait()

    @pl.loop(1, 32)
    def _(k):
        param(k).wait_send()


def forward(
    x, params, qkv, out_p, dm, gate, up, down_p, freq, orow, ocol, lengths, valid, collective
):
    rows, width = x.shape
    w3 = qkv.shape[1] // 8
    part, wide = gate.shape[0], gate.shape[1] // 4
    w = w3 // 3
    group = 8 * rows
    heads = w // HEAD_DIM

    def out(shape, dtype=jnp.bfloat16):
        return jax.ShapeDtypeStruct(shape, dtype)

    return pl.pallas_call(
        forward_kernel,
        out_shape=(
            out((8, rows, width)),
            out((width, w3)),
            out((8, width), jnp.float32),
            out((4,) + out_p.shape),
            out((valid, w3)),
            out((heads, valid, 1), jnp.float32),
            out((8, rows, width)),
            out((width, wide)),
            out((4,) + down_p.shape),
            out((8, rows, w)),
            out((rows, width), jnp.float32),
            out((rows, width), jnp.float32),
            out((rows, width)),
        ),
        in_specs=[HBM_SPEC, VMEM_SPEC] + [HBM_SPEC] * 6 + [VMEM_SPEC] * 3 + [SMEM_SPEC],
        out_specs=(ANY_SPEC,) * 2 + (VMEM_SPEC,) + (ANY_SPEC,) * 7 + (VMEM_SPEC,) * 3,
        scratch_shapes=[
            pltpu.VMEM((8, rows, width), jnp.bfloat16),
            pltpu.VMEM((width, w3), jnp.bfloat16),
            pltpu.VMEM((32,) + out_p.shape, jnp.bfloat16),
            pltpu.VMEM((8, rows, w), jnp.bfloat16),
            pltpu.VMEM((valid, w3), jnp.bfloat16),
            pltpu.VMEM((heads, valid, 1), jnp.float32),
            pltpu.VMEM((8, rows, w), jnp.bfloat16),
        ]
        + [pltpu.VMEM(v.shape, v.dtype) for v in (x, out_p, dm, gate, up, down_p)]
        + [
            pltpu.VMEM((8, rows, width), jnp.bfloat16),
            pltpu.VMEM((32, 8, 128), jnp.float32),
            pltpu.VMEM((group, w3), jnp.bfloat16),
            pltpu.VMEM((valid, w), jnp.bfloat16),
            pltpu.VMEM((8, part, w3), jnp.bfloat16),
            pltpu.VMEM((8, part, wide), jnp.bfloat16),
            DMA((30,)),
            DMA((6,)),
            DMA((32,)),
            DMA((32,)),
        ]
        + SeqGather.scratch()
        + ColGather.scratch()
        + WholeGather.scratch()
        + SeqGather.scratch()
        + ColGather.scratch()
        + FsdpGather.scratch()
        + RowExchange.scratch(),
        compiler_params=comm_params(collective),
    )(x, params, qkv, out_p, dm, gate, up, down_p, freq, orow, ocol, lengths)


def tall(rows, step=16):
    def wrap(fn):
        @pl.loop(0, rows // step)
        def _(i):
            fn(row_at(i, step))

    return wrap


def middle_kernel(
    cloc,
    n_ref,
    ww_hbm,
    dw_hbm,
    dm_hbm,
    res_hbm,
    rg_ref,
    vec_ref,
    mp_hbm,
    dg_hbm,
    h_hbm,
    ww_ref,
    dw_ref,
    dm_ref,
    res_ref,
    mp_ref,
    dg_ref,
    h_ref,
    big,
    c_ref,
    hid,
    act,
    part,
    second,
    load,
    store,
    *scratch,
):
    s, f, z, y = where_am_i()
    rows, width = cloc.shape
    lf = dw_ref.shape[0]
    operands = [(ww_hbm, ww_ref), (dw_hbm, dw_ref), (dm_hbm, dm_ref), (res_hbm, res_ref)]
    loads = fetch(operands, load)
    greet_columns(s, f)
    gather = SeqGather(cloc, c_ref, *scratch[:5])
    reduce = SeqReduce(part, second, *scratch[5:11])
    sums = ColSum(big, h_ref, *scratch[11:])
    gain = n_ref[2:3]
    gather.start()
    gather.own.wait()
    for copy in loads:
        copy.wait()

    def block(b):
        at = pl.ds(pl.multiple_of(b * rows, rows), rows)
        wide = dot(c_ref[b], ww_ref[...])
        gate, upper = wide[:, :lf], wide[:, lf:]
        hidden, sigma = mlp_forward(gate, upper)
        hid[at] = hidden
        grad = dot(dm_ref[b], dw_ref[...], 1, 1)
        gate_act, up_act = mlp_backward(grad, gate, upper, sigma)
        act[at] = jnp.concatenate([gate_act, up_act], 1)
        part[b] = dot(act[at], ww_ref[...], 1, 1).astype(jnp.bfloat16)

    def wide_grad(i):
        at = row_at(i, 256)
        left = jnp.concatenate([c_ref[b, :, at] for b in range(8)], 0)
        big[at, 0 : 2 * lf] = dot(left, act[...], 0, 0).astype(jnp.bfloat16)
        sums.send(i)

    def mlp_part(i):
        for k in range(2):
            b = 2 * i + k
            at = pl.ds(pl.multiple_of(b * rows, rows), rows)
            mp_ref[b] = dot(hid[at], dw_ref[...]).astype(jnp.bfloat16)

    def down_grad(i):
        cols = row_at(i, 256)
        right = jnp.concatenate([dm_ref[b, :, cols] for b in range(8)], 0)
        dg_ref[:, cols] = dot(hid[...], right, 0, 0).astype(jnp.bfloat16)

    def norm_backward():
        vec_ref[...] = jnp.zeros_like(vec_ref)

        @tall(rows)
        def _(r):
            grad = second[r]
            normed, rstd = normalize(res_ref[r])
            inner, gain_part, shift_part = norm_back(grad, normed, rstd, gain)
            rg_ref[r] = dm_ref[s, r].astype(jnp.float32) + inner
            vec_ref[0:1] += gain_part[None]
            vec_ref[1:2] += shift_part[None]

    p = functools.partial
    each = range(8)
    out_copies = [
        pltpu.make_async_copy(mp_ref, mp_hbm, store.at[0]),
        pltpu.make_async_copy(dg_ref, dg_hbm, store.at[1]),
        pltpu.make_async_copy(h_ref, h_hbm, store.at[2]),
    ]
    left = dict(
        g=gather.steps(),
        r=[p(reduce.send, k) for k in range(4)],
        t=reduce.steps(),
        e=[p(sums.step, i) for i in each],
        h=[p(sums.total, i) for i in each],
        z=[norm_backward],
        M=[out_copies[0].start],
        L=[out_copies[1].start],
        H=[out_copies[2].start],
    )
    left = looped(MIDDLE_PLAN[0], "b", lambda j: block(gather.turn(j)), left)
    left = looped(MIDDLE_PLAN[1], "a", wide_grad, left)
    left = looped(MIDDLE_PLAN[2], "m", mlp_part, left)
    left = looped(MIDDLE_PLAN[3], "l", down_grad, left)
    perform(MIDDLE_PLAN[4], left)
    for copy in out_copies:
        copy.wait()
    gather.finish(False)
    reduce.finish()
    sums.finish()


def middle(second, norms, wide_w, down_w, dm, res, collective):
    rows, width = second.shape
    lf = down_w.shape[0]
    group = 8 * rows
    part = width // 32

    def out(shape, dtype=jnp.bfloat16):
        return jax.ShapeDtypeStruct(shape, dtype)

    def vm(shape, dtype=jnp.bfloat16):
        return pltpu.VMEM(shape, dtype)

    wide = (rows, width)
    return pl.pallas_call(
        middle_kernel,
        out_shape=(
            out(wide, jnp.float32),
            out((8, width), jnp.float32),
            out((8,) + wide),
            out((lf, width)),
            out((8, part, 2 * lf)),
        ),
        in_specs=[VMEM_SPEC] * 2 + [HBM_SPEC] * 4,
        out_specs=(VMEM_SPEC,) * 2 + (ANY_SPEC,) * 3,
        scratch_shapes=[
            vm(wide_w.shape),
            vm(down_w.shape),
            vm(dm.shape),
            vm(wide, jnp.float32),
            vm((8,) + wide),
            vm((lf, width)),
            vm((8, part, 2 * lf)),
            vm((width, 2 * lf)),
            vm((8,) + wide),
            vm((group, lf)),
            vm((group, 2 * lf)),
            vm((8,) + wide),
            vm(wide, jnp.float32),
            DMA((4,)),
            DMA((3,)),
        ]
        + SeqGather.scratch(2)
        + SeqReduce.scratch(rows, width)
        + ColSum.scratch(part, 2 * lf),
        compiler_params=comm_params(collective),
    )(second, norms, wide_w, down_w, dm, res)


def backward_kernel(
    rg_ref,
    freq_ref,
    orow_ref,
    ocol_ref,
    len_ref,
    ow_hbm,
    mix_hbm,
    pk_hbm,
    lse_hbm,
    attn_hbm,
    res_hbm,
    mp_hbm,
    dg_hbm,
    h_hbm,
    g_ref,
    b_ref,
    lo_ref,
    sum_ref,
    got,
    down_hbm,
    out_ref,
    or_ref,
    mix_ref,
    pk_ref,
    lse_ref,
    attn_ref,
    res_ref,
    mp_ref,
    dg_ref,
    h_ref,
    down_ref,
    da,
    full,
    do_ref,
    og,
    mlp,
    dpk,
    dq,
    dk,
    dv,
    gpk,
    load,
    store,
    *scratch,
):
    s, f, z, y = where_am_i()
    rows, width = rg_ref.shape
    part = out_ref.shape[0]
    valid = pk_ref.shape[0]
    loads = fetch(
        [
            (ow_hbm, or_ref),
            (dg_hbm, dg_ref),
            (mp_hbm, mp_ref),
            (h_hbm, h_ref),
            (pk_hbm, pk_ref),
            (lse_hbm, lse_ref),
            (mix_hbm, mix_ref),
            (attn_hbm, attn_ref),
            (res_hbm, res_ref),
        ],
        load,
    )
    greet_columns(s, f)
    gather = EvenGather(da, full, *scratch[:6])
    reduce = SeqReduce(mp_ref, mlp, *scratch[6:12])
    swap = RowExchange(h_ref, got, *scratch[12:15])
    down = FsdpReduce(dg_ref, down_ref, *scratch[15:19])
    outer_sum = FsdpReduce(og, out_ref, *scratch[19:])

    @tall(rows)
    def _(r):
        da[r] = rg_ref[r].astype(jnp.bfloat16)

    gather.start()
    gather.own.wait()
    loads[0].wait()

    def block(b):
        at = pl.ds(pl.multiple_of(b * rows, rows), rows)
        out_rows = jnp.concatenate([or_ref[k] for k in range(4)], 0)
        do_ref[at] = dot(full[b], out_rows, 1, 1).astype(jnp.bfloat16)

    def before(copies, then):
        def run():
            for copy in copies:
                copy.wait()
            then()

        return run

    out_copies = [pltpu.make_async_copy(down_ref, down_hbm, store)]

    def down_total():
        down.total()
        out_copies[0].start()

    def out_grad(i):
        cols = slice(i * 256, i * 256 + 256)
        right = jnp.concatenate([full[b, :, cols] for b in range(8)], 0)
        value = dot(mix_ref[...], right, 0, 0).astype(jnp.bfloat16)
        for k in range(4):
            og[k, :, cols] = value[k * part : k * part + part]

    p = functools.partial
    work = attend_back(
        pk_ref,
        do_ref,
        lse_ref,
        freq_ref,
        orow_ref,
        ocol_ref,
        len_ref,
        g_ref,
        b_ref,
        dpk,
        dq,
        dk,
        dv,
        gpk,
    )
    def results():
        sum_ref[...] = jnp.zeros_like(sum_ref)

        step = 16

        @pl.loop(0, rows // step)
        def _(i):
            r = row_at(i, step)
            m = mlp[r]
            result = res_ref[r] + m
            lo_ref[r] = result.astype(jnp.bfloat16)
            pos = ocol_ref[pl.ds(pl.multiple_of(s * rows + i * step, step), step)]
            keep = jnp.where(pos < valid, 1.0, 0.0)
            for n, v in enumerate((result, attn_ref[r], m)):
                total = jnp.sum(jnp.sum(v * v, -1, keepdims=True) * keep, 0, keepdims=True)
                sum_ref[n : n + 1] += jnp.broadcast_to(total, (1, 128))

    sends = [p(reduce.send, k) for k in range(4)]
    outs = [p(out_grad, i) for i in range(8)]
    queues = dict(
        F=[before(loads[1:2], down.start)],
        f=[down.step],
        q=[down_total],
        g=gather.steps(),
        K=[gather.lead],
        S=[gather.follow],
        r=[before(loads[2:3], sends[0])] + sends[1:],
        t=reduce.steps(),
        X=[before(loads[3:4], swap.start)],
        Z=[swap.finish],
        c=[before(loads[4:6], work[0])] + work[1:],
        o=[before(loads[6:7], outs[0])] + outs[1:],
        O=[outer_sum.start],
        p=[outer_sum.step],
        P=[outer_sum.total],
        z=[before(loads[7:9], results)],
    )
    left = looped(BACKWARD_PLAN[0], "b", lambda j: block(gather.turn(j)), queues)
    perform(BACKWARD_PLAN[1], left)
    gather.finish()
    reduce.finish()
    down.finish()
    outer_sum.finish()
    for copy in out_copies:
        copy.wait()


def backward(
    rg, freq, orow, ocol, lengths, out_w, mixed, pk, lse, attn, res, mp, dg, h, collective
):
    rows, width = rg.shape
    group, w = mixed.shape
    valid = pk.shape[0]
    part = h.shape[1]

    def out(shape, dtype=jnp.float32):
        return jax.ShapeDtypeStruct(shape, dtype)

    def vm(shape, dtype=jnp.bfloat16):
        return pltpu.VMEM(shape, dtype)

    return pl.pallas_call(
        backward_kernel,
        out_shape=(
            out((group, 3 * w), jnp.bfloat16),
            out((1, 3 * w)),
            out((rows, width), jnp.bfloat16),
            out((8, 128)),
            out(h.shape, jnp.bfloat16),
            out(dg.shape[1:]),
            out((part, width)),
        ),
        in_specs=[VMEM_SPEC] * 4 + [SMEM_SPEC] + [HBM_SPEC] * 9,
        out_specs=(VMEM_SPEC,) * 4 + (ANY_SPEC,) * 2 + (VMEM_SPEC,),
        scratch_shapes=[
            vm((4, part, width)),
            vm(mixed.shape),
            vm(pk.shape),
            vm(lse.shape, jnp.float32),
            vm(attn.shape, jnp.float32),
            vm(res.shape, jnp.float32),
            vm(mp.shape),
            vm(dg.shape),
            vm(h.shape),
            vm(dg.shape[1:], jnp.float32),
            vm((rows, width)),
            vm((8, rows, width)),
            vm((group, w)),
            vm((4, part, width)),
            vm((rows, width), jnp.float32),
            vm((valid, w)),
            vm((valid, w), jnp.float32),
            vm((valid, w), jnp.float32),
            vm((valid, w), jnp.float32),
            vm((valid, 3 * w)),
            DMA((9,)),
            DMA,
        ]
        + EvenGather.scratch()
        + SeqReduce.scratch(rows, width)
        + RowExchange.scratch()
        + FsdpReduce.scratch(*dg.shape[1:])
        + FsdpReduce.scratch(part, width),
        compiler_params=comm_params(collective),
    )(rg, freq, orow, ocol, lengths, out_w, mixed, pk, lse, attn, res, mp, dg, h)


def last_kernel(
    g_ref,
    b_ref,
    n_ref,
    vec_ref,
    sum_ref,
    qw_hbm,
    a_hbm,
    x_hbm,
    rg_hbm,
    ig_ref,
    got,
    total_ref,
    qw_ref,
    a_ref,
    x_ref,
    rg_ref,
    load,
    part,
    first,
    grad,
    h,
    msg,
    inbox,
    vec,
    msend,
    mrecv,
    *scratch,
):
    s, f, z, y = where_am_i()
    me = s * 4 + f
    rows, width = x_ref.shape
    w3 = g_ref.shape[1]
    w = w3 // 3
    loads = fetch([(qw_hbm, qw_ref), (a_hbm, a_ref), (x_hbm, x_ref), (rg_hbm, rg_ref)], load)
    greet_all(s, f)
    loads[0].wait()
    reduce = SeqReduce(part, first, *scratch[:6])
    sums = ColSum(grad, h, *scratch[6:12])
    swap = RowExchange(h, got, *scratch[12:])

    def block(b):
        at = pl.ds(pl.multiple_of(b * rows, rows), rows)
        part[b] = dot(g_ref[at], qw_ref[...], 1, 1).astype(jnp.bfloat16)

    def block_at(j):
        far = j < 4
        zb = reduce.order(j % 4)
        block(2 * zb + jnp.where(far, 1 - y, y))

        @pl.when(far)
        def _():
            reduce.send(j)

    def qkv_grad(n):
        i = peer_at(s, 7 - n)
        at = row_at(i, 256)
        left = jnp.concatenate([a_ref[b, :, at] for b in range(8)], 0)
        grad[at] = dot(left, g_ref[...], 0, 0).astype(jnp.bfloat16)
        sums.send(i)

    def hand_over(k):
        sums.total(peer(s, k))
        if k:
            swap.piece(k).start()
        else:
            swap.mine.start()

    def message(k):
        i = (me + k) % 32
        return remote(msg.at[i // 2], inbox.at[k], msend.at[k], mrecv.at[k], dealer(i))

    def norm_backward():
        vec[0:2] = jnp.zeros((2, width), jnp.float32)
        vec[2:4] = vec_ref[0:2]
        gain = n_ref[0:1]
        loads[2].wait()
        loads[3].wait()

        @tall(rows)
        def _(r):
            normed, rstd = normalize(x_ref[r].astype(jnp.float32))
            inner, gain_part, shift_part = norm_back(first[r], normed, rstd, gain)
            ig_ref[r] = rg_ref[r] + inner
            vec[0:1] += gain_part[None]
            vec[1:2] += shift_part[None]

        lane = lax.broadcasted_iota(jnp.int32, (1, 128), 1)
        scalars = jnp.where(lane == 0, sum_ref[0:1], jnp.where(lane == 1, sum_ref[1:2], sum_ref[2:3]))
        for i in range(16):
            cols = slice(i * 128, i * 128 + 128)
            msg[i, 0:4] = vec[0:4, cols]
            msg[i, 4:5] = scalars
            at = (i % 2) * 128
            for n in range(3):
                piece = b_ref[0:1, n * w + at : n * w + at + 128]
                msg[i, 5 + n : 6 + n] = jnp.where(s == i // 2, piece, jnp.zeros_like(piece))

        @pl.loop(1, 32)
        def _(k):
            message(k).start()

    p = functools.partial
    ks = [7, 6, 5, 4, 3, 2, 1, 0]
    queues = dict(
        t=reduce.steps(),
        e=[lambda k=k: sums.step(peer(s, k)) for k in ks],
        h=[p(hand_over, k) for k in ks],
        z=[norm_backward],
        Z=[swap.finish],
    )
    pl.loop(0, 8)(block_at)
    loads[1].wait()
    left = looped(LAST_PLAN[0], "a", qkv_grad, queues)
    perform(LAST_PLAN[1], left)
    reduce.finish()
    sums.finish()
    total_ref[...] = msg[me // 2]

    @pl.loop(1, 32)
    def _(k):
        message(k).wait_recv()
        total_ref[...] += inbox[k]

    @pl.loop(1, 32)
    def _(k):
        message(k).wait_send()


def last(g, b, qkv_w, a, x, rg, norms, vec, sums, collective):
    rows, width = x.shape
    w3 = g.shape[1]
    pr = width // 32

    def out(shape, dtype=jnp.float32):
        return jax.ShapeDtypeStruct(shape, dtype)

    def vm(shape, dtype=jnp.bfloat16):
        return pltpu.VMEM(shape, dtype)

    return pl.pallas_call(
        last_kernel,
        out_shape=(out((rows, width)), out((8, pr, w3), jnp.bfloat16), out((8, 128))),
        in_specs=[VMEM_SPEC] * 5 + [HBM_SPEC] * 4,
        out_specs=(VMEM_SPEC, ANY_SPEC, VMEM_SPEC),
        scratch_shapes=[
            vm(qkv_w.shape),
            vm(a.shape),
            vm(x.shape),
            vm(rg.shape, jnp.float32),
            DMA((4,)),
            vm((8, rows, width)),
            vm((rows, width), jnp.float32),
            vm((width, w3)),
            vm((8, pr, w3)),
            vm((16, 8, 128), jnp.float32),
            vm((32, 8, 128), jnp.float32),
            vm((4, width), jnp.float32),
            DMA((32,)),
            DMA((32,)),
        ]
        + SeqReduce.scratch(rows, width)
        + ColSum.scratch(pr, w3)
        + RowExchange.scratch(),
        compiler_params=comm_params(collective),
    )(g, b, norms, vec, sums, qkv_w, a, x, rg)


def results_kernel(*refs):
    same, pieces, outs = refs[:4], refs[4:6], refs[6:13]
    bufs, wide, qkv, spread, load, store = refs[13:17], refs[17], refs[18], refs[19:22], refs[22], refs[23]
    moves = list(zip(same, bufs)) + [(pieces[0], wide), (pieces[1], qkv)]
    loads = fetch(moves, load)
    stores = [pltpu.make_async_copy(bufs[i], outs[i], store.at[i]) for i in range(4)]
    stores += [pltpu.make_async_copy(spread[i], outs[4 + i], store.at[4 + i]) for i in range(3)]
    for i in range(4):
        loads[i].wait()
        stores[i].start()
    loads[4].wait()
    lf = wide.shape[2] // 2
    for n in range(2):
        for i in range(8):
            value = wide[i, :, n * lf : n * lf + lf]
            spread[n][:, i * lf : i * lf + lf] = value.astype(jnp.float32)
        stores[4 + n].start()
    loads[5].wait()
    w = qkv.shape[2] // 3
    for i in range(8):
        for n in range(3):
            at = (n * 8 + i) * w
            spread[2][:, at : at + w] = qkv[i, :, n * w : n * w + w].astype(jnp.float32)
    stores[6].start()
    for copy in stores:
        copy.wait()


def results(same, wide, qkv):
    part = wide.shape[1]
    spread = [(part, 4 * wide.shape[2])] * 2 + [(part, 8 * qkv.shape[2])]
    return pl.pallas_call(
        results_kernel,
        out_shape=[jax.ShapeDtypeStruct(v.shape, v.dtype) for v in same]
        + [jax.ShapeDtypeStruct(v, jnp.float32) for v in spread],
        in_specs=[HBM_SPEC] * 6,
        out_specs=[ANY_SPEC] * 7,
        scratch_shapes=[pltpu.VMEM(v.shape, v.dtype) for v in (*same, wide, qkv)]
        + [pltpu.VMEM(v, jnp.float32) for v in spread]
        + [DMA((6,)), DMA((7,))],
        compiler_params=pltpu.CompilerParams(vmem_limit_bytes=63 << 20),
    )(*same, wide, qkv)


def line_body(
    hidden_in,
    ln1_gain,
    ln1_bias,
    qkv_weight,
    qkv_bias,
    out_weight,
    ln2_gain,
    ln2_bias,
    gate_weight,
    up_weight,
    down_weight,
    seq_lengths,
    deal_order,
    out_grad,
):
    rows = hidden_in.shape[1]
    width = hidden_in.shape[2]
    nseq = lax.axis_size("seq")
    nfsdp = lax.axis_size("fsdp")
    lw = width // nseq
    part = qkv_weight.shape[0]
    ff = gate_weight.shape[1]
    lf = ff // nseq
    seq_at, fsdp_at = lax.axis_index("seq"), lax.axis_index("fsdp")
    order = deal_order[0]
    group_rows = order.shape[0]
    valid_rows = group_rows * 5 // 8
    orow, ocol = order[None, :], order[:, None]
    lane = jnp.arange(128, dtype=jnp.int32) % HEAD_DIM % (ROT // 2)
    freq = 10000.0 ** (-2.0 * lane.astype(jnp.float32) / ROT)
    freq = freq[None, :]
    params = jnp.stack([ln1_gain, ln1_bias, ln2_gain, ln2_bias, *qkv_bias])
    params = jnp.pad(params.astype(jnp.float32), ((0, 1), (0, 64)))
    params = jnp.where(fsdp_at % 2 == 0, params, jnp.roll(params, part, 1))
    (
        first_in,
        qkv_w,
        norms,
        out_rows,
        packed,
        lse,
        mlp_grad,
        wide_w,
        down_w,
        mixed,
        attn,
        resid,
        second,
    ) = forward(
        hidden_in[0],
        params,
        qkv_weight,
        out_weight,
        out_grad[0],
        gate_weight,
        up_weight,
        down_weight,
        freq,
        orow,
        ocol,
        seq_lengths,
        valid_rows,
        1,
    )
    resid_grad, norm2_grads, mlp_part, down_part, wide_sum = middle(
        second, norms, wide_w, down_w.reshape(lf, width), mlp_grad, resid, 3
    )
    qkv_act, bias_sums, result, sums, wide_pieces, down_grad, out_grad_w = backward(
        resid_grad,
        freq,
        orow,
        ocol,
        seq_lengths,
        out_rows,
        mixed.reshape(group_rows, lw),
        packed,
        lse,
        attn,
        resid,
        mlp_part,
        down_part.reshape(nfsdp, -1, width),
        wide_sum,
        4,
    )
    input_grad, qkv_pieces, total = last(
        qkv_act, bias_sums, qkv_w, first_in, hidden_in[0], resid_grad, norms, norm2_grads, sums, 5
    )
    result, input_grad, down_grad, out_grad_w, gate_grad, up_grad, qkv_grad = results(
        (result, input_grad, down_grad, out_grad_w), wide_pieces, qkv_pieces
    )
    count = valid_rows * nfsdp * width
    rms = jnp.sqrt(total[4, :3] / count)
    halves = lax.dynamic_slice_in_dim(total, (fsdp_at % 2) * part, part, 1)
    shards = halves[:4]
    qkv_bias_grad = halves[5:8]
    return (
        result[None],
        input_grad[None],
        shards[0],
        shards[1],
        qkv_grad,
        qkv_bias_grad,
        out_grad_w,
        shards[2],
        shards[3],
        gate_grad,
        up_grad,
        down_grad,
        rms,
    )


def solution(mesh):
    in_specs = (
        P("fsdp", "seq", None),
        P(("seq", "fsdp")),
        P(("seq", "fsdp")),
        P(("seq", "fsdp"), None),
        P(None, ("seq", "fsdp")),
        P(("seq", "fsdp"), None),
        P(("seq", "fsdp")),
        P(("seq", "fsdp")),
        P(("seq", "fsdp"), None),
        P(("seq", "fsdp"), None),
        P(("seq", "fsdp"), None),
        P("fsdp", None),
        P("fsdp", None),
        P("fsdp", "seq", None),
    )
    out_specs = (
        P("fsdp", "seq", None),
        P("fsdp", "seq", None),
        P(("seq", "fsdp")),
        P(("seq", "fsdp")),
        P(("seq", "fsdp"), None),
        P(None, ("seq", "fsdp")),
        P(("seq", "fsdp"), None),
        P(("seq", "fsdp")),
        P(("seq", "fsdp")),
        P(("seq", "fsdp"), None),
        P(("seq", "fsdp"), None),
        P(("seq", "fsdp"), None),
        P(),
    )
    line = dict(mesh.shape) == {"seq": 8, "fsdp": 4}
    return jax.shard_map(
        line_body if line else body,
        mesh=mesh,
        in_specs=in_specs,
        out_specs=out_specs,
        check_vma=False,
    )
```
